32 devices in a mesh: dp: 8 (over y, x, core), tensor: 4 (over z).
Axes of the slice: x: 2, y: 2, z: 4, core: 2. Of those that a mesh axis runs over, the one named last changes fastest.
Arguments:
- tokens: bfloat16 [4096, 2048], P(('dp', 'tensor')), may hold values from -6 to 6
- cotangent: bfloat16 [4096, 2048], P(('dp', 'tensor')), may hold values from -6 to 6
- lengths: int32 [8, 2], P('dp'), may hold values from 1 to 384, 512 in all within a row
- seq_order: int32 [8, 512], P('dp'), may hold values from 0 to 511, each once within a row
- routes: int32 [4096, 8], P(('dp', 'tensor')), may hold values from 0 to 63, all different within a row; in each aligned block of 128 rows (0 to 127, 128 to 255, ...) at most 18 rows name the same one
- attn_gain: bfloat16 [2048], P('dp'), may hold values from 0.099609375 to 1.8984375
- w_query: bfloat16 [2048, 2048], P('dp', 'tensor'), may hold values from -0.125 to 0.125
- w_key: bfloat16 [2048, 2048], P('dp', 'tensor'), may hold values from -0.125 to 0.125
- w_value: bfloat16 [2048, 2048], P('dp', 'tensor'), may hold values from -0.125 to 0.125
- w_output: bfloat16 [2048, 2048], P('tensor', 'dp'), may hold values from -0.5 to 0.5
- query_gain: bfloat16 [128], P('dp'), may hold values from 1 to 1.796875
- key_gain: bfloat16 [128], P('dp'), may hold values from 1 to 1.796875
- ffn_gain: bfloat16 [2048], P('dp'), may hold values from 0.099609375 to 1.8984375
- router: bfloat16 [2048, 64], P('dp'), may hold values from -0.0625 to 0.0625
- w_gate: bfloat16 [64, 2048, 1024], P('dp', None, 'tensor'), may hold values from -0.125 to 0.125
- w_up: bfloat16 [64, 2048, 1024], P('dp', None, 'tensor'), may hold values from -0.125 to 0.125
- w_down: bfloat16 [64, 1024, 2048], P('dp', 'tensor'), may hold values from -0.75 to 0.75
Outputs:
- layer_out: bfloat16 [4096, 2048], P(('dp', 'tensor'))
- grad_tokens: float32 [4096, 2048], P(('dp', 'tensor'))
- grad_attn_gain: float32 [2048], P('dp')
- grad_w_query: float32 [2048, 2048], P('dp', 'tensor')
- grad_w_key: float32 [2048, 2048], P('dp', 'tensor')
- grad_w_value: float32 [2048, 2048], P('dp', 'tensor')
- grad_w_output: float32 [2048, 2048], P('tensor', 'dp')
- grad_query_gain: float32 [128], P('dp')
- grad_key_gain: float32 [128], P('dp')
- grad_ffn_gain: float32 [2048], P('dp')
- grad_router: float32 [2048, 64], P('dp')
- grad_w_gate: float32 [64, 2048, 1024], P('dp', None, 'tensor')
- grad_w_up: float32 [64, 2048, 1024], P('dp', None, 'tensor')
- grad_w_down: float32 [64, 1024, 2048], P('dp', 'tensor')
- rms_stats: float32 [8, 3], P('dp')
The draws below stay inside these ranges and needn't reach their ends.
Inputs may be any that keep to these rules, and one draw needn't show every extreme that they name: Each group's lengths sum to 512, and none is longer than 384. `seq_order`: each row holds every number of 0 to 511 once. `routes`: each row names 8 different experts. Among the rows of one device (aligned blocks of 128 rows) no expert is named more than 18 times, and in every draw some expert is named exactly 18 times by the rows of some device.
All inputs are finite; a program needn't handle non-finite values.
Results may differ from the reference program's by a relative error of at most 0.024.
Values may be sent and summed in bfloat16 or wider, within the bound.
A program may use at most 512 MiB of HBM per device.

```python
import math
import jax
import jax.numpy as jnp
import numpy as np
from jax import lax

D = 2048
HEADS = 16
HD = 128
EXPERTS = 64
FF = 1024
TOPK = 8
TOK_DEV = 128
SEQS = 2
GROUP_TOK = 512
GROUPS = 8
TOKENS = 4096
MAXLEN = 384
CAP = 18


def draw_tokens(key, part):
    first_key = jax.random.fold_in(key, 0)
    within = (jnp.arange(TOKENS, dtype=jnp.int32) % GROUP_TOK).astype(jnp.float32)
    row_scale = 0.5 + within / GROUP_TOK
    base_draw = jax.random.truncated_normal(first_key, -4.0, 4.0, (TOKENS, D), jnp.float32)
    return (base_draw * row_scale[:, None]).astype(jnp.bfloat16)


def levels(own_key, dims, pieces, least, high):
    gain, own = 1.0, jax.random.fold_in(own_key, 6)
    for dim, blocks in pieces:
        steps = jnp.exp(jax.random.uniform(jax.random.fold_in(own, dim), (blocks,), jnp.float32, least / len(pieces), high / len(pieces)))
        gain = gain * jnp.repeat(steps, dims[dim] // blocks).reshape([-1 if axis == dim else 1 for axis in range(len(dims))])
    return gain


def length_profile(number_of, total, bound, lean):
    portions = [(1 << 20) // math.isqrt(standing ** lean) + 1 for standing in range(2, number_of + 1)]
    spare, holding = total - bound - (number_of - 1), [1] * (number_of - 1)
    while spare > 0:
        movable = [i for i in range(number_of - 1) if holding[i] < bound]
        whole, remaining = sum([portions[i] for i in movable]), spare
        for i in movable:
            extra = min(bound - holding[i], max(1, remaining * portions[i] // whole), spare)
            holding[i] = holding[i] + extra
            spare = spare - extra
    return np.array([bound] + holding)


def uneven(rng, number_of, total, reach, skew):
    if number_of == 2:
        one = jax.random.randint(rng, (), max(1, total - reach), min(reach, total - 1) + 1)
        return jnp.stack([one, total - one])
    sizes = jnp.asarray(length_profile(number_of, total, reach, skew), jnp.int32)
    twos = (number_of - 1) // 2
    donor, receiver = sizes[1:1 + 2 * twos:2], sizes[2:2 + 2 * twos:2]
    room = jnp.minimum(donor - 1, reach - receiver)
    shifted = jax.random.randint(jax.random.fold_in(rng, 1), (twos,), 0, 1 << 20) % (room + 1)
    sizes = sizes.at[1:1 + 2 * twos:2].set(donor - shifted).at[2:2 + 2 * twos:2].set(receiver + shifted)
    return sizes[jax.random.permutation(jax.random.fold_in(rng, 2), number_of)]


def shared_out(key, own, number, rows, amount, top, reach, skew):
    sequence = jax.random.permutation(key, amount)
    packed, usual = portions_of(amount, rows * top, reach, skew, True), portions_of(amount, rows * top, reach, skew, False)
    places = jnp.arange(amount)

    def named(tallies, offset_by):
        used = int((tallies > 0).sum())
        fixed = max(1, used // 4)
        passed = fixed + (places - fixed + offset_by * (used - fixed)) % max(1, amount - fixed)
        return jnp.zeros((amount,), jnp.int32).at[sequence[jnp.where(places < fixed, places, passed)]].set(jnp.asarray(tallies, jnp.int32))

    tallies = jnp.where(number % 4 == 0, named(packed, number // 4), named(usual, number - number // 4 - 1))
    mixed = jax.random.permutation(jax.random.fold_in(own, 3), amount)
    source_of, taker = mixed[0:amount // 2 * 2:2], mixed[1:amount // 2 * 2:2]
    slack = jnp.minimum(tallies[source_of] - 1, reach - tallies[taker]) // 2
    slack = jnp.where((source_of == sequence[0]) | (taker == sequence[0]) | (tallies[taker] == 0), 0, jnp.maximum(slack, 0))
    passed = jax.random.randint(jax.random.fold_in(own, 4), (amount // 2,), 0, 1 << 20) % (slack + 1)
    tallies = tallies.at[source_of].add(-passed).at[taker].add(passed)
    members = jnp.searchsorted(jnp.cumsum(tallies), jnp.arange(rows * top), side="right").astype(jnp.int32)
    grid = members.reshape(top, rows).T
    grid = grid[jax.random.permutation(jax.random.fold_in(own, 1), rows)]
    offset_by = jax.random.randint(jax.random.fold_in(own, 2), (rows, 1), 0, top)
    return jnp.take_along_axis(grid, (jnp.arange(top)[None, :] + offset_by) % top, axis=1)


def portions_of(number_of, total, limit, skew, full):
    weights = [(1 << 20) // math.isqrt(standing ** skew) + 1 for standing in range(1, number_of + 1)]
    largest = limit if full else min(limit, max(-(-total // number_of), total * weights[0] // sum(weights)))
    least = 1 if total - largest >= number_of - 1 else 0
    holding, rest = [largest] + [least] * (number_of - 1), total - largest - least * (number_of - 1)
    while rest > 0:
        movable = [i for i in range(1, number_of) if holding[i] < largest] or [i for i in range(1, number_of) if holding[i] < limit]
        pool, left = sum([weights[i] for i in movable]), rest
        for i in movable:
            more = min(limit - holding[i], max(1, left * weights[i] // pool), rest)
            holding[i] = holding[i] + more
            rest = rest - more
    return np.array(holding)


def gaussian(rng, extent, spread, limit, cuts=(), held_as=jnp.bfloat16):
    values = jax.random.normal(rng, extent, jnp.float32) * spread
    if len(cuts) > 0:
        values = levels(rng, extent, cuts, -0.22, 0.18) * values
    return jnp.clip(values, min=-limit, max=limit).astype(held_as)


def setup_inputs(seed: int = 0) -> dict:
    splits = jax.random.split(jax.random.key(seed), 18)
    tokens = draw_tokens(jax.random.fold_in(splits[17], 71), 0)
    cotangent = gaussian(splits[1], (TOKENS, D), 1.0, 6.0, ((0, 32),))
    lengths = jax.vmap(lambda own: uneven(own, SEQS, GROUP_TOK, MAXLEN, 2))(jax.random.split(splits[2], GROUPS)).reshape((GROUPS, SEQS)).astype(jnp.int32)
    seq_order = jax.vmap(lambda own: jax.random.permutation(own, GROUP_TOK))(jax.random.split(splits[3], GROUPS)).reshape((GROUPS, GROUP_TOK)).astype(jnp.int32)
    routes_keys = jax.random.split(jax.random.fold_in(splits[4], 1), TOKENS // TOK_DEV)
    routes_turns = jax.random.permutation(jax.random.fold_in(splits[4], 3), TOKENS // TOK_DEV)
    routes = jax.vmap(lambda own, number: shared_out(jax.random.fold_in(splits[4], 2), own, number, TOK_DEV, EXPERTS, TOPK, CAP, 1))(routes_keys, routes_turns).reshape((TOKENS, TOPK))
    attn_gain = jnp.clip(1.0 + 0.18 * jax.random.normal(splits[5], (D,), jnp.float32), 0.099609375, 1.8984375).astype(jnp.bfloat16)
    w_query = gaussian(splits[6], (D, D), D ** -0.5, 0.125, ((0, 8), (1, 4)))
    w_key = gaussian(splits[7], (D, D), D ** -0.5, 0.125, ((0, 8), (1, 4)))
    w_value = gaussian(splits[8], (D, D), D ** -0.5, 0.125, ((0, 8), (1, 4)))
    w_output = gaussian(splits[9], (D, D), (D // 16) ** -0.5, 0.5, ((0, 4), (1, 8)))
    query_gain = jnp.clip(1.0 + 0.796875 * jax.random.uniform(splits[10], (HD,), jnp.float32) ** levels(splits[10], (HD,), ((0, 8),), -0.2, 0.2), 1.0, 1.796875).astype(jnp.bfloat16)
    key_gain = jnp.clip(1.0 + 0.796875 * jax.random.uniform(splits[11], (HD,), jnp.float32) ** levels(splits[11], (HD,), ((0, 8),), -0.2, 0.2), 1.0, 1.796875).astype(jnp.bfloat16)
    ffn_gain = jnp.clip(1.0 + 0.18 * jax.random.normal(splits[12], (D,), jnp.float32), 0.099609375, 1.8984375).astype(jnp.bfloat16)
    router = gaussian(splits[13], (D, EXPERTS), (4 * D) ** -0.5, 0.0625, ((0, 8),))
    w_gate = gaussian(splits[14], (EXPERTS, D, FF), D ** -0.5, 0.125, ((0, 8), (2, 4)))
    w_up = gaussian(splits[15], (EXPERTS, D, FF), D ** -0.5, 0.125, ((0, 8), (2, 4)))
    w_down = gaussian(splits[16], (EXPERTS, FF, D), (FF // 16) ** -0.5, 0.75, ((0, 8), (1, 4)))
    return {"tokens": tokens, "cotangent": cotangent, "lengths": lengths, "seq_order": seq_order, "routes": routes, "attn_gain": attn_gain, "w_query": w_query, "w_key": w_key, "w_value": w_value, "w_output": w_output, "query_gain": query_gain, "key_gain": key_gain, "ffn_gain": ffn_gain, "router": router, "w_gate": w_gate, "w_up": w_up, "w_down": w_down}


EPSILON = 1e-05
THETA = 10000.0
NEGATIVE = -1e+30
PRECISE = lax.Precision.HIGHEST

@jax.custom_vjp
def low(v):
    return lax.optimization_barrier(v.astype(jnp.bfloat16)).astype(jnp.float32)

@jax.custom_vjp
def low_back(v):
    return v

def low_keep(v):
    return (low(v), None)

def low_pass(kept, grad):
    return (grad,)

def back_keep(v):
    return (v, None)

def back_low(kept, grad):
    return (low(grad),)
low.defvjp(low_keep, low_pass)
low_back.defvjp(back_keep, back_low)

def inv_rms(values):
    return lax.rsqrt(lax.optimization_barrier(jnp.mean(values * values, axis=-1, keepdims=True)) + EPSILON)

def norm_apply(values, scale_gain):
    return values * inv_rms(values) * scale_gain

def arrival_layout(seq_lengths, order_row):
    row_total = order_row.shape[0]
    placed = jnp.arange(row_total, dtype=jnp.int32)
    seq_ends = jnp.cumsum(seq_lengths).astype(jnp.int32)
    seq_starts = seq_ends - seq_lengths
    member = lax.optimization_barrier(jnp.sum((placed[:, None] >= seq_ends[None, :]).astype(jnp.int32), axis=1))
    chosen = member[:, None] == jnp.arange(seq_lengths.shape[0], dtype=jnp.int32)[None, :]
    seq_begin = lax.optimization_barrier(jnp.sum(jnp.where(chosen, seq_starts[None, :], 0), axis=1)).astype(jnp.int32)
    seq_ids = jnp.zeros((row_total,), jnp.int32).at[order_row].set(member)
    positions = jnp.zeros((row_total,), jnp.int32).at[order_row].set(placed - seq_begin)
    return (seq_ids, positions)

def rope_tables(positions):
    half_dim = HD // 2
    frequency = THETA ** (-jnp.arange(half_dim, dtype=jnp.float32) / half_dim)
    angles = positions.astype(jnp.float32)[:, None] * frequency[None, :]
    return (jnp.cos(angles)[:, None, :], jnp.sin(angles)[:, None, :])

def head_norm_rope(projected, head_gain, cosines, sines):
    shaped = projected.reshape(projected.shape[0], -1, HD)
    normed_heads = norm_apply(shaped, head_gain)
    first_half = normed_heads[..., :HD // 2]
    second_half = normed_heads[..., HD // 2:]
    return jnp.concatenate([first_half * cosines - second_half * sines, second_half * cosines + first_half * sines], axis=-1)

def attention_group(query, key_heads, value_heads, seq_ids):
    score_scale = HD ** (-0.5)
    raw_scores = jnp.einsum('qhd,khd->hqk', query, key_heads, precision=PRECISE) * score_scale
    same_seq = (seq_ids[:, None] == seq_ids[None, :])[None]
    scores = low_back(jnp.where(same_seq, raw_scores, NEGATIVE))
    row_peak = lax.optimization_barrier(jnp.max(scores, axis=-1, keepdims=True))
    raised = jnp.exp(scores - row_peak)
    probs = low(raised / lax.optimization_barrier(jnp.sum(raised, axis=-1, keepdims=True)))
    context = jnp.einsum('hqk,khd->qhd', probs, value_heads, precision=PRECISE)
    return low_back(low(context.reshape(context.shape[0], -1)))

def route_tables(routes):
    flat_routes = routes.reshape(-1)
    onehot = (flat_routes[:, None] == jnp.arange(EXPERTS, dtype=jnp.int32)[None, :]).astype(jnp.int32)
    blocked = onehot.reshape(-1, TOK_DEV * TOPK, EXPERTS)
    earlier = jnp.cumsum(blocked, axis=1) - blocked
    slot_of = lax.optimization_barrier(jnp.sum(earlier * blocked, axis=2)).reshape(-1).astype(jnp.int32)
    route_ids = jnp.arange(flat_routes.shape[0], dtype=jnp.int32)
    source = (route_ids // (TOK_DEV * TOPK)).astype(jnp.int32)
    tables = jnp.full((EXPERTS, TOKENS // TOK_DEV, CAP), -1, jnp.int32)
    tables = tables.at[flat_routes, source, slot_of].set(route_ids)
    return tables.reshape(EXPERTS, -1)

def layer_forward(tokens, attn_gain, w_query, w_key, w_value, w_output, query_gain, key_gain, ffn_gain, router, w_gate, w_up, w_down, seq_ids, positions, routes, tables):
    normed = low(norm_apply(tokens, attn_gain))
    proj_query = low_back(jnp.dot(normed, w_query, precision=PRECISE))
    proj_key = low_back(jnp.dot(normed, w_key, precision=PRECISE))
    value = low_back(low(jnp.dot(normed, w_value, precision=PRECISE)))
    cosines, sines = rope_tables(positions.reshape(-1))
    query = low(head_norm_rope(proj_query, query_gain, cosines, sines))
    key_heads = low(head_norm_rope(proj_key, key_gain, cosines, sines))
    shape_groups = (GROUPS, GROUP_TOK, HEADS, HD)
    group_fn = jax.checkpoint(attention_group)
    context = lax.map(lambda parts: group_fn(*parts), (query.reshape(shape_groups), key_heads.reshape(shape_groups), value.reshape(shape_groups), seq_ids))
    context = context.reshape(TOKENS, D)
    attn_out = low_back(jnp.dot(context, w_output, precision=PRECISE))
    resid_mid = tokens + attn_out
    moe_in = low(norm_apply(resid_mid, ffn_gain))
    logits = low_back(jnp.dot(moe_in, router, precision=PRECISE))
    picked = jnp.take_along_axis(logits, routes, axis=1)
    gate_peak = lax.optimization_barrier(jnp.max(picked, axis=1, keepdims=True))
    gate_raw = jnp.exp(picked - gate_peak)
    gates = gate_raw / lax.optimization_barrier(jnp.sum(gate_raw, axis=1, keepdims=True))
    gate_flat = gates.reshape(-1)

    def expert_rows(parts):
        route_ids, gate_matrix, up_matrix, down_matrix = parts
        valid = route_ids >= 0
        safe_ids = jnp.where(valid, route_ids, 0)
        token_ids = safe_ids // TOPK
        rows_in = low_back(jnp.where(valid[:, None], moe_in[token_ids], 0.0))
        gate_pre = low_back(jnp.dot(rows_in, gate_matrix, precision=PRECISE))
        up_pre = low_back(jnp.dot(rows_in, up_matrix, precision=PRECISE))
        hidden = low(jax.nn.silu(gate_pre) * up_pre)
        expert_out = low_back(low(jnp.dot(hidden, down_matrix, precision=PRECISE)))
        weight = jnp.where(valid, gate_flat[safe_ids], 0.0)
        return weight[:, None] * expert_out
    stacked = lax.map(jax.checkpoint(expert_rows), (tables, w_gate, w_up, w_down))
    token_all = (jnp.where(tables >= 0, tables, 0) // TOPK).reshape(-1)
    moe_out = jnp.zeros((TOKENS, D), jnp.float32).at[token_all].add(stacked.reshape(-1, D))
    layer_sum = resid_mid + moe_out

    def group_rms(values):
        return jnp.sqrt(lax.optimization_barrier(jnp.mean((values * values).reshape(GROUPS, -1), axis=1)))
    stats = jnp.stack([group_rms(resid_mid), group_rms(attn_out), group_rms(moe_out)], axis=1)
    return (layer_sum, stats)

def reference(tokens, cotangent, lengths, seq_order, routes, attn_gain, w_query, w_key, w_value, w_output, query_gain, key_gain, ffn_gain, router, w_gate, w_up, w_down):
    seq_ids, positions = jax.vmap(arrival_layout)(lengths, seq_order)
    tables = route_tables(routes)
    floats = tuple((param.astype(jnp.float32) for param in (tokens, attn_gain, w_query, w_key, w_value, w_output, query_gain, key_gain, ffn_gain, router, w_gate, w_up, w_down)))

    def forward(*params):
        return layer_forward(*params, seq_ids, positions, routes, tables)
    layer_sum, pullback, stats = jax.vjp(forward, *floats, has_aux=True)
    grads = pullback(cotangent.astype(jnp.float32))
    return (layer_sum.astype(jnp.bfloat16), grads[0], grads[1], grads[2], grads[3], grads[4], grads[5], grads[6], grads[7], grads[8], grads[9], grads[10], grads[11], grads[12], stats)
```

```python
import functools

import jax
import jax.numpy as jnp
from jax import lax
from jax.experimental import pallas as pl
from jax.experimental.pallas import tpu as pltpu
from jax.sharding import PartitionSpec as P

HD = 128
EXPERTS = 64
TOPK = 8
CAP = 18


EPSILON = 1e-05
THETA = 10000.0
NEGATIVE = -1e30


def inv_rms(values):
    return lax.rsqrt(jnp.mean(values * values, axis=-1, keepdims=True) + EPSILON)


def norm_apply(values, scale_gain):
    return values * inv_rms(values) * scale_gain


def arrival_layout(seq_lengths, order_row):
    row_total = order_row.shape[0]
    placed = jnp.arange(row_total, dtype=jnp.int32)
    order = jnp.arange(seq_lengths.shape[0], dtype=jnp.int32)
    upto = order[None, :] <= order[:, None]
    seq_ends = jnp.sum(jnp.where(upto, seq_lengths[None, :], 0), axis=1)
    seq_starts = seq_ends - seq_lengths
    member = jnp.sum((placed[:, None] >= seq_ends[None, :]).astype(jnp.int32), axis=1)
    chosen = member[:, None] == jnp.arange(seq_lengths.shape[0], dtype=jnp.int32)[None, :]
    seq_begin = jnp.sum(jnp.where(chosen, seq_starts[None, :], 0), axis=1)
    here = order_row[None, :] == placed[:, None]
    seq_ids = jnp.sum(jnp.where(here, member[None, :], 0), axis=1)
    positions = jnp.sum(jnp.where(here, (placed - seq_begin)[None, :], 0), axis=1)
    return (seq_ids, positions)


def rope_tables(positions):
    half_dim = HD // 2
    frequency = THETA ** (-jnp.arange(half_dim, dtype=jnp.float32) / half_dim)
    angles = positions.astype(jnp.float32)[:, None] * frequency[None, :]
    return (jnp.cos(angles)[:, None, :], jnp.sin(angles)[:, None, :])


def head_norm_rope(projected, head_gain, cosines, sines):
    shaped = projected.reshape(projected.shape[0], -1, HD)
    normed_heads = norm_apply(shaped, head_gain)
    first_half = normed_heads[..., : HD // 2]
    second_half = normed_heads[..., HD // 2 :]
    return jnp.concatenate(
        [first_half * cosines - second_half * sines, second_half * cosines + first_half * sines],
        axis=-1,
    )


def masked_scores(query_block, key_low, seq_block, seq_ids):
    score_scale = HD ** (-0.5)
    scores = (
        jnp.einsum("qhd,khd->hqk", query_block, key_low, preferred_element_type=jnp.float32)
        * score_scale
    )
    same_seq = (seq_block[:, None] == seq_ids[None, :])[None]
    return jnp.where(same_seq, scores, NEGATIVE)


def attend(query_low, key_low, value_low, seq_ids, block_rows):
    num_blocks = query_low.shape[0] // block_rows
    query_blocks = query_low.reshape(num_blocks, block_rows, query_low.shape[1], HD)
    seq_blocks = seq_ids.reshape(num_blocks, block_rows)

    def one_block(inputs):
        query_block, seq_block = inputs
        scores = masked_scores(query_block, key_low, seq_block, seq_ids)
        row_peak = jnp.max(scores, axis=-1, keepdims=True)
        raised = jnp.exp(scores - row_peak)
        row_total = jnp.sum(raised, axis=-1, keepdims=True)
        probs_low = (raised / row_total).astype(jnp.bfloat16)
        context = jnp.einsum(
            "hqk,khd->qhd", probs_low, value_low, preferred_element_type=jnp.float32
        )
        return (context, row_peak + jnp.log(row_total))

    context, row_lse = lax.map(one_block, (query_blocks, seq_blocks))
    return (context.reshape(query_low.shape), row_lse)


def attend_back(query_low, key_low, value_low, seq_ids, row_lse, grad_ctx_low, block_rows):
    score_scale = HD ** (-0.5)
    num_blocks = query_low.shape[0] // block_rows
    block_shape = (num_blocks, block_rows, query_low.shape[1], HD)

    def one_block(carry, inputs):
        grad_key_sum, grad_value_sum = carry
        query_block, seq_block, lse_block, grad_block = inputs
        scores = masked_scores(query_block, key_low, seq_block, seq_ids)
        probs = jnp.exp(scores - lse_block)
        probs_low = probs.astype(jnp.bfloat16)
        grad_value_sum = grad_value_sum + jnp.einsum(
            "hqk,qhd->khd", probs_low, grad_block, preferred_element_type=jnp.float32
        )
        grad_probs = jnp.einsum(
            "qhd,khd->hqk", grad_block, value_low, preferred_element_type=jnp.float32
        )
        inner_sum = jnp.sum(probs * grad_probs, axis=-1, keepdims=True)
        grad_scores = (probs * (grad_probs - inner_sum)).astype(jnp.bfloat16)
        grad_query_block = (
            jnp.einsum("hqk,khd->qhd", grad_scores, key_low, preferred_element_type=jnp.float32)
            * score_scale
        )
        grad_key_sum = (
            grad_key_sum
            + jnp.einsum(
                "hqk,qhd->khd", grad_scores, query_block, preferred_element_type=jnp.float32
            )
            * score_scale
        )
        return ((grad_key_sum, grad_value_sum), grad_query_block)

    zeros_heads = jnp.zeros(query_low.shape, jnp.float32)
    carried, grad_query = lax.scan(
        one_block,
        (zeros_heads, zeros_heads),
        (
            query_low.reshape(block_shape),
            seq_ids.reshape(num_blocks, block_rows),
            row_lse,
            grad_ctx_low.reshape(block_shape),
        ),
    )
    return (grad_query.reshape(query_low.shape), carried[0], carried[1])


MESH = pl.DeviceIdType.MESH
VMEM_LIMIT = 60 * 1024 * 1024
MAIN = 16
SPARE = CAP - MAIN


def at(dp_index, z_index):
    return {"dp": dp_index, "tensor": z_index}


def place():
    dp = lax.axis_index("dp")
    z = lax.axis_index("tensor")
    core, x, y = dp % 2, (dp // 2) % 2, dp // 4
    return dp, z, 1 - 2 * core, 2 - 4 * x, 4 - 8 * y


def greet(peers, extra=None, has_extra=None, count=0):
    barrier = pltpu.get_barrier_semaphore()
    for peer in peers:
        pl.semaphore_signal(barrier, inc=1, device_id=at(*peer), device_id_type=MESH)
    if extra is not None:

        @pl.when(has_extra)
        def _():
            pl.semaphore_signal(barrier, inc=1, device_id=at(*extra), device_id_type=MESH)

    pl.semaphore_wait(barrier, len(peers) + count)


def when_or_now(cond, action):
    if cond is None:
        action()
    else:
        pl.when(cond)(action)


def slot_matrix(routes_block, source, first_expert):
    experts = lax.broadcasted_iota(jnp.int32, (8, 128), 0) + first_expert
    member = jnp.zeros((8, 128), jnp.float32)
    for j in range(TOPK):
        member = member + (routes_block[j : j + 1, :] == experts.astype(jnp.float32)).astype(jnp.float32)
    earlier = (
        lax.broadcasted_iota(jnp.int32, (128, 128), 0)
        < lax.broadcasted_iota(jnp.int32, (128, 128), 1)
    ).astype(jnp.bfloat16)
    rank = jnp.dot(member.astype(jnp.bfloat16), earlier, preferred_element_type=jnp.float32)
    rank = jnp.where(member > 0.5, rank, -1.0).astype(jnp.int32)
    spread = jnp.broadcast_to(rank[:, None, :], (8, MAIN, 128)).reshape(128, 128)
    row = lax.broadcasted_iota(jnp.int32, (128, 128), 0) % MAIN
    main = spread == row
    spare = jnp.logical_and(row // SPARE == source % 8, spread == MAIN + row % SPARE)
    return jnp.concatenate(
        [main.astype(jnp.float32), spare.astype(jnp.float32)], axis=0
    ).astype(jnp.bfloat16)


class LineScatter:
    def __init__(self, dp, z, blocks, rze, rzm, rzf, zsend, zrecv):
        self.dp, self.z = dp, z
        self.zr, self.zo = z + 1 - 2 * (z % 2), 3 - z
        self.mid, self.end = z * (3 - z) > 0, z * (3 - z) < 1
        self.zs = [3 - 3 * (z // 2), 2 - z // 2, self.zr, z]
        self.blocks, self.rze, self.rzm, self.rzf = blocks, rze, rzm, rzf
        self.zsend, self.zrecv = zsend, zrecv
        self.outward = [self.copy(blocks.at[k], rze.at[k], k, self.zr) for k in range(3)]
        self.sends = []

    def copy(self, src, dst, index, z_to):
        return pltpu.make_async_remote_copy(
            src, dst, self.zsend.at[index], self.zrecv.at[index],
            device_id=at(self.dp, z_to), device_id_type=MESH,
        )

    def ready(self, k):
        pl.when(self.end)(functools.partial(self.outward[k].start))
        self.sends.append((self.outward[k], self.end))

    def add(self, k, part):
        total = self.blocks[k].astype(jnp.float32) + part[...].astype(jnp.float32)
        self.blocks[k] = total.astype(jnp.bfloat16)

    def onward(self, k):
        if k < 2:
            copy = self.copy(self.blocks.at[k], self.rzm.at[k], 3 + k, self.zo)
        else:
            copy = self.copy(self.blocks.at[k], self.rzf, 5, self.zr)
        self.sends.append((copy, self.mid))

        @pl.when(self.mid)
        def _():
            if k < 2:
                self.outward[k].wait_recv()
                self.add(k, self.rze.at[k])
            else:
                self.copy(self.blocks.at[0], self.rzm.at[0], 3, self.zo).wait_recv()
                self.add(k, self.rzm.at[0])
            copy.start()

    def last(self, out_ref):
        @pl.when(self.end)
        def _():
            self.copy(self.blocks.at[2], self.rzf, 5, self.zr).wait_recv()
            out_ref[...] = out_ref[...] + self.rzf[...].astype(jnp.float32)

        @pl.when(self.mid)
        def _():
            self.outward[2].wait_recv()
            self.copy(self.blocks.at[1], self.rzm.at[1], 4, self.zo).wait_recv()
            out_ref[...] = (
                out_ref[...]
                + self.rze[2].astype(jnp.float32)
                + self.rzm[1].astype(jnp.float32)
            )

    def drain(self):
        for copy, cond in self.sends:
            pl.when(cond)(functools.partial(copy.wait_send))

    @staticmethod
    def scratch(width):
        low, dma = jnp.bfloat16, pltpu.SemaphoreType.DMA
        return [
            pltpu.VMEM((3, 128, width), low),
            pltpu.VMEM((3, 128, width), low),
            pltpu.VMEM((2, 128, width), low),
            pltpu.VMEM((128, width), low),
            dma((6,)),
            dma((6,)),
        ]


class AllGather:
    def __init__(self, held, own_ref, ssem, rsem, metas=None, own_meta=None, msem=None, mrsem=None):
        self.dp, self.z, self.dc, self.dx, self.dy = place()
        z = self.z
        self.zr, self.zo = z + 1 - 2 * (z % 2), 3 - z
        self.mid = z * (3 - z) > 0
        self.zs = [z, self.zr, 2 - z // 2, 3 - 3 * (z // 2)]
        self.held, self.own_ref, self.ssem, self.rsem = held, own_ref, ssem, rsem
        self.metas, self.own_meta, self.msem, self.mrsem = metas, own_meta, msem, mrsem
        self.sends = []

    def send(self, block, part, dp_to, z_to, cond=None, own=False):
        half = pl.ds(part * 64, 64)
        view = self.held.at[block, half]
        source = self.own_ref.at[half] if own else view
        index = len(self.sends)
        copies = [
            pltpu.make_async_remote_copy(
                source, view, self.ssem.at[index], self.rsem.at[block, part],
                device_id=at(dp_to, z_to), device_id_type=MESH,
            )
        ]
        if part == 0 and self.metas is not None:
            copies.append(
                pltpu.make_async_remote_copy(
                    self.own_meta if own else self.metas.at[block], self.metas.at[block],
                    self.msem.at[index], self.mrsem.at[block],
                    device_id=at(dp_to, z_to), device_id_type=MESH,
                )
            )
        self.sends.append((copies, cond))

        def go():
            for copy in copies:
                copy.start()

        when_or_now(cond, go)

    def arrive(self, block, part):
        view = self.held.at[block, pl.ds(part * 64, 64)]
        here = dict(device_id=at(self.dp, self.zr), device_id_type=MESH)
        pltpu.make_async_remote_copy(
            view, view, self.ssem.at[0], self.rsem.at[block, part], **here
        ).wait_recv()
        if part == 0 and self.metas is not None:
            pltpu.make_async_remote_copy(
                self.metas.at[block], self.metas.at[block], self.msem.at[0], self.mrsem.at[block],
                **here
            ).wait_recv()

    def first(self, k):
        dp, z, dx, dy, dc = self.dp, self.z, self.dx, self.dy, self.dc
        block = dp * 4 + self.zs[k]
        own = k == 0
        for part in (0, 1):
            if k > 0:
                self.arrive(block, part)
            if k == 0:
                self.send(block, part, dp, self.zr, None, own)
                self.send(block, part, dp, self.zo, self.mid, own)
            else:
                self.send(block, part, dp, self.zo if k == 1 else self.zr, self.mid)
            self.send(block, part, dp + (dx if part == 0 else dy), z, None, own)
        self.send(block, 1, dp + dx, z, None, own)
        self.send(block, 0, dp + dy, z, None, own)
        self.send(block, 0, dp + dc, z, None, own)
        self.send(block, 1, dp + dc, z, None, own)

    def second(self, k):
        dp, z, dx, dy, dc = self.dp, self.z, self.dx, self.dy, self.dc
        bx, by = (dp + dx) * 4 + self.zs[k], (dp + dy) * 4 + self.zs[k]
        self.arrive(bx, 0)
        self.send(bx, 0, dp + dy, z)
        self.send(bx, 0, dp + dc, z)
        self.arrive(by, 1)
        self.send(by, 1, dp + dx, z)
        self.send(by, 1, dp + dc, z)
        self.arrive(bx, 1)
        self.send(bx, 1, dp + dc, z)
        self.arrive(by, 0)
        self.send(by, 0, dp + dc, z)

    def third(self, k):
        block = (self.dp + self.dx + self.dy) * 4 + self.zs[k]
        for part in (0, 1):
            self.arrive(block, part)
            self.send(block, part, self.dp + self.dc, self.z)

    def across(self, k, step):
        block = (self.dp + self.dc + step) * 4 + self.zs[k]
        self.arrive(block, 0)
        self.arrive(block, 1)

    def drain(self):
        for copies, cond in self.sends:

            def done(copies=copies):
                for copy in copies:
                    copy.wait_send()

            when_or_now(cond, done)


class Dispatcher:
    def __init__(self, held, stage, spare, slots_ref, osem):
        self.held, self.stage, self.spare = held, stage, spare
        self.slots_ref, self.osem = slots_ref, osem
        self.count = 0

    def put(self, start, slot):
        return pltpu.make_async_copy(
            self.stage.at[slot], self.slots_ref.at[:, pl.ds(start, MAIN), :], self.osem.at[slot]
        )

    def block(self, block, onehot):
        slot, group = self.count % 2, block // 8
        width = self.held.shape[2]
        if self.count >= 2:
            self.put(block * MAIN, slot).wait()

        def tile(step, carry):
            lanes = pl.ds(pl.multiple_of(step * 512, 512), 512)
            rows = jnp.dot(onehot, self.held[block, :, lanes], preferred_element_type=jnp.float32)
            self.stage[slot, :, :, lanes] = rows[:128].astype(jnp.bfloat16).reshape(8, MAIN, 512)
            extra = rows[128:].astype(jnp.bfloat16)
            self.spare[group, :, lanes] = self.spare[group, :, lanes] + extra
            return carry

        lax.fori_loop(0, width // 512, tile, 0)
        self.put(block * MAIN, slot).start()
        self.count += 1

    def end(self):
        width = self.held.shape[2]
        for group in range(4):
            slot = group % 2
            self.put(512 + group * MAIN, slot).wait()
            self.stage[slot] = self.spare[group].reshape(8, MAIN, width)
            self.put(512 + group * MAIN, slot).start()
        for slot in range(2):
            self.put(512, slot).wait()


def arrival_order(gather):
    dp, dc, dx, dy, zs = gather.dp, gather.dc, gather.dx, gather.dy, gather.zs
    order = []
    for k in range(6):
        column = []
        if k < 4:
            column.append((k, 0))
        if 1 <= k < 5:
            column += [(k - 1, dx), (k - 1, dy)]
        if k >= 2:
            column.append((k - 2, dx + dy))
        across = [(k - 1, dc)] if 1 <= k < 5 else []
        if k >= 2:
            across += [(k - 2, dc + step) for step in (dx, dy, dx + dy)]
        order.append([[(dp + to) * 4 + zs[j] for j, to in part] for part in (column, across)])
    return order


def gather_step(gather, order, k, process):
    if k < 4:
        gather.first(k)
    if 1 <= k < 5:
        gather.second(k - 1)
    if k >= 2:
        gather.third(k - 2)
    for block in order[k][0]:
        process(block)
    for block in order[k][1]:
        gather.arrive(block, 0)
        gather.arrive(block, 1)
        process(block)


def rotate(values, cosines, sines):
    return values * cosines + pltpu.roll(values, HD // 2, 1) * sines


def head_probs(query, key, seq_column, seq_row):
    scores = lax.dot_general(
        query, key, (((1,), (1,)), ((), ())), preferred_element_type=jnp.float32
    ) * (HD ** (-0.5))
    scores = jnp.where(seq_column == seq_row, scores, NEGATIVE)
    raised = jnp.exp(scores - jnp.max(scores, axis=1, keepdims=True))
    return raised / jnp.sum(raised, axis=1, keepdims=True)


def head_gain(gains_ref, first):
    lane = lax.broadcasted_iota(jnp.int32, (8, 128), 1)
    keep = jnp.logical_and(lane >= first, lane < first + 16)
    total = jnp.zeros((8, 128), jnp.float32)
    for block in range(8):
        part = jnp.where(keep, jnp.broadcast_to(gains_ref[block, 4:5, :], (8, 128)), 0.0)
        shift = (16 * block - first) % 128
        total = total + (pltpu.roll(part, shift, 1) if shift else part)
    return total[:1]


def front_kernel(
    wq_ref, wk_ref, wv_ref, wo_ref, router_ref, tok_ref, cot_ref, routes_in, gains_in, cos_ref, sin_ref, seqc_ref, seqr_ref,
    weights_ref, group_ref, slots_ref, gains_ref, onehot_ref, routes_ref, normed_ref, projq_ref, projk_ref,
    query_ref, key_ref, value_ref, ctx_ref, out_ref,
    wheld, theld, gheld, held, metas, stage, spare, lsem, wsend, wrecv, gsend, grecv, zsend, zrecv,
    dsend, drecv, msend, mrecv, osem, fsem, *line_refs
):
    dp, z, dc, dx, dy = place()
    zr, zo = z + 1 - 2 * (z % 2), 3 - z
    mid = z * (3 - z) > 0
    f32, low = jnp.float32, jnp.bfloat16
    heads = query_ref.shape[1]
    width = tok_ref.shape[1]
    line = LineScatter(dp, z, *line_refs)
    gather = AllGather(held, cot_ref, dsend, drecv, metas, routes_in, msend, mrecv)
    order = arrival_order(gather)
    picker = Dispatcher(held, stage, spare, slots_ref, osem)
    own_block = dp * 4 + z
    own_rows = pl.ds(pl.multiple_of(dp * 256, 256), 256)
    fill = []
    for source, column, count in (
        (wq_ref, 0, heads), (wk_ref, heads, heads), (wv_ref, 2 * heads, heads),
        (wo_ref.at[pl.ds(0, 256)], 3 * heads, 256), (wo_ref.at[pl.ds(256, 256)], 3 * heads + 256, 256),
        (router_ref, 4 * heads, 128),
    ):
        target = wheld.at[own_rows, pl.ds(column, count)]
        fill.append(pltpu.make_async_copy(source, target, fsem.at[len(fill)]))
    for copy in fill:
        copy.start()
    greet([(dp + dc, z), (dp + dx, z), (dp + dy, z), (dp, zr)], (dp, zo), mid, z * (3 - z) // 2)
    sends = []

    def spot(block, part):
        return wheld.at[pl.ds(pl.multiple_of(block * 256 + part * 128, 128), 128)]

    def send(block, part, dp_to, own=False):
        source = spot(block, part)
        index = len(sends)
        copies = [
            pltpu.make_async_remote_copy(
                source, spot(block, part), wsend.at[index], wrecv.at[block, part],
                device_id=at(dp_to, z), device_id_type=MESH,
            )
        ]
        if part == 0:
            copies.append(
                pltpu.make_async_remote_copy(
                    gains_in if own else gheld.at[block], gheld.at[block],
                    gsend.at[index], grecv.at[block],
                    device_id=at(dp_to, z), device_id_type=MESH,
                )
            )
        for copy in copies:
            copy.start()
        sends.append(copies)

    def arrive(block, part):
        here = dict(device_id=at(dp + dx, z), device_id_type=MESH)
        pltpu.make_async_remote_copy(
            spot(block, part), spot(block, part), wsend.at[0], wrecv.at[block, part], **here
        ).wait_recv()
        if part == 0:
            pltpu.make_async_remote_copy(
                gheld.at[block], gheld.at[block], gsend.at[0], grecv.at[block], **here
            ).wait_recv()

    zsends = []

    def z_send(source, block, z_to, cond=None):
        copy = pltpu.make_async_remote_copy(
            source, theld.at[block], zsend.at[len(zsends)], zrecv.at[block],
            device_id=at(dp, z_to), device_id_type=MESH,
        )
        when_or_now(cond, functools.partial(copy.start))
        zsends.append((copy, cond))

    def z_arrive(block):
        pltpu.make_async_remote_copy(
            theld.at[block], theld.at[block], zsend.at[0], zrecv.at[block],
            device_id=at(dp, zr), device_id_type=MESH,
        ).wait_recv()

    z_send(tok_ref, z, zr)
    z_send(tok_ref, z, zo, mid)
    for copy in fill:
        copy.wait()
    send(dp, 0, dp + dx, True)
    send(dp, 1, dp + dy, True)
    send(dp, 1, dp + dx, True)
    send(dp, 0, dp + dy, True)
    send(dp, 0, dp + dc, True)
    send(dp, 1, dp + dc, True)
    local = [
        pltpu.make_async_copy(tok_ref, theld.at[z], lsem.at[1]),
        pltpu.make_async_copy(gains_in, gheld.at[dp], lsem.at[2]),
        pltpu.make_async_copy(cot_ref, held.at[own_block], lsem.at[3]),
        pltpu.make_async_copy(routes_in, metas.at[own_block], lsem.at[4]),
    ]
    for copy in local:
        copy.start()
    spare[...] = jnp.zeros_like(spare)
    z_arrive(zr)
    z_send(theld.at[zr], zr, zo, mid)
    bx, by, bxy = dp + dx, dp + dy, dp + dx + dy
    arrive(bx, 0)
    send(bx, 0, dp + dy)
    send(bx, 0, dp + dc)
    arrive(by, 1)
    send(by, 1, dp + dx)
    send(by, 1, dp + dc)
    far = 2 - z // 2
    z_arrive(far)
    z_send(theld.at[far], far, zr, mid)
    arrive(bx, 1)
    send(bx, 1, dp + dc)
    arrive(by, 0)
    send(by, 0, dp + dc)
    last = 3 - 3 * (z // 2)
    z_arrive(last)
    z_send(theld.at[last], last, zr, mid)
    for part in (0, 1):
        arrive(bxy, part)
        send(bxy, part, dp + dc)
    gather.first(0)
    for block in (dp, bx, by, bxy):
        for part in (0, 1):
            arrive(block + dc, part)
    for copy in local:
        copy.wait()
    kept = [
        pltpu.make_async_copy(wheld, weights_ref, lsem.at[0]),
        pltpu.make_async_copy(theld, group_ref, lsem.at[1]),
    ]
    for copy in kept:
        copy.start()

    def process(block):
        onehot = slot_matrix(metas[block], block, dp * 8)
        onehot_ref[block] = onehot
        picker.block(block, onehot)

    scale = jnp.concatenate(
        [gheld[j // 2, j % 2 : j % 2 + 1, :] for j in range(width // 128)], axis=1
    )

    def norm_rows(step, carry):
        values = theld[step].astype(f32)
        inverse = lax.rsqrt(jnp.mean(values * values, axis=1, keepdims=True) + EPSILON)
        rows = pl.ds(pl.multiple_of(step * 128, 128), 128)
        normed_ref[rows, :] = (values * inverse * scale).astype(low)
        return carry

    gains_ref[...] = gheld[...]
    lax.fori_loop(0, 4, norm_rows, 0)

    def project(column):
        cols = slice(column * heads, column * heads + heads)
        return jnp.dot(normed_ref[...], wheld[:, cols], preferred_element_type=f32)

    projq_ref[...] = project(0)
    projk_ref[...] = project(1)
    value_ref[...] = project(2).astype(low)
    process(own_block)
    gather_step(gather, order, 1, process)
    cosines, sines = cos_ref[...], sin_ref[...]
    query_gain, key_gain = head_gain(gheld, 0), head_gain(gheld, 16)

    def one_head(h, carry):
        cols = pl.ds(pl.multiple_of(h * HD, HD), HD)
        for source, gain, target in (
            (projq_ref, query_gain, query_ref), (projk_ref, key_gain, key_ref),
        ):
            values = source[:, cols]
            inverse = lax.rsqrt(jnp.mean(values * values, axis=1, keepdims=True) + EPSILON)
            target[:, cols] = rotate(values * inverse * gain, cosines, sines).astype(low)
        for start in range(0, 512, 256):
            rows = slice(start, start + 256)
            probs = head_probs(
                query_ref[rows, cols], key_ref[:, cols], seqc_ref[rows, :1], seqr_ref[:1, :]
            )
            ctx_ref[rows, cols] = jnp.dot(
                probs.astype(low), value_ref[:, cols], preferred_element_type=f32
            ).astype(low)
        return carry

    lax.fori_loop(0, heads // HD, one_head, 0)
    for k in range(4):
        rows = pl.ds(pl.multiple_of(line.zs[k] * 128, 128), 128)
        for start in range(0, width, 256):
            lanes = slice(start, start + 256)
            piece = jnp.dot(
                ctx_ref[rows, :256], wheld[lanes, 3 * heads : 3 * heads + 256],
                preferred_element_type=f32,
            ) + jnp.dot(
                ctx_ref[rows, 256:], wheld[lanes, 3 * heads + 256 : 4 * heads],
                preferred_element_type=f32,
            )
            if k < 3:
                line.blocks[k, :, lanes] = piece.astype(low)
            else:
                out_ref[:, lanes] = piece
        if k < 3:
            line.ready(k)
    gather_step(gather, order, 2, process)
    line.onward(0)
    line.onward(1)
    gather_step(gather, order, 3, process)
    line.onward(2)
    gather_step(gather, order, 4, process)
    line.last(out_ref)
    gather_step(gather, order, 5, process)
    picker.end()
    routes_ref[...] = metas[...]
    for copy in kept:
        copy.wait()
    for copies in sends:
        for copy in copies:
            copy.wait_send()
    for copy, cond in zsends:
        when_or_now(cond, functools.partial(copy.wait_send))
    gather.drain()
    line.drain()


def front(shards, tokens, cotangent, routes, gains, cosines, sines, seq_column, seq_row, heads):
    width = tokens.shape[1]
    rows = 4 * tokens.shape[0]
    f32, low = jnp.float32, jnp.bfloat16
    anywhere = pl.BlockSpec(memory_space=pl.ANY)
    vmem = pl.BlockSpec(memory_space=pltpu.VMEM)
    dma = pltpu.SemaphoreType.DMA
    narrow = jax.ShapeDtypeStruct((rows, heads), low)
    return pl.pallas_call(
        front_kernel,
        name="front",
        out_shape=(
            jax.ShapeDtypeStruct((width, 4 * heads + 128), low),
            jax.ShapeDtypeStruct((4, 128, width), low),
            jax.ShapeDtypeStruct((8, 576, width), low),
            jax.ShapeDtypeStruct((8, 8, 128), f32),
            jax.ShapeDtypeStruct((32, 256, 128), low),
            jax.ShapeDtypeStruct((32, 8, 128), f32),
            jax.ShapeDtypeStruct((rows, width), low),
            jax.ShapeDtypeStruct((rows, heads), f32),
            jax.ShapeDtypeStruct((rows, heads), f32),
            narrow, narrow, narrow, narrow,
            jax.ShapeDtypeStruct((128, width), f32),
        ),
        in_specs=[anywhere] * 5 + [vmem] * 8,
        out_specs=(anywhere,) * 3 + (vmem,) * 11,
        scratch_shapes=[
            pltpu.VMEM((width, 4 * heads + 128), low),
            pltpu.VMEM((4, 128, width), low),
            pltpu.VMEM((8, 8, 128), f32),
            pltpu.VMEM((32, 128, width), low),
            pltpu.VMEM((32, 8, 128), f32),
            pltpu.VMEM((2, 8, MAIN, width), low),
            pltpu.VMEM((4, 128, width), low),
            dma((9,)), dma((14,)), dma((8, 2)), dma((14,)), dma((8,)), dma((5,)), dma((4,)),
            dma((72,)), dma((32, 2)), dma((72,)), dma((32,)), dma((2,)), dma((6,)),
        ]
        + LineScatter.scratch(width),
        compiler_params=pltpu.CompilerParams(
            collective_id=0, has_side_effects=True, vmem_limit_bytes=VMEM_LIMIT
        ),
        cost_estimate=pl.CostEstimate(
            flops=5_000_000_000, bytes_accessed=100_000_000, transcendentals=2_000_000
        ),
    )(*shards, tokens, cotangent, routes, gains, cosines, sines, seq_column, seq_row)


def gather_kernel(
    x_ref, meta_ref, onehot_ref, routes_ref, slots_ref, gate_ref,
    held, metas, stage, spare, lsem, ssem, rsem, msem, mrsem, osem,
):
    dp, z, dc, dx, dy = place()
    own = dp * 4 + z
    gather = AllGather(held, held.at[own], ssem, rsem, metas, metas.at[own], msem, mrsem)
    order = arrival_order(gather)
    picker = Dispatcher(held, stage, spare, slots_ref, osem)
    local = [
        pltpu.make_async_copy(x_ref, held.at[own], lsem.at[0]),
        pltpu.make_async_copy(meta_ref, metas.at[own], lsem.at[1]),
    ]
    for copy in local:
        copy.start()
    greet(
        [(dp + dc, z), (dp + dx, z), (dp + dy, z), (dp, gather.zr)],
        (dp, gather.zo), gather.mid, z * (3 - z) // 2,
    )
    spare[...] = jnp.zeros_like(spare)
    gate_ref[:, 512:576, :] = jnp.zeros((8, 64, 128), jnp.float32)
    for copy in local:
        copy.wait()
    experts = (lax.broadcasted_iota(jnp.int32, (8, 128), 0) + dp * 8).astype(jnp.float32)

    def process(block):
        onehot = onehot_ref[block]
        gates_here = jnp.zeros((8, 128), jnp.float32)
        for j in range(TOPK):
            gates_here = gates_here + jnp.where(
                routes_ref[block, j : j + 1, :] == experts, metas[block, j : j + 1, :], 0.0
            )
        wide = jnp.broadcast_to(gates_here[:, None, :], (8, MAIN, 128)).reshape(128, 128)
        taken = onehot.astype(jnp.float32)
        main_gate = jnp.sum(taken[:128] * wide, axis=1, keepdims=True)
        spare_gate = jnp.sum(taken[128:] * wide, axis=1, keepdims=True)
        gate_ref[:, pl.ds(pl.multiple_of(block * MAIN, MAIN), MAIN), :] = jnp.broadcast_to(
            main_gate, (128, 128)
        ).reshape(8, MAIN, 128)
        spare_rows = pl.ds(pl.multiple_of(512 + (block // 8) * MAIN, MAIN), MAIN)
        gate_ref[:, spare_rows, :] = gate_ref[:, spare_rows, :] + jnp.broadcast_to(
            spare_gate, (128, 128)
        ).reshape(8, MAIN, 128)
        picker.block(block, onehot)

    for k in range(6):
        gather_step(gather, order, k, process)
    picker.end()
    gather.drain()


def gather_slots(rows, meta, onehot, routes):
    count, width = rows.shape
    anywhere = pl.BlockSpec(memory_space=pl.ANY)
    vmem = pl.BlockSpec(memory_space=pltpu.VMEM)
    dma = pltpu.SemaphoreType.DMA
    return pl.pallas_call(
        gather_kernel,
        name="gather_x",
        out_shape=(
            jax.ShapeDtypeStruct((8, 576, width), jnp.bfloat16),
            jax.ShapeDtypeStruct((8, 576, 128), jnp.float32),
        ),
        in_specs=[anywhere, anywhere, vmem, vmem],
        out_specs=(anywhere, vmem),
        scratch_shapes=[
            pltpu.VMEM((32, count, width), jnp.bfloat16),
            pltpu.VMEM((32, 8, 128), jnp.float32),
            pltpu.VMEM((2, 8, MAIN, width), jnp.bfloat16),
            pltpu.VMEM((4, 128, width), jnp.bfloat16),
            dma((2,)), dma((72,)), dma((32, 2)), dma((72,)), dma((32,)), dma((2,)),
        ],
        compiler_params=pltpu.CompilerParams(
            collective_id=1, has_side_effects=True, vmem_limit_bytes=VMEM_LIMIT
        ),
        cost_estimate=pl.CostEstimate(
            flops=4_300_000_000, bytes_accessed=100_000_000, transcendentals=0
        ),
    )(rows, meta, onehot, routes)


def return_kernel(
    y_ref, onehot_ref, out_ref,
    rows_in, to_core, from_core, sums, ry0, rx1, rx0, ry1, rze, rzm, rzf,
    ysem, csend, crecv, xsend, xrecv, zsend, zrecv,
):
    dp, z, dc, dx, dy = place()
    zr, zo = z + 1 - 2 * (z % 2), 3 - z
    mid = z * (3 - z) > 0
    end = z * (3 - z) < 1
    half = 64
    width = y_ref.shape[2]
    zs = [3 - 3 * (z // 2), 2 - z // 2, zr, z]
    greet([(dp + dc, z), (dp + dx, z), (dp + dy, z), (dp, zr)], (dp, zo), mid, z * (3 - z) // 2)

    def dest(k, step):
        r = 3 - step % 4
        base = dp + dc - dc * (step // 4)
        return (base + (r % 2) * dx + (r // 2) * dy) * 4 + zs[k]

    def fetch(block, slot):
        return [
            pltpu.make_async_copy(
                y_ref.at[:, pl.ds(block * MAIN, MAIN), :], rows_in.at[slot, pl.ds(0, 8)], ysem.at[slot, 0]
            ),
            pltpu.make_async_copy(
                y_ref.at[:, pl.ds(512 + (block // 8) * MAIN, MAIN), :],
                rows_in.at[slot, pl.ds(8, 8)], ysem.at[slot, 1],
            ),
        ]

    def partial_tile(block, slot, lanes):
        size = lanes.stop - lanes.start
        return lax.dot_general(
            onehot_ref[block], rows_in[slot, :, :, lanes].reshape(256, size),
            (((0,), (0,)), ((), ())), preferred_element_type=jnp.float32,
        )

    tiles = [slice(s, min(s + 512, width)) for s in range(0, width, 512)]
    lo, hi = pl.ds(0, half), pl.ds(half, half)
    xsends, zsends = [[] for _ in range(4)], []

    def core_copy(r, k):
        return pltpu.make_async_remote_copy(
            to_core.at[k, r], from_core.at[k, r], csend.at[k, r], crecv.at[k, r],
            device_id=at(dp + dc, z), device_id_type=MESH,
        )

    def xy_copy(src, dst, index, k, dp_to):
        return pltpu.make_async_remote_copy(
            src, dst, xsend.at[index, k], xrecv.at[index, k],
            device_id=at(dp_to, z), device_id_type=MESH,
        )

    def z_copy(src, dst, index, z_to):
        return pltpu.make_async_remote_copy(
            src, dst, zsend.at[index], zrecv.at[index],
            device_id=at(dp, z_to), device_id_type=MESH,
        )

    def add_to(target, rows, *others):
        total = target[rows, :].astype(jnp.float32)
        for other in others:
            total = total + other[...].astype(jnp.float32)
        target[rows, :] = total.astype(jnp.bfloat16)

    def stage_core(k):
        def load(block, slot, following=None):
            for copy in fetch(block, slot):
                copy.wait()
            if following is not None:
                for copy in fetch(following, 1 - slot):
                    copy.start()

        def partner(step, slot, following):
            r = 3 - step
            block = dest(k, step)
            load(block, slot, following)
            for lanes in tiles:
                to_core[k, r, :, lanes] = partial_tile(block, slot, lanes).astype(jnp.bfloat16)
            core_copy(r, k).start()

        batch = [
            xy_copy(sums.at[k, 3, lo], ry0.at[1, k], 0, k, dp + dy),
            xy_copy(sums.at[k, 3, hi], rx1.at[1, k], 1, k, dp + dx),
            xy_copy(sums.at[k, 2, lo], ry0.at[0, k], 2, k, dp + dy),
            xy_copy(sums.at[k, 1, hi], rx1.at[0, k], 3, k, dp + dx),
        ]
        xsends[k].extend(batch)

        def both(i, carry):
            r = 3 - i
            block = dest(k, 4 + i)

            @pl.when(i < 3)
            def _():
                partner(i + 1, 1, block)

            late = i // 2
            following = (1 - late) * dest(k, i + 2) + late * dest(k, 5 + i)
            slot = i // 3
            if k < 3:
                last = i // 3
                load(block, slot, (1 - last) * following + last * dest(k + 1, 0))
            else:
                load(block, slot)

                @pl.when(i < 3)
                def _():
                    for copy in fetch(following, 1):
                        copy.start()

            core_copy(r, k).wait_recv()
            for lanes in tiles:
                sums[k, r, :, lanes] = (
                    partial_tile(block, slot, lanes) + from_core[k, r, :, lanes].astype(jnp.float32)
                ).astype(jnp.bfloat16)
            for when, copies in enumerate((batch[:2], batch[2:3], batch[3:])):

                @pl.when(i == when)
                def _():
                    for copy in copies:
                        copy.start()

            return carry

        partner(0, 0, dest(k, 1))
        lax.fori_loop(0, 4, both, 0)

    def stage_cross(k):
        xsends[k][0].wait_recv()
        add_to(sums.at[k, 1], lo, ry0.at[1, k])
        across = xy_copy(sums.at[k, 1, lo], rx0.at[k], 4, k, dp + dx)
        across.start()
        xsends[k][1].wait_recv()
        add_to(sums.at[k, 2], hi, rx1.at[1, k])
        down = xy_copy(sums.at[k, 2, hi], ry1.at[k], 5, k, dp + dy)
        down.start()
        xsends[k].extend([across, down])

    outward = [z_copy(sums.at[k, 0], rze.at[k], k, zr) for k in range(3)]

    def stage_line(k):
        for j in range(2, 6):
            xsends[k][j].wait_recv()
        if k < 3:
            add_to(sums.at[k, 0], lo, ry0.at[0, k], rx0.at[k])
            add_to(sums.at[k, 0], hi, rx1.at[0, k], ry1.at[k])
            zsends.append((outward[k], end))
            pl.when(end)(functools.partial(outward[k].start))
        else:

            def total(part, *others):
                value = sums[k, 0, part, :].astype(jnp.float32)
                for other in others:
                    value = value + other.astype(jnp.float32)
                return value

            out_ref[lo, :] = total(lo, ry0[0, k], rx0[k])
            out_ref[hi, :] = total(hi, rx1[0, k], ry1[k])

    def stage_onward(k):
        if k < 2:
            onward = z_copy(sums.at[k, 0], rzm.at[k], 3 + k, zo)
        else:
            onward = z_copy(sums.at[k, 0], rzf, 5, zr)
        zsends.append((onward, mid))

        @pl.when(mid)
        def _():
            if k < 2:
                outward[k].wait_recv()
                add_to(sums.at[k, 0], slice(None), rze.at[k])
            else:
                z_copy(sums.at[0, 0], rzm.at[0], 3, zo).wait_recv()
                add_to(sums.at[k, 0], slice(None), rzm.at[0])
            onward.start()

    def stage_last():
        @pl.when(end)
        def _():
            z_copy(sums.at[2, 0], rzf, 5, zr).wait_recv()
            out_ref[...] = out_ref[...] + rzf[...].astype(jnp.float32)

        @pl.when(mid)
        def _():
            outward[2].wait_recv()
            z_copy(sums.at[1, 0], rzm.at[1], 4, zo).wait_recv()
            out_ref[...] = out_ref[...] + rze[2].astype(jnp.float32) + rzm[1].astype(jnp.float32)

    for copy in fetch(dest(0, 0), 0):
        copy.start()
    for k in range(6):
        if k < 4:
            stage_core(k)
        if 1 <= k < 5:
            stage_cross(k - 1)
        if 2 <= k < 5:
            stage_line(k - 2)
        if k == 3:
            stage_onward(0)
        if k == 4:
            stage_onward(2)
            stage_onward(1)
    stage_line(3)
    stage_last()
    for k in range(4):
        for r in range(4):
            core_copy(r, k).wait_send()
    for batch in xsends:
        for copy in batch:
            copy.wait_send()
    for copy, cond in zsends:
        pl.when(cond)(functools.partial(copy.wait_send))


def return_rows(partial_slots, onehot, collective_id):
    width = partial_slots.shape[2]
    anywhere = pl.BlockSpec(memory_space=pl.ANY)
    vmem = pl.BlockSpec(memory_space=pltpu.VMEM)
    dma = pltpu.SemaphoreType.DMA
    low = jnp.bfloat16
    return pl.pallas_call(
        return_kernel,
        name="return_rows_%d" % collective_id,
        out_shape=jax.ShapeDtypeStruct((128, width), jnp.float32),
        in_specs=[anywhere, vmem],
        out_specs=vmem,
        scratch_shapes=[
            pltpu.VMEM((2, 16, MAIN, width), low),
            pltpu.VMEM((4, 4, 128, width), low),
            pltpu.VMEM((4, 4, 128, width), low),
            pltpu.VMEM((4, 4, 128, width), low),
            pltpu.VMEM((2, 4, 64, width), low),
            pltpu.VMEM((2, 4, 64, width), low),
            pltpu.VMEM((4, 64, width), low),
            pltpu.VMEM((4, 64, width), low),
            pltpu.VMEM((3, 128, width), low),
            pltpu.VMEM((2, 128, width), low),
            pltpu.VMEM((128, width), low),
            dma((2, 2)), dma((4, 4)), dma((4, 4)), dma((6, 4)), dma((6, 4)), dma((6,)), dma((6,)),
        ],
        compiler_params=pltpu.CompilerParams(
            collective_id=collective_id, has_side_effects=True, vmem_limit_bytes=VMEM_LIMIT
        ),
        cost_estimate=pl.CostEstimate(
            flops=4_300_000_000, bytes_accessed=300_000_000, transcendentals=0
        ),
    )(partial_slots, onehot)


def finish_kernel(
    rows_ref, tok_ref, projq_ref, projk_ref, query_ref, key_ref, value_ref, ctx_ref, ga_ref, w_ref,
    gains_ref, cos_ref, sin_ref, seqc_ref, seqr_ref, side_ref, stat_ref,
    gw_ref, gwo_ref, dx_ref, small_ref,
    gqkv_ref, gctx_ref, to_core, from_core, sums, ry0, rx1, rx0, ry1, gain, zside,
    csend, crecv, xsend, xrecv, ssend, srecv, *line_refs,
):
    dp, z, dc, dx, dy = place()
    line = LineScatter(dp, z, *line_refs)
    dxs = line.blocks
    f32, low = jnp.float32, jnp.bfloat16
    half = 128
    heads = query_ref.shape[1]
    width = rows_ref.shape[1]
    others = [(z + i) % 4 for i in (1, 2, 3)]
    greet([(dp + dc, z), (dp + dx, z), (dp + dy, z)] + [(dp, other) for other in others])
    nt = (((1,), (1,)), ((), ()))
    tn = (((0,), (0,)), ((), ()))
    lo, hi = pl.ds(0, half), pl.ds(half, half)
    xsends = []

    def mm(a, b, dims):
        return lax.dot_general(a, b, dims, preferred_element_type=f32)

    def core_copy(r):
        return pltpu.make_async_remote_copy(
            to_core.at[r], from_core.at[r], csend.at[r], crecv.at[r],
            device_id=at(dp + dc, z), device_id_type=MESH,
        )

    def xy_copy(src, dst, index, dp_to):
        return pltpu.make_async_remote_copy(
            src, dst, xsend.at[index], xrecv.at[index], device_id=at(dp_to, z), device_id_type=MESH
        )

    def add_to(target, rows, *parts):
        total = target[rows, :].astype(f32)
        for part in parts:
            total = total + part[...].astype(f32)
        target[rows, :] = total.astype(low)

    gain[...] = jnp.zeros_like(gain)
    cosines, sines = cos_ref[...], sin_ref[...]
    query_gain, key_gain = head_gain(gains_ref, 0), head_gain(gains_ref, 16)
    for i in range(2):
        column = 3 * heads + i * 256
        total_ctx = jnp.zeros((512, 256), f32)
        for start in range(0, width, 256):
            lanes = slice(start, start + 256)
            total_ctx = total_ctx + mm(ga_ref[:, lanes], w_ref[lanes, column : column + 256], nt)
        gctx_ref[:, i * 256 : i * 256 + 256] = total_ctx.astype(low)
    score_scale = HD ** (-0.5)

    def head_back(grad, source, rows, cols, gain_values, column):
        values = source[rows, cols]
        inverse = lax.rsqrt(jnp.mean(values * values, axis=1, keepdims=True) + EPSILON)
        turned = grad * cosines[rows] - pltpu.roll(grad, HD // 2, 1) * sines[rows]
        scaled = turned * gain_values
        inner = jnp.mean(scaled * values, axis=1, keepdims=True)
        target = pl.ds(pl.multiple_of(cols.start + column, HD), HD)
        gqkv_ref[rows, target] = ((scaled - values * inner * inverse * inverse) * inverse).astype(low)
        return jnp.sum(turned * values * inverse, axis=0, keepdims=True)

    def one_head(h, carry):
        query_part, key_part = carry
        cols = pl.ds(pl.multiple_of(h * HD, HD), HD)
        key, value = key_ref[:, cols], value_ref[:, cols]
        grad_key = jnp.zeros((key.shape[0], HD), f32)
        grad_value = jnp.zeros((key.shape[0], HD), f32)
        for start in range(0, 512, 256):
            rows = slice(start, start + 256)
            query, grad_ctx = query_ref[rows, cols], gctx_ref[rows, cols]
            probs = head_probs(query, key, seqc_ref[rows, :1], seqr_ref[:1, :])
            grad_value = grad_value + mm(probs.astype(low), grad_ctx, tn)
            grad_probs = mm(grad_ctx, value, nt)
            inner = jnp.sum(probs * grad_probs, axis=1, keepdims=True)
            grad_scores = (probs * (grad_probs - inner)).astype(low)
            grad_query = jnp.dot(grad_scores, key, preferred_element_type=f32) * score_scale
            grad_key = grad_key + mm(grad_scores, query, tn)
            query_part = query_part + head_back(
                grad_query, projq_ref, rows, cols, query_gain, 0
            )
        key_part = key_part + head_back(
            grad_key * score_scale, projk_ref, slice(0, 512), cols, key_gain, heads
        )
        target = pl.ds(pl.multiple_of(cols.start + 2 * heads, HD), HD)
        gqkv_ref[:, target] = grad_value.astype(low)
        return query_part, key_part

    zero_row = jnp.zeros((1, HD), f32)
    query_part, key_part = lax.fori_loop(0, heads // HD, one_head, (zero_row, zero_row))
    for to in range(8):
        gain[to, 4:5, :] = query_part
        gain[to, 5:6, :] = key_part
    for k in range(4):
        rows = pl.ds(pl.multiple_of(line.zs[k] * 128, 128), 128)
        square = jnp.zeros((128, 1), f32)
        for start in range(0, width, 512):
            values = tok_ref[rows, start : start + 512].astype(f32)
            square = square + jnp.sum(values * values, axis=1, keepdims=True)
        inverse = lax.rsqrt(square * (1.0 / width) + EPSILON)
        for start in range(0, width, 512):
            lanes = slice(start, start + 512)
            piece = mm(gqkv_ref[rows, :], w_ref[lanes, : 3 * heads], nt)
            scaled = tok_ref[rows, lanes].astype(f32) * inverse
            column = jnp.sum(piece * scaled, axis=0, keepdims=True)
            for j in range(4):
                to = start // 256 + j // 2
                row = slice(j % 2, j % 2 + 1)
                gain[to, row, :] = gain[to, row, :] + column[:, j * 128 : j * 128 + 128]
            if k < 3:
                dxs[k, :, lanes] = piece.astype(low)
            else:
                dx_ref[:, lanes] = piece
        if k < 3:
            line.ready(k)

    def pieces(to):
        cols = pl.ds(pl.multiple_of(to * 256, 256), 256)
        mine = rows_ref[:, cols]
        yield slice(0, 3 * heads), mm(mine, gqkv_ref[...], tn)
        out = mm(ctx_ref[...], ga_ref[:, cols], tn)
        yield slice(3 * heads, 3 * heads + 256), out[:256]
        yield slice(3 * heads + 256, 4 * heads), out[256:]
        yield slice(4 * heads, 4 * heads + 128), jnp.concatenate(
            [
                side_ref[to, :128, :].astype(f32),
                side_ref[to, 128:144, :].astype(f32) + gain[to],
                jnp.zeros((112, 128), f32),
            ],
            axis=0,
        )

    def dest(step):
        r = 3 - step % 4
        base = dp + dc - dc * (step // 4)
        return base + (r % 2) * dx + (r // 2) * dy

    def partner(step, carry):
        r = 3 - step
        for lanes, value in pieces(dest(step)):
            to_core[r, :, lanes] = value.astype(low)
        core_copy(r).start()
        return carry

    def own(step, carry):
        r = 7 - step
        core_copy(r).wait_recv()
        for lanes, value in pieces(dest(step)):
            sums[r, :, lanes] = (value + from_core[r, :, lanes].astype(f32)).astype(low)
        return carry

    lax.fori_loop(0, 4, partner, 0)
    lax.fori_loop(4, 8, own, 0)
    xsends += [
        xy_copy(sums.at[3, lo], ry0.at[1], 0, dp + dy),
        xy_copy(sums.at[3, hi], rx1.at[1], 1, dp + dx),
        xy_copy(sums.at[2, lo], ry0.at[0], 2, dp + dy),
        xy_copy(sums.at[1, hi], rx1.at[0], 3, dp + dx),
    ]
    for copy in xsends:
        copy.start()

    line.onward(0)
    line.onward(1)
    xsends[0].wait_recv()
    add_to(sums.at[1], lo, ry0.at[1])
    xsends.append(xy_copy(sums.at[1, lo], rx0, 4, dp + dx))
    xsends[4].start()
    xsends[1].wait_recv()
    add_to(sums.at[2], hi, rx1.at[1])
    xsends.append(xy_copy(sums.at[2, hi], ry1, 5, dp + dy))
    xsends[5].start()
    line.onward(2)
    for j in (2, 3, 4, 5):
        xsends[j].wait_recv()

    def side_copy(i, source):
        return pltpu.make_async_remote_copy(
            zside.at[source], zside.at[source], ssend.at[i], srecv.at[source],
            device_id=at(dp, others[i]), device_id_type=MESH,
        )

    def total(part, lanes, first, second):
        return (
            sums[0, part, lanes].astype(f32)
            + first[:, lanes].astype(f32)
            + second[:, lanes].astype(f32)
        )

    sides = slice(4 * heads, 4 * heads + 128)
    zside[z, :128, :] = total(lo, sides, ry0.at[0], rx0)
    zside[z, 128:144, :] = total(hi, sides, rx1.at[0], ry1)[:16] + stat_ref[...]
    for i in range(3):
        side_copy(i, z).start()
    for rows, first, second in ((lo, ry0.at[0], rx0), (hi, rx1.at[0], ry1)):
        gw_ref[rows, :] = total(rows, slice(0, 3 * heads), first, second)
        gwo_ref[rows, :] = total(rows, slice(3 * heads, 3 * heads + 256), first, second)
        below = pl.ds(256 + rows.start, half)
        gwo_ref[below, :] = total(rows, slice(3 * heads + 256, 4 * heads), first, second)

    line.last(dx_ref)
    for i in range(3):
        side_copy(i, others[i]).wait_recv()
    small_ref[...] = (zside[0] + zside[1]) + (zside[2] + zside[3])
    for r in range(4):
        core_copy(r).wait_send()
    for copy in xsends:
        copy.wait_send()
    line.drain()
    for i in range(3):
        side_copy(i, z).wait_send()


def finish(rows, tok, attention, grad_attn, weights, tables, side, stats):
    width = rows.shape[1]
    heads = attention[0].shape[1]
    f32, low = jnp.float32, jnp.bfloat16
    vmem = pl.BlockSpec(memory_space=pltpu.VMEM)
    dma = pltpu.SemaphoreType.DMA
    packed = 4 * heads + 128
    return pl.pallas_call(
        finish_kernel,
        name="finish",
        out_shape=(
            jax.ShapeDtypeStruct((256, 3 * heads), f32),
            jax.ShapeDtypeStruct((heads, 256), f32),
            jax.ShapeDtypeStruct((128, width), f32),
            jax.ShapeDtypeStruct((144, 128), f32),
        ),
        in_specs=[vmem] * 17,
        out_specs=(vmem,) * 4,
        scratch_shapes=[pltpu.VMEM((512, 3 * heads), low), pltpu.VMEM((512, heads), low)]
        + [
            pltpu.VMEM((4, 256, packed), low),
            pltpu.VMEM((4, 256, packed), low),
            pltpu.VMEM((4, 256, packed), low),
            pltpu.VMEM((2, 128, packed), low),
            pltpu.VMEM((2, 128, packed), low),
            pltpu.VMEM((128, packed), low),
            pltpu.VMEM((128, packed), low),
            pltpu.VMEM((8, 16, 128), f32),
            pltpu.VMEM((4, 144, 128), f32),
            dma((4,)), dma((4,)), dma((6,)), dma((6,)), dma((3,)), dma((4,)),
        ]
        + LineScatter.scratch(width),
        compiler_params=pltpu.CompilerParams(
            collective_id=4, has_side_effects=True, vmem_limit_bytes=VMEM_LIMIT
        ),
        cost_estimate=pl.CostEstimate(
            flops=8_000_000_000, bytes_accessed=100_000_000, transcendentals=0
        ),
    )(rows, tok, *attention, grad_attn, weights, *tables, side, stats)


def expert_kernel(
    x_ref, dy_ref, gate_ref, wg_ref, wu_ref, wd_ref, y_ref, gin_ref, dgate_ref, dup_ref, hgated_ref,
    gate_pre_ref, up_pre_ref, raw_ref,
):
    rows, ff = dgate_ref.shape[1:]
    width = x_ref.shape[2]
    expert = lax.axis_index("dp") * 8 + pl.program_id(0)
    nt = (((1,), (1,)), ((), ()))

    def mm(a, b, dims):
        return lax.dot_general(a, b, dims, preferred_element_type=jnp.float32)

    gate_pre_ref[...] = jnp.dot(x_ref[0], wg_ref[0], preferred_element_type=jnp.float32)
    up_pre_ref[...] = jnp.dot(x_ref[0], wu_ref[0], preferred_element_type=jnp.float32)
    raw_ref[...] = mm(dy_ref[0], wd_ref[0], nt)
    step = 96

    def pointwise(index, carry):
        part = pl.ds(pl.multiple_of(index * step, step), step)
        gate_pre, up_pre, raw = gate_pre_ref[part, :], up_pre_ref[part, :], raw_ref[part, :]
        weight = jnp.concatenate([gate_ref[0, part, :]] * (ff // 128), axis=1)
        sig = jax.nn.sigmoid(gate_pre)
        silu = gate_pre * sig
        hidden = silu * up_pre
        route_grad = jnp.sum(hidden * raw, axis=1, keepdims=True)
        grad_hidden = weight * raw
        lane = lax.broadcasted_iota(jnp.int32, (step, 128), 1)
        high = route_grad.astype(jnp.bfloat16).astype(jnp.float32)
        extra = jnp.where(lane == expert, high, 0.0) + jnp.where(
            lane == expert + 64, route_grad - high, 0.0
        )
        hgated_ref[0, part, :] = (weight * hidden).astype(jnp.bfloat16)
        dgate_ref[0, part, :] = (
            grad_hidden * up_pre * sig * (1.0 + gate_pre * (1.0 - sig))
        ).astype(jnp.bfloat16)
        dup_ref[0, part, :] = (grad_hidden * silu).astype(jnp.bfloat16)
        y_ref[0, part, width:] = extra.astype(jnp.bfloat16)
        return carry

    lax.fori_loop(0, rows // step, pointwise, 0)
    for start in range(0, width, 512):
        lanes = slice(start, start + 512)
        y_ref[0, :, lanes] = jnp.dot(
            hgated_ref[0], wd_ref[0, :, lanes], preferred_element_type=jnp.float32
        ).astype(jnp.bfloat16)
        gin_ref[0, :, lanes] = (
            mm(dgate_ref[0], wg_ref[0, lanes, :], nt) + mm(dup_ref[0], wu_ref[0, lanes, :], nt)
        ).astype(jnp.bfloat16)


def weights_kernel(x_ref, dy_ref, dgate_ref, dup_ref, hgated_ref, gwg_ref, gwu_ref, gwd_ref):
    width = x_ref.shape[2]
    tn = (((0,), (0,)), ((), ()))

    def mm(a, b):
        return lax.dot_general(a, b, tn, preferred_element_type=jnp.float32)

    for start in range(0, width, 512):
        part = slice(start, start + 512)
        gwd_ref[0, :, part] = mm(hgated_ref[0], dy_ref[0, :, part])
        xs = x_ref[0, :, part]
        gwg_ref[0, part, :] = mm(xs, dgate_ref[0])
        gwu_ref[0, part, :] = mm(xs, dup_ref[0])


def expert_spec(*shape):
    return pl.BlockSpec((1,) + shape, lambda e: (e, 0, 0))


def run_experts(x_slots, dy_slots, gate_slots, w_gate, w_up, w_down):
    experts, rows, width = x_slots.shape
    ff = w_gate.shape[2]
    spec, low = expert_spec, jnp.bfloat16
    middle = jax.ShapeDtypeStruct((experts, rows, ff), low)
    return pl.pallas_call(
        expert_kernel,
        name="experts",
        grid=(experts,),
        in_specs=[
            spec(rows, width), spec(rows, width), spec(rows, 128),
            spec(width, ff), spec(width, ff), spec(ff, width),
        ],
        out_specs=(spec(rows, width + 128), spec(rows, width)) + (spec(rows, ff),) * 3,
        out_shape=(
            jax.ShapeDtypeStruct((experts, rows, width + 128), low),
            jax.ShapeDtypeStruct((experts, rows, width), low),
            middle, middle, middle,
        ),
        scratch_shapes=[pltpu.VMEM((rows, ff), jnp.float32)] * 3,
        compiler_params=pltpu.CompilerParams(vmem_limit_bytes=VMEM_LIMIT),
        cost_estimate=pl.CostEstimate(
            flops=29_000_000_000, bytes_accessed=100_000_000, transcendentals=2_000_000
        ),
    )(x_slots, dy_slots, gate_slots, w_gate, w_up, w_down)


def run_weights(x_slots, dy_slots, dgate, dup, hgated):
    experts, rows, width = x_slots.shape
    ff = dgate.shape[2]
    spec, f32 = expert_spec, jnp.float32
    wide = jax.ShapeDtypeStruct((experts, width, ff), f32)
    return pl.pallas_call(
        weights_kernel,
        name="expert_weights",
        grid=(experts,),
        in_specs=[spec(rows, width)] * 2 + [spec(rows, ff)] * 3,
        out_specs=(spec(width, ff), spec(width, ff), spec(ff, width)),
        out_shape=(wide, wide, jax.ShapeDtypeStruct((experts, ff, width), f32)),
        compiler_params=pltpu.CompilerParams(vmem_limit_bytes=VMEM_LIMIT),
        cost_estimate=pl.CostEstimate(
            flops=15_000_000_000, bytes_accessed=100_000_000, transcendentals=0
        ),
    )(x_slots, dy_slots, dgate, dup, hgated)


def plain_onehot(routes_all, first_expert, local_experts):
    sources, rows = routes_all.shape[0], routes_all.shape[1]
    experts = jnp.arange(local_experts, dtype=jnp.int32) + first_expert
    member = jnp.any(routes_all[:, :, :, None] == experts, axis=2).astype(jnp.int32)
    rank = jnp.cumsum(member, axis=1) - member
    rank = jnp.where(member > 0, rank, -1)
    return (
        rank.transpose(0, 2, 1)[:, :, None, :] == jnp.arange(CAP, dtype=jnp.int32)[:, None]
    ).astype(jnp.bfloat16)


def plain_experts(moe_low, cotangent, routes, gates, w_gate, w_up, w_down):
    both = ("dp", "tensor")
    local_experts = w_gate.shape[0]
    width = moe_low.shape[1]
    f32 = jnp.float32
    routes_all = lax.all_gather(routes, both, axis=0)
    x_all = lax.all_gather(moe_low, both, axis=0)
    dy_all = lax.all_gather(cotangent, both, axis=0)
    gates_all = lax.all_gather(gates, both, axis=0)
    first_expert = lax.axis_index("dp") * local_experts
    onehot = plain_onehot(routes_all, first_expert, local_experts)
    take = functools.partial(jnp.einsum, "sect,std->escd")
    flat = (local_experts, -1, width)
    x_slots = take(onehot, x_all).reshape(flat)
    dy_slots = take(onehot, dy_all).reshape(flat)
    experts = jnp.arange(local_experts, dtype=jnp.int32) + first_expert
    gates_here = jnp.sum(
        jnp.where(routes_all[..., None] == experts, gates_all[..., None], 0.0), axis=2
    )
    weight = jnp.einsum(
        "sect,ste->esc", onehot.astype(f32), gates_here, precision=lax.Precision.HIGHEST
    ).reshape(local_experts, -1)[..., None]
    mm = functools.partial(jnp.einsum, preferred_element_type=f32)
    gate_pre = mm("ecd,edf->ecf", x_slots, w_gate)
    up_pre = mm("ecd,edf->ecf", x_slots, w_up)
    raw = mm("ecd,efd->ecf", dy_slots, w_down)
    sig = jax.nn.sigmoid(gate_pre)
    silu = gate_pre * sig
    hidden = silu * up_pre
    hgated = (weight * hidden).astype(jnp.bfloat16)
    route_grad = jnp.sum(hidden * raw, axis=2).reshape(local_experts, -1, CAP)
    grad_hidden = weight * raw
    dgate = (grad_hidden * up_pre * sig * (1.0 + gate_pre * (1.0 - sig))).astype(jnp.bfloat16)
    dup = (grad_hidden * silu).astype(jnp.bfloat16)
    y_slots = mm("ecf,efd->ecd", hgated, w_down).astype(jnp.bfloat16)
    gin_slots = (mm("ecf,edf->ecd", dgate, w_gate) + mm("ecf,edf->ecd", dup, w_up)).astype(
        jnp.bfloat16
    )
    grads = (
        mm("ecd,ecf->edf", x_slots, dgate),
        mm("ecd,ecf->edf", x_slots, dup),
        mm("ecf,ecd->efd", hgated, dy_slots),
    )

    def give_back(slots):
        slots = slots.reshape(local_experts, -1, CAP, width)
        rows = mm("sect,escd->std", onehot, slots).astype(jnp.bfloat16)
        return lax.psum_scatter(
            rows.reshape(-1, width), both, scatter_dimension=0, tiled=True
        ).astype(f32)

    here = jnp.einsum(
        "sect,esc->ste", onehot.astype(f32), route_grad, precision=lax.Precision.HIGHEST
    )
    spread = jnp.zeros(here.shape[:2] + (EXPERTS,), f32)
    spread = lax.dynamic_update_slice(spread, here, (0, 0, first_expert))
    grad_gates = lax.psum_scatter(
        spread.reshape(-1, EXPERTS), both, scatter_dimension=0, tiled=True
    )
    return (give_back(y_slots), grad_gates, give_back(gin_slots), lambda own_rows: grads)


def routed_experts(moe_low, cotangent, routes, gates, w_gate, w_up, w_down, dispatched):
    if dispatched is None:
        return plain_experts(moe_low, cotangent, routes, gates, w_gate, w_up, w_down)
    dy_slots, onehot, all_routes = dispatched
    width = moe_low.shape[1]
    x_slots, gate_slots = gather_slots(moe_low, gates.T, onehot, all_routes)
    y_slots, gin_slots, *middle = run_experts(
        x_slots, dy_slots, gate_slots, w_gate, w_up, w_down
    )
    sums = return_rows(y_slots, onehot, 2)
    grad_in = return_rows(gin_slots, onehot, 3)
    grad_gates = sums[:, width : width + EXPERTS] + sums[:, width + EXPERTS :]

    def weight_grads(own_rows):
        hgated, unused = lax.optimization_barrier((middle[2], own_rows))
        return run_weights(x_slots, dy_slots, middle[0], middle[1], hgated)

    return (sums[:, :width], grad_gates, grad_in, weight_grads)


def own_kernels(tokens, w_gate):
    return (
        lax.axis_size("dp") == 8
        and lax.axis_size("tensor") == 4
        and tokens.shape == (128, 2048)
        and w_gate.shape[0] == 8
    )


def side_columns(pieces, rows):
    filled = [jnp.pad(p, ((0, rows - p.shape[0]), (0, 0))) for p in pieces]
    used = sum(p.shape[1] for p in filled)
    return jnp.concatenate(filled + [jnp.zeros((rows, 128 - used), filled[0].dtype)], axis=1)


def body(
    tokens,
    cotangent,
    lengths,
    seq_order,
    routes,
    attn_gain,
    w_query,
    w_key,
    w_value,
    w_output,
    query_gain,
    key_gain,
    ffn_gain,
    router,
    w_gate,
    w_up,
    w_down,
):
    tok_rows, model_width = tokens.shape
    tensor_count = lax.axis_size("tensor")
    data_count = lax.axis_size("dp")
    group_rows_count = tok_rows * tensor_count
    block_rows = min(group_rows_count, 512)
    shard = w_query.shape[0]
    heads_width = w_query.shape[1]
    gain_rows = query_gain.shape[0]
    low = jnp.bfloat16
    f32 = jnp.float32

    own = own_kernels(tokens, w_gate)

    seq_ids, positions = arrival_layout(lengths[0], seq_order[0])
    resid_in = tokens.astype(f32)
    if own:
        gain_list = [attn_gain, ffn_gain, query_gain, key_gain]
        filled = sum(part.shape[0] for part in gain_list)
        gains = jnp.concatenate(gain_list + [jnp.zeros((1024 - filled,), low)])
        gains = gains.reshape(8, 128).astype(f32)
        shards = (w_query, w_key, w_value, w_output, jnp.pad(router, ((0, 0), (0, 128 - EXPERTS))))
        seq_float = seq_ids.astype(f32)
        lane = jnp.arange(HD, dtype=jnp.int32)
        frequency = THETA ** (-(lane % (HD // 2)).astype(f32) / (HD // 2))
        angles = positions.astype(f32)[:, None] * frequency[None, :]
        tables = (
            jnp.cos(angles),
            jnp.sin(angles) * jnp.where(lane < HD // 2, -1.0, 1.0),
            jnp.broadcast_to(seq_float[:, None], (group_rows_count, 128)),
            jnp.broadcast_to(seq_float[None, :], (8, group_rows_count)),
        )
        (
            weights, group_tokens, dy_slots, all_gains, onehot, all_routes, group_rows,
            *attention, attn_out,
        ) = front(shards, tokens, cotangent, routes.T.astype(f32), gains, *tables, heads_width)
        dispatched = (dy_slots, onehot, all_routes)
        group_tokens = group_tokens.reshape(-1, model_width)
        full_router = weights[:, 4 * heads_width : 4 * heads_width + EXPERTS]
        attn_scale = all_gains[:, :2].reshape(-1)
        ffn_scale = all_gains[:, 2:4].reshape(-1)
    else:
        side = side_columns(
            [router, attn_gain[:, None], ffn_gain[:, None], query_gain[:, None], key_gain[:, None]],
            shard,
        )
        packed = jnp.concatenate([w_query, w_key, w_value, w_output.T, side], axis=1)
        weights = lax.all_gather(packed, "dp", axis=0, tiled=True)
        group_tokens = lax.all_gather(tokens, "tensor", axis=0, tiled=True)
        dispatched = None
        full_query = weights[:, :heads_width]
        full_key = weights[:, heads_width : 2 * heads_width]
        full_value = weights[:, 2 * heads_width : 3 * heads_width]
        output_t = weights[:, 3 * heads_width : 4 * heads_width]
        extras = weights[:, 4 * heads_width :]
        full_router = extras[:, :EXPERTS]
        attn_scale = extras[:, EXPERTS].astype(f32)
        ffn_scale = extras[:, EXPERTS + 1].astype(f32)
        gain_columns = extras.reshape(data_count, shard, 128)[:, :gain_rows, EXPERTS + 2 : EXPERTS + 4]
        query_scale = gain_columns[:, :, 0].reshape(-1).astype(f32)
        key_scale = gain_columns[:, :, 1].reshape(-1).astype(f32)

        cosines, sines = rope_tables(positions)
        group_rows = norm_apply(group_tokens.astype(f32), attn_scale).astype(low)
        proj_query = jnp.dot(group_rows, full_query, preferred_element_type=f32)
        proj_key = jnp.dot(group_rows, full_key, preferred_element_type=f32)
        value_flat = jnp.dot(group_rows, full_value, preferred_element_type=f32).astype(low)
        value_low = value_flat.reshape(group_rows_count, -1, HD)
        query_low = head_norm_rope(proj_query, query_scale, cosines, sines).astype(low)
        key_low = head_norm_rope(proj_key, key_scale, cosines, sines).astype(low)
        context, row_lse = attend(query_low, key_low, value_low, seq_ids, block_rows)
        context_low = context.reshape(group_rows_count, -1).astype(low)
        attn_out = lax.psum_scatter(
            lax.dot_general(
                context_low, output_t, (((1,), (1,)), ((), ())), preferred_element_type=f32
            ).astype(low),
            "tensor",
            scatter_dimension=0,
            tiled=True,
        ).astype(f32)
    resid_mid = resid_in + attn_out
    moe_low = norm_apply(resid_mid, ffn_scale).astype(low)
    logits = jnp.dot(moe_low, full_router, preferred_element_type=f32)
    route_match = routes[:, :, None] == jnp.arange(EXPERTS, dtype=jnp.int32)[None, None, :]
    picked_logits = jnp.sum(jnp.where(route_match, logits[:, None, :], 0.0), axis=-1)
    gate_peak = jnp.max(picked_logits, axis=1, keepdims=True)
    gate_raw = jnp.exp(picked_logits - gate_peak)
    gates = gate_raw / jnp.sum(gate_raw, axis=1, keepdims=True)
    dense_gates = jnp.sum(jnp.where(route_match, gates[:, :, None], 0.0), axis=1)

    moe_out, grad_gates, grad_from_experts, expert_weight_grads = routed_experts(
        moe_low, cotangent, routes, gates, w_gate, w_up, w_down, dispatched
    )
    layer_out = (resid_mid + moe_out).astype(low)
    stat_terms = jnp.stack(
        [jnp.sum(resid_mid * resid_mid), jnp.sum(attn_out * attn_out), jnp.sum(moe_out * moe_out)]
    )
    grad_out = cotangent.astype(f32)
    inner_gate = jnp.sum(dense_gates * grad_gates, axis=1, keepdims=True)
    grad_logits_low = (dense_gates * (grad_gates - inner_gate)).astype(low)
    grad_router_part = jnp.dot(moe_low.T, grad_logits_low, preferred_element_type=f32)
    grad_moe_in = grad_from_experts + jnp.dot(
        grad_logits_low, full_router.T, preferred_element_type=f32
    )
    unused_mid, ffn_back = jax.vjp(norm_apply, resid_mid, ffn_scale)
    grad_mid_norm, grad_ffn_part = ffn_back(grad_moe_in)
    grad_mid = grad_out + grad_mid_norm
    grad_attn_low = grad_mid.astype(low)
    grad_attn_rows = lax.all_gather(grad_attn_low, "tensor", axis=0, tiled=True)
    grad_gate_w, grad_up_w, grad_down = expert_weight_grads(grad_attn_low)
    tn = (((0,), (0,)), ((), ()))
    if own:
        router_side = grad_router_part.reshape(8, 2, 128, EXPERTS).swapaxes(1, 2).reshape(8, 128, 128)

        side = jnp.concatenate(
            [
                router_side,
                jnp.zeros((8, 2, 128), f32),
                grad_ffn_part.reshape(8, 2, 128),
                jnp.zeros((8, 12, 128), f32),
            ],
            axis=1,
        ).astype(low)
        stats = jnp.pad(stat_terms[None, :], ((6, 9), (0, 125)))
        grads_qkv, grad_out_w, grad_normed, small = finish(
            group_rows, group_tokens, attention, grad_attn_rows, weights, (all_gains,) + tables, side, stats
        )
        grad_router = small[:128].reshape(128, 2, EXPERTS).swapaxes(0, 1).reshape(256, EXPERTS)
        grad_attn_gain = small[128:130].reshape(-1)
        grad_ffn_gain = small[130:132].reshape(-1)
        first_lane = lax.axis_index("dp") * gain_rows
        grad_query_gain = lax.dynamic_slice(small[132], (first_lane,), (gain_rows,))
        grad_key_gain = lax.dynamic_slice(small[133], (first_lane,), (gain_rows,))
        stat_totals = small[134, :3]
        unused_in, attn_back = jax.vjp(lambda values: norm_apply(values, attn_scale), resid_in)
        (grad_in_norm,) = attn_back(grad_normed)
    else:
        grad_ctx_low = jnp.dot(grad_attn_rows, output_t, preferred_element_type=f32).astype(low)
        grad_query, grad_key, grad_value = attend_back(
            query_low,
            key_low,
            value_low,
            seq_ids,
            row_lse,
            grad_ctx_low.reshape(value_low.shape),
            block_rows,
        )
        grad_value_low = grad_value.reshape(group_rows_count, -1).astype(low)
        unused_query, query_back = jax.vjp(
            lambda projected, head_gain: head_norm_rope(projected, head_gain, cosines, sines),
            proj_query,
            query_scale,
        )
        grad_proj_query, grad_query_gain_part = query_back(grad_query)
        unused_key, key_back = jax.vjp(
            lambda projected, head_gain: head_norm_rope(projected, head_gain, cosines, sines),
            proj_key,
            key_scale,
        )
        grad_proj_key, grad_key_gain_part = key_back(grad_key)
        grad_query_low = grad_proj_query.astype(low)
        grad_key_low = grad_proj_key.astype(low)
        head_grads = (grad_query_low, grad_key_low, grad_value_low)
        weight_grads = [
            lax.dot_general(group_rows, part, tn, preferred_element_type=f32) for part in head_grads
        ]
        grad_output_t = lax.dot_general(grad_attn_rows, context_low, tn, preferred_element_type=f32)
        total_rows = jnp.dot(grad_query_low, full_query.T, preferred_element_type=f32)
        total_rows = total_rows + jnp.dot(grad_key_low, full_key.T, preferred_element_type=f32)
        total_rows = total_rows + jnp.dot(grad_value_low, full_value.T, preferred_element_type=f32)
        grad_normed = lax.psum_scatter(
            total_rows.astype(low), "tensor", scatter_dimension=0, tiled=True
        ).astype(f32)
        unused_in, attn_back = jax.vjp(norm_apply, resid_in, attn_scale)
        grad_in_norm, grad_attn_part = attn_back(grad_normed)

        def gain_column(part):
            cut = part.astype(low).reshape(data_count, gain_rows, 1)
            return jnp.pad(cut, ((0, 0), (0, shard - gain_rows), (0, 0))).reshape(-1, 1)

        side_grads = side_columns(
            [
                grad_router_part.astype(low),
                grad_attn_part.astype(low)[:, None],
                grad_ffn_part.astype(low)[:, None],
                gain_column(grad_query_gain_part),
                gain_column(grad_key_gain_part),
            ],
            model_width,
        )
        packed_grads = jnp.concatenate(
            [part.astype(low) for part in weight_grads] + [grad_output_t.astype(low), side_grads],
            axis=1,
        )
        reduced = lax.psum_scatter(packed_grads, "dp", scatter_dimension=0, tiled=True).astype(f32)
        side_total, stat_totals = lax.psum(
            (reduced[:, 4 * heads_width : 4 * heads_width + EXPERTS + 4], stat_terms), "tensor"
        )
        grads_qkv = reduced[:, : 3 * heads_width]
        grad_out_w = reduced[:, 3 * heads_width : 4 * heads_width].T
        grad_attn_gain = side_total[:, EXPERTS]
        grad_ffn_gain = side_total[:, EXPERTS + 1]
        grad_query_gain = side_total[:gain_rows, EXPERTS + 2]
        grad_key_gain = side_total[:gain_rows, EXPERTS + 3]
        grad_router = side_total[:, :EXPERTS]
    grad_tokens = grad_mid + grad_in_norm
    rms_stats = jnp.sqrt(stat_totals / (group_rows_count * model_width))[None, :]
    return (
        layer_out,
        grad_tokens,
        grad_attn_gain,
        grads_qkv[:, :heads_width],
        grads_qkv[:, heads_width : 2 * heads_width],
        grads_qkv[:, 2 * heads_width :],
        grad_out_w,
        grad_query_gain,
        grad_key_gain,
        grad_ffn_gain,
        grad_router,
        grad_gate_w,
        grad_up_w,
        grad_down,
        rms_stats,
    )


def solution(mesh):
    in_specs = (
        P(("dp", "tensor"), None),
        P(("dp", "tensor"), None),
        P("dp", None),
        P("dp", None),
        P(("dp", "tensor"), None),
        P("dp"),
        P("dp", "tensor"),
        P("dp", "tensor"),
        P("dp", "tensor"),
        P("tensor", "dp"),
        P("dp"),
        P("dp"),
        P("dp"),
        P("dp", None),
        P("dp", None, "tensor"),
        P("dp", None, "tensor"),
        P("dp", "tensor", None),
    )
    out_specs = (
        P(("dp", "tensor"), None),
        P(("dp", "tensor"), None),
        P("dp"),
        P("dp", "tensor"),
        P("dp", "tensor"),
        P("dp", "tensor"),
        P("tensor", "dp"),
        P("dp"),
        P("dp"),
        P("dp"),
        P("dp", None),
        P("dp", None, "tensor"),
        P("dp", None, "tensor"),
        P("dp", "tensor", None),
        P("dp", None),
    )
    return jax.shard_map(body, mesh=mesh, in_specs=in_specs, out_specs=out_specs, check_vma=False)
```

```python
import functools

import jax
import jax.numpy as jnp
from jax import lax
from jax.experimental import pallas as pl
from jax.experimental.pallas import tpu as pltpu
from jax.sharding import PartitionSpec as P

HD = 128
EXPERTS = 64
TOPK = 8
CAP = 18


EPSILON = 1e-05
THETA = 10000.0
NEGATIVE = -1e30


def inv_rms(values):
    return lax.rsqrt(jnp.mean(values * values, axis=-1, keepdims=True) + EPSILON)


def norm_apply(values, scale_gain):
    return values * inv_rms(values) * scale_gain


def arrival_layout(seq_lengths, order_row):
    row_total = order_row.shape[0]
    placed = jnp.arange(row_total, dtype=jnp.int32)
    order = jnp.arange(seq_lengths.shape[0], dtype=jnp.int32)
    upto = order[None, :] <= order[:, None]
    seq_ends = jnp.sum(jnp.where(upto, seq_lengths[None, :], 0), axis=1)
    seq_starts = seq_ends - seq_lengths
    member = jnp.sum((placed[:, None] >= seq_ends[None, :]).astype(jnp.int32), axis=1)
    chosen = member[:, None] == jnp.arange(seq_lengths.shape[0], dtype=jnp.int32)[None, :]
    seq_begin = jnp.sum(jnp.where(chosen, seq_starts[None, :], 0), axis=1)
    here = order_row[None, :] == placed[:, None]
    seq_ids = jnp.sum(jnp.where(here, member[None, :], 0), axis=1)
    positions = jnp.sum(jnp.where(here, (placed - seq_begin)[None, :], 0), axis=1)
    return (seq_ids, positions)


def rope_tables(positions):
    half_dim = HD // 2
    frequency = THETA ** (-jnp.arange(half_dim, dtype=jnp.float32) / half_dim)
    angles = positions.astype(jnp.float32)[:, None] * frequency[None, :]
    return (jnp.cos(angles)[:, None, :], jnp.sin(angles)[:, None, :])


def head_norm_rope(projected, head_gain, cosines, sines):
    shaped = projected.reshape(projected.shape[0], -1, HD)
    normed_heads = norm_apply(shaped, head_gain)
    first_half = normed_heads[..., : HD // 2]
    second_half = normed_heads[..., HD // 2 :]
    return jnp.concatenate(
        [first_half * cosines - second_half * sines, second_half * cosines + first_half * sines],
        axis=-1,
    )


def masked_scores(query_block, key_low, seq_block, seq_ids):
    score_scale = HD ** (-0.5)
    scores = (
        jnp.einsum("qhd,khd->hqk", query_block, key_low, preferred_element_type=jnp.float32)
        * score_scale
    )
    same_seq = (seq_block[:, None] == seq_ids[None, :])[None]
    return jnp.where(same_seq, scores, NEGATIVE)


def attend(query_low, key_low, value_low, seq_ids, block_rows):
    num_blocks = query_low.shape[0] // block_rows
    query_blocks = query_low.reshape(num_blocks, block_rows, query_low.shape[1], HD)
    seq_blocks = seq_ids.reshape(num_blocks, block_rows)

    def one_block(inputs):
        query_block, seq_block = inputs
        scores = masked_scores(query_block, key_low, seq_block, seq_ids)
        row_peak = jnp.max(scores, axis=-1, keepdims=True)
        raised = jnp.exp(scores - row_peak)
        row_total = jnp.sum(raised, axis=-1, keepdims=True)
        probs_low = (raised / row_total).astype(jnp.bfloat16)
        context = jnp.einsum(
            "hqk,khd->qhd", probs_low, value_low, preferred_element_type=jnp.float32
        )
        return (context, row_peak + jnp.log(row_total))

    context, row_lse = lax.map(one_block, (query_blocks, seq_blocks))
    return (context.reshape(query_low.shape), row_lse)


def attend_back(query_low, key_low, value_low, seq_ids, row_lse, grad_ctx_low, block_rows):
    score_scale = HD ** (-0.5)
    num_blocks = query_low.shape[0] // block_rows
    block_shape = (num_blocks, block_rows, query_low.shape[1], HD)

    def one_block(carry, inputs):
        grad_key_sum, grad_value_sum = carry
        query_block, seq_block, lse_block, grad_block = inputs
        scores = masked_scores(query_block, key_low, seq_block, seq_ids)
        probs = jnp.exp(scores - lse_block)
        probs_low = probs.astype(jnp.bfloat16)
        grad_value_sum = grad_value_sum + jnp.einsum(
            "hqk,qhd->khd", probs_low, grad_block, preferred_element_type=jnp.float32
        )
        grad_probs = jnp.einsum(
            "qhd,khd->hqk", grad_block, value_low, preferred_element_type=jnp.float32
        )
        inner_sum = jnp.sum(probs * grad_probs, axis=-1, keepdims=True)
        grad_scores = (probs * (grad_probs - inner_sum)).astype(jnp.bfloat16)
        grad_query_block = (
            jnp.einsum("hqk,khd->qhd", grad_scores, key_low, preferred_element_type=jnp.float32)
            * score_scale
        )
        grad_key_sum = (
            grad_key_sum
            + jnp.einsum(
                "hqk,qhd->khd", grad_scores, query_block, preferred_element_type=jnp.float32
            )
            * score_scale
        )
        return ((grad_key_sum, grad_value_sum), grad_query_block)

    zeros_heads = jnp.zeros(query_low.shape, jnp.float32)
    carried, grad_query = lax.scan(
        one_block,
        (zeros_heads, zeros_heads),
        (
            query_low.reshape(block_shape),
            seq_ids.reshape(num_blocks, block_rows),
            row_lse,
            grad_ctx_low.reshape(block_shape),
        ),
    )
    return (grad_query.reshape(query_low.shape), carried[0], carried[1])


MESH = pl.DeviceIdType.MESH
VMEM_LIMIT = 60 * 1024 * 1024
MAIN = 16
SPARE = CAP - MAIN


def at(dp_index, z_index):
    return {"dp": dp_index, "tensor": z_index}


def place():
    dp = lax.axis_index("dp")
    z = lax.axis_index("tensor")
    core, x, y = dp % 2, (dp // 2) % 2, dp // 4
    return dp, z, 1 - 2 * core, 2 - 4 * x, 4 - 8 * y


def greet(peers, extra=None, has_extra=None, count=0):
    barrier = pltpu.get_barrier_semaphore()
    for peer in peers:
        pl.semaphore_signal(barrier, inc=1, device_id=at(*peer), device_id_type=MESH)
    if extra is not None:

        @pl.when(has_extra)
        def _():
            pl.semaphore_signal(barrier, inc=1, device_id=at(*extra), device_id_type=MESH)

    pl.semaphore_wait(barrier, len(peers) + count)


def when_or_now(cond, action):
    if cond is None:
        action()
    else:
        pl.when(cond)(action)


def slot_matrix(routes_block, source, first_expert):
    experts = lax.broadcasted_iota(jnp.int32, (8, 128), 0) + first_expert
    member = jnp.zeros((8, 128), jnp.float32)
    for j in range(TOPK):
        member = member + (routes_block[j : j + 1, :] == experts.astype(jnp.float32)).astype(jnp.float32)
    earlier = (
        lax.broadcasted_iota(jnp.int32, (128, 128), 0)
        < lax.broadcasted_iota(jnp.int32, (128, 128), 1)
    ).astype(jnp.bfloat16)
    rank = jnp.dot(member.astype(jnp.bfloat16), earlier, preferred_element_type=jnp.float32)
    rank = jnp.where(member > 0.5, rank, -1.0).astype(jnp.int32)
    spread = jnp.broadcast_to(rank[:, None, :], (8, MAIN, 128)).reshape(128, 128)
    row = lax.broadcasted_iota(jnp.int32, (128, 128), 0) % MAIN
    main = spread == row
    spare = jnp.logical_and(row // SPARE == source % 8, spread == MAIN + row % SPARE)
    return jnp.concatenate(
        [main.astype(jnp.float32), spare.astype(jnp.float32)], axis=0
    ).astype(jnp.bfloat16)


class LineScatter:
    def __init__(self, dp, z, blocks, rze, rzm, rzf, zsend, zrecv):
        self.dp, self.z = dp, z
        self.zr, self.zo = z + 1 - 2 * (z % 2), 3 - z
        self.mid, self.end = z * (3 - z) > 0, z * (3 - z) < 1
        self.zs = [3 - 3 * (z // 2), 2 - z // 2, self.zr, z]
        self.blocks, self.rze, self.rzm, self.rzf = blocks, rze, rzm, rzf
        self.zsend, self.zrecv = zsend, zrecv
        self.outward = [self.copy(blocks.at[k], rze.at[k], k, self.zr) for k in range(3)]
        self.sends = []

    def copy(self, src, dst, index, z_to):
        return pltpu.make_async_remote_copy(
            src, dst, self.zsend.at[index], self.zrecv.at[index],
            device_id=at(self.dp, z_to), device_id_type=MESH,
        )

    def ready(self, k):
        pl.when(self.end)(functools.partial(self.outward[k].start))
        self.sends.append((self.outward[k], self.end))

    def add(self, k, part):
        total = self.blocks[k].astype(jnp.float32) + part[...].astype(jnp.float32)
        self.blocks[k] = total.astype(jnp.bfloat16)

    def onward(self, k):
        if k < 2:
            copy = self.copy(self.blocks.at[k], self.rzm.at[k], 3 + k, self.zo)
        else:
            copy = self.copy(self.blocks.at[k], self.rzf, 5, self.zr)
        self.sends.append((copy, self.mid))

        @pl.when(self.mid)
        def _():
            if k < 2:
                self.outward[k].wait_recv()
                self.add(k, self.rze.at[k])
            else:
                self.copy(self.blocks.at[0], self.rzm.at[0], 3, self.zo).wait_recv()
                self.add(k, self.rzm.at[0])
            copy.start()

    def last(self, out_ref):
        @pl.when(self.end)
        def _():
            self.copy(self.blocks.at[2], self.rzf, 5, self.zr).wait_recv()
            out_ref[...] = out_ref[...] + self.rzf[...].astype(jnp.float32)

        @pl.when(self.mid)
        def _():
            self.outward[2].wait_recv()
            self.copy(self.blocks.at[1], self.rzm.at[1], 4, self.zo).wait_recv()
            out_ref[...] = (
                out_ref[...]
                + self.rze[2].astype(jnp.float32)
                + self.rzm[1].astype(jnp.float32)
            )

    def drain(self):
        for copy, cond in self.sends:
            pl.when(cond)(functools.partial(copy.wait_send))

    @staticmethod
    def scratch(width):
        low, dma = jnp.bfloat16, pltpu.SemaphoreType.DMA
        return [
            pltpu.VMEM((3, 128, width), low),
            pltpu.VMEM((3, 128, width), low),
            pltpu.VMEM((2, 128, width), low),
            pltpu.VMEM((128, width), low),
            dma((6,)),
            dma((6,)),
        ]


class AllGather:
    def __init__(self, held, own_ref, ssem, rsem, metas=None, own_meta=None, msem=None, mrsem=None):
        self.dp, self.z, self.dc, self.dx, self.dy = place()
        z = self.z
        self.zr, self.zo = z + 1 - 2 * (z % 2), 3 - z
        self.mid = z * (3 - z) > 0
        self.zs = [z, self.zr, 2 - z // 2, 3 - 3 * (z // 2)]
        self.held, self.own_ref, self.ssem, self.rsem = held, own_ref, ssem, rsem
        self.metas, self.own_meta, self.msem, self.mrsem = metas, own_meta, msem, mrsem
        self.sends = []

    def send(self, block, part, dp_to, z_to, cond=None, own=False):
        half = pl.ds(part * 64, 64)
        view = self.held.at[block, half]
        source = self.own_ref.at[half] if own else view
        index = len(self.sends)
        copies = [
            pltpu.make_async_remote_copy(
                source, view, self.ssem.at[index], self.rsem.at[block, part],
                device_id=at(dp_to, z_to), device_id_type=MESH,
            )
        ]
        if part == 0 and self.metas is not None:
            copies.append(
                pltpu.make_async_remote_copy(
                    self.own_meta if own else self.metas.at[block], self.metas.at[block],
                    self.msem.at[index], self.mrsem.at[block],
                    device_id=at(dp_to, z_to), device_id_type=MESH,
                )
            )
        self.sends.append((copies, cond))

        def go():
            for copy in copies:
                copy.start()

        when_or_now(cond, go)

    def arrive(self, block, part):
        view = self.held.at[block, pl.ds(part * 64, 64)]
        here = dict(device_id=at(self.dp, self.zr), device_id_type=MESH)
        pltpu.make_async_remote_copy(
            view, view, self.ssem.at[0], self.rsem.at[block, part], **here
        ).wait_recv()
        if part == 0 and self.metas is not None:
            pltpu.make_async_remote_copy(
                self.metas.at[block], self.metas.at[block], self.msem.at[0], self.mrsem.at[block],
                **here
            ).wait_recv()

    def first(self, k):
        dp, z, dx, dy, dc = self.dp, self.z, self.dx, self.dy, self.dc
        block = dp * 4 + self.zs[k]
        own = k == 0
        for part in (0, 1):
            if k > 0:
                self.arrive(block, part)
            if k == 0:
                self.send(block, part, dp, self.zr, None, own)
                self.send(block, part, dp, self.zo, self.mid, own)
            else:
                self.send(block, part, dp, self.zo if k == 1 else self.zr, self.mid)
            self.send(block, part, dp + (dx if part == 0 else dy), z, None, own)
        self.send(block, 1, dp + dx, z, None, own)
        self.send(block, 0, dp + dy, z, None, own)
        self.send(block, 0, dp + dc, z, None, own)
        self.send(block, 1, dp + dc, z, None, own)

    def second(self, k):
        dp, z, dx, dy, dc = self.dp, self.z, self.dx, self.dy, self.dc
        bx, by = (dp + dx) * 4 + self.zs[k], (dp + dy) * 4 + self.zs[k]
        self.arrive(bx, 0)
        self.send(bx, 0, dp + dy, z)
        self.send(bx, 0, dp + dc, z)
        self.arrive(by, 1)
        self.send(by, 1, dp + dx, z)
        self.send(by, 1, dp + dc, z)
        self.arrive(bx, 1)
        self.send(bx, 1, dp + dc, z)
        self.arrive(by, 0)
        self.send(by, 0, dp + dc, z)

    def third(self, k):
        block = (self.dp + self.dx + self.dy) * 4 + self.zs[k]
        for part in (0, 1):
            self.arrive(block, part)
            self.send(block, part, self.dp + self.dc, self.z)

    def across(self, k, step):
        block = (self.dp + self.dc + step) * 4 + self.zs[k]
        self.arrive(block, 0)
        self.arrive(block, 1)

    def drain(self):
        for copies, cond in self.sends:

            def done(copies=copies):
                for copy in copies:
                    copy.wait_send()

            when_or_now(cond, done)


class Dispatcher:
    def __init__(self, held, stage, spare, slots_ref, osem):
        self.held, self.stage, self.spare = held, stage, spare
        self.slots_ref, self.osem = slots_ref, osem
        self.count = 0

    def put(self, start, slot):
        return pltpu.make_async_copy(
            self.stage.at[slot], self.slots_ref.at[:, pl.ds(start, MAIN), :], self.osem.at[slot]
        )

    def block(self, block, onehot):
        slot, group = self.count % 2, block // 8
        width = self.held.shape[2]
        if self.count >= 2:
            self.put(block * MAIN, slot).wait()

        def tile(step, carry):
            lanes = pl.ds(pl.multiple_of(step * 512, 512), 512)
            rows = jnp.dot(onehot, self.held[block, :, lanes], preferred_element_type=jnp.float32)
            self.stage[slot, :, :, lanes] = rows[:128].astype(jnp.bfloat16).reshape(8, MAIN, 512)
            extra = rows[128:].astype(jnp.bfloat16)
            self.spare[group, :, lanes] = self.spare[group, :, lanes] + extra
            return carry

        lax.fori_loop(0, width // 512, tile, 0)
        self.put(block * MAIN, slot).start()
        self.count += 1

    def end(self):
        width = self.held.shape[2]
        for group in range(4):
            slot = group % 2
            self.put(512 + group * MAIN, slot).wait()
            self.stage[slot] = self.spare[group].reshape(8, MAIN, width)
            self.put(512 + group * MAIN, slot).start()
        for slot in range(2):
            self.put(512, slot).wait()


def arrival_order(gather):
    dp, dc, dx, dy, zs = gather.dp, gather.dc, gather.dx, gather.dy, gather.zs
    order = []
    for k in range(6):
        column = []
        if k < 4:
            column.append((k, 0))
        if 1 <= k < 5:
            column += [(k - 1, dx), (k - 1, dy)]
        if k >= 2:
            column.append((k - 2, dx + dy))
        across = [(k - 1, dc)] if 1 <= k < 5 else []
        if k >= 2:
            across += [(k - 2, dc + step) for step in (dx, dy, dx + dy)]
        order.append([[(dp + to) * 4 + zs[j] for j, to in part] for part in (column, across)])
    return order


def gather_forward(gather, k):
    if k < 4:
        gather.first(k)
    if 1 <= k < 5:
        gather.second(k - 1)
    if k >= 2:
        gather.third(k - 2)


def gather_process(gather, order, k, process):
    for block in order[k][0]:
        process(block)
    for block in order[k][1]:
        gather.arrive(block, 0)
        gather.arrive(block, 1)
        process(block)


def rotate(values, cosines, sines):
    return values * cosines + pltpu.roll(values, HD // 2, 1) * sines


def head_probs(query, key, seq_column, seq_row):
    scores = lax.dot_general(
        query, key, (((1,), (1,)), ((), ())), preferred_element_type=jnp.float32
    ) * (HD ** (-0.5))
    scores = jnp.where(seq_column == seq_row, scores, NEGATIVE)
    raised = jnp.exp(scores - jnp.max(scores, axis=1, keepdims=True))
    return raised / jnp.sum(raised, axis=1, keepdims=True)


def head_gain(gains_ref, first):
    lane = lax.broadcasted_iota(jnp.int32, (8, 128), 1)
    keep = jnp.logical_and(lane >= first, lane < first + 16)
    total = jnp.zeros((8, 128), jnp.float32)
    for block in range(8):
        part = jnp.where(keep, jnp.broadcast_to(gains_ref[block, 4:5, :], (8, 128)), 0.0)
        shift = (16 * block - first) % 128
        total = total + (pltpu.roll(part, shift, 1) if shift else part)
    return total[:1]


def front_kernel(
    wq_ref, wk_ref, wv_ref, wo_ref, router_ref, tok_ref, cot_ref, routes_in, gains_in, cos_ref, sin_ref, seqc_ref, seqr_ref,
    weights_ref, group_ref, slots_ref, gains_ref, onehot_ref, routes_ref, normed_ref, projq_ref, projk_ref,
    query_ref, key_ref, value_ref, ctx_ref, out_ref,
    wheld, theld, gheld, held, metas, stage, spare, lsem, wsend, wrecv, gsend, grecv, zsend, zrecv,
    dsend, drecv, msend, mrecv, osem, fsem, *line_refs
):
    dp, z, dc, dx, dy = place()
    zr, zo = z + 1 - 2 * (z % 2), 3 - z
    mid = z * (3 - z) > 0
    f32, low = jnp.float32, jnp.bfloat16
    heads = query_ref.shape[1]
    width = tok_ref.shape[1]
    line = LineScatter(dp, z, *line_refs)
    gather = AllGather(held, cot_ref, dsend, drecv, metas, routes_in, msend, mrecv)
    order = arrival_order(gather)
    picker = Dispatcher(held, stage, spare, slots_ref, osem)
    own_block = dp * 4 + z
    own_rows = pl.ds(pl.multiple_of(dp * 256, 256), 256)
    fill = []
    for source, column, count in (
        (wq_ref, 0, heads), (wk_ref, heads, heads), (wv_ref, 2 * heads, heads),
        (wo_ref.at[pl.ds(0, 256)], 3 * heads, 256), (wo_ref.at[pl.ds(256, 256)], 3 * heads + 256, 256),
        (router_ref, 4 * heads, 128),
    ):
        target = wheld.at[own_rows, pl.ds(column, count)]
        fill.append(pltpu.make_async_copy(source, target, fsem.at[len(fill)]))
    for copy in fill:
        copy.start()
    greet([(dp + dc, z), (dp + dx, z), (dp + dy, z), (dp, zr)], (dp, zo), mid, z * (3 - z) // 2)
    sends = []

    def spot(block, part):
        return wheld.at[pl.ds(pl.multiple_of(block * 256 + part * 128, 128), 128)]

    def send(block, part, dp_to, own=False):
        source = spot(block, part)
        index = len(sends)
        copies = [
            pltpu.make_async_remote_copy(
                source, spot(block, part), wsend.at[index], wrecv.at[block, part],
                device_id=at(dp_to, z), device_id_type=MESH,
            )
        ]
        if part == 0:
            copies.append(
                pltpu.make_async_remote_copy(
                    gains_in if own else gheld.at[block], gheld.at[block],
                    gsend.at[index], grecv.at[block],
                    device_id=at(dp_to, z), device_id_type=MESH,
                )
            )
        for copy in copies:
            copy.start()
        sends.append(copies)

    def arrive(block, part):
        here = dict(device_id=at(dp + dx, z), device_id_type=MESH)
        pltpu.make_async_remote_copy(
            spot(block, part), spot(block, part), wsend.at[0], wrecv.at[block, part], **here
        ).wait_recv()
        if part == 0:
            pltpu.make_async_remote_copy(
                gheld.at[block], gheld.at[block], gsend.at[0], grecv.at[block], **here
            ).wait_recv()

    zsends = []

    def z_send(source, block, z_to, cond=None):
        copy = pltpu.make_async_remote_copy(
            source, theld.at[block], zsend.at[len(zsends)], zrecv.at[block],
            device_id=at(dp, z_to), device_id_type=MESH,
        )
        when_or_now(cond, functools.partial(copy.start))
        zsends.append((copy, cond))

    def z_arrive(block):
        pltpu.make_async_remote_copy(
            theld.at[block], theld.at[block], zsend.at[0], zrecv.at[block],
            device_id=at(dp, zr), device_id_type=MESH,
        ).wait_recv()

    z_send(tok_ref, z, zr)
    z_send(tok_ref, z, zo, mid)
    for copy in fill:
        copy.wait()
    send(dp, 0, dp + dx, True)
    send(dp, 1, dp + dy, True)
    send(dp, 1, dp + dx, True)
    send(dp, 0, dp + dy, True)
    send(dp, 0, dp + dc, True)
    send(dp, 1, dp + dc, True)
    local = [
        pltpu.make_async_copy(tok_ref, theld.at[z], lsem.at[1]),
        pltpu.make_async_copy(gains_in, gheld.at[dp], lsem.at[2]),
        pltpu.make_async_copy(cot_ref, held.at[own_block], lsem.at[3]),
        pltpu.make_async_copy(routes_in, metas.at[own_block], lsem.at[4]),
    ]
    for copy in local:
        copy.start()
    spare[...] = jnp.zeros_like(spare)
    z_arrive(zr)
    z_send(theld.at[zr], zr, zo, mid)
    bx, by, bxy = dp + dx, dp + dy, dp + dx + dy
    arrive(bx, 0)
    send(bx, 0, dp + dy)
    send(bx, 0, dp + dc)
    arrive(by, 1)
    send(by, 1, dp + dx)
    send(by, 1, dp + dc)
    far = 2 - z // 2
    z_arrive(far)
    z_send(theld.at[far], far, zr, mid)
    arrive(bx, 1)
    send(bx, 1, dp + dc)
    arrive(by, 0)
    send(by, 0, dp + dc)
    last = 3 - 3 * (z // 2)
    z_arrive(last)
    z_send(theld.at[last], last, zr, mid)
    for part in (0, 1):
        arrive(bxy, part)
        send(bxy, part, dp + dc)
    gather.first(0)
    for block in (dp, bx, by, bxy):
        for part in (0, 1):
            arrive(block + dc, part)
    for copy in local:
        copy.wait()
    kept = [
        pltpu.make_async_copy(wheld, weights_ref, lsem.at[0]),
        pltpu.make_async_copy(theld, group_ref, lsem.at[1]),
    ]
    for copy in kept:
        copy.start()

    def process(block):
        onehot = slot_matrix(metas[block], block, dp * 8)
        onehot_ref[block] = onehot
        picker.block(block, onehot)

    scale = jnp.concatenate(
        [gheld[j // 2, j % 2 : j % 2 + 1, :] for j in range(width // 128)], axis=1
    )

    def norm_rows(step, carry):
        values = theld[step].astype(f32)
        inverse = lax.rsqrt(jnp.mean(values * values, axis=1, keepdims=True) + EPSILON)
        rows = pl.ds(pl.multiple_of(step * 128, 128), 128)
        normed_ref[rows, :] = (values * inverse * scale).astype(low)
        return carry

    gains_ref[...] = gheld[...]
    lax.fori_loop(0, 4, norm_rows, 0)

    def project(column):
        cols = slice(column * heads, column * heads + heads)
        return jnp.dot(normed_ref[...], wheld[:, cols], preferred_element_type=f32)

    projq_ref[...] = project(0)
    projk_ref[...] = project(1)
    value_ref[...] = project(2).astype(low)
    gather_forward(gather, 1)
    process(own_block)
    cosines, sines = cos_ref[...], sin_ref[...]
    query_gain, key_gain = head_gain(gheld, 0), head_gain(gheld, 16)

    def one_head(h, carry):
        cols = pl.ds(pl.multiple_of(h * HD, HD), HD)
        for source, gain, target in (
            (projq_ref, query_gain, query_ref), (projk_ref, key_gain, key_ref),
        ):
            values = source[:, cols]
            inverse = lax.rsqrt(jnp.mean(values * values, axis=1, keepdims=True) + EPSILON)
            target[:, cols] = rotate(values * inverse * gain, cosines, sines).astype(low)
        for start in range(0, 512, 256):
            rows = slice(start, start + 256)
            probs = head_probs(
                query_ref[rows, cols], key_ref[:, cols], seqc_ref[rows, :1], seqr_ref[:1, :]
            )
            ctx_ref[rows, cols] = jnp.dot(
                probs.astype(low), value_ref[:, cols], preferred_element_type=f32
            ).astype(low)
        return carry

    lax.fori_loop(0, heads // HD // 2, one_head, 0)
    gather_forward(gather, 2)
    lax.fori_loop(heads // HD // 2, heads // HD, one_head, 0)
    for k in range(4):
        rows = pl.ds(pl.multiple_of(line.zs[k] * 128, 128), 128)
        for start in range(0, width, 256):
            lanes = slice(start, start + 256)
            piece = jnp.dot(
                ctx_ref[rows, :256], wheld[lanes, 3 * heads : 3 * heads + 256],
                preferred_element_type=f32,
            ) + jnp.dot(
                ctx_ref[rows, 256:], wheld[lanes, 3 * heads + 256 : 4 * heads],
                preferred_element_type=f32,
            )
            if k < 3:
                line.blocks[k, :, lanes] = piece.astype(low)
            else:
                out_ref[:, lanes] = piece
        if k < 3:
            line.ready(k)
    gather_forward(gather, 3)
    gather_process(gather, order, 1, process)
    line.onward(0)
    line.onward(1)
    gather_process(gather, order, 2, process)
    gather_forward(gather, 4)
    line.onward(2)
    gather_process(gather, order, 3, process)
    gather_forward(gather, 5)
    line.last(out_ref)
    gather_process(gather, order, 4, process)
    gather_process(gather, order, 5, process)
    picker.end()
    routes_ref[...] = metas[...]
    for copy in kept:
        copy.wait()
    for copies in sends:
        for copy in copies:
            copy.wait_send()
    for copy, cond in zsends:
        when_or_now(cond, functools.partial(copy.wait_send))
    gather.drain()
    line.drain()


def front(shards, tokens, cotangent, routes, gains, cosines, sines, seq_column, seq_row, heads):
    width = tokens.shape[1]
    rows = 4 * tokens.shape[0]
    f32, low = jnp.float32, jnp.bfloat16
    anywhere = pl.BlockSpec(memory_space=pl.ANY)
    vmem = pl.BlockSpec(memory_space=pltpu.VMEM)
    dma = pltpu.SemaphoreType.DMA
    narrow = jax.ShapeDtypeStruct((rows, heads), low)
    return pl.pallas_call(
        front_kernel,
        name="front",
        out_shape=(
            jax.ShapeDtypeStruct((width, 4 * heads + 128), low),
            jax.ShapeDtypeStruct((4, 128, width), low),
            jax.ShapeDtypeStruct((8, 576, width), low),
            jax.ShapeDtypeStruct((8, 8, 128), f32),
            jax.ShapeDtypeStruct((32, 256, 128), low),
            jax.ShapeDtypeStruct((32, 8, 128), f32),
            jax.ShapeDtypeStruct((rows, width), low),
            jax.ShapeDtypeStruct((rows, heads), f32),
            jax.ShapeDtypeStruct((rows, heads), f32),
            narrow, narrow, narrow, narrow,
            jax.ShapeDtypeStruct((128, width), f32),
        ),
        in_specs=[anywhere] * 5 + [vmem] * 8,
        out_specs=(anywhere,) * 3 + (vmem,) * 11,
        scratch_shapes=[
            pltpu.VMEM((width, 4 * heads + 128), low),
            pltpu.VMEM((4, 128, width), low),
            pltpu.VMEM((8, 8, 128), f32),
            pltpu.VMEM((32, 128, width), low),
            pltpu.VMEM((32, 8, 128), f32),
            pltpu.VMEM((2, 8, MAIN, width), low),
            pltpu.VMEM((4, 128, width), low),
            dma((9,)), dma((14,)), dma((8, 2)), dma((14,)), dma((8,)), dma((5,)), dma((4,)),
            dma((72,)), dma((32, 2)), dma((72,)), dma((32,)), dma((2,)), dma((6,)),
        ]
        + LineScatter.scratch(width),
        compiler_params=pltpu.CompilerParams(
            collective_id=0, has_side_effects=True, vmem_limit_bytes=VMEM_LIMIT
        ),
        cost_estimate=pl.CostEstimate(
            flops=5_000_000_000, bytes_accessed=100_000_000, transcendentals=2_000_000
        ),
    )(*shards, tokens, cotangent, routes, gains, cosines, sines, seq_column, seq_row)


def gather_kernel(
    x_ref, meta_ref, onehot_ref, routes_ref, slots_ref, gate_ref,
    held, metas, stage, spare, lsem, ssem, rsem, msem, mrsem, osem,
):
    dp, z, dc, dx, dy = place()
    own = dp * 4 + z
    gather = AllGather(held, held.at[own], ssem, rsem, metas, metas.at[own], msem, mrsem)
    order = arrival_order(gather)
    picker = Dispatcher(held, stage, spare, slots_ref, osem)
    local = [
        pltpu.make_async_copy(x_ref, held.at[own], lsem.at[0]),
        pltpu.make_async_copy(meta_ref, metas.at[own], lsem.at[1]),
    ]
    for copy in local:
        copy.start()
    greet(
        [(dp + dc, z), (dp + dx, z), (dp + dy, z), (dp, gather.zr)],
        (dp, gather.zo), gather.mid, z * (3 - z) // 2,
    )
    spare[...] = jnp.zeros_like(spare)
    gate_ref[:, 512:576, :] = jnp.zeros((8, 64, 128), jnp.float32)
    for copy in local:
        copy.wait()
    experts = (lax.broadcasted_iota(jnp.int32, (8, 128), 0) + dp * 8).astype(jnp.float32)

    def process(block):
        onehot = onehot_ref[block]
        gates_here = jnp.zeros((8, 128), jnp.float32)
        for j in range(TOPK):
            gates_here = gates_here + jnp.where(
                routes_ref[block, j : j + 1, :] == experts, metas[block, j : j + 1, :], 0.0
            )
        wide = jnp.broadcast_to(gates_here[:, None, :], (8, MAIN, 128)).reshape(128, 128)
        taken = onehot.astype(jnp.float32)
        main_gate = jnp.sum(taken[:128] * wide, axis=1, keepdims=True)
        spare_gate = jnp.sum(taken[128:] * wide, axis=1, keepdims=True)
        gate_ref[:, pl.ds(pl.multiple_of(block * MAIN, MAIN), MAIN), :] = jnp.broadcast_to(
            main_gate, (128, 128)
        ).reshape(8, MAIN, 128)
        spare_rows = pl.ds(pl.multiple_of(512 + (block // 8) * MAIN, MAIN), MAIN)
        gate_ref[:, spare_rows, :] = gate_ref[:, spare_rows, :] + jnp.broadcast_to(
            spare_gate, (128, 128)
        ).reshape(8, MAIN, 128)
        picker.block(block, onehot)

    for k in range(6):
        gather_forward(gather, k)
        gather_process(gather, order, k, process)
    picker.end()
    gather.drain()


def gather_slots(rows, meta, onehot, routes):
    count, width = rows.shape
    anywhere = pl.BlockSpec(memory_space=pl.ANY)
    vmem = pl.BlockSpec(memory_space=pltpu.VMEM)
    dma = pltpu.SemaphoreType.DMA
    return pl.pallas_call(
        gather_kernel,
        name="gather_x",
        out_shape=(
            jax.ShapeDtypeStruct((8, 576, width), jnp.bfloat16),
            jax.ShapeDtypeStruct((8, 576, 128), jnp.float32),
        ),
        in_specs=[anywhere, anywhere, vmem, vmem],
        out_specs=(anywhere, vmem),
        scratch_shapes=[
            pltpu.VMEM((32, count, width), jnp.bfloat16),
            pltpu.VMEM((32, 8, 128), jnp.float32),
            pltpu.VMEM((2, 8, MAIN, width), jnp.bfloat16),
            pltpu.VMEM((4, 128, width), jnp.bfloat16),
            dma((2,)), dma((72,)), dma((32, 2)), dma((72,)), dma((32,)), dma((2,)),
        ],
        compiler_params=pltpu.CompilerParams(
            collective_id=1, has_side_effects=True, vmem_limit_bytes=VMEM_LIMIT
        ),
        cost_estimate=pl.CostEstimate(
            flops=4_300_000_000, bytes_accessed=100_000_000, transcendentals=0
        ),
    )(rows, meta, onehot, routes)


def return_kernel(
    y_ref, g_ref, onehot_ref, outy_ref, outg_ref,
    rows_in, to_core, sums, ry0, rx1, rx0, ry1, rze, rzm, rzf,
    ysem, csend, crecv, xsend, xrecv, zsend, zrecv,
):
    dp, z, dc, dx, dy = place()
    zr, zo = z + 1 - 2 * (z % 2), 3 - z
    mid = z * (3 - z) > 0
    end = z * (3 - z) < 1
    half = 64
    sources, outs = (y_ref, g_ref), (outy_ref, outg_ref)
    zs = [3 - 3 * (z // 2), 2 - z // 2, zr, z]
    greet([(dp + dc, z), (dp + dx, z), (dp + dy, z), (dp, zr)], (dp, zo), mid, z * (3 - z) // 2)
    lo, hi = pl.ds(0, half), pl.ds(half, half)
    xsends, zsends = [[] for _ in range(8)], []

    def lanes_of(s):
        return pl.ds(0, sources[s // 4].shape[2])

    def tiles_of(s):
        width = sources[s // 4].shape[2]
        return [slice(i, min(i + 512, width)) for i in range(0, width, 512)]

    def dest(s, step):
        r = 3 - step % 4
        base = dp + dc - dc * (step // 4)
        return (base + (r % 2) * dx + (r // 2) * dy) * 4 + zs[s % 4]

    def fetch(s, block, slot):
        source, lanes = sources[s // 4], lanes_of(s)
        return [
            pltpu.make_async_copy(
                source.at[:, pl.ds(block * MAIN, MAIN), :],
                rows_in.at[slot, pl.ds(0, 8), :, lanes], ysem.at[slot, 0],
            ),
            pltpu.make_async_copy(
                source.at[:, pl.ds(512 + (block // 8) * MAIN, MAIN), :],
                rows_in.at[slot, pl.ds(8, 8), :, lanes], ysem.at[slot, 1],
            ),
        ]

    def partial_tile(block, slot, lanes):
        return lax.dot_general(
            onehot_ref[block], rows_in[slot, :, :, lanes].reshape(256, lanes.stop - lanes.start),
            (((0,), (0,)), ((), ())), preferred_element_type=jnp.float32,
        )

    def core_copy(r, s):
        lanes = lanes_of(s)
        return pltpu.make_async_remote_copy(
            to_core.at[s % 4, r, :, lanes], sums.at[s, r, :, lanes], csend.at[s, r], crecv.at[s, r],
            device_id=at(dp + dc, z), device_id_type=MESH,
        )

    def xy_copy(r, rows, target, index, s, dp_to):
        lanes = lanes_of(s)
        return pltpu.make_async_remote_copy(
            sums.at[s, r, rows, lanes], target.at[:, lanes], xsend.at[index, s], xrecv.at[index, s],
            device_id=at(dp_to, z), device_id_type=MESH,
        )

    def z_copy(s, target, index, z_to):
        lanes = lanes_of(s)
        index = 6 * (s // 4) + index
        return pltpu.make_async_remote_copy(
            sums.at[s, 0, :, lanes], target.at[:, lanes], zsend.at[index], zrecv.at[index],
            device_id=at(dp, z_to), device_id_type=MESH,
        )

    def add_to(s, r, rows, *others):
        lanes = lanes_of(s)
        total = sums[s, r, rows, lanes].astype(jnp.float32)
        for other in others:
            total = total + other[:, lanes].astype(jnp.float32)
        sums[s, r, rows, lanes] = total.astype(jnp.bfloat16)

    def stage_core(s):
        def load(block, slot, following=None):
            for copy in fetch(s, block, slot):
                copy.wait()
            if following is not None:
                for copy in fetch(s, following, 1 - slot):
                    copy.start()

        def partner(step, slot, following):
            r = 3 - step
            block = dest(s, step)
            load(block, slot, following)
            if s >= 4:
                core_copy(r, s - 4).wait_send()
            for lanes in tiles_of(s):
                to_core[s % 4, r, :, lanes] = partial_tile(block, slot, lanes).astype(jnp.bfloat16)
            core_copy(r, s).start()

        batch = [
            xy_copy(3, lo, ry0.at[1, s], 0, s, dp + dy),
            xy_copy(3, hi, rx1.at[1, s], 1, s, dp + dx),
            xy_copy(2, lo, ry0.at[0, s], 2, s, dp + dy),
            xy_copy(1, hi, rx1.at[0, s], 3, s, dp + dx),
        ]
        xsends[s].extend(batch)

        def both(i, carry):
            r = 3 - i
            block = dest(s, 4 + i)

            @pl.when(i < 3)
            def _():
                partner(i + 1, 1, block)

            late = i // 2
            following = (1 - late) * dest(s, i + 2) + late * dest(s, 5 + i)
            slot = i // 3
            load(block, slot)

            @pl.when(i < 3)
            def _():
                for copy in fetch(s, following, 1):
                    copy.start()

            if s < 7:

                @pl.when(i == 3)
                def _():
                    for copy in fetch(s + 1, dest(s + 1, 0), 0):
                        copy.start()

            core_copy(r, s).wait_recv()
            for lanes in tiles_of(s):
                sums[s, r, :, lanes] = (
                    partial_tile(block, slot, lanes) + sums[s, r, :, lanes].astype(jnp.float32)
                ).astype(jnp.bfloat16)
            for when, copies in enumerate((batch[:2], batch[2:3], batch[3:])):

                @pl.when(i == when)
                def _():
                    for copy in copies:
                        copy.start()

            return carry

        partner(0, 0, dest(s, 1))
        lax.fori_loop(0, 4, both, 0)

    def stage_cross(s):
        xsends[s][0].wait_recv()
        add_to(s, 1, lo, ry0.at[1, s])
        across = xy_copy(1, lo, rx0.at[s], 4, s, dp + dx)
        across.start()
        xsends[s][1].wait_recv()
        add_to(s, 2, hi, rx1.at[1, s])
        down = xy_copy(2, hi, ry1.at[s], 5, s, dp + dy)
        down.start()
        xsends[s].extend([across, down])

    def outward(s):
        return z_copy(s, rze.at[3 * (s // 4) + s % 4], s % 4, zr)

    def stage_line(s):
        for j in range(2, 6):
            xsends[s][j].wait_recv()
        if s % 4 < 3:
            add_to(s, 0, lo, ry0.at[0, s], rx0.at[s])
            add_to(s, 0, hi, rx1.at[0, s], ry1.at[s])
            copy = outward(s)
            zsends.append((copy, end))
            pl.when(end)(functools.partial(copy.start))
        else:
            out_ref, lanes = outs[s // 4], lanes_of(s)
            for rows, first, second in ((lo, ry0.at[0, s], rx0.at[s]), (hi, rx1.at[0, s], ry1.at[s])):
                out_ref[rows, :] = (
                    sums[s, 0, rows, lanes].astype(jnp.float32)
                    + first[:, lanes].astype(jnp.float32)
                    + second[:, lanes].astype(jnp.float32)
                )

    def stage_onward(s):
        p, k = s // 4, s % 4
        if k < 2:
            onward = z_copy(s, rzm.at[2 * p + k], 3 + k, zo)
        else:
            onward = z_copy(s, rzf.at[p], 5, zr)
        zsends.append((onward, mid))

        @pl.when(mid)
        def _():
            if k < 2:
                outward(s).wait_recv()
                add_to(s, 0, slice(None), rze.at[3 * p + k])
            else:
                z_copy(4 * p, rzm.at[2 * p], 3, zo).wait_recv()
                add_to(s, 0, slice(None), rzm.at[2 * p])
            onward.start()

    def stage_last(p):
        out_ref, lanes = outs[p], lanes_of(4 * p)

        @pl.when(end)
        def _():
            z_copy(4 * p + 2, rzf.at[p], 5, zr).wait_recv()
            out_ref[...] = out_ref[...] + rzf[p, :, lanes].astype(jnp.float32)

        @pl.when(mid)
        def _():
            outward(4 * p + 2).wait_recv()
            z_copy(4 * p + 1, rzm.at[2 * p + 1], 4, zo).wait_recv()
            out_ref[...] = (
                out_ref[...]
                + rze[3 * p + 2, :, lanes].astype(jnp.float32)
                + rzm[2 * p + 1, :, lanes].astype(jnp.float32)
            )

    for copy in fetch(0, dest(0, 0), 0):
        copy.start()
    for t in range(10):
        if t < 8:
            stage_core(t)
        if 1 <= t < 9:
            stage_cross(t - 1)
        if t >= 2:
            stage_line(t - 2)
        if t % 4 == 3:
            stage_onward(t - 3)
        if t >= 4 and t % 4 == 0:
            stage_onward(t - 2)
            stage_onward(t - 3)
        if t >= 5 and t % 4 == 1:
            stage_last(t // 4 - 1)
    for s in range(4, 8):
        for r in range(4):
            core_copy(r, s).wait_send()
    for batch in xsends:
        for copy in batch:
            copy.wait_send()
    for copy, cond in zsends:
        pl.when(cond)(functools.partial(copy.wait_send))


def return_rows(y_slots, gin_slots, onehot):
    width, narrow = y_slots.shape[2], gin_slots.shape[2]
    anywhere = pl.BlockSpec(memory_space=pl.ANY)
    vmem = pl.BlockSpec(memory_space=pltpu.VMEM)
    dma = pltpu.SemaphoreType.DMA
    low = jnp.bfloat16
    return pl.pallas_call(
        return_kernel,
        name="return_rows",
        out_shape=(
            jax.ShapeDtypeStruct((128, width), jnp.float32),
            jax.ShapeDtypeStruct((128, narrow), jnp.float32),
        ),
        in_specs=[anywhere, anywhere, vmem],
        out_specs=(vmem, vmem),
        scratch_shapes=[
            pltpu.VMEM((2, 16, MAIN, width), low),
            pltpu.VMEM((4, 4, 128, width), low),
            pltpu.VMEM((8, 4, 128, width), low),
            pltpu.VMEM((2, 8, 64, width), low),
            pltpu.VMEM((2, 8, 64, width), low),
            pltpu.VMEM((8, 64, width), low),
            pltpu.VMEM((8, 64, width), low),
            pltpu.VMEM((6, 128, width), low),
            pltpu.VMEM((4, 128, width), low),
            pltpu.VMEM((2, 128, width), low),
            dma((2, 2)), dma((8, 4)), dma((8, 4)), dma((6, 8)), dma((6, 8)), dma((12,)), dma((12,)),
        ],
        compiler_params=pltpu.CompilerParams(
            collective_id=2, has_side_effects=True, vmem_limit_bytes=VMEM_LIMIT
        ),
        cost_estimate=pl.CostEstimate(
            flops=8_600_000_000, bytes_accessed=300_000_000, transcendentals=0
        ),
    )(y_slots, gin_slots, onehot)


def finish_kernel(
    rows_ref, tok_ref, projq_ref, projk_ref, query_ref, key_ref, value_ref, ctx_ref, ga_ref, w_ref,
    gains_ref, cos_ref, sin_ref, seqc_ref, seqr_ref, side_ref, stat_ref,
    gw_ref, gwo_ref, dx_ref, small_ref,
    gqkv_ref, gctx_ref, to_core, from_core, sums, ry0, rx1, rx0, ry1, gain, zside,
    csend, crecv, xsend, xrecv, ssend, srecv, *line_refs,
):
    dp, z, dc, dx, dy = place()
    line = LineScatter(dp, z, *line_refs)
    dxs = line.blocks
    f32, low = jnp.float32, jnp.bfloat16
    half = 128
    heads = query_ref.shape[1]
    width = rows_ref.shape[1]
    others = [(z + i) % 4 for i in (1, 2, 3)]
    greet([(dp + dc, z), (dp + dx, z), (dp + dy, z)] + [(dp, other) for other in others])
    nt = (((1,), (1,)), ((), ()))
    tn = (((0,), (0,)), ((), ()))
    lo, hi = pl.ds(0, half), pl.ds(half, half)
    xsends = []

    def mm(a, b, dims):
        return lax.dot_general(a, b, dims, preferred_element_type=f32)

    def core_copy(r):
        return pltpu.make_async_remote_copy(
            to_core.at[r], from_core.at[r], csend.at[r], crecv.at[r],
            device_id=at(dp + dc, z), device_id_type=MESH,
        )

    def xy_copy(src, dst, index, dp_to):
        return pltpu.make_async_remote_copy(
            src, dst, xsend.at[index], xrecv.at[index], device_id=at(dp_to, z), device_id_type=MESH
        )

    def add_to(target, rows, *parts):
        total = target[rows, :].astype(f32)
        for part in parts:
            total = total + part[...].astype(f32)
        target[rows, :] = total.astype(low)

    gain[...] = jnp.zeros_like(gain)
    cosines, sines = cos_ref[...], sin_ref[...]
    query_gain, key_gain = head_gain(gains_ref, 0), head_gain(gains_ref, 16)
    for i in range(2):
        column = 3 * heads + i * 256
        total_ctx = jnp.zeros((512, 256), f32)
        for start in range(0, width, 256):
            lanes = slice(start, start + 256)
            total_ctx = total_ctx + mm(ga_ref[:, lanes], w_ref[lanes, column : column + 256], nt)
        gctx_ref[:, i * 256 : i * 256 + 256] = total_ctx.astype(low)
    score_scale = HD ** (-0.5)

    def head_back(grad, source, rows, cols, gain_values, column):
        values = source[rows, cols]
        inverse = lax.rsqrt(jnp.mean(values * values, axis=1, keepdims=True) + EPSILON)
        turned = grad * cosines[rows] - pltpu.roll(grad, HD // 2, 1) * sines[rows]
        scaled = turned * gain_values
        inner = jnp.mean(scaled * values, axis=1, keepdims=True)
        target = pl.ds(pl.multiple_of(cols.start + column, HD), HD)
        gqkv_ref[rows, target] = ((scaled - values * inner * inverse * inverse) * inverse).astype(low)
        return jnp.sum(turned * values * inverse, axis=0, keepdims=True)

    def one_head(h, carry):
        query_part, key_part = carry
        cols = pl.ds(pl.multiple_of(h * HD, HD), HD)
        key, value = key_ref[:, cols], value_ref[:, cols]
        grad_key = jnp.zeros((key.shape[0], HD), f32)
        grad_value = jnp.zeros((key.shape[0], HD), f32)
        for start in range(0, 512, 256):
            rows = slice(start, start + 256)
            query, grad_ctx = query_ref[rows, cols], gctx_ref[rows, cols]
            probs = head_probs(query, key, seqc_ref[rows, :1], seqr_ref[:1, :])
            grad_value = grad_value + mm(probs.astype(low), grad_ctx, tn)
            grad_probs = mm(grad_ctx, value, nt)
            inner = jnp.sum(probs * grad_probs, axis=1, keepdims=True)
            grad_scores = (probs * (grad_probs - inner)).astype(low)
            grad_query = jnp.dot(grad_scores, key, preferred_element_type=f32) * score_scale
            grad_key = grad_key + mm(grad_scores, query, tn)
            query_part = query_part + head_back(
                grad_query, projq_ref, rows, cols, query_gain, 0
            )
        key_part = key_part + head_back(
            grad_key * score_scale, projk_ref, slice(0, 512), cols, key_gain, heads
        )
        target = pl.ds(pl.multiple_of(cols.start + 2 * heads, HD), HD)
        gqkv_ref[:, target] = grad_value.astype(low)
        return query_part, key_part

    zero_row = jnp.zeros((1, HD), f32)
    query_part, key_part = lax.fori_loop(0, heads // HD, one_head, (zero_row, zero_row))
    for to in range(8):
        gain[to, 4:5, :] = query_part
        gain[to, 5:6, :] = key_part
    for k in range(4):
        rows = pl.ds(pl.multiple_of(line.zs[k] * 128, 128), 128)
        square = jnp.zeros((128, 1), f32)
        for start in range(0, width, 512):
            values = tok_ref[rows, start : start + 512].astype(f32)
            square = square + jnp.sum(values * values, axis=1, keepdims=True)
        inverse = lax.rsqrt(square * (1.0 / width) + EPSILON)
        for start in range(0, width, 512):
            lanes = slice(start, start + 512)
            piece = mm(gqkv_ref[rows, :], w_ref[lanes, : 3 * heads], nt)
            scaled = tok_ref[rows, lanes].astype(f32) * inverse
            column = jnp.sum(piece * scaled, axis=0, keepdims=True)
            for j in range(4):
                to = start // 256 + j // 2
                row = slice(j % 2, j % 2 + 1)
                gain[to, row, :] = gain[to, row, :] + column[:, j * 128 : j * 128 + 128]
            if k < 3:
                dxs[k, :, lanes] = piece.astype(low)
            else:
                dx_ref[:, lanes] = piece
        if k < 3:
            line.ready(k)

    def pieces(to):
        cols = pl.ds(pl.multiple_of(to * 256, 256), 256)
        mine = rows_ref[:, cols]
        yield slice(0, 3 * heads), mm(mine, gqkv_ref[...], tn)
        out = mm(ctx_ref[...], ga_ref[:, cols], tn)
        yield slice(3 * heads, 3 * heads + 256), out[:256]
        yield slice(3 * heads + 256, 4 * heads), out[256:]
        yield slice(4 * heads, 4 * heads + 128), jnp.concatenate(
            [
                side_ref[to, :128, :].astype(f32),
                side_ref[to, 128:144, :].astype(f32) + gain[to],
                jnp.zeros((112, 128), f32),
            ],
            axis=0,
        )

    def dest(step):
        r = 3 - step % 4
        base = dp + dc - dc * (step // 4)
        return base + (r % 2) * dx + (r // 2) * dy

    def partner(step, carry):
        r = 3 - step
        for lanes, value in pieces(dest(step)):
            to_core[r, :, lanes] = value.astype(low)
        core_copy(r).start()
        return carry

    def own(step, carry):
        r = 7 - step
        core_copy(r).wait_recv()
        for lanes, value in pieces(dest(step)):
            sums[r, :, lanes] = (value + from_core[r, :, lanes].astype(f32)).astype(low)
        return carry

    lax.fori_loop(0, 4, partner, 0)
    lax.fori_loop(4, 8, own, 0)
    xsends += [
        xy_copy(sums.at[3, lo], ry0.at[1], 0, dp + dy),
        xy_copy(sums.at[3, hi], rx1.at[1], 1, dp + dx),
        xy_copy(sums.at[2, lo], ry0.at[0], 2, dp + dy),
        xy_copy(sums.at[1, hi], rx1.at[0], 3, dp + dx),
    ]
    for copy in xsends:
        copy.start()

    line.onward(0)
    line.onward(1)
    xsends[0].wait_recv()
    add_to(sums.at[1], lo, ry0.at[1])
    xsends.append(xy_copy(sums.at[1, lo], rx0, 4, dp + dx))
    xsends[4].start()
    xsends[1].wait_recv()
    add_to(sums.at[2], hi, rx1.at[1])
    xsends.append(xy_copy(sums.at[2, hi], ry1, 5, dp + dy))
    xsends[5].start()
    line.onward(2)
    for j in (2, 3, 4, 5):
        xsends[j].wait_recv()

    def side_copy(i, source):
        return pltpu.make_async_remote_copy(
            zside.at[source], zside.at[source], ssend.at[i], srecv.at[source],
            device_id=at(dp, others[i]), device_id_type=MESH,
        )

    def total(part, lanes, first, second):
        return (
            sums[0, part, lanes].astype(f32)
            + first[:, lanes].astype(f32)
            + second[:, lanes].astype(f32)
        )

    sides = slice(4 * heads, 4 * heads + 128)
    zside[z, :128, :] = total(lo, sides, ry0.at[0], rx0)
    zside[z, 128:144, :] = total(hi, sides, rx1.at[0], ry1)[:16] + stat_ref[...]
    for i in range(3):
        side_copy(i, z).start()
    for rows, first, second in ((lo, ry0.at[0], rx0), (hi, rx1.at[0], ry1)):
        gw_ref[rows, :] = total(rows, slice(0, 3 * heads), first, second)
        gwo_ref[rows, :] = total(rows, slice(3 * heads, 3 * heads + 256), first, second)
        below = pl.ds(256 + rows.start, half)
        gwo_ref[below, :] = total(rows, slice(3 * heads + 256, 4 * heads), first, second)

    line.last(dx_ref)
    for i in range(3):
        side_copy(i, others[i]).wait_recv()
    small_ref[...] = (zside[0] + zside[1]) + (zside[2] + zside[3])
    for r in range(4):
        core_copy(r).wait_send()
    for copy in xsends:
        copy.wait_send()
    line.drain()
    for i in range(3):
        side_copy(i, z).wait_send()


def finish(rows, tok, attention, grad_attn, weights, tables, side, stats):
    width = rows.shape[1]
    heads = attention[0].shape[1]
    f32, low = jnp.float32, jnp.bfloat16
    vmem = pl.BlockSpec(memory_space=pltpu.VMEM)
    dma = pltpu.SemaphoreType.DMA
    packed = 4 * heads + 128
    return pl.pallas_call(
        finish_kernel,
        name="finish",
        out_shape=(
            jax.ShapeDtypeStruct((256, 3 * heads), f32),
            jax.ShapeDtypeStruct((heads, 256), f32),
            jax.ShapeDtypeStruct((128, width), f32),
            jax.ShapeDtypeStruct((144, 128), f32),
        ),
        in_specs=[vmem] * 17,
        out_specs=(vmem,) * 4,
        scratch_shapes=[pltpu.VMEM((512, 3 * heads), low), pltpu.VMEM((512, heads), low)]
        + [
            pltpu.VMEM((4, 256, packed), low),
            pltpu.VMEM((4, 256, packed), low),
            pltpu.VMEM((4, 256, packed), low),
            pltpu.VMEM((2, 128, packed), low),
            pltpu.VMEM((2, 128, packed), low),
            pltpu.VMEM((128, packed), low),
            pltpu.VMEM((128, packed), low),
            pltpu.VMEM((8, 16, 128), f32),
            pltpu.VMEM((4, 144, 128), f32),
            dma((4,)), dma((4,)), dma((6,)), dma((6,)), dma((3,)), dma((4,)),
        ]
        + LineScatter.scratch(width),
        compiler_params=pltpu.CompilerParams(
            collective_id=4, has_side_effects=True, vmem_limit_bytes=VMEM_LIMIT
        ),
        cost_estimate=pl.CostEstimate(
            flops=8_000_000_000, bytes_accessed=100_000_000, transcendentals=0
        ),
    )(rows, tok, *attention, grad_attn, weights, *tables, side, stats)


def expert_kernel(
    x_ref, dy_ref, gate_ref, wg_ref, wu_ref, wd_ref, y_ref, gin_ref, dgate_ref, dup_ref, hgated_ref,
    gate_pre_ref, up_pre_ref, raw_ref,
):
    rows, ff = dgate_ref.shape[1:]
    width = x_ref.shape[2]
    expert = lax.axis_index("dp") * 8 + pl.program_id(0)
    nt = (((1,), (1,)), ((), ()))

    def mm(a, b, dims):
        return lax.dot_general(a, b, dims, preferred_element_type=jnp.float32)

    gate_pre_ref[...] = jnp.dot(x_ref[0], wg_ref[0], preferred_element_type=jnp.float32)
    up_pre_ref[...] = jnp.dot(x_ref[0], wu_ref[0], preferred_element_type=jnp.float32)
    raw_ref[...] = mm(dy_ref[0], wd_ref[0], nt)
    step = 96

    def pointwise(index, carry):
        part = pl.ds(pl.multiple_of(index * step, step), step)
        gate_pre, up_pre, raw = gate_pre_ref[part, :], up_pre_ref[part, :], raw_ref[part, :]
        weight = jnp.concatenate([gate_ref[0, part, :]] * (ff // 128), axis=1)
        sig = jax.nn.sigmoid(gate_pre)
        silu = gate_pre * sig
        hidden = silu * up_pre
        route_grad = jnp.sum(hidden * raw, axis=1, keepdims=True)
        grad_hidden = weight * raw
        lane = lax.broadcasted_iota(jnp.int32, (step, 128), 1)
        high = route_grad.astype(jnp.bfloat16).astype(jnp.float32)
        extra = jnp.where(lane == expert, high, 0.0) + jnp.where(
            lane == expert + 64, route_grad - high, 0.0
        )
        hgated_ref[0, part, :] = (weight * hidden).astype(jnp.bfloat16)
        dgate_ref[0, part, :] = (
            grad_hidden * up_pre * sig * (1.0 + gate_pre * (1.0 - sig))
        ).astype(jnp.bfloat16)
        dup_ref[0, part, :] = (grad_hidden * silu).astype(jnp.bfloat16)
        y_ref[0, part, width:] = extra.astype(jnp.bfloat16)
        return carry

    lax.fori_loop(0, rows // step, pointwise, 0)
    for start in range(0, width, 512):
        lanes = slice(start, start + 512)
        y_ref[0, :, lanes] = jnp.dot(
            hgated_ref[0], wd_ref[0, :, lanes], preferred_element_type=jnp.float32
        ).astype(jnp.bfloat16)
        gin_ref[0, :, lanes] = (
            mm(dgate_ref[0], wg_ref[0, lanes, :], nt) + mm(dup_ref[0], wu_ref[0, lanes, :], nt)
        ).astype(jnp.bfloat16)


def weights_kernel(x_ref, dy_ref, dgate_ref, dup_ref, hgated_ref, gwg_ref, gwu_ref, gwd_ref):
    width = x_ref.shape[2]
    tn = (((0,), (0,)), ((), ()))

    def mm(a, b):
        return lax.dot_general(a, b, tn, preferred_element_type=jnp.float32)

    for start in range(0, width, 512):
        part = slice(start, start + 512)
        gwd_ref[0, :, part] = mm(hgated_ref[0], dy_ref[0, :, part])
        xs = x_ref[0, :, part]
        gwg_ref[0, part, :] = mm(xs, dgate_ref[0])
        gwu_ref[0, part, :] = mm(xs, dup_ref[0])


def expert_spec(*shape):
    return pl.BlockSpec((1,) + shape, lambda e: (e, 0, 0))


def run_experts(x_slots, dy_slots, gate_slots, w_gate, w_up, w_down):
    experts, rows, width = x_slots.shape
    ff = w_gate.shape[2]
    spec, low = expert_spec, jnp.bfloat16
    middle = jax.ShapeDtypeStruct((experts, rows, ff), low)
    return pl.pallas_call(
        expert_kernel,
        name="experts",
        grid=(experts,),
        in_specs=[
            spec(rows, width), spec(rows, width), spec(rows, 128),
            spec(width, ff), spec(width, ff), spec(ff, width),
        ],
        out_specs=(spec(rows, width + 128), spec(rows, width)) + (spec(rows, ff),) * 3,
        out_shape=(
            jax.ShapeDtypeStruct((experts, rows, width + 128), low),
            jax.ShapeDtypeStruct((experts, rows, width), low),
            middle, middle, middle,
        ),
        scratch_shapes=[pltpu.VMEM((rows, ff), jnp.float32)] * 3,
        compiler_params=pltpu.CompilerParams(vmem_limit_bytes=VMEM_LIMIT),
        cost_estimate=pl.CostEstimate(
            flops=29_000_000_000, bytes_accessed=100_000_000, transcendentals=2_000_000
        ),
    )(x_slots, dy_slots, gate_slots, w_gate, w_up, w_down)


def run_weights(x_slots, dy_slots, dgate, dup, hgated):
    experts, rows, width = x_slots.shape
    ff = dgate.shape[2]
    spec, f32 = expert_spec, jnp.float32
    wide = jax.ShapeDtypeStruct((experts, width, ff), f32)
    return pl.pallas_call(
        weights_kernel,
        name="expert_weights",
        grid=(experts,),
        in_specs=[spec(rows, width)] * 2 + [spec(rows, ff)] * 3,
        out_specs=(spec(width, ff), spec(width, ff), spec(ff, width)),
        out_shape=(wide, wide, jax.ShapeDtypeStruct((experts, ff, width), f32)),
        compiler_params=pltpu.CompilerParams(vmem_limit_bytes=VMEM_LIMIT),
        cost_estimate=pl.CostEstimate(
            flops=15_000_000_000, bytes_accessed=100_000_000, transcendentals=0
        ),
    )(x_slots, dy_slots, dgate, dup, hgated)


def plain_onehot(routes_all, first_expert, local_experts):
    sources, rows = routes_all.shape[0], routes_all.shape[1]
    experts = jnp.arange(local_experts, dtype=jnp.int32) + first_expert
    member = jnp.any(routes_all[:, :, :, None] == experts, axis=2).astype(jnp.int32)
    rank = jnp.cumsum(member, axis=1) - member
    rank = jnp.where(member > 0, rank, -1)
    return (
        rank.transpose(0, 2, 1)[:, :, None, :] == jnp.arange(CAP, dtype=jnp.int32)[:, None]
    ).astype(jnp.bfloat16)


def plain_experts(moe_low, cotangent, routes, gates, w_gate, w_up, w_down):
    both = ("dp", "tensor")
    local_experts = w_gate.shape[0]
    width = moe_low.shape[1]
    f32 = jnp.float32
    routes_all = lax.all_gather(routes, both, axis=0)
    x_all = lax.all_gather(moe_low, both, axis=0)
    dy_all = lax.all_gather(cotangent, both, axis=0)
    gates_all = lax.all_gather(gates, both, axis=0)
    first_expert = lax.axis_index("dp") * local_experts
    onehot = plain_onehot(routes_all, first_expert, local_experts)
    take = functools.partial(jnp.einsum, "sect,std->escd")
    flat = (local_experts, -1, width)
    x_slots = take(onehot, x_all).reshape(flat)
    dy_slots = take(onehot, dy_all).reshape(flat)
    experts = jnp.arange(local_experts, dtype=jnp.int32) + first_expert
    gates_here = jnp.sum(
        jnp.where(routes_all[..., None] == experts, gates_all[..., None], 0.0), axis=2
    )
    weight = jnp.einsum(
        "sect,ste->esc", onehot.astype(f32), gates_here, precision=lax.Precision.HIGHEST
    ).reshape(local_experts, -1)[..., None]
    mm = functools.partial(jnp.einsum, preferred_element_type=f32)
    gate_pre = mm("ecd,edf->ecf", x_slots, w_gate)
    up_pre = mm("ecd,edf->ecf", x_slots, w_up)
    raw = mm("ecd,efd->ecf", dy_slots, w_down)
    sig = jax.nn.sigmoid(gate_pre)
    silu = gate_pre * sig
    hidden = silu * up_pre
    hgated = (weight * hidden).astype(jnp.bfloat16)
    route_grad = jnp.sum(hidden * raw, axis=2).reshape(local_experts, -1, CAP)
    grad_hidden = weight * raw
    dgate = (grad_hidden * up_pre * sig * (1.0 + gate_pre * (1.0 - sig))).astype(jnp.bfloat16)
    dup = (grad_hidden * silu).astype(jnp.bfloat16)
    y_slots = mm("ecf,efd->ecd", hgated, w_down).astype(jnp.bfloat16)
    gin_slots = (mm("ecf,edf->ecd", dgate, w_gate) + mm("ecf,edf->ecd", dup, w_up)).astype(
        jnp.bfloat16
    )
    grads = (
        mm("ecd,ecf->edf", x_slots, dgate),
        mm("ecd,ecf->edf", x_slots, dup),
        mm("ecf,ecd->efd", hgated, dy_slots),
    )

    def give_back(slots):
        slots = slots.reshape(local_experts, -1, CAP, width)
        rows = mm("sect,escd->std", onehot, slots).astype(jnp.bfloat16)
        return lax.psum_scatter(
            rows.reshape(-1, width), both, scatter_dimension=0, tiled=True
        ).astype(f32)

    here = jnp.einsum(
        "sect,esc->ste", onehot.astype(f32), route_grad, precision=lax.Precision.HIGHEST
    )
    spread = jnp.zeros(here.shape[:2] + (EXPERTS,), f32)
    spread = lax.dynamic_update_slice(spread, here, (0, 0, first_expert))
    grad_gates = lax.psum_scatter(
        spread.reshape(-1, EXPERTS), both, scatter_dimension=0, tiled=True
    )
    return (give_back(y_slots), grad_gates, give_back(gin_slots), lambda own_rows: grads)


def routed_experts(moe_low, cotangent, routes, gates, w_gate, w_up, w_down, dispatched):
    if dispatched is None:
        return plain_experts(moe_low, cotangent, routes, gates, w_gate, w_up, w_down)
    dy_slots, onehot, all_routes = dispatched
    width = moe_low.shape[1]
    x_slots, gate_slots = gather_slots(moe_low, gates.T, onehot, all_routes)
    y_slots, gin_slots, *middle = run_experts(
        x_slots, dy_slots, gate_slots, w_gate, w_up, w_down
    )
    sums, grad_in = return_rows(y_slots, gin_slots, onehot)
    grad_gates = sums[:, width : width + EXPERTS] + sums[:, width + EXPERTS :]

    def weight_grads(own_rows):
        hgated, unused = lax.optimization_barrier((middle[2], own_rows))
        return run_weights(x_slots, dy_slots, middle[0], middle[1], hgated)

    return (sums[:, :width], grad_gates, grad_in, weight_grads)


def own_kernels(tokens, w_gate):
    return (
        lax.axis_size("dp") == 8
        and lax.axis_size("tensor") == 4
        and tokens.shape == (128, 2048)
        and w_gate.shape[0] == 8
    )


def side_columns(pieces, rows):
    filled = [jnp.pad(p, ((0, rows - p.shape[0]), (0, 0))) for p in pieces]
    used = sum(p.shape[1] for p in filled)
    return jnp.concatenate(filled + [jnp.zeros((rows, 128 - used), filled[0].dtype)], axis=1)


def body(
    tokens,
    cotangent,
    lengths,
    seq_order,
    routes,
    attn_gain,
    w_query,
    w_key,
    w_value,
    w_output,
    query_gain,
    key_gain,
    ffn_gain,
    router,
    w_gate,
    w_up,
    w_down,
):
    tok_rows, model_width = tokens.shape
    tensor_count = lax.axis_size("tensor")
    data_count = lax.axis_size("dp")
    group_rows_count = tok_rows * tensor_count
    block_rows = min(group_rows_count, 512)
    shard = w_query.shape[0]
    heads_width = w_query.shape[1]
    gain_rows = query_gain.shape[0]
    low = jnp.bfloat16
    f32 = jnp.float32

    own = own_kernels(tokens, w_gate)

    seq_ids, positions = arrival_layout(lengths[0], seq_order[0])
    resid_in = tokens.astype(f32)
    if own:
        gain_list = [attn_gain, ffn_gain, query_gain, key_gain]
        filled = sum(part.shape[0] for part in gain_list)
        gains = jnp.concatenate(gain_list + [jnp.zeros((1024 - filled,), low)])
        gains = gains.reshape(8, 128).astype(f32)
        shards = (w_query, w_key, w_value, w_output, jnp.pad(router, ((0, 0), (0, 128 - EXPERTS))))
        seq_float = seq_ids.astype(f32)
        lane = jnp.arange(HD, dtype=jnp.int32)
        frequency = THETA ** (-(lane % (HD // 2)).astype(f32) / (HD // 2))
        angles = positions.astype(f32)[:, None] * frequency[None, :]
        tables = (
            jnp.cos(angles),
            jnp.sin(angles) * jnp.where(lane < HD // 2, -1.0, 1.0),
            jnp.broadcast_to(seq_float[:, None], (group_rows_count, 128)),
            jnp.broadcast_to(seq_float[None, :], (8, group_rows_count)),
        )
        (
            weights, group_tokens, dy_slots, all_gains, onehot, all_routes, group_rows,
            *attention, attn_out,
        ) = front(shards, tokens, cotangent, routes.T.astype(f32), gains, *tables, heads_width)
        dispatched = (dy_slots, onehot, all_routes)
        group_tokens = group_tokens.reshape(-1, model_width)
        full_router = weights[:, 4 * heads_width : 4 * heads_width + EXPERTS]
        attn_scale = all_gains[:, :2].reshape(-1)
        ffn_scale = all_gains[:, 2:4].reshape(-1)
    else:
        side = side_columns(
            [router, attn_gain[:, None], ffn_gain[:, None], query_gain[:, None], key_gain[:, None]],
            shard,
        )
        packed = jnp.concatenate([w_query, w_key, w_value, w_output.T, side], axis=1)
        weights = lax.all_gather(packed, "dp", axis=0, tiled=True)
        group_tokens = lax.all_gather(tokens, "tensor", axis=0, tiled=True)
        dispatched = None
        full_query = weights[:, :heads_width]
        full_key = weights[:, heads_width : 2 * heads_width]
        full_value = weights[:, 2 * heads_width : 3 * heads_width]
        output_t = weights[:, 3 * heads_width : 4 * heads_width]
        extras = weights[:, 4 * heads_width :]
        full_router = extras[:, :EXPERTS]
        attn_scale = extras[:, EXPERTS].astype(f32)
        ffn_scale = extras[:, EXPERTS + 1].astype(f32)
        gain_columns = extras.reshape(data_count, shard, 128)[:, :gain_rows, EXPERTS + 2 : EXPERTS + 4]
        query_scale = gain_columns[:, :, 0].reshape(-1).astype(f32)
        key_scale = gain_columns[:, :, 1].reshape(-1).astype(f32)

        cosines, sines = rope_tables(positions)
        group_rows = norm_apply(group_tokens.astype(f32), attn_scale).astype(low)
        proj_query = jnp.dot(group_rows, full_query, preferred_element_type=f32)
        proj_key = jnp.dot(group_rows, full_key, preferred_element_type=f32)
        value_flat = jnp.dot(group_rows, full_value, preferred_element_type=f32).astype(low)
        value_low = value_flat.reshape(group_rows_count, -1, HD)
        query_low = head_norm_rope(proj_query, query_scale, cosines, sines).astype(low)
        key_low = head_norm_rope(proj_key, key_scale, cosines, sines).astype(low)
        context, row_lse = attend(query_low, key_low, value_low, seq_ids, block_rows)
        context_low = context.reshape(group_rows_count, -1).astype(low)
        attn_out = lax.psum_scatter(
            lax.dot_general(
                context_low, output_t, (((1,), (1,)), ((), ())), preferred_element_type=f32
            ).astype(low),
            "tensor",
            scatter_dimension=0,
            tiled=True,
        ).astype(f32)
    resid_mid = resid_in + attn_out
    moe_low = norm_apply(resid_mid, ffn_scale).astype(low)
    logits = jnp.dot(moe_low, full_router, preferred_element_type=f32)
    route_match = routes[:, :, None] == jnp.arange(EXPERTS, dtype=jnp.int32)[None, None, :]
    picked_logits = jnp.sum(jnp.where(route_match, logits[:, None, :], 0.0), axis=-1)
    gate_peak = jnp.max(picked_logits, axis=1, keepdims=True)
    gate_raw = jnp.exp(picked_logits - gate_peak)
    gates = gate_raw / jnp.sum(gate_raw, axis=1, keepdims=True)
    dense_gates = jnp.sum(jnp.where(route_match, gates[:, :, None], 0.0), axis=1)

    moe_out, grad_gates, grad_from_experts, expert_weight_grads = routed_experts(
        moe_low, cotangent, routes, gates, w_gate, w_up, w_down, dispatched
    )
    layer_out = (resid_mid + moe_out).astype(low)
    stat_terms = jnp.stack(
        [jnp.sum(resid_mid * resid_mid), jnp.sum(attn_out * attn_out), jnp.sum(moe_out * moe_out)]
    )
    grad_out = cotangent.astype(f32)
    inner_gate = jnp.sum(dense_gates * grad_gates, axis=1, keepdims=True)
    grad_logits_low = (dense_gates * (grad_gates - inner_gate)).astype(low)
    grad_router_part = jnp.dot(moe_low.T, grad_logits_low, preferred_element_type=f32)
    grad_moe_in = grad_from_experts + jnp.dot(
        grad_logits_low, full_router.T, preferred_element_type=f32
    )
    unused_mid, ffn_back = jax.vjp(norm_apply, resid_mid, ffn_scale)
    grad_mid_norm, grad_ffn_part = ffn_back(grad_moe_in)
    grad_mid = grad_out + grad_mid_norm
    grad_attn_low = grad_mid.astype(low)
    grad_attn_rows = lax.all_gather(grad_attn_low, "tensor", axis=0, tiled=True)
    grad_gate_w, grad_up_w, grad_down = expert_weight_grads(grad_attn_low)
    tn = (((0,), (0,)), ((), ()))
    if own:
        router_side = grad_router_part.reshape(8, 2, 128, EXPERTS).swapaxes(1, 2).reshape(8, 128, 128)

        side = jnp.concatenate(
            [
                router_side,
                jnp.zeros((8, 2, 128), f32),
                grad_ffn_part.reshape(8, 2, 128),
                jnp.zeros((8, 12, 128), f32),
            ],
            axis=1,
        ).astype(low)
        stats = jnp.pad(stat_terms[None, :], ((6, 9), (0, 125)))
        grads_qkv, grad_out_w, grad_normed, small = finish(
            group_rows, group_tokens, attention, grad_attn_rows, weights, (all_gains,) + tables, side, stats
        )
        grad_router = small[:128].reshape(128, 2, EXPERTS).swapaxes(0, 1).reshape(256, EXPERTS)
        grad_attn_gain = small[128:130].reshape(-1)
        grad_ffn_gain = small[130:132].reshape(-1)
        first_lane = lax.axis_index("dp") * gain_rows
        grad_query_gain = lax.dynamic_slice(small[132], (first_lane,), (gain_rows,))
        grad_key_gain = lax.dynamic_slice(small[133], (first_lane,), (gain_rows,))
        stat_totals = small[134, :3]
        unused_in, attn_back = jax.vjp(lambda values: norm_apply(values, attn_scale), resid_in)
        (grad_in_norm,) = attn_back(grad_normed)
    else:
        grad_ctx_low = jnp.dot(grad_attn_rows, output_t, preferred_element_type=f32).astype(low)
        grad_query, grad_key, grad_value = attend_back(
            query_low,
            key_low,
            value_low,
            seq_ids,
            row_lse,
            grad_ctx_low.reshape(value_low.shape),
            block_rows,
        )
        grad_value_low = grad_value.reshape(group_rows_count, -1).astype(low)
        unused_query, query_back = jax.vjp(
            lambda projected, head_gain: head_norm_rope(projected, head_gain, cosines, sines),
            proj_query,
            query_scale,
        )
        grad_proj_query, grad_query_gain_part = query_back(grad_query)
        unused_key, key_back = jax.vjp(
            lambda projected, head_gain: head_norm_rope(projected, head_gain, cosines, sines),
            proj_key,
            key_scale,
        )
        grad_proj_key, grad_key_gain_part = key_back(grad_key)
        grad_query_low = grad_proj_query.astype(low)
        grad_key_low = grad_proj_key.astype(low)
        head_grads = (grad_query_low, grad_key_low, grad_value_low)
        weight_grads = [
            lax.dot_general(group_rows, part, tn, preferred_element_type=f32) for part in head_grads
        ]
        grad_output_t = lax.dot_general(grad_attn_rows, context_low, tn, preferred_element_type=f32)
        total_rows = jnp.dot(grad_query_low, full_query.T, preferred_element_type=f32)
        total_rows = total_rows + jnp.dot(grad_key_low, full_key.T, preferred_element_type=f32)
        total_rows = total_rows + jnp.dot(grad_value_low, full_value.T, preferred_element_type=f32)
        grad_normed = lax.psum_scatter(
            total_rows.astype(low), "tensor", scatter_dimension=0, tiled=True
        ).astype(f32)
        unused_in, attn_back = jax.vjp(norm_apply, resid_in, attn_scale)
        grad_in_norm, grad_attn_part = attn_back(grad_normed)

        def gain_column(part):
            cut = part.astype(low).reshape(data_count, gain_rows, 1)
            return jnp.pad(cut, ((0, 0), (0, shard - gain_rows), (0, 0))).reshape(-1, 1)

        side_grads = side_columns(
            [
                grad_router_part.astype(low),
                grad_attn_part.astype(low)[:, None],
                grad_ffn_part.astype(low)[:, None],
                gain_column(grad_query_gain_part),
                gain_column(grad_key_gain_part),
            ],
            model_width,
        )
        packed_grads = jnp.concatenate(
            [part.astype(low) for part in weight_grads] + [grad_output_t.astype(low), side_grads],
            axis=1,
        )
        reduced = lax.psum_scatter(packed_grads, "dp", scatter_dimension=0, tiled=True).astype(f32)
        side_total, stat_totals = lax.psum(
            (reduced[:, 4 * heads_width : 4 * heads_width + EXPERTS + 4], stat_terms), "tensor"
        )
        grads_qkv = reduced[:, : 3 * heads_width]
        grad_out_w = reduced[:, 3 * heads_width : 4 * heads_width].T
        grad_attn_gain = side_total[:, EXPERTS]
        grad_ffn_gain = side_total[:, EXPERTS + 1]
        grad_query_gain = side_total[:gain_rows, EXPERTS + 2]
        grad_key_gain = side_total[:gain_rows, EXPERTS + 3]
        grad_router = side_total[:, :EXPERTS]
    grad_tokens = grad_mid + grad_in_norm
    rms_stats = jnp.sqrt(stat_totals / (group_rows_count * model_width))[None, :]
    return (
        layer_out,
        grad_tokens,
        grad_attn_gain,
        grads_qkv[:, :heads_width],
        grads_qkv[:, heads_width : 2 * heads_width],
        grads_qkv[:, 2 * heads_width :],
        grad_out_w,
        grad_query_gain,
        grad_key_gain,
        grad_ffn_gain,
        grad_router,
        grad_gate_w,
        grad_up_w,
        grad_down,
        rms_stats,
    )


def solution(mesh):
    in_specs = (
        P(("dp", "tensor"), None),
        P(("dp", "tensor"), None),
        P("dp", None),
        P("dp", None),
        P(("dp", "tensor"), None),
        P("dp"),
        P("dp", "tensor"),
        P("dp", "tensor"),
        P("dp", "tensor"),
        P("tensor", "dp"),
        P("dp"),
        P("dp"),
        P("dp"),
        P("dp", None),
        P("dp", None, "tensor"),
        P("dp", None, "tensor"),
        P("dp", "tensor", None),
    )
    out_specs = (
        P(("dp", "tensor"), None),
        P(("dp", "tensor"), None),
        P("dp"),
        P("dp", "tensor"),
        P("dp", "tensor"),
        P("dp", "tensor"),
        P("tensor", "dp"),
        P("dp"),
        P("dp"),
        P("dp"),
        P("dp", None),
        P("dp", None, "tensor"),
        P("dp", None, "tensor"),
        P("dp", "tensor", None),
        P("dp", None),
    )
    return jax.shard_map(body, mesh=mesh, in_specs=in_specs, out_specs=out_specs, check_vma=False)
```

```python
import functools

import jax
import jax.numpy as jnp
from jax import lax
from jax.experimental import pallas as pl
from jax.experimental.pallas import tpu as pltpu
from jax.sharding import PartitionSpec as P

HD = 128
EXPERTS = 64
TOPK = 8
CAP = 18


EPSILON = 1e-05
THETA = 10000.0
NEGATIVE = -1e30


def inv_rms(values):
    return lax.rsqrt(jnp.mean(values * values, axis=-1, keepdims=True) + EPSILON)


def norm_apply(values, scale_gain):
    return values * inv_rms(values) * scale_gain


def arrival_layout(seq_lengths, order_row):
    row_total = order_row.shape[0]
    placed = jnp.arange(row_total, dtype=jnp.int32)
    order = jnp.arange(seq_lengths.shape[0], dtype=jnp.int32)
    upto = order[None, :] <= order[:, None]
    seq_ends = jnp.sum(jnp.where(upto, seq_lengths[None, :], 0), axis=1)
    seq_starts = seq_ends - seq_lengths
    member = jnp.sum((placed[:, None] >= seq_ends[None, :]).astype(jnp.int32), axis=1)
    chosen = member[:, None] == jnp.arange(seq_lengths.shape[0], dtype=jnp.int32)[None, :]
    seq_begin = jnp.sum(jnp.where(chosen, seq_starts[None, :], 0), axis=1)
    here = order_row[None, :] == placed[:, None]
    seq_ids = jnp.sum(jnp.where(here, member[None, :], 0), axis=1)
    positions = jnp.sum(jnp.where(here, (placed - seq_begin)[None, :], 0), axis=1)
    return (seq_ids, positions)


def rope_tables(positions):
    half_dim = HD // 2
    frequency = THETA ** (-jnp.arange(half_dim, dtype=jnp.float32) / half_dim)
    angles = positions.astype(jnp.float32)[:, None] * frequency[None, :]
    return (jnp.cos(angles)[:, None, :], jnp.sin(angles)[:, None, :])


def head_norm_rope(projected, head_gain, cosines, sines):
    shaped = projected.reshape(projected.shape[0], -1, HD)
    normed_heads = norm_apply(shaped, head_gain)
    first_half = normed_heads[..., : HD // 2]
    second_half = normed_heads[..., HD // 2 :]
    return jnp.concatenate(
        [first_half * cosines - second_half * sines, second_half * cosines + first_half * sines],
        axis=-1,
    )


def masked_scores(query_block, key_low, seq_block, seq_ids):
    score_scale = HD ** (-0.5)
    scores = (
        jnp.einsum("qhd,khd->hqk", query_block, key_low, preferred_element_type=jnp.float32)
        * score_scale
    )
    same_seq = (seq_block[:, None] == seq_ids[None, :])[None]
    return jnp.where(same_seq, scores, NEGATIVE)


def attend(query_low, key_low, value_low, seq_ids, block_rows):
    num_blocks = query_low.shape[0] // block_rows
    query_blocks = query_low.reshape(num_blocks, block_rows, query_low.shape[1], HD)
    seq_blocks = seq_ids.reshape(num_blocks, block_rows)

    def one_block(inputs):
        query_block, seq_block = inputs
        scores = masked_scores(query_block, key_low, seq_block, seq_ids)
        row_peak = jnp.max(scores, axis=-1, keepdims=True)
        raised = jnp.exp(scores - row_peak)
        row_total = jnp.sum(raised, axis=-1, keepdims=True)
        probs_low = (raised / row_total).astype(jnp.bfloat16)
        context = jnp.einsum(
            "hqk,khd->qhd", probs_low, value_low, preferred_element_type=jnp.float32
        )
        return (context, row_peak + jnp.log(row_total))

    context, row_lse = lax.map(one_block, (query_blocks, seq_blocks))
    return (context.reshape(query_low.shape), row_lse)


def attend_back(query_low, key_low, value_low, seq_ids, row_lse, grad_ctx_low, block_rows):
    score_scale = HD ** (-0.5)
    num_blocks = query_low.shape[0] // block_rows
    block_shape = (num_blocks, block_rows, query_low.shape[1], HD)

    def one_block(carry, inputs):
        grad_key_sum, grad_value_sum = carry
        query_block, seq_block, lse_block, grad_block = inputs
        scores = masked_scores(query_block, key_low, seq_block, seq_ids)
        probs = jnp.exp(scores - lse_block)
        probs_low = probs.astype(jnp.bfloat16)
        grad_value_sum = grad_value_sum + jnp.einsum(
            "hqk,qhd->khd", probs_low, grad_block, preferred_element_type=jnp.float32
        )
        grad_probs = jnp.einsum(
            "qhd,khd->hqk", grad_block, value_low, preferred_element_type=jnp.float32
        )
        inner_sum = jnp.sum(probs * grad_probs, axis=-1, keepdims=True)
        grad_scores = (probs * (grad_probs - inner_sum)).astype(jnp.bfloat16)
        grad_query_block = (
            jnp.einsum("hqk,khd->qhd", grad_scores, key_low, preferred_element_type=jnp.float32)
            * score_scale
        )
        grad_key_sum = (
            grad_key_sum
            + jnp.einsum(
                "hqk,qhd->khd", grad_scores, query_block, preferred_element_type=jnp.float32
            )
            * score_scale
        )
        return ((grad_key_sum, grad_value_sum), grad_query_block)

    zeros_heads = jnp.zeros(query_low.shape, jnp.float32)
    carried, grad_query = lax.scan(
        one_block,
        (zeros_heads, zeros_heads),
        (
            query_low.reshape(block_shape),
            seq_ids.reshape(num_blocks, block_rows),
            row_lse,
            grad_ctx_low.reshape(block_shape),
        ),
    )
    return (grad_query.reshape(query_low.shape), carried[0], carried[1])


MESH = pl.DeviceIdType.MESH
VMEM_LIMIT = 60 * 1024 * 1024
MAIN = 16
SPARE = CAP - MAIN


def at(dp_index, z_index):
    return {"dp": dp_index, "tensor": z_index}


def place():
    dp = lax.axis_index("dp")
    z = lax.axis_index("tensor")
    core, x, y = dp % 2, (dp // 2) % 2, dp // 4
    return dp, z, 1 - 2 * core, 2 - 4 * x, 4 - 8 * y


def greet(peers, extra=None, has_extra=None, count=0):
    barrier = pltpu.get_barrier_semaphore()
    for peer in peers:
        pl.semaphore_signal(barrier, inc=1, device_id=at(*peer), device_id_type=MESH)
    if extra is not None:

        @pl.when(has_extra)
        def _():
            pl.semaphore_signal(barrier, inc=1, device_id=at(*extra), device_id_type=MESH)

    pl.semaphore_wait(barrier, len(peers) + count)


def when_or_now(cond, action):
    if cond is None:
        action()
    else:
        pl.when(cond)(action)


def slot_matrix(routes_block, source, first_expert):
    experts = lax.broadcasted_iota(jnp.int32, (8, 128), 0) + first_expert
    member = jnp.zeros((8, 128), jnp.float32)
    for j in range(TOPK):
        member = member + (routes_block[j : j + 1, :] == experts.astype(jnp.float32)).astype(jnp.float32)
    earlier = (
        lax.broadcasted_iota(jnp.int32, (128, 128), 0)
        < lax.broadcasted_iota(jnp.int32, (128, 128), 1)
    ).astype(jnp.bfloat16)
    rank = jnp.dot(member.astype(jnp.bfloat16), earlier, preferred_element_type=jnp.float32)
    rank = jnp.where(member > 0.5, rank, -1.0).astype(jnp.int32)
    spread = jnp.broadcast_to(rank[:, None, :], (8, MAIN, 128)).reshape(128, 128)
    row = lax.broadcasted_iota(jnp.int32, (128, 128), 0) % MAIN
    main = spread == row
    spare = jnp.logical_and(row // SPARE == source % 8, spread == MAIN + row % SPARE)
    return jnp.concatenate(
        [main.astype(jnp.float32), spare.astype(jnp.float32)], axis=0
    ).astype(jnp.bfloat16)


class LineScatter:
    def __init__(self, dp, z, blocks, rze, rzm, rzf, zsend, zrecv):
        self.dp, self.z = dp, z
        self.zr, self.zo = z + 1 - 2 * (z % 2), 3 - z
        self.mid, self.end = z * (3 - z) > 0, z * (3 - z) < 1
        self.zs = [3 - 3 * (z // 2), 2 - z // 2, self.zr, z]
        self.blocks, self.rze, self.rzm, self.rzf = blocks, rze, rzm, rzf
        self.zsend, self.zrecv = zsend, zrecv
        self.outward = [self.copy(blocks.at[k], rze.at[k], k, self.zr) for k in range(3)]
        self.sends = []

    def copy(self, src, dst, index, z_to):
        return pltpu.make_async_remote_copy(
            src, dst, self.zsend.at[index], self.zrecv.at[index],
            device_id=at(self.dp, z_to), device_id_type=MESH,
        )

    def ready(self, k):
        pl.when(self.end)(functools.partial(self.outward[k].start))
        self.sends.append((self.outward[k], self.end))

    def add(self, k, part):
        total = self.blocks[k].astype(jnp.float32) + part[...].astype(jnp.float32)
        self.blocks[k] = total.astype(jnp.bfloat16)

    def onward(self, k):
        if k < 2:
            copy = self.copy(self.blocks.at[k], self.rzm.at[k], 3 + k, self.zo)
        else:
            copy = self.copy(self.blocks.at[k], self.rzf, 5, self.zr)
        self.sends.append((copy, self.mid))

        @pl.when(self.mid)
        def _():
            if k < 2:
                self.outward[k].wait_recv()
                self.add(k, self.rze.at[k])
            else:
                self.copy(self.blocks.at[0], self.rzm.at[0], 3, self.zo).wait_recv()
                self.add(k, self.rzm.at[0])
            copy.start()

    def last(self, out_ref):
        @pl.when(self.end)
        def _():
            self.copy(self.blocks.at[2], self.rzf, 5, self.zr).wait_recv()
            out_ref[...] = out_ref[...] + self.rzf[...].astype(jnp.float32)

        @pl.when(self.mid)
        def _():
            self.outward[2].wait_recv()
            self.copy(self.blocks.at[1], self.rzm.at[1], 4, self.zo).wait_recv()
            out_ref[...] = (
                out_ref[...]
                + self.rze[2].astype(jnp.float32)
                + self.rzm[1].astype(jnp.float32)
            )

    def drain(self):
        for copy, cond in self.sends:
            pl.when(cond)(functools.partial(copy.wait_send))

    @staticmethod
    def scratch(width):
        low, dma = jnp.bfloat16, pltpu.SemaphoreType.DMA
        return [
            pltpu.VMEM((3, 128, width), low),
            pltpu.VMEM((3, 128, width), low),
            pltpu.VMEM((2, 128, width), low),
            pltpu.VMEM((128, width), low),
            dma((6,)),
            dma((6,)),
        ]


class AllGather:
    def __init__(self, held, own_ref, ssem, rsem, metas=None, own_meta=None, msem=None, mrsem=None):
        self.dp, self.z, self.dc, self.dx, self.dy = place()
        z = self.z
        self.zr, self.zo = z + 1 - 2 * (z % 2), 3 - z
        self.mid = z * (3 - z) > 0
        self.zs = [z, self.zr, 2 - z // 2, 3 - 3 * (z // 2)]
        self.held, self.own_ref, self.ssem, self.rsem = held, own_ref, ssem, rsem
        self.metas, self.own_meta, self.msem, self.mrsem = metas, own_meta, msem, mrsem
        self.sends = []

    def send(self, block, part, dp_to, z_to, cond=None, own=False):
        half = pl.ds(part * 64, 64)
        view = self.held.at[block, half]
        source = self.own_ref.at[half] if own else view
        index = len(self.sends)
        copies = [
            pltpu.make_async_remote_copy(
                source, view, self.ssem.at[index], self.rsem.at[block, part],
                device_id=at(dp_to, z_to), device_id_type=MESH,
            )
        ]
        if part == 0 and self.metas is not None:
            copies.append(
                pltpu.make_async_remote_copy(
                    self.own_meta if own else self.metas.at[block], self.metas.at[block],
                    self.msem.at[index], self.mrsem.at[block],
                    device_id=at(dp_to, z_to), device_id_type=MESH,
                )
            )
        self.sends.append((copies, cond))

        def go():
            for copy in copies:
                copy.start()

        when_or_now(cond, go)

    def arrive(self, block, part):
        view = self.held.at[block, pl.ds(part * 64, 64)]
        here = dict(device_id=at(self.dp, self.zr), device_id_type=MESH)
        pltpu.make_async_remote_copy(
            view, view, self.ssem.at[0], self.rsem.at[block, part], **here
        ).wait_recv()
        if part == 0 and self.metas is not None:
            pltpu.make_async_remote_copy(
                self.metas.at[block], self.metas.at[block], self.msem.at[0], self.mrsem.at[block],
                **here
            ).wait_recv()

    def first(self, k):
        dp, z, dx, dy, dc = self.dp, self.z, self.dx, self.dy, self.dc
        block = dp * 4 + self.zs[k]
        own = k == 0
        for part in (0, 1):
            if k > 0:
                self.arrive(block, part)
            if k == 0:
                self.send(block, part, dp, self.zr, None, own)
                self.send(block, part, dp, self.zo, self.mid, own)
            else:
                self.send(block, part, dp, self.zo if k == 1 else self.zr, self.mid)
            self.send(block, part, dp + (dx if part == 0 else dy), z, None, own)
        self.send(block, 1, dp + dx, z, None, own)
        self.send(block, 0, dp + dy, z, None, own)
        self.send(block, 0, dp + dc, z, None, own)
        self.send(block, 1, dp + dc, z, None, own)

    def second(self, k):
        dp, z, dx, dy, dc = self.dp, self.z, self.dx, self.dy, self.dc
        bx, by = (dp + dx) * 4 + self.zs[k], (dp + dy) * 4 + self.zs[k]
        self.arrive(bx, 0)
        self.send(bx, 0, dp + dy, z)
        self.send(bx, 0, dp + dc, z)
        self.arrive(by, 1)
        self.send(by, 1, dp + dx, z)
        self.send(by, 1, dp + dc, z)
        self.arrive(bx, 1)
        self.send(bx, 1, dp + dc, z)
        self.arrive(by, 0)
        self.send(by, 0, dp + dc, z)

    def third(self, k):
        block = (self.dp + self.dx + self.dy) * 4 + self.zs[k]
        for part in (0, 1):
            self.arrive(block, part)
            self.send(block, part, self.dp + self.dc, self.z)

    def across(self, k, step):
        block = (self.dp + self.dc + step) * 4 + self.zs[k]
        self.arrive(block, 0)
        self.arrive(block, 1)

    def drain(self):
        for copies, cond in self.sends:

            def done(copies=copies):
                for copy in copies:
                    copy.wait_send()

            when_or_now(cond, done)


class Dispatcher:
    def __init__(self, held, stage, spare, slots_ref, osem):
        self.held, self.stage, self.spare = held, stage, spare
        self.slots_ref, self.osem = slots_ref, osem
        self.count = 0

    def put(self, start, slot):
        return pltpu.make_async_copy(
            self.stage.at[slot], self.slots_ref.at[:, pl.ds(start, MAIN), :], self.osem.at[slot]
        )

    def block(self, block, onehot):
        slot, group = self.count % 2, block // 8
        width = self.held.shape[2]
        if self.count >= 2:
            self.put(block * MAIN, slot).wait()

        def tile(step, carry):
            lanes = pl.ds(pl.multiple_of(step * 1024, 1024), 1024)
            rows = jnp.dot(onehot, self.held[block, :, lanes], preferred_element_type=jnp.float32)
            self.stage[slot, :, :, lanes] = rows[:128].astype(jnp.bfloat16).reshape(8, MAIN, 1024)
            extra = rows[128:].astype(jnp.bfloat16)
            self.spare[group, :, lanes] = self.spare[group, :, lanes] + extra
            return carry

        lax.fori_loop(0, width // 1024, tile, 0)
        self.put(block * MAIN, slot).start()
        self.count += 1

    def end(self):
        width = self.held.shape[2]
        for group in range(4):
            slot = group % 2
            self.put(512 + group * MAIN, slot).wait()
            self.stage[slot] = self.spare[group].reshape(8, MAIN, width)
            self.put(512 + group * MAIN, slot).start()
        for slot in range(2):
            self.put(512, slot).wait()


def arrival_order(gather):
    dp, dc, dx, dy, zs = gather.dp, gather.dc, gather.dx, gather.dy, gather.zs
    order = []
    for k in range(6):
        column = []
        if k < 4:
            column.append((k, 0))
        if 1 <= k < 5:
            column += [(k - 1, dx), (k - 1, dy)]
        if k >= 2:
            column.append((k - 2, dx + dy))
        across = [(k - 1, dc)] if 1 <= k < 5 else []
        if k >= 2:
            across += [(k - 2, dc + step) for step in (dx, dy, dx + dy)]
        order.append([[(dp + to) * 4 + zs[j] for j, to in part] for part in (column, across)])
    return order


def gather_forward(gather, k):
    if k < 4:
        gather.first(k)
    if 1 <= k < 5:
        gather.second(k - 1)
    if k >= 2:
        gather.third(k - 2)


def gather_process(gather, order, k, process):
    for block in order[k][0]:
        process(block)
    for block in order[k][1]:
        gather.arrive(block, 0)
        gather.arrive(block, 1)
        process(block)


def rotate(values, cosines, sines):
    return values * cosines + pltpu.roll(values, HD // 2, 1) * sines


def head_probs(query, key, seq_column, seq_row):
    scores = lax.dot_general(
        query, key, (((1,), (1,)), ((), ())), preferred_element_type=jnp.float32
    ) * (HD ** (-0.5))
    scores = jnp.where(seq_column == seq_row, scores, NEGATIVE)
    raised = jnp.exp(scores - jnp.max(scores, axis=1, keepdims=True))
    return raised / jnp.sum(raised, axis=1, keepdims=True)


def head_gain(gains_ref, first):
    lane = lax.broadcasted_iota(jnp.int32, (8, 128), 1)
    keep = jnp.logical_and(lane >= first, lane < first + 16)
    total = jnp.zeros((8, 128), jnp.float32)
    for block in range(8):
        part = jnp.where(keep, jnp.broadcast_to(gains_ref[block, 4:5, :], (8, 128)), 0.0)
        shift = (16 * block - first) % 128
        total = total + (pltpu.roll(part, shift, 1) if shift else part)
    return total[:1]


def front_kernel(
    wq_ref, wk_ref, wv_ref, wo_ref, router_ref, tok_ref, cot_ref, routes_in, gains_in, cos_ref, sin_ref, seqc_ref, seqr_ref,
    weights_ref, group_ref, slots_ref, gains_ref, onehot_ref, routes_ref, normed_ref, projq_ref, projk_ref,
    query_ref, key_ref, value_ref, ctx_ref, out_ref,
    wheld, theld, gheld, held, metas, stage, spare, lsem, wsend, wrecv, gsend, grecv, zsend, zrecv,
    dsend, drecv, msend, mrecv, osem, fsem, *line_refs
):
    dp, z, dc, dx, dy = place()
    zr, zo = z + 1 - 2 * (z % 2), 3 - z
    mid = z * (3 - z) > 0
    f32, low = jnp.float32, jnp.bfloat16
    heads = query_ref.shape[1]
    width = tok_ref.shape[1]
    line = LineScatter(dp, z, *line_refs)
    gather = AllGather(held, cot_ref, dsend, drecv, metas, routes_in, msend, mrecv)
    order = arrival_order(gather)
    picker = Dispatcher(held, stage, spare, slots_ref, osem)
    own_block = dp * 4 + z
    own_rows = pl.ds(pl.multiple_of(dp * 256, 256), 256)
    fill = []
    for source, column, count in (
        (wq_ref, 0, heads), (wk_ref, heads, heads), (wv_ref, 2 * heads, heads),
        (wo_ref.at[pl.ds(0, 256)], 3 * heads, 256), (wo_ref.at[pl.ds(256, 256)], 3 * heads + 256, 256),
        (router_ref, 4 * heads, 128),
    ):
        target = wheld.at[own_rows, pl.ds(column, count)]
        fill.append(pltpu.make_async_copy(source, target, fsem.at[len(fill)]))
    for copy in fill:
        copy.start()
    greet([(dp + dc, z), (dp + dx, z), (dp + dy, z), (dp, zr)], (dp, zo), mid, z * (3 - z) // 2)
    sends = []

    def spot(block, part):
        return wheld.at[pl.ds(pl.multiple_of(block * 256 + part * 128, 128), 128)]

    def send(block, part, dp_to, own=False):
        source = spot(block, part)
        index = len(sends)
        copies = [
            pltpu.make_async_remote_copy(
                source, spot(block, part), wsend.at[index], wrecv.at[block, part],
                device_id=at(dp_to, z), device_id_type=MESH,
            )
        ]
        if part == 0:
            copies.append(
                pltpu.make_async_remote_copy(
                    gains_in if own else gheld.at[block], gheld.at[block],
                    gsend.at[index], grecv.at[block],
                    device_id=at(dp_to, z), device_id_type=MESH,
                )
            )
        for copy in copies:
            copy.start()
        sends.append(copies)

    def arrive(block, part):
        here = dict(device_id=at(dp + dx, z), device_id_type=MESH)
        pltpu.make_async_remote_copy(
            spot(block, part), spot(block, part), wsend.at[0], wrecv.at[block, part], **here
        ).wait_recv()
        if part == 0:
            pltpu.make_async_remote_copy(
                gheld.at[block], gheld.at[block], gsend.at[0], grecv.at[block], **here
            ).wait_recv()

    zsends = []

    def z_send(source, block, z_to, cond=None):
        copy = pltpu.make_async_remote_copy(
            source, theld.at[block], zsend.at[len(zsends)], zrecv.at[block],
            device_id=at(dp, z_to), device_id_type=MESH,
        )
        when_or_now(cond, functools.partial(copy.start))
        zsends.append((copy, cond))

    def z_arrive(block):
        pltpu.make_async_remote_copy(
            theld.at[block], theld.at[block], zsend.at[0], zrecv.at[block],
            device_id=at(dp, zr), device_id_type=MESH,
        ).wait_recv()

    z_send(tok_ref, z, zr)
    z_send(tok_ref, z, zo, mid)
    for copy in fill:
        copy.wait()
    send(dp, 0, dp + dx, True)
    send(dp, 1, dp + dy, True)
    send(dp, 1, dp + dx, True)
    send(dp, 0, dp + dy, True)
    send(dp, 0, dp + dc, True)
    send(dp, 1, dp + dc, True)
    local = [
        pltpu.make_async_copy(tok_ref, theld.at[z], lsem.at[1]),
        pltpu.make_async_copy(gains_in, gheld.at[dp], lsem.at[2]),
        pltpu.make_async_copy(cot_ref, held.at[own_block], lsem.at[3]),
        pltpu.make_async_copy(routes_in, metas.at[own_block], lsem.at[4]),
    ]
    for copy in local:
        copy.start()
    spare[...] = jnp.zeros_like(spare)
    z_arrive(zr)
    z_send(theld.at[zr], zr, zo, mid)
    bx, by, bxy = dp + dx, dp + dy, dp + dx + dy
    arrive(bx, 0)
    send(bx, 0, dp + dy)
    send(bx, 0, dp + dc)
    arrive(by, 1)
    send(by, 1, dp + dx)
    send(by, 1, dp + dc)
    gather.first(0)
    far = 2 - z // 2
    z_arrive(far)
    z_send(theld.at[far], far, zr, mid)
    arrive(bx, 1)
    send(bx, 1, dp + dc)
    arrive(by, 0)
    send(by, 0, dp + dc)
    last = 3 - 3 * (z // 2)
    z_arrive(last)
    z_send(theld.at[last], last, zr, mid)
    for part in (0, 1):
        arrive(bxy, part)
        send(bxy, part, dp + dc)
    for block in (dp, bx, by, bxy):
        for part in (0, 1):
            arrive(block + dc, part)
    for copy in local:
        copy.wait()
    kept = [
        pltpu.make_async_copy(wheld, weights_ref, lsem.at[0]),
        pltpu.make_async_copy(theld, group_ref, lsem.at[1]),
    ]
    for copy in kept:
        copy.start()

    def process(block):
        onehot = slot_matrix(metas[block], block, dp * 8)
        onehot_ref[block] = onehot
        picker.block(block, onehot)

    scale = jnp.concatenate(
        [gheld[j // 2, j % 2 : j % 2 + 1, :] for j in range(width // 128)], axis=1
    )

    def norm_rows(step, carry):
        values = theld[step].astype(f32)
        inverse = lax.rsqrt(jnp.mean(values * values, axis=1, keepdims=True) + EPSILON)
        rows = pl.ds(pl.multiple_of(step * 128, 128), 128)
        normed_ref[rows, :] = (values * inverse * scale).astype(low)
        return carry

    gains_ref[...] = gheld[...]
    lax.fori_loop(0, 4, norm_rows, 0)

    def project(column):
        cols = slice(column * heads, column * heads + heads)
        return jnp.dot(normed_ref[...], wheld[:, cols], preferred_element_type=f32)

    projq_ref[...] = project(0)
    projk_ref[...] = project(1)
    value_ref[...] = project(2).astype(low)
    gather_forward(gather, 1)
    process(own_block)
    cosines, sines = cos_ref[...], sin_ref[...]
    query_gain, key_gain = head_gain(gheld, 0), head_gain(gheld, 16)

    def one_head(h, carry):
        cols = pl.ds(pl.multiple_of(h * HD, HD), HD)
        for source, gain, target in (
            (projq_ref, query_gain, query_ref), (projk_ref, key_gain, key_ref),
        ):
            values = source[:, cols]
            inverse = lax.rsqrt(jnp.mean(values * values, axis=1, keepdims=True) + EPSILON)
            target[:, cols] = rotate(values * inverse * gain, cosines, sines).astype(low)
        for start in range(0, 512, 256):
            rows = slice(start, start + 256)
            probs = head_probs(
                query_ref[rows, cols], key_ref[:, cols], seqc_ref[rows, :1], seqr_ref[:1, :]
            )
            ctx_ref[rows, cols] = jnp.dot(
                probs.astype(low), value_ref[:, cols], preferred_element_type=f32
            ).astype(low)
        return carry

    lax.fori_loop(0, heads // HD // 2, one_head, 0)
    gather_forward(gather, 2)
    lax.fori_loop(heads // HD // 2, heads // HD, one_head, 0)
    for k in range(4):
        rows = pl.ds(pl.multiple_of(line.zs[k] * 128, 128), 128)
        for start in range(0, width, 256):
            lanes = slice(start, start + 256)
            piece = jnp.dot(
                ctx_ref[rows, :256], wheld[lanes, 3 * heads : 3 * heads + 256],
                preferred_element_type=f32,
            ) + jnp.dot(
                ctx_ref[rows, 256:], wheld[lanes, 3 * heads + 256 : 4 * heads],
                preferred_element_type=f32,
            )
            if k < 3:
                line.blocks[k, :, lanes] = piece.astype(low)
            else:
                out_ref[:, lanes] = piece
        if k < 3:
            line.ready(k)
    gather_forward(gather, 3)
    gather_process(gather, order, 1, process)
    line.onward(0)
    line.onward(1)
    gather_process(gather, order, 2, process)
    gather_forward(gather, 4)
    line.onward(2)
    gather_process(gather, order, 3, process)
    gather_process(gather, order, 4, process)
    gather_forward(gather, 5)
    line.last(out_ref)
    gather_process(gather, order, 5, process)
    picker.end()
    routes_ref[...] = metas[...]
    for copy in kept:
        copy.wait()
    for copies in sends:
        for copy in copies:
            copy.wait_send()
    for copy, cond in zsends:
        when_or_now(cond, functools.partial(copy.wait_send))
    gather.drain()
    line.drain()


def front(shards, tokens, cotangent, routes, gains, cosines, sines, seq_column, seq_row, heads):
    width = tokens.shape[1]
    rows = 4 * tokens.shape[0]
    f32, low = jnp.float32, jnp.bfloat16
    anywhere = pl.BlockSpec(memory_space=pl.ANY)
    vmem = pl.BlockSpec(memory_space=pltpu.VMEM)
    dma = pltpu.SemaphoreType.DMA
    narrow = jax.ShapeDtypeStruct((rows, heads), low)
    return pl.pallas_call(
        front_kernel,
        name="front",
        out_shape=(
            jax.ShapeDtypeStruct((width, 4 * heads + 128), low),
            jax.ShapeDtypeStruct((4, 128, width), low),
            jax.ShapeDtypeStruct((8, 576, width), low),
            jax.ShapeDtypeStruct((8, 8, 128), f32),
            jax.ShapeDtypeStruct((32, 256, 128), low),
            jax.ShapeDtypeStruct((32, 8, 128), f32),
            jax.ShapeDtypeStruct((rows, width), low),
            jax.ShapeDtypeStruct((rows, heads), f32),
            jax.ShapeDtypeStruct((rows, heads), f32),
            narrow, narrow, narrow, narrow,
            jax.ShapeDtypeStruct((128, width), f32),
        ),
        in_specs=[anywhere] * 5 + [vmem] * 8,
        out_specs=(anywhere,) * 3 + (vmem,) * 11,
        scratch_shapes=[
            pltpu.VMEM((width, 4 * heads + 128), low),
            pltpu.VMEM((4, 128, width), low),
            pltpu.VMEM((8, 8, 128), f32),
            pltpu.VMEM((32, 128, width), low),
            pltpu.VMEM((32, 8, 128), f32),
            pltpu.VMEM((2, 8, MAIN, width), low),
            pltpu.VMEM((4, 128, width), low),
            dma((9,)), dma((14,)), dma((8, 2)), dma((14,)), dma((8,)), dma((5,)), dma((4,)),
            dma((72,)), dma((32, 2)), dma((72,)), dma((32,)), dma((2,)), dma((6,)),
        ]
        + LineScatter.scratch(width),
        compiler_params=pltpu.CompilerParams(
            collective_id=0, has_side_effects=True, vmem_limit_bytes=VMEM_LIMIT
        ),
        cost_estimate=pl.CostEstimate(
            flops=5_000_000_000, bytes_accessed=100_000_000, transcendentals=2_000_000
        ),
    )(*shards, tokens, cotangent, routes, gains, cosines, sines, seq_column, seq_row)


def gather_kernel(
    x_ref, meta_ref, onehot_ref, routes_ref, slots_ref, gate_ref,
    held, metas, stage, spare, lsem, ssem, rsem, msem, mrsem, osem,
):
    dp, z, dc, dx, dy = place()
    own = dp * 4 + z
    gather = AllGather(held, held.at[own], ssem, rsem, metas, metas.at[own], msem, mrsem)
    order = arrival_order(gather)
    picker = Dispatcher(held, stage, spare, slots_ref, osem)
    local = [
        pltpu.make_async_copy(x_ref, held.at[own], lsem.at[0]),
        pltpu.make_async_copy(meta_ref, metas.at[own], lsem.at[1]),
    ]
    for copy in local:
        copy.start()
    greet(
        [(dp + dc, z), (dp + dx, z), (dp + dy, z), (dp, gather.zr)],
        (dp, gather.zo), gather.mid, z * (3 - z) // 2,
    )
    spare[...] = jnp.zeros_like(spare)
    gate_ref[:, 512:576, :] = jnp.zeros((8, 64, 128), jnp.float32)
    for copy in local:
        copy.wait()
    experts = (lax.broadcasted_iota(jnp.int32, (8, 128), 0) + dp * 8).astype(jnp.float32)

    def process(block):
        onehot = onehot_ref[block]
        gates_here = jnp.zeros((8, 128), jnp.float32)
        for j in range(TOPK):
            gates_here = gates_here + jnp.where(
                routes_ref[block, j : j + 1, :] == experts, metas[block, j : j + 1, :], 0.0
            )
        wide = jnp.broadcast_to(gates_here[:, None, :], (8, MAIN, 128)).reshape(128, 128)
        taken = onehot.astype(jnp.float32)
        main_gate = jnp.sum(taken[:128] * wide, axis=1, keepdims=True)
        spare_gate = jnp.sum(taken[128:] * wide, axis=1, keepdims=True)
        gate_ref[:, pl.ds(pl.multiple_of(block * MAIN, MAIN), MAIN), :] = jnp.broadcast_to(
            main_gate, (128, 128)
        ).reshape(8, MAIN, 128)
        spare_rows = pl.ds(pl.multiple_of(512 + (block // 8) * MAIN, MAIN), MAIN)
        gate_ref[:, spare_rows, :] = gate_ref[:, spare_rows, :] + jnp.broadcast_to(
            spare_gate, (128, 128)
        ).reshape(8, MAIN, 128)
        picker.block(block, onehot)

    for k in range(6):
        gather_forward(gather, k)
        gather_process(gather, order, k, process)
    picker.end()
    gather.drain()


def gather_slots(rows, meta, onehot, routes):
    count, width = rows.shape
    anywhere = pl.BlockSpec(memory_space=pl.ANY)
    vmem = pl.BlockSpec(memory_space=pltpu.VMEM)
    dma = pltpu.SemaphoreType.DMA
    return pl.pallas_call(
        gather_kernel,
        name="gather_x",
        out_shape=(
            jax.ShapeDtypeStruct((8, 576, width), jnp.bfloat16),
            jax.ShapeDtypeStruct((8, 576, 128), jnp.float32),
        ),
        in_specs=[anywhere, anywhere, vmem, vmem],
        out_specs=(anywhere, vmem),
        scratch_shapes=[
            pltpu.VMEM((32, count, width), jnp.bfloat16),
            pltpu.VMEM((32, 8, 128), jnp.float32),
            pltpu.VMEM((2, 8, MAIN, width), jnp.bfloat16),
            pltpu.VMEM((4, 128, width), jnp.bfloat16),
            dma((2,)), dma((72,)), dma((32, 2)), dma((72,)), dma((32,)), dma((2,)),
        ],
        compiler_params=pltpu.CompilerParams(
            collective_id=1, has_side_effects=True, vmem_limit_bytes=VMEM_LIMIT
        ),
        cost_estimate=pl.CostEstimate(
            flops=4_300_000_000, bytes_accessed=100_000_000, transcendentals=0
        ),
    )(rows, meta, onehot, routes)


def return_kernel(
    y_ref, g_ref, onehot_ref, outy_ref, outg_ref,
    rows_in, to_core, sums, ry0, rx1, rx0, ry1, rze, rzm, rzf,
    ysem, csend, crecv, xsend, xrecv, zsend, zrecv,
):
    dp, z, dc, dx, dy = place()
    zr, zo = z + 1 - 2 * (z % 2), 3 - z
    mid = z * (3 - z) > 0
    end = z * (3 - z) < 1
    half = 64
    sources, outs = (y_ref, g_ref), (outy_ref, outg_ref)
    zs = [3 - 3 * (z // 2), 2 - z // 2, zr, z]
    greet([(dp + dc, z), (dp + dx, z), (dp + dy, z), (dp, zr)], (dp, zo), mid, z * (3 - z) // 2)
    lo, hi = pl.ds(0, half), pl.ds(half, half)
    xsends, zsends = [[] for _ in range(8)], []

    def lanes_of(s):
        return pl.ds(0, sources[s // 4].shape[2])

    def tiles_of(s):
        width = sources[s // 4].shape[2]
        return [slice(i, min(i + 512, width)) for i in range(0, width, 512)]

    def dest(s, step):
        r = 3 - step % 4
        base = dp + dc - dc * (step // 4)
        return (base + (r % 2) * dx + (r // 2) * dy) * 4 + zs[s % 4]

    def fetch(s, block, slot):
        source, lanes = sources[s // 4], lanes_of(s)
        return [
            pltpu.make_async_copy(
                source.at[:, pl.ds(block * MAIN, MAIN), :],
                rows_in.at[slot, pl.ds(0, 8), :, lanes], ysem.at[slot, 0],
            ),
            pltpu.make_async_copy(
                source.at[:, pl.ds(512 + (block // 8) * MAIN, MAIN), :],
                rows_in.at[slot, pl.ds(8, 8), :, lanes], ysem.at[slot, 1],
            ),
        ]

    def partial_tile(block, slot, lanes):
        return lax.dot_general(
            onehot_ref[block], rows_in[slot, :, :, lanes].reshape(256, lanes.stop - lanes.start),
            (((0,), (0,)), ((), ())), preferred_element_type=jnp.float32,
        )

    def core_copy(r, s):
        lanes = lanes_of(s)
        return pltpu.make_async_remote_copy(
            to_core.at[s % 4, r, :, lanes], sums.at[s, r, :, lanes], csend.at[s, r], crecv.at[s, r],
            device_id=at(dp + dc, z), device_id_type=MESH,
        )

    def xy_copy(r, rows, target, index, s, dp_to):
        lanes = lanes_of(s)
        return pltpu.make_async_remote_copy(
            sums.at[s, r, rows, lanes], target.at[:, lanes], xsend.at[index, s], xrecv.at[index, s],
            device_id=at(dp_to, z), device_id_type=MESH,
        )

    def z_copy(s, target, index, z_to):
        lanes = lanes_of(s)
        index = 6 * (s // 4) + index
        return pltpu.make_async_remote_copy(
            sums.at[s, 0, :, lanes], target.at[:, lanes], zsend.at[index], zrecv.at[index],
            device_id=at(dp, z_to), device_id_type=MESH,
        )

    def add_to(s, r, rows, *others):
        lanes = lanes_of(s)
        total = sums[s, r, rows, lanes].astype(jnp.float32)
        for other in others:
            total = total + other[:, lanes].astype(jnp.float32)
        sums[s, r, rows, lanes] = total.astype(jnp.bfloat16)

    def stage_core(s):
        def load(block, slot, following=None):
            for copy in fetch(s, block, slot):
                copy.wait()
            if following is not None:
                for copy in fetch(s, following, 1 - slot):
                    copy.start()

        def partner(step, slot, following):
            r = 3 - step
            block = dest(s, step)
            load(block, slot, following)
            if s >= 4:
                core_copy(r, s - 4).wait_send()
            for lanes in tiles_of(s):
                to_core[s % 4, r, :, lanes] = partial_tile(block, slot, lanes).astype(jnp.bfloat16)
            core_copy(r, s).start()

        batch = [
            xy_copy(3, lo, ry0.at[1, s], 0, s, dp + dy),
            xy_copy(3, hi, rx1.at[1, s], 1, s, dp + dx),
            xy_copy(2, lo, ry0.at[0, s], 2, s, dp + dy),
            xy_copy(1, hi, rx1.at[0, s], 3, s, dp + dx),
        ]
        xsends[s].extend(batch)

        def both(i, carry):
            r = 3 - i
            block = dest(s, 4 + i)

            @pl.when(i < 3)
            def _():
                partner(i + 1, 1, block)

            late = i // 2
            following = (1 - late) * dest(s, i + 2) + late * dest(s, 5 + i)
            slot = i // 3
            load(block, slot)

            @pl.when(i < 3)
            def _():
                for copy in fetch(s, following, 1):
                    copy.start()

            if s < 7:

                @pl.when(i == 3)
                def _():
                    for copy in fetch(s + 1, dest(s + 1, 0), 0):
                        copy.start()

            core_copy(r, s).wait_recv()
            for lanes in tiles_of(s):
                sums[s, r, :, lanes] = (
                    partial_tile(block, slot, lanes) + sums[s, r, :, lanes].astype(jnp.float32)
                ).astype(jnp.bfloat16)
            for when, copies in enumerate((batch[:2], batch[2:3], batch[3:])):

                @pl.when(i == when)
                def _():
                    for copy in copies:
                        copy.start()

            return carry

        partner(0, 0, dest(s, 1))
        lax.fori_loop(0, 4, both, 0)

    def stage_cross(s):
        xsends[s][0].wait_recv()
        add_to(s, 1, lo, ry0.at[1, s])
        across = xy_copy(1, lo, rx0.at[s], 4, s, dp + dx)
        across.start()
        xsends[s][1].wait_recv()
        add_to(s, 2, hi, rx1.at[1, s])
        down = xy_copy(2, hi, ry1.at[s], 5, s, dp + dy)
        down.start()
        xsends[s].extend([across, down])

    def outward(s):
        return z_copy(s, rze.at[3 * (s // 4) + s % 4], s % 4, zr)

    def stage_line(s):
        for j in range(2, 6):
            xsends[s][j].wait_recv()
        if s % 4 < 3:
            add_to(s, 0, lo, ry0.at[0, s], rx0.at[s])
            add_to(s, 0, hi, rx1.at[0, s], ry1.at[s])
            copy = outward(s)
            zsends.append((copy, end))
            pl.when(end)(functools.partial(copy.start))
        else:
            out_ref, lanes = outs[s // 4], lanes_of(s)
            for rows, first, second in ((lo, ry0.at[0, s], rx0.at[s]), (hi, rx1.at[0, s], ry1.at[s])):
                out_ref[rows, :] = (
                    sums[s, 0, rows, lanes].astype(jnp.float32)
                    + first[:, lanes].astype(jnp.float32)
                    + second[:, lanes].astype(jnp.float32)
                )

    def stage_onward(s):
        p, k = s // 4, s % 4
        if k < 2:
            onward = z_copy(s, rzm.at[2 * p + k], 3 + k, zo)
        else:
            onward = z_copy(s, rzf.at[p], 5, zr)
        zsends.append((onward, mid))

        @pl.when(mid)
        def _():
            if k < 2:
                outward(s).wait_recv()
                add_to(s, 0, slice(None), rze.at[3 * p + k])
            else:
                z_copy(4 * p, rzm.at[2 * p], 3, zo).wait_recv()
                add_to(s, 0, slice(None), rzm.at[2 * p])
            onward.start()

    def stage_last(p):
        out_ref, lanes = outs[p], lanes_of(4 * p)

        @pl.when(end)
        def _():
            z_copy(4 * p + 2, rzf.at[p], 5, zr).wait_recv()
            out_ref[...] = out_ref[...] + rzf[p, :, lanes].astype(jnp.float32)

        @pl.when(mid)
        def _():
            outward(4 * p + 2).wait_recv()
            z_copy(4 * p + 1, rzm.at[2 * p + 1], 4, zo).wait_recv()
            out_ref[...] = (
                out_ref[...]
                + rze[3 * p + 2, :, lanes].astype(jnp.float32)
                + rzm[2 * p + 1, :, lanes].astype(jnp.float32)
            )

    for copy in fetch(0, dest(0, 0), 0):
        copy.start()
    for t in range(10):
        if t < 8:
            stage_core(t)
        if 1 <= t < 9:
            stage_cross(t - 1)
        if t >= 2:
            stage_line(t - 2)
        if t % 4 == 3:
            stage_onward(t - 3)
        if t >= 4 and t % 4 == 0:
            stage_onward(t - 2)
            stage_onward(t - 3)
        if t >= 5 and t % 4 == 1:
            stage_last(t // 4 - 1)
    for s in range(4, 8):
        for r in range(4):
            core_copy(r, s).wait_send()
    for batch in xsends:
        for copy in batch:
            copy.wait_send()
    for copy, cond in zsends:
        pl.when(cond)(functools.partial(copy.wait_send))


def return_rows(y_slots, gin_slots, onehot):
    width, narrow = y_slots.shape[2], gin_slots.shape[2]
    anywhere = pl.BlockSpec(memory_space=pl.ANY)
    vmem = pl.BlockSpec(memory_space=pltpu.VMEM)
    dma = pltpu.SemaphoreType.DMA
    low = jnp.bfloat16
    return pl.pallas_call(
        return_kernel,
        name="return_rows",
        out_shape=(
            jax.ShapeDtypeStruct((128, width), jnp.float32),
            jax.ShapeDtypeStruct((128, narrow), jnp.float32),
        ),
        in_specs=[anywhere, anywhere, vmem],
        out_specs=(vmem, vmem),
        scratch_shapes=[
            pltpu.VMEM((2, 16, MAIN, width), low),
            pltpu.VMEM((4, 4, 128, width), low),
            pltpu.VMEM((8, 4, 128, width), low),
            pltpu.VMEM((2, 8, 64, width), low),
            pltpu.VMEM((2, 8, 64, width), low),
            pltpu.VMEM((8, 64, width), low),
            pltpu.VMEM((8, 64, width), low),
            pltpu.VMEM((6, 128, width), low),
            pltpu.VMEM((4, 128, width), low),
            pltpu.VMEM((2, 128, width), low),
            dma((2, 2)), dma((8, 4)), dma((8, 4)), dma((6, 8)), dma((6, 8)), dma((12,)), dma((12,)),
        ],
        compiler_params=pltpu.CompilerParams(
            collective_id=2, has_side_effects=True, vmem_limit_bytes=VMEM_LIMIT
        ),
        cost_estimate=pl.CostEstimate(
            flops=8_600_000_000, bytes_accessed=300_000_000, transcendentals=0
        ),
    )(y_slots, gin_slots, onehot)


def finish_kernel(
    rows_ref, tok_ref, projq_ref, projk_ref, query_ref, key_ref, value_ref, ctx_ref, ga_ref, w_ref,
    gains_ref, cos_ref, sin_ref, seqc_ref, seqr_ref, side_ref, stat_ref,
    gw_ref, gwo_ref, dx_ref, small_ref,
    gqkv_ref, gctx_ref, dx_all, to_core, from_core, sums, ry0, rx1, rx0, ry1, gain, zside,
    csend, crecv, xsend, xrecv, ssend, srecv, *line_refs,
):
    dp, z, dc, dx, dy = place()
    line = LineScatter(dp, z, *line_refs)
    dxs = line.blocks
    f32, low = jnp.float32, jnp.bfloat16
    half = 128
    heads = query_ref.shape[1]
    width = rows_ref.shape[1]
    others = [(z + i) % 4 for i in (1, 2, 3)]
    greet([(dp + dc, z), (dp + dx, z), (dp + dy, z)] + [(dp, other) for other in others])
    nt = (((1,), (1,)), ((), ()))
    tn = (((0,), (0,)), ((), ()))
    lo, hi = pl.ds(0, half), pl.ds(half, half)
    early = 3 * heads + 128

    def mm(a, b, dims):
        return lax.dot_general(a, b, dims, preferred_element_type=f32)

    def dest(step):
        r = 3 - step % 4
        base = dp + dc - dc * (step // 4)
        return base + (r % 2) * dx + (r // 2) * dy

    def scatter(index, first, count, pieces):
        lanes = pl.ds(first, count)

        def core_copy(r):
            return pltpu.make_async_remote_copy(
                to_core.at[r, :, lanes], from_core.at[r, :, lanes],
                csend.at[index, r], crecv.at[index, r],
                device_id=at(dp + dc, z), device_id_type=MESH,
            )

        def xy_copy(r, rows, target, j, dp_to):
            return pltpu.make_async_remote_copy(
                sums.at[r, rows, lanes], target.at[:, lanes], xsend.at[index, j], xrecv.at[index, j],
                device_id=at(dp_to, z), device_id_type=MESH,
            )

        def add_to(r, rows, part):
            total = sums[r, rows, lanes].astype(f32) + part[:, lanes].astype(f32)
            sums[r, rows, lanes] = total.astype(low)

        copies = [
            xy_copy(3, lo, ry0.at[1], 0, dp + dy),
            xy_copy(3, hi, rx1.at[1], 1, dp + dx),
            xy_copy(2, lo, ry0.at[0], 2, dp + dy),
            xy_copy(1, hi, rx1.at[0], 3, dp + dx),
            xy_copy(1, lo, rx0, 4, dp + dx),
            xy_copy(2, hi, ry1, 5, dp + dy),
        ]

        def partner(step):
            r = 3 - step
            for part, value in pieces(dest(step)):
                to_core[r, :, part] = value.astype(low)
            core_copy(r).start()

        def both(i, carry):
            @pl.when(i < 3)
            def _():
                partner(i + 1)

            r = 3 - i
            core_copy(r).wait_recv()
            for part, value in pieces(dest(4 + i)):
                sums[r, :, part] = (value + from_core[r, :, part].astype(f32)).astype(low)
            for when, batch in enumerate((copies[:2], copies[2:3], copies[3:4])):

                @pl.when(i == when)
                def _():
                    for copy in batch:
                        copy.start()

            return carry

        def core():
            partner(0)
            lax.fori_loop(0, 4, both, 0)

        def cross():
            copies[0].wait_recv()
            add_to(1, lo, ry0.at[1])
            copies[4].start()
            copies[1].wait_recv()
            add_to(2, hi, rx1.at[1])
            copies[5].start()

        def wait():
            for copy in copies[2:]:
                copy.wait_recv()

        def drain():
            for r in range(4):
                core_copy(r).wait_send()
            for copy in copies:
                copy.wait_send()

        return core, cross, wait, drain

    def out_pieces(to):
        cols = pl.ds(pl.multiple_of(to * 256, 256), 256)
        out = mm(ctx_ref[...], ga_ref[:, cols], tn)
        yield slice(early, early + 256), out[:256]
        yield slice(early + 256, early + 512), out[256:]

    def head_pieces(to):
        cols = pl.ds(pl.multiple_of(to * 256, 256), 256)
        yield slice(0, 3 * heads), mm(rows_ref[:, cols], gqkv_ref[...], tn)
        yield slice(3 * heads, early), jnp.concatenate(
            [
                side_ref[to, :128, :].astype(f32),
                side_ref[to, 128:144, :].astype(f32) + gain[to],
                jnp.zeros((112, 128), f32),
            ],
            axis=0,
        )

    core_out, cross_out, wait_out, drain_out = scatter(0, early, heads, out_pieces)
    core_heads, cross_heads, wait_heads, drain_heads = scatter(1, 0, early, head_pieces)
    core_out()
    gain[...] = jnp.zeros_like(gain)
    cosines, sines = cos_ref[...], sin_ref[...]
    query_gain, key_gain = head_gain(gains_ref, 0), head_gain(gains_ref, 16)
    for i in range(2):
        column = 3 * heads + i * 256
        total_ctx = jnp.zeros((512, 256), f32)
        for start in range(0, width, 256):
            lanes = slice(start, start + 256)
            total_ctx = total_ctx + mm(ga_ref[:, lanes], w_ref[lanes, column : column + 256], nt)
        gctx_ref[:, i * 256 : i * 256 + 256] = total_ctx.astype(low)
    score_scale = HD ** (-0.5)

    def head_back(grad, source, rows, cols, gain_values, column):
        values = source[rows, cols]
        inverse = lax.rsqrt(jnp.mean(values * values, axis=1, keepdims=True) + EPSILON)
        turned = grad * cosines[rows] - pltpu.roll(grad, HD // 2, 1) * sines[rows]
        scaled = turned * gain_values
        inner = jnp.mean(scaled * values, axis=1, keepdims=True)
        target = pl.ds(pl.multiple_of(cols.start + column, HD), HD)
        gqkv_ref[rows, target] = ((scaled - values * inner * inverse * inverse) * inverse).astype(low)
        return jnp.sum(turned * values * inverse, axis=0, keepdims=True)

    def one_head(h, carry):
        query_part, key_part = carry
        cols = pl.ds(pl.multiple_of(h * HD, HD), HD)
        key, value = key_ref[:, cols], value_ref[:, cols]
        grad_key = jnp.zeros((key.shape[0], HD), f32)
        grad_value = jnp.zeros((key.shape[0], HD), f32)
        for start in range(0, 512, 256):
            rows = slice(start, start + 256)
            query, grad_ctx = query_ref[rows, cols], gctx_ref[rows, cols]
            probs = head_probs(query, key, seqc_ref[rows, :1], seqr_ref[:1, :])
            grad_value = grad_value + mm(probs.astype(low), grad_ctx, tn)
            grad_probs = mm(grad_ctx, value, nt)
            inner = jnp.sum(probs * grad_probs, axis=1, keepdims=True)
            grad_scores = (probs * (grad_probs - inner)).astype(low)
            grad_query = jnp.dot(grad_scores, key, preferred_element_type=f32) * score_scale
            grad_key = grad_key + mm(grad_scores, query, tn)
            query_part = query_part + head_back(
                grad_query, projq_ref, rows, cols, query_gain, 0
            )
        key_part = key_part + head_back(
            grad_key * score_scale, projk_ref, slice(0, 512), cols, key_gain, heads
        )
        target = pl.ds(pl.multiple_of(cols.start + 2 * heads, HD), HD)
        gqkv_ref[:, target] = grad_value.astype(low)
        return query_part, key_part

    zero_row = jnp.zeros((1, HD), f32)
    query_part, key_part = lax.fori_loop(0, heads // HD, one_head, (zero_row, zero_row))
    for to in range(8):
        gain[to, 4:5, :] = query_part
        gain[to, 5:6, :] = key_part
    cross_out()
    for start in range(0, width, 512):
        lanes = slice(start, start + 512)
        dx_all[:, lanes] = mm(gqkv_ref[...], w_ref[lanes, : 3 * heads], nt)
    for k in range(4):
        rows = pl.ds(pl.multiple_of(line.zs[k] * 128, 128), 128)
        square = jnp.zeros((128, 1), f32)
        for start in range(0, width, 512):
            values = tok_ref[rows, start : start + 512].astype(f32)
            square = square + jnp.sum(values * values, axis=1, keepdims=True)
        inverse = lax.rsqrt(square * (1.0 / width) + EPSILON)
        for start in range(0, width, 512):
            lanes = slice(start, start + 512)
            piece = dx_all[rows, lanes]
            scaled = tok_ref[rows, lanes].astype(f32) * inverse
            column = jnp.sum(piece * scaled, axis=0, keepdims=True)
            for j in range(4):
                to = start // 256 + j // 2
                row = slice(j % 2, j % 2 + 1)
                gain[to, row, :] = gain[to, row, :] + column[:, j * 128 : j * 128 + 128]
            if k < 3:
                dxs[k, :, lanes] = piece.astype(low)
            else:
                dx_ref[:, lanes] = piece
        if k < 3:
            line.ready(k)

    core_heads()
    line.onward(0)
    cross_heads()
    line.onward(1)
    line.onward(2)
    wait_out()
    wait_heads()

    def side_copy(i, source):
        return pltpu.make_async_remote_copy(
            zside.at[source], zside.at[source], ssend.at[i], srecv.at[source],
            device_id=at(dp, others[i]), device_id_type=MESH,
        )

    def total(part, lanes, first, second):
        return (
            sums[0, part, lanes].astype(f32)
            + first[:, lanes].astype(f32)
            + second[:, lanes].astype(f32)
        )

    sides = slice(3 * heads, early)
    zside[z, :128, :] = total(lo, sides, ry0.at[0], rx0)
    zside[z, 128:144, :] = total(hi, sides, rx1.at[0], ry1)[:16] + stat_ref[...]
    for i in range(3):
        side_copy(i, z).start()
    for rows, first, second in ((lo, ry0.at[0], rx0), (hi, rx1.at[0], ry1)):
        gw_ref[rows, :] = total(rows, slice(0, 3 * heads), first, second)
        gwo_ref[rows, :] = total(rows, slice(early, early + 256), first, second)
        below = pl.ds(256 + rows.start, half)
        gwo_ref[below, :] = total(rows, slice(early + 256, early + 512), first, second)

    line.last(dx_ref)
    for i in range(3):
        side_copy(i, others[i]).wait_recv()
    small_ref[...] = (zside[0] + zside[1]) + (zside[2] + zside[3])
    drain_out()
    drain_heads()
    line.drain()
    for i in range(3):
        side_copy(i, z).wait_send()


def finish(rows, tok, attention, grad_attn, weights, tables, side, stats):
    width = rows.shape[1]
    heads = attention[0].shape[1]
    f32, low = jnp.float32, jnp.bfloat16
    vmem = pl.BlockSpec(memory_space=pltpu.VMEM)
    dma = pltpu.SemaphoreType.DMA
    packed = 4 * heads + 128
    return pl.pallas_call(
        finish_kernel,
        name="finish",
        out_shape=(
            jax.ShapeDtypeStruct((256, 3 * heads), f32),
            jax.ShapeDtypeStruct((heads, 256), f32),
            jax.ShapeDtypeStruct((128, width), f32),
            jax.ShapeDtypeStruct((144, 128), f32),
        ),
        in_specs=[vmem] * 17,
        out_specs=(vmem,) * 4,
        scratch_shapes=[
            pltpu.VMEM((512, 3 * heads), low),
            pltpu.VMEM((512, heads), low),
            pltpu.VMEM((512, width), f32),
        ]
        + [
            pltpu.VMEM((4, 256, packed), low),
            pltpu.VMEM((4, 256, packed), low),
            pltpu.VMEM((4, 256, packed), low),
            pltpu.VMEM((2, 128, packed), low),
            pltpu.VMEM((2, 128, packed), low),
            pltpu.VMEM((128, packed), low),
            pltpu.VMEM((128, packed), low),
            pltpu.VMEM((8, 16, 128), f32),
            pltpu.VMEM((4, 144, 128), f32),
            dma((2, 4)), dma((2, 4)), dma((2, 6)), dma((2, 6)), dma((3,)), dma((4,)),
        ]
        + LineScatter.scratch(width),
        compiler_params=pltpu.CompilerParams(
            collective_id=4, has_side_effects=True, vmem_limit_bytes=VMEM_LIMIT
        ),
        cost_estimate=pl.CostEstimate(
            flops=8_000_000_000, bytes_accessed=100_000_000, transcendentals=0
        ),
    )(rows, tok, *attention, grad_attn, weights, *tables, side, stats)


def expert_kernel(
    x_ref, dy_ref, gate_ref, wg_ref, wu_ref, wd_ref, y_ref, gin_ref, dgate_ref, dup_ref, hgated_ref,
    gate_pre_ref, up_pre_ref, raw_ref,
):
    rows, ff = dgate_ref.shape[1:]
    width = x_ref.shape[2]
    expert = lax.axis_index("dp") * 8 + pl.program_id(0)
    nt = (((1,), (1,)), ((), ()))

    def mm(a, b, dims):
        return lax.dot_general(a, b, dims, preferred_element_type=jnp.float32)

    gate_pre_ref[...] = jnp.dot(x_ref[0], wg_ref[0], preferred_element_type=jnp.float32)
    up_pre_ref[...] = jnp.dot(x_ref[0], wu_ref[0], preferred_element_type=jnp.float32)
    raw_ref[...] = mm(dy_ref[0], wd_ref[0], nt)
    step = 96

    def pointwise(index, carry):
        part = pl.ds(pl.multiple_of(index * step, step), step)
        gate_pre, up_pre, raw = gate_pre_ref[part, :], up_pre_ref[part, :], raw_ref[part, :]
        weight = jnp.concatenate([gate_ref[0, part, :]] * (ff // 128), axis=1)
        sig = jax.nn.sigmoid(gate_pre)
        silu = gate_pre * sig
        hidden = silu * up_pre
        route_grad = jnp.sum(hidden * raw, axis=1, keepdims=True)
        grad_hidden = weight * raw
        lane = lax.broadcasted_iota(jnp.int32, (step, 128), 1)
        high = route_grad.astype(jnp.bfloat16).astype(jnp.float32)
        extra = jnp.where(lane == expert, high, 0.0) + jnp.where(
            lane == expert + 64, route_grad - high, 0.0
        )
        hgated_ref[0, part, :] = (weight * hidden).astype(jnp.bfloat16)
        dgate_ref[0, part, :] = (
            grad_hidden * up_pre * sig * (1.0 + gate_pre * (1.0 - sig))
        ).astype(jnp.bfloat16)
        dup_ref[0, part, :] = (grad_hidden * silu).astype(jnp.bfloat16)
        y_ref[0, part, width:] = extra.astype(jnp.bfloat16)
        return carry

    lax.fori_loop(0, rows // step, pointwise, 0)
    for start in range(0, width, 512):
        lanes = slice(start, start + 512)
        y_ref[0, :, lanes] = jnp.dot(
            hgated_ref[0], wd_ref[0, :, lanes], preferred_element_type=jnp.float32
        ).astype(jnp.bfloat16)
        gin_ref[0, :, lanes] = (
            mm(dgate_ref[0], wg_ref[0, lanes, :], nt) + mm(dup_ref[0], wu_ref[0, lanes, :], nt)
        ).astype(jnp.bfloat16)


def weights_kernel(x_ref, dy_ref, dgate_ref, dup_ref, hgated_ref, gwg_ref, gwu_ref, gwd_ref):
    width = x_ref.shape[2]
    tn = (((0,), (0,)), ((), ()))

    def mm(a, b):
        return lax.dot_general(a, b, tn, preferred_element_type=jnp.float32)

    for start in range(0, width, 512):
        part = slice(start, start + 512)
        gwd_ref[0, :, part] = mm(hgated_ref[0], dy_ref[0, :, part])
        xs = x_ref[0, :, part]
        gwg_ref[0, part, :] = mm(xs, dgate_ref[0])
        gwu_ref[0, part, :] = mm(xs, dup_ref[0])


def expert_spec(*shape):
    return pl.BlockSpec((1,) + shape, lambda e: (e, 0, 0))


def run_experts(x_slots, dy_slots, gate_slots, w_gate, w_up, w_down):
    experts, rows, width = x_slots.shape
    ff = w_gate.shape[2]
    spec, low = expert_spec, jnp.bfloat16
    middle = jax.ShapeDtypeStruct((experts, rows, ff), low)
    return pl.pallas_call(
        expert_kernel,
        name="experts",
        grid=(experts,),
        in_specs=[
            spec(rows, width), spec(rows, width), spec(rows, 128),
            spec(width, ff), spec(width, ff), spec(ff, width),
        ],
        out_specs=(spec(rows, width + 128), spec(rows, width)) + (spec(rows, ff),) * 3,
        out_shape=(
            jax.ShapeDtypeStruct((experts, rows, width + 128), low),
            jax.ShapeDtypeStruct((experts, rows, width), low),
            middle, middle, middle,
        ),
        scratch_shapes=[pltpu.VMEM((rows, ff), jnp.float32)] * 3,
        compiler_params=pltpu.CompilerParams(vmem_limit_bytes=VMEM_LIMIT),
        cost_estimate=pl.CostEstimate(
            flops=29_000_000_000, bytes_accessed=100_000_000, transcendentals=2_000_000
        ),
    )(x_slots, dy_slots, gate_slots, w_gate, w_up, w_down)


def run_weights(x_slots, dy_slots, dgate, dup, hgated):
    experts, rows, width = x_slots.shape
    ff = dgate.shape[2]
    spec, f32 = expert_spec, jnp.float32
    wide = jax.ShapeDtypeStruct((experts, width, ff), f32)
    return pl.pallas_call(
        weights_kernel,
        name="expert_weights",
        grid=(experts,),
        in_specs=[spec(rows, width)] * 2 + [spec(rows, ff)] * 3,
        out_specs=(spec(width, ff), spec(width, ff), spec(ff, width)),
        out_shape=(wide, wide, jax.ShapeDtypeStruct((experts, ff, width), f32)),
        compiler_params=pltpu.CompilerParams(vmem_limit_bytes=VMEM_LIMIT),
        cost_estimate=pl.CostEstimate(
            flops=15_000_000_000, bytes_accessed=100_000_000, transcendentals=0
        ),
    )(x_slots, dy_slots, dgate, dup, hgated)


def plain_onehot(routes_all, first_expert, local_experts):
    sources, rows = routes_all.shape[0], routes_all.shape[1]
    experts = jnp.arange(local_experts, dtype=jnp.int32) + first_expert
    member = jnp.any(routes_all[:, :, :, None] == experts, axis=2).astype(jnp.int32)
    rank = jnp.cumsum(member, axis=1) - member
    rank = jnp.where(member > 0, rank, -1)
    return (
        rank.transpose(0, 2, 1)[:, :, None, :] == jnp.arange(CAP, dtype=jnp.int32)[:, None]
    ).astype(jnp.bfloat16)


def plain_experts(moe_low, cotangent, routes, gates, w_gate, w_up, w_down):
    both = ("dp", "tensor")
    local_experts = w_gate.shape[0]
    width = moe_low.shape[1]
    f32 = jnp.float32
    routes_all = lax.all_gather(routes, both, axis=0)
    x_all = lax.all_gather(moe_low, both, axis=0)
    dy_all = lax.all_gather(cotangent, both, axis=0)
    gates_all = lax.all_gather(gates, both, axis=0)
    first_expert = lax.axis_index("dp") * local_experts
    onehot = plain_onehot(routes_all, first_expert, local_experts)
    take = functools.partial(jnp.einsum, "sect,std->escd")
    flat = (local_experts, -1, width)
    x_slots = take(onehot, x_all).reshape(flat)
    dy_slots = take(onehot, dy_all).reshape(flat)
    experts = jnp.arange(local_experts, dtype=jnp.int32) + first_expert
    gates_here = jnp.sum(
        jnp.where(routes_all[..., None] == experts, gates_all[..., None], 0.0), axis=2
    )
    weight = jnp.einsum(
        "sect,ste->esc", onehot.astype(f32), gates_here, precision=lax.Precision.HIGHEST
    ).reshape(local_experts, -1)[..., None]
    mm = functools.partial(jnp.einsum, preferred_element_type=f32)
    gate_pre = mm("ecd,edf->ecf", x_slots, w_gate)
    up_pre = mm("ecd,edf->ecf", x_slots, w_up)
    raw = mm("ecd,efd->ecf", dy_slots, w_down)
    sig = jax.nn.sigmoid(gate_pre)
    silu = gate_pre * sig
    hidden = silu * up_pre
    hgated = (weight * hidden).astype(jnp.bfloat16)
    route_grad = jnp.sum(hidden * raw, axis=2).reshape(local_experts, -1, CAP)
    grad_hidden = weight * raw
    dgate = (grad_hidden * up_pre * sig * (1.0 + gate_pre * (1.0 - sig))).astype(jnp.bfloat16)
    dup = (grad_hidden * silu).astype(jnp.bfloat16)
    y_slots = mm("ecf,efd->ecd", hgated, w_down).astype(jnp.bfloat16)
    gin_slots = (mm("ecf,edf->ecd", dgate, w_gate) + mm("ecf,edf->ecd", dup, w_up)).astype(
        jnp.bfloat16
    )
    grads = (
        mm("ecd,ecf->edf", x_slots, dgate),
        mm("ecd,ecf->edf", x_slots, dup),
        mm("ecf,ecd->efd", hgated, dy_slots),
    )

    def give_back(slots):
        slots = slots.reshape(local_experts, -1, CAP, width)
        rows = mm("sect,escd->std", onehot, slots).astype(jnp.bfloat16)
        return lax.psum_scatter(
            rows.reshape(-1, width), both, scatter_dimension=0, tiled=True
        ).astype(f32)

    here = jnp.einsum(
        "sect,esc->ste", onehot.astype(f32), route_grad, precision=lax.Precision.HIGHEST
    )
    spread = jnp.zeros(here.shape[:2] + (EXPERTS,), f32)
    spread = lax.dynamic_update_slice(spread, here, (0, 0, first_expert))
    grad_gates = lax.psum_scatter(
        spread.reshape(-1, EXPERTS), both, scatter_dimension=0, tiled=True
    )
    return (give_back(y_slots), grad_gates, give_back(gin_slots), lambda own_rows: grads)


def routed_experts(moe_low, cotangent, routes, gates, w_gate, w_up, w_down, dispatched):
    if dispatched is None:
        return plain_experts(moe_low, cotangent, routes, gates, w_gate, w_up, w_down)
    dy_slots, onehot, all_routes = dispatched
    width = moe_low.shape[1]
    x_slots, gate_slots = gather_slots(moe_low, gates.T, onehot, all_routes)
    y_slots, gin_slots, *middle = run_experts(
        x_slots, dy_slots, gate_slots, w_gate, w_up, w_down
    )
    sums, grad_in = return_rows(y_slots, gin_slots, onehot)
    grad_gates = sums[:, width : width + EXPERTS] + sums[:, width + EXPERTS :]

    def weight_grads(own_rows):
        hgated, unused = lax.optimization_barrier((middle[2], own_rows))
        return run_weights(x_slots, dy_slots, middle[0], middle[1], hgated)

    return (sums[:, :width], grad_gates, grad_in, weight_grads)


def own_kernels(tokens, w_gate):
    return (
        lax.axis_size("dp") == 8
        and lax.axis_size("tensor") == 4
        and tokens.shape == (128, 2048)
        and w_gate.shape[0] == 8
    )


def side_columns(pieces, rows):
    filled = [jnp.pad(p, ((0, rows - p.shape[0]), (0, 0))) for p in pieces]
    used = sum(p.shape[1] for p in filled)
    return jnp.concatenate(filled + [jnp.zeros((rows, 128 - used), filled[0].dtype)], axis=1)


def body(
    tokens,
    cotangent,
    lengths,
    seq_order,
    routes,
    attn_gain,
    w_query,
    w_key,
    w_value,
    w_output,
    query_gain,
    key_gain,
    ffn_gain,
    router,
    w_gate,
    w_up,
    w_down,
):
    tok_rows, model_width = tokens.shape
    tensor_count = lax.axis_size("tensor")
    data_count = lax.axis_size("dp")
    group_rows_count = tok_rows * tensor_count
    block_rows = min(group_rows_count, 512)
    shard = w_query.shape[0]
    heads_width = w_query.shape[1]
    gain_rows = query_gain.shape[0]
    low = jnp.bfloat16
    f32 = jnp.float32

    own = own_kernels(tokens, w_gate)

    seq_ids, positions = arrival_layout(lengths[0], seq_order[0])
    resid_in = tokens.astype(f32)
    if own:
        gain_list = [attn_gain, ffn_gain, query_gain, key_gain]
        filled = sum(part.shape[0] for part in gain_list)
        gains = jnp.concatenate(gain_list + [jnp.zeros((1024 - filled,), low)])
        gains = gains.reshape(8, 128).astype(f32)
        shards = (w_query, w_key, w_value, w_output, jnp.pad(router, ((0, 0), (0, 128 - EXPERTS))))
        seq_float = seq_ids.astype(f32)
        lane = jnp.arange(HD, dtype=jnp.int32)
        frequency = THETA ** (-(lane % (HD // 2)).astype(f32) / (HD // 2))
        angles = positions.astype(f32)[:, None] * frequency[None, :]
        tables = (
            jnp.cos(angles),
            jnp.sin(angles) * jnp.where(lane < HD // 2, -1.0, 1.0),
            jnp.broadcast_to(seq_float[:, None], (group_rows_count, 128)),
            jnp.broadcast_to(seq_float[None, :], (8, group_rows_count)),
        )
        (
            weights, group_tokens, dy_slots, all_gains, onehot, all_routes, group_rows,
            *attention, attn_out,
        ) = front(shards, tokens, cotangent, routes.T.astype(f32), gains, *tables, heads_width)
        dispatched = (dy_slots, onehot, all_routes)
        group_tokens = group_tokens.reshape(-1, model_width)
        full_router = weights[:, 4 * heads_width : 4 * heads_width + EXPERTS]
        attn_scale = all_gains[:, :2].reshape(-1)
        ffn_scale = all_gains[:, 2:4].reshape(-1)
    else:
        side = side_columns(
            [router, attn_gain[:, None], ffn_gain[:, None], query_gain[:, None], key_gain[:, None]],
            shard,
        )
        packed = jnp.concatenate([w_query, w_key, w_value, w_output.T, side], axis=1)
        weights = lax.all_gather(packed, "dp", axis=0, tiled=True)
        group_tokens = lax.all_gather(tokens, "tensor", axis=0, tiled=True)
        dispatched = None
        full_query = weights[:, :heads_width]
        full_key = weights[:, heads_width : 2 * heads_width]
        full_value = weights[:, 2 * heads_width : 3 * heads_width]
        output_t = weights[:, 3 * heads_width : 4 * heads_width]
        extras = weights[:, 4 * heads_width :]
        full_router = extras[:, :EXPERTS]
        attn_scale = extras[:, EXPERTS].astype(f32)
        ffn_scale = extras[:, EXPERTS + 1].astype(f32)
        gain_columns = extras.reshape(data_count, shard, 128)[:, :gain_rows, EXPERTS + 2 : EXPERTS + 4]
        query_scale = gain_columns[:, :, 0].reshape(-1).astype(f32)
        key_scale = gain_columns[:, :, 1].reshape(-1).astype(f32)

        cosines, sines = rope_tables(positions)
        group_rows = norm_apply(group_tokens.astype(f32), attn_scale).astype(low)
        proj_query = jnp.dot(group_rows, full_query, preferred_element_type=f32)
        proj_key = jnp.dot(group_rows, full_key, preferred_element_type=f32)
        value_flat = jnp.dot(group_rows, full_value, preferred_element_type=f32).astype(low)
        value_low = value_flat.reshape(group_rows_count, -1, HD)
        query_low = head_norm_rope(proj_query, query_scale, cosines, sines).astype(low)
        key_low = head_norm_rope(proj_key, key_scale, cosines, sines).astype(low)
        context, row_lse = attend(query_low, key_low, value_low, seq_ids, block_rows)
        context_low = context.reshape(group_rows_count, -1).astype(low)
        attn_out = lax.psum_scatter(
            lax.dot_general(
                context_low, output_t, (((1,), (1,)), ((), ())), preferred_element_type=f32
            ).astype(low),
            "tensor",
            scatter_dimension=0,
            tiled=True,
        ).astype(f32)
    resid_mid = resid_in + attn_out
    moe_low = norm_apply(resid_mid, ffn_scale).astype(low)
    logits = jnp.dot(moe_low, full_router, preferred_element_type=f32)
    route_match = routes[:, :, None] == jnp.arange(EXPERTS, dtype=jnp.int32)[None, None, :]
    picked_logits = jnp.sum(jnp.where(route_match, logits[:, None, :], 0.0), axis=-1)
    gate_peak = jnp.max(picked_logits, axis=1, keepdims=True)
    gate_raw = jnp.exp(picked_logits - gate_peak)
    gates = gate_raw / jnp.sum(gate_raw, axis=1, keepdims=True)
    dense_gates = jnp.sum(jnp.where(route_match, gates[:, :, None], 0.0), axis=1)

    moe_out, grad_gates, grad_from_experts, expert_weight_grads = routed_experts(
        moe_low, cotangent, routes, gates, w_gate, w_up, w_down, dispatched
    )
    layer_out = (resid_mid + moe_out).astype(low)
    stat_terms = jnp.stack(
        [jnp.sum(resid_mid * resid_mid), jnp.sum(attn_out * attn_out), jnp.sum(moe_out * moe_out)]
    )
    grad_out = cotangent.astype(f32)
    inner_gate = jnp.sum(dense_gates * grad_gates, axis=1, keepdims=True)
    grad_logits_low = (dense_gates * (grad_gates - inner_gate)).astype(low)
    grad_router_part = jnp.dot(moe_low.T, grad_logits_low, preferred_element_type=f32)
    grad_moe_in = grad_from_experts + jnp.dot(
        grad_logits_low, full_router.T, preferred_element_type=f32
    )
    unused_mid, ffn_back = jax.vjp(norm_apply, resid_mid, ffn_scale)
    grad_mid_norm, grad_ffn_part = ffn_back(grad_moe_in)
    grad_mid = grad_out + grad_mid_norm
    grad_attn_low = grad_mid.astype(low)
    grad_attn_rows = lax.all_gather(grad_attn_low, "tensor", axis=0, tiled=True)
    grad_gate_w, grad_up_w, grad_down = expert_weight_grads(grad_attn_low)
    tn = (((0,), (0,)), ((), ()))
    if own:
        router_side = grad_router_part.reshape(8, 2, 128, EXPERTS).swapaxes(1, 2).reshape(8, 128, 128)

        side = jnp.concatenate(
            [
                router_side,
                jnp.zeros((8, 2, 128), f32),
                grad_ffn_part.reshape(8, 2, 128),
                jnp.zeros((8, 12, 128), f32),
            ],
            axis=1,
        ).astype(low)
        stats = jnp.pad(stat_terms[None, :], ((6, 9), (0, 125)))
        grads_qkv, grad_out_w, grad_normed, small = finish(
            group_rows, group_tokens, attention, grad_attn_rows, weights, (all_gains,) + tables, side, stats
        )
        grad_router = small[:128].reshape(128, 2, EXPERTS).swapaxes(0, 1).reshape(256, EXPERTS)
        grad_attn_gain = small[128:130].reshape(-1)
        grad_ffn_gain = small[130:132].reshape(-1)
        first_lane = lax.axis_index("dp") * gain_rows
        grad_query_gain = lax.dynamic_slice(small[132], (first_lane,), (gain_rows,))
        grad_key_gain = lax.dynamic_slice(small[133], (first_lane,), (gain_rows,))
        stat_totals = small[134, :3]
        unused_in, attn_back = jax.vjp(lambda values: norm_apply(values, attn_scale), resid_in)
        (grad_in_norm,) = attn_back(grad_normed)
    else:
        grad_ctx_low = jnp.dot(grad_attn_rows, output_t, preferred_element_type=f32).astype(low)
        grad_query, grad_key, grad_value = attend_back(
            query_low,
            key_low,
            value_low,
            seq_ids,
            row_lse,
            grad_ctx_low.reshape(value_low.shape),
            block_rows,
        )
        grad_value_low = grad_value.reshape(group_rows_count, -1).astype(low)
        unused_query, query_back = jax.vjp(
            lambda projected, head_gain: head_norm_rope(projected, head_gain, cosines, sines),
            proj_query,
            query_scale,
        )
        grad_proj_query, grad_query_gain_part = query_back(grad_query)
        unused_key, key_back = jax.vjp(
            lambda projected, head_gain: head_norm_rope(projected, head_gain, cosines, sines),
            proj_key,
            key_scale,
        )
        grad_proj_key, grad_key_gain_part = key_back(grad_key)
        grad_query_low = grad_proj_query.astype(low)
        grad_key_low = grad_proj_key.astype(low)
        head_grads = (grad_query_low, grad_key_low, grad_value_low)
        weight_grads = [
            lax.dot_general(group_rows, part, tn, preferred_element_type=f32) for part in head_grads
        ]
        grad_output_t = lax.dot_general(grad_attn_rows, context_low, tn, preferred_element_type=f32)
        total_rows = jnp.dot(grad_query_low, full_query.T, preferred_element_type=f32)
        total_rows = total_rows + jnp.dot(grad_key_low, full_key.T, preferred_element_type=f32)
        total_rows = total_rows + jnp.dot(grad_value_low, full_value.T, preferred_element_type=f32)
        grad_normed = lax.psum_scatter(
            total_rows.astype(low), "tensor", scatter_dimension=0, tiled=True
        ).astype(f32)
        unused_in, attn_back = jax.vjp(norm_apply, resid_in, attn_scale)
        grad_in_norm, grad_attn_part = attn_back(grad_normed)

        def gain_column(part):
            cut = part.astype(low).reshape(data_count, gain_rows, 1)
            return jnp.pad(cut, ((0, 0), (0, shard - gain_rows), (0, 0))).reshape(-1, 1)

        side_grads = side_columns(
            [
                grad_router_part.astype(low),
                grad_attn_part.astype(low)[:, None],
                grad_ffn_part.astype(low)[:, None],
                gain_column(grad_query_gain_part),
                gain_column(grad_key_gain_part),
            ],
            model_width,
        )
        packed_grads = jnp.concatenate(
            [part.astype(low) for part in weight_grads] + [grad_output_t.astype(low), side_grads],
            axis=1,
        )
        reduced = lax.psum_scatter(packed_grads, "dp", scatter_dimension=0, tiled=True).astype(f32)
        side_total, stat_totals = lax.psum(
            (reduced[:, 4 * heads_width : 4 * heads_width + EXPERTS + 4], stat_terms), "tensor"
        )
        grads_qkv = reduced[:, : 3 * heads_width]
        grad_out_w = reduced[:, 3 * heads_width : 4 * heads_width].T
        grad_attn_gain = side_total[:, EXPERTS]
        grad_ffn_gain = side_total[:, EXPERTS + 1]
        grad_query_gain = side_total[:gain_rows, EXPERTS + 2]
        grad_key_gain = side_total[:gain_rows, EXPERTS + 3]
        grad_router = side_total[:, :EXPERTS]
    grad_tokens = grad_mid + grad_in_norm
    rms_stats = jnp.sqrt(stat_totals / (group_rows_count * model_width))[None, :]
    return (
        layer_out,
        grad_tokens,
        grad_attn_gain,
        grads_qkv[:, :heads_width],
        grads_qkv[:, heads_width : 2 * heads_width],
        grads_qkv[:, 2 * heads_width :],
        grad_out_w,
        grad_query_gain,
        grad_key_gain,
        grad_ffn_gain,
        grad_router,
        grad_gate_w,
        grad_up_w,
        grad_down,
        rms_stats,
    )


def solution(mesh):
    in_specs = (
        P(("dp", "tensor"), None),
        P(("dp", "tensor"), None),
        P("dp", None),
        P("dp", None),
        P(("dp", "tensor"), None),
        P("dp"),
        P("dp", "tensor"),
        P("dp", "tensor"),
        P("dp", "tensor"),
        P("tensor", "dp"),
        P("dp"),
        P("dp"),
        P("dp"),
        P("dp", None),
        P("dp", None, "tensor"),
        P("dp", None, "tensor"),
        P("dp", "tensor", None),
    )
    out_specs = (
        P(("dp", "tensor"), None),
        P(("dp", "tensor"), None),
        P("dp"),
        P("dp", "tensor"),
        P("dp", "tensor"),
        P("dp", "tensor"),
        P("tensor", "dp"),
        P("dp"),
        P("dp"),
        P("dp"),
        P("dp", None),
        P("dp", None, "tensor"),
        P("dp", None, "tensor"),
        P("dp", "tensor", None),
        P("dp", None),
    )
    return jax.shard_map(body, mesh=mesh, in_specs=in_specs, out_specs=out_specs, check_vma=False)
```

```python
import functools

import jax
import jax.numpy as jnp
from jax import lax
from jax.experimental import pallas as pl
from jax.experimental.pallas import tpu as pltpu
from jax.sharding import PartitionSpec as P

HD = 128
EXPERTS = 64
TOPK = 8
CAP = 18


EPSILON = 1e-05
THETA = 10000.0
NEGATIVE = -1e30


def inv_rms(values):
    return lax.rsqrt(jnp.mean(values * values, axis=-1, keepdims=True) + EPSILON)


def norm_apply(values, scale_gain):
    return values * inv_rms(values) * scale_gain


def arrival_layout(seq_lengths, order_row):
    row_total = order_row.shape[0]
    placed = jnp.arange(row_total, dtype=jnp.int32)
    order = jnp.arange(seq_lengths.shape[0], dtype=jnp.int32)
    upto = order[None, :] <= order[:, None]
    seq_ends = jnp.sum(jnp.where(upto, seq_lengths[None, :], 0), axis=1)
    seq_starts = seq_ends - seq_lengths
    member = jnp.sum((placed[:, None] >= seq_ends[None, :]).astype(jnp.int32), axis=1)
    chosen = member[:, None] == jnp.arange(seq_lengths.shape[0], dtype=jnp.int32)[None, :]
    seq_begin = jnp.sum(jnp.where(chosen, seq_starts[None, :], 0), axis=1)
    here = order_row[None, :] == placed[:, None]
    seq_ids = jnp.sum(jnp.where(here, member[None, :], 0), axis=1)
    positions = jnp.sum(jnp.where(here, (placed - seq_begin)[None, :], 0), axis=1)
    return (seq_ids, positions)


def rope_tables(positions):
    half_dim = HD // 2
    frequency = THETA ** (-jnp.arange(half_dim, dtype=jnp.float32) / half_dim)
    angles = positions.astype(jnp.float32)[:, None] * frequency[None, :]
    return (jnp.cos(angles)[:, None, :], jnp.sin(angles)[:, None, :])


def head_norm_rope(projected, head_gain, cosines, sines):
    shaped = projected.reshape(projected.shape[0], -1, HD)
    normed_heads = norm_apply(shaped, head_gain)
    first_half = normed_heads[..., : HD // 2]
    second_half = normed_heads[..., HD // 2 :]
    return jnp.concatenate(
        [first_half * cosines - second_half * sines, second_half * cosines + first_half * sines],
        axis=-1,
    )


def masked_scores(query_block, key_low, seq_block, seq_ids):
    score_scale = HD ** (-0.5)
    scores = (
        jnp.einsum("qhd,khd->hqk", query_block, key_low, preferred_element_type=jnp.float32)
        * score_scale
    )
    same_seq = (seq_block[:, None] == seq_ids[None, :])[None]
    return jnp.where(same_seq, scores, NEGATIVE)


def attend(query_low, key_low, value_low, seq_ids, block_rows):
    num_blocks = query_low.shape[0] // block_rows
    query_blocks = query_low.reshape(num_blocks, block_rows, query_low.shape[1], HD)
    seq_blocks = seq_ids.reshape(num_blocks, block_rows)

    def one_block(inputs):
        query_block, seq_block = inputs
        scores = masked_scores(query_block, key_low, seq_block, seq_ids)
        row_peak = jnp.max(scores, axis=-1, keepdims=True)
        raised = jnp.exp(scores - row_peak)
        row_total = jnp.sum(raised, axis=-1, keepdims=True)
        probs_low = (raised / row_total).astype(jnp.bfloat16)
        context = jnp.einsum(
            "hqk,khd->qhd", probs_low, value_low, preferred_element_type=jnp.float32
        )
        return (context, row_peak + jnp.log(row_total))

    context, row_lse = lax.map(one_block, (query_blocks, seq_blocks))
    return (context.reshape(query_low.shape), row_lse)


def attend_back(query_low, key_low, value_low, seq_ids, row_lse, grad_ctx_low, block_rows):
    score_scale = HD ** (-0.5)
    num_blocks = query_low.shape[0] // block_rows
    block_shape = (num_blocks, block_rows, query_low.shape[1], HD)

    def one_block(carry, inputs):
        grad_key_sum, grad_value_sum = carry
        query_block, seq_block, lse_block, grad_block = inputs
        scores = masked_scores(query_block, key_low, seq_block, seq_ids)
        probs = jnp.exp(scores - lse_block)
        probs_low = probs.astype(jnp.bfloat16)
        grad_value_sum = grad_value_sum + jnp.einsum(
            "hqk,qhd->khd", probs_low, grad_block, preferred_element_type=jnp.float32
        )
        grad_probs = jnp.einsum(
            "qhd,khd->hqk", grad_block, value_low, preferred_element_type=jnp.float32
        )
        inner_sum = jnp.sum(probs * grad_probs, axis=-1, keepdims=True)
        grad_scores = (probs * (grad_probs - inner_sum)).astype(jnp.bfloat16)
        grad_query_block = (
            jnp.einsum("hqk,khd->qhd", grad_scores, key_low, preferred_element_type=jnp.float32)
            * score_scale
        )
        grad_key_sum = (
            grad_key_sum
            + jnp.einsum(
                "hqk,qhd->khd", grad_scores, query_block, preferred_element_type=jnp.float32
            )
            * score_scale
        )
        return ((grad_key_sum, grad_value_sum), grad_query_block)

    zeros_heads = jnp.zeros(query_low.shape, jnp.float32)
    carried, grad_query = lax.scan(
        one_block,
        (zeros_heads, zeros_heads),
        (
            query_low.reshape(block_shape),
            seq_ids.reshape(num_blocks, block_rows),
            row_lse,
            grad_ctx_low.reshape(block_shape),
        ),
    )
    return (grad_query.reshape(query_low.shape), carried[0], carried[1])


MESH = pl.DeviceIdType.MESH
VMEM_LIMIT = 60 * 1024 * 1024
MAIN = 16
SPARE = CAP - MAIN


def at(dp_index, z_index):
    return {"dp": dp_index, "tensor": z_index}


def place():
    dp = lax.axis_index("dp")
    z = lax.axis_index("tensor")
    core, x, y = dp % 2, (dp // 2) % 2, dp // 4
    return dp, z, 1 - 2 * core, 2 - 4 * x, 4 - 8 * y


def greet(peers, extra=None, has_extra=None, count=0):
    barrier = pltpu.get_barrier_semaphore()
    for peer in peers:
        pl.semaphore_signal(barrier, inc=1, device_id=at(*peer), device_id_type=MESH)
    if extra is not None:

        @pl.when(has_extra)
        def _():
            pl.semaphore_signal(barrier, inc=1, device_id=at(*extra), device_id_type=MESH)

    pl.semaphore_wait(barrier, len(peers) + count)


def when_or_now(cond, action):
    if cond is None:
        action()
    else:
        pl.when(cond)(action)


def slot_matrix(routes_block, source, first_expert):
    experts = lax.broadcasted_iota(jnp.int32, (8, 128), 0) + first_expert
    member = jnp.zeros((8, 128), jnp.float32)
    for j in range(TOPK):
        member = member + (routes_block[j : j + 1, :] == experts.astype(jnp.float32)).astype(jnp.float32)
    earlier = (
        lax.broadcasted_iota(jnp.int32, (128, 128), 0)
        < lax.broadcasted_iota(jnp.int32, (128, 128), 1)
    ).astype(jnp.bfloat16)
    rank = jnp.dot(member.astype(jnp.bfloat16), earlier, preferred_element_type=jnp.float32)
    rank = jnp.where(member > 0.5, rank, -1.0).astype(jnp.int32)
    spread = jnp.broadcast_to(rank[:, None, :], (8, MAIN, 128)).reshape(128, 128)
    row = lax.broadcasted_iota(jnp.int32, (128, 128), 0) % MAIN
    main = spread == row
    spare = jnp.logical_and(row // SPARE == source % 8, spread == MAIN + row % SPARE)
    return jnp.concatenate(
        [main.astype(jnp.float32), spare.astype(jnp.float32)], axis=0
    ).astype(jnp.bfloat16)


class LineScatter:
    def __init__(self, dp, z, blocks, rze, rzm, rzf, zsend, zrecv):
        self.dp, self.z = dp, z
        self.zr, self.zo = z + 1 - 2 * (z % 2), 3 - z
        self.mid, self.end = z * (3 - z) > 0, z * (3 - z) < 1
        self.zs = [3 - 3 * (z // 2), 2 - z // 2, self.zr, z]
        self.blocks, self.rze, self.rzm, self.rzf = blocks, rze, rzm, rzf
        self.zsend, self.zrecv = zsend, zrecv
        self.outward = [self.copy(blocks.at[k], rze.at[k], k, self.zr) for k in range(3)]
        self.sends = []

    def copy(self, src, dst, index, z_to):
        return pltpu.make_async_remote_copy(
            src, dst, self.zsend.at[index], self.zrecv.at[index],
            device_id=at(self.dp, z_to), device_id_type=MESH,
        )

    def ready(self, k):
        pl.when(self.end)(functools.partial(self.outward[k].start))
        self.sends.append((self.outward[k], self.end))

    def add(self, k, part):
        total = self.blocks[k].astype(jnp.float32) + part[...].astype(jnp.float32)
        self.blocks[k] = total.astype(jnp.bfloat16)

    def onward(self, k):
        if k < 2:
            copy = self.copy(self.blocks.at[k], self.rzm.at[k], 3 + k, self.zo)
        else:
            copy = self.copy(self.blocks.at[k], self.rzf, 5, self.zr)
        self.sends.append((copy, self.mid))

        @pl.when(self.mid)
        def _():
            if k < 2:
                self.outward[k].wait_recv()
                self.add(k, self.rze.at[k])
            else:
                self.copy(self.blocks.at[0], self.rzm.at[0], 3, self.zo).wait_recv()
                self.add(k, self.rzm.at[0])
            copy.start()

    def last(self, out_ref):
        @pl.when(self.end)
        def _():
            self.copy(self.blocks.at[2], self.rzf, 5, self.zr).wait_recv()
            out_ref[...] = out_ref[...] + self.rzf[...].astype(jnp.float32)

        @pl.when(self.mid)
        def _():
            self.outward[2].wait_recv()
            self.copy(self.blocks.at[1], self.rzm.at[1], 4, self.zo).wait_recv()
            out_ref[...] = (
                out_ref[...]
                + self.rze[2].astype(jnp.float32)
                + self.rzm[1].astype(jnp.float32)
            )

    def drain(self):
        for copy, cond in self.sends:
            pl.when(cond)(functools.partial(copy.wait_send))

    @staticmethod
    def scratch(width):
        low, dma = jnp.bfloat16, pltpu.SemaphoreType.DMA
        return [
            pltpu.VMEM((3, 128, width), low),
            pltpu.VMEM((3, 128, width), low),
            pltpu.VMEM((2, 128, width), low),
            pltpu.VMEM((128, width), low),
            dma((6,)),
            dma((6,)),
        ]


class AllGather:
    def __init__(self, held, own_ref, ssem, rsem, metas=None, own_meta=None, msem=None, mrsem=None):
        self.dp, self.z, self.dc, self.dx, self.dy = place()
        z = self.z
        self.zr, self.zo = z + 1 - 2 * (z % 2), 3 - z
        self.mid = z * (3 - z) > 0
        self.zs = [z, self.zr, 2 - z // 2, 3 - 3 * (z // 2)]
        self.held, self.own_ref, self.ssem, self.rsem = held, own_ref, ssem, rsem
        self.metas, self.own_meta, self.msem, self.mrsem = metas, own_meta, msem, mrsem
        self.sends = []

    def send(self, block, part, dp_to, z_to, cond=None, own=False):
        half = pl.ds(part * 64, 64)
        view = self.held.at[block, half]
        source = self.own_ref.at[half] if own else view
        index = len(self.sends)
        copies = [
            pltpu.make_async_remote_copy(
                source, view, self.ssem.at[index], self.rsem.at[block, part],
                device_id=at(dp_to, z_to), device_id_type=MESH,
            )
        ]
        if part == 0 and self.metas is not None:
            copies.append(
                pltpu.make_async_remote_copy(
                    self.own_meta if own else self.metas.at[block], self.metas.at[block],
                    self.msem.at[index], self.mrsem.at[block],
                    device_id=at(dp_to, z_to), device_id_type=MESH,
                )
            )
        self.sends.append((copies, cond))

        def go():
            for copy in copies:
                copy.start()

        when_or_now(cond, go)

    def arrive(self, block, part):
        view = self.held.at[block, pl.ds(part * 64, 64)]
        here = dict(device_id=at(self.dp, self.zr), device_id_type=MESH)
        pltpu.make_async_remote_copy(
            view, view, self.ssem.at[0], self.rsem.at[block, part], **here
        ).wait_recv()
        if part == 0 and self.metas is not None:
            pltpu.make_async_remote_copy(
                self.metas.at[block], self.metas.at[block], self.msem.at[0], self.mrsem.at[block],
                **here
            ).wait_recv()

    def first(self, k):
        dp, z, dx, dy, dc = self.dp, self.z, self.dx, self.dy, self.dc
        block = dp * 4 + self.zs[k]
        own = k == 0
        for part in (0, 1):
            if k > 0:
                self.arrive(block, part)
            if k == 0:
                self.send(block, part, dp, self.zr, None, own)
                self.send(block, part, dp, self.zo, self.mid, own)
            else:
                self.send(block, part, dp, self.zo if k == 1 else self.zr, self.mid)
            self.send(block, part, dp + (dx if part == 0 else dy), z, None, own)
        self.send(block, 1, dp + dx, z, None, own)
        self.send(block, 0, dp + dy, z, None, own)
        self.send(block, 0, dp + dc, z, None, own)
        self.send(block, 1, dp + dc, z, None, own)

    def second(self, k):
        dp, z, dx, dy, dc = self.dp, self.z, self.dx, self.dy, self.dc
        bx, by = (dp + dx) * 4 + self.zs[k], (dp + dy) * 4 + self.zs[k]
        self.arrive(bx, 0)
        self.send(bx, 0, dp + dy, z)
        self.send(bx, 0, dp + dc, z)
        self.arrive(by, 1)
        self.send(by, 1, dp + dx, z)
        self.send(by, 1, dp + dc, z)
        self.arrive(bx, 1)
        self.send(bx, 1, dp + dc, z)
        self.arrive(by, 0)
        self.send(by, 0, dp + dc, z)

    def third(self, k):
        block = (self.dp + self.dx + self.dy) * 4 + self.zs[k]
        for part in (0, 1):
            self.arrive(block, part)
            self.send(block, part, self.dp + self.dc, self.z)

    def across(self, k, step):
        block = (self.dp + self.dc + step) * 4 + self.zs[k]
        self.arrive(block, 0)
        self.arrive(block, 1)

    def drain(self):
        for copies, cond in self.sends:

            def done(copies=copies):
                for copy in copies:
                    copy.wait_send()

            when_or_now(cond, done)


class Dispatcher:
    def __init__(self, held, stage, spare, slots_ref, osem):
        self.held, self.stage, self.spare = held, stage, spare
        self.slots_ref, self.osem = slots_ref, osem
        self.count = 0

    def put(self, start, slot):
        return pltpu.make_async_copy(
            self.stage.at[slot], self.slots_ref.at[:, pl.ds(start, MAIN), :], self.osem.at[slot]
        )

    def block(self, block, onehot):
        slot, group = self.count % 2, block // 8
        width = self.held.shape[2]
        if self.count >= 2:
            self.put(block * MAIN, slot).wait()

        def tile(step, carry):
            lanes = pl.ds(pl.multiple_of(step * 1024, 1024), 1024)
            rows = jnp.dot(onehot, self.held[block, :, lanes], preferred_element_type=jnp.float32)
            self.stage[slot, :, :, lanes] = rows[:128].astype(jnp.bfloat16).reshape(8, MAIN, 1024)
            extra = rows[128:].astype(jnp.bfloat16)
            self.spare[group, :, lanes] = self.spare[group, :, lanes] + extra
            return carry

        lax.fori_loop(0, width // 1024, tile, 0)
        self.put(block * MAIN, slot).start()
        self.count += 1

    def end(self):
        width = self.held.shape[2]
        for group in range(4):
            slot = group % 2
            self.put(512 + group * MAIN, slot).wait()
            self.stage[slot] = self.spare[group].reshape(8, MAIN, width)
            self.put(512 + group * MAIN, slot).start()
        for slot in range(2):
            self.put(512, slot).wait()


def arrival_order(gather):
    dp, dc, dx, dy, zs = gather.dp, gather.dc, gather.dx, gather.dy, gather.zs
    order = []
    for k in range(6):
        column = []
        if k < 4:
            column.append((k, 0))
        if 1 <= k < 5:
            column += [(k - 1, dx), (k - 1, dy)]
        if k >= 2:
            column.append((k - 2, dx + dy))
        across = [(k - 1, dc)] if 1 <= k < 5 else []
        if k >= 2:
            across += [(k - 2, dc + step) for step in (dx, dy, dx + dy)]
        order.append([[(dp + to) * 4 + zs[j] for j, to in part] for part in (column, across)])
    return order


def gather_forward(gather, k):
    if k < 4:
        gather.first(k)
    if 1 <= k < 5:
        gather.second(k - 1)
    if k >= 2:
        gather.third(k - 2)


def gather_process(gather, order, k, process):
    for block in order[k][0]:
        process(block)
    for block in order[k][1]:
        gather.arrive(block, 0)
        gather.arrive(block, 1)
        process(block)


def rotate(values, cosines, sines):
    return values * cosines + pltpu.roll(values, HD // 2, 1) * sines


def head_probs(query, key, seq_column, seq_row):
    scores = lax.dot_general(
        query, key, (((1,), (1,)), ((), ())), preferred_element_type=jnp.float32
    ) * (HD ** (-0.5))
    scores = jnp.where(seq_column == seq_row, scores, NEGATIVE)
    raised = jnp.exp(scores - jnp.max(scores, axis=1, keepdims=True))
    return raised / jnp.sum(raised, axis=1, keepdims=True)


def head_gain(gains_ref, first):
    lane = lax.broadcasted_iota(jnp.int32, (8, 128), 1)
    keep = jnp.logical_and(lane >= first, lane < first + 16)
    total = jnp.zeros((8, 128), jnp.float32)
    for block in range(8):
        part = jnp.where(keep, jnp.broadcast_to(gains_ref[block, 4:5, :], (8, 128)), 0.0)
        shift = (16 * block - first) % 128
        total = total + (pltpu.roll(part, shift, 1) if shift else part)
    return total[:1]


def front_kernel(
    wq_ref, wk_ref, wv_ref, wo_ref, router_ref, tok_ref, cot_ref, routes_in, gains_in, cos_ref, sin_ref, seqc_ref, seqr_ref,
    weights_ref, group_ref, slots_ref, gains_ref, onehot_ref, routes_ref, normed_ref, projq_ref, projk_ref,
    query_ref, key_ref, value_ref, ctx_ref, out_ref,
    wheld, theld, gheld, held, metas, stage, spare, lsem, wsend, wrecv, gsend, grecv, zsend, zrecv,
    dsend, drecv, msend, mrecv, osem, fsem, *line_refs
):
    dp, z, dc, dx, dy = place()
    zr, zo = z + 1 - 2 * (z % 2), 3 - z
    mid = z * (3 - z) > 0
    f32, low = jnp.float32, jnp.bfloat16
    heads = query_ref.shape[1]
    width = tok_ref.shape[1]
    line = LineScatter(dp, z, *line_refs)
    gather = AllGather(held, cot_ref, dsend, drecv, metas, routes_in, msend, mrecv)
    order = arrival_order(gather)
    picker = Dispatcher(held, stage, spare, slots_ref, osem)
    own_block = dp * 4 + z
    own_rows = pl.ds(pl.multiple_of(dp * 256, 256), 256)
    fill = []
    for source, column, count in (
        (wq_ref, 0, heads), (wk_ref, heads, heads), (wv_ref, 2 * heads, heads),
        (wo_ref.at[pl.ds(0, 256)], 3 * heads, 256), (wo_ref.at[pl.ds(256, 256)], 3 * heads + 256, 256),
        (router_ref, 4 * heads, 128),
    ):
        target = wheld.at[own_rows, pl.ds(column, count)]
        fill.append(pltpu.make_async_copy(source, target, fsem.at[len(fill)]))
    for copy in fill:
        copy.start()
    greet([(dp + dc, z), (dp + dx, z), (dp + dy, z), (dp, zr)], (dp, zo), mid, z * (3 - z) // 2)
    sends = []

    def spot(block, part):
        return wheld.at[pl.ds(pl.multiple_of(block * 256 + part * 128, 128), 128)]

    def send(block, part, dp_to, own=False):
        source = spot(block, part)
        index = len(sends)
        copies = [
            pltpu.make_async_remote_copy(
                source, spot(block, part), wsend.at[index], wrecv.at[block, part],
                device_id=at(dp_to, z), device_id_type=MESH,
            )
        ]
        if part == 0:
            copies.append(
                pltpu.make_async_remote_copy(
                    gains_in if own else gheld.at[block], gheld.at[block],
                    gsend.at[index], grecv.at[block],
                    device_id=at(dp_to, z), device_id_type=MESH,
                )
            )
        for copy in copies:
            copy.start()
        sends.append(copies)

    def arrive(block, part):
        here = dict(device_id=at(dp + dx, z), device_id_type=MESH)
        pltpu.make_async_remote_copy(
            spot(block, part), spot(block, part), wsend.at[0], wrecv.at[block, part], **here
        ).wait_recv()
        if part == 0:
            pltpu.make_async_remote_copy(
                gheld.at[block], gheld.at[block], gsend.at[0], grecv.at[block], **here
            ).wait_recv()

    zsends = []

    def z_send(source, block, z_to, cond=None):
        copy = pltpu.make_async_remote_copy(
            source, theld.at[block], zsend.at[len(zsends)], zrecv.at[block],
            device_id=at(dp, z_to), device_id_type=MESH,
        )
        when_or_now(cond, functools.partial(copy.start))
        zsends.append((copy, cond))

    def z_arrive(block):
        pltpu.make_async_remote_copy(
            theld.at[block], theld.at[block], zsend.at[0], zrecv.at[block],
            device_id=at(dp, zr), device_id_type=MESH,
        ).wait_recv()

    z_send(tok_ref, z, zr)
    z_send(tok_ref, z, zo, mid)
    for copy in fill:
        copy.wait()
    send(dp, 0, dp + dx, True)
    send(dp, 1, dp + dy, True)
    send(dp, 1, dp + dx, True)
    send(dp, 0, dp + dy, True)
    send(dp, 0, dp + dc, True)
    send(dp, 1, dp + dc, True)
    local = [
        pltpu.make_async_copy(tok_ref, theld.at[z], lsem.at[1]),
        pltpu.make_async_copy(gains_in, gheld.at[dp], lsem.at[2]),
        pltpu.make_async_copy(cot_ref, held.at[own_block], lsem.at[3]),
        pltpu.make_async_copy(routes_in, metas.at[own_block], lsem.at[4]),
    ]
    for copy in local:
        copy.start()
    spare[...] = jnp.zeros_like(spare)
    z_arrive(zr)
    z_send(theld.at[zr], zr, zo, mid)
    bx, by, bxy = dp + dx, dp + dy, dp + dx + dy
    arrive(bx, 0)
    send(bx, 0, dp + dy)
    send(bx, 0, dp + dc)
    arrive(by, 1)
    send(by, 1, dp + dx)
    send(by, 1, dp + dc)
    gather.first(0)
    far = 2 - z // 2
    z_arrive(far)
    z_send(theld.at[far], far, zr, mid)
    arrive(bx, 1)
    send(bx, 1, dp + dc)
    arrive(by, 0)
    send(by, 0, dp + dc)
    last = 3 - 3 * (z // 2)
    z_arrive(last)
    z_send(theld.at[last], last, zr, mid)
    for part in (0, 1):
        arrive(bxy, part)
        send(bxy, part, dp + dc)
    for block in (dp, bx, by, bxy):
        for part in (0, 1):
            arrive(block + dc, part)
    for copy in local:
        copy.wait()
    kept = [
        pltpu.make_async_copy(wheld, weights_ref, lsem.at[0]),
        pltpu.make_async_copy(theld, group_ref, lsem.at[1]),
    ]
    for copy in kept:
        copy.start()

    def process(block):
        onehot = slot_matrix(metas[block], block, dp * 8)
        onehot_ref[block] = onehot
        picker.block(block, onehot)

    scale = jnp.concatenate(
        [gheld[j // 2, j % 2 : j % 2 + 1, :] for j in range(width // 128)], axis=1
    )

    def norm_rows(step, carry):
        values = theld[step].astype(f32)
        inverse = lax.rsqrt(jnp.mean(values * values, axis=1, keepdims=True) + EPSILON)
        rows = pl.ds(pl.multiple_of(step * 128, 128), 128)
        normed_ref[rows, :] = (values * inverse * scale).astype(low)
        return carry

    gains_ref[...] = gheld[...]
    lax.fori_loop(0, 4, norm_rows, 0)

    def project(column):
        cols = slice(column * heads, column * heads + heads)
        return jnp.dot(normed_ref[...], wheld[:, cols], preferred_element_type=f32)

    projq_ref[...] = project(0)
    projk_ref[...] = project(1)
    value_ref[...] = project(2).astype(low)
    gather_forward(gather, 1)
    cosines, sines = cos_ref[...], sin_ref[...]
    query_gain, key_gain = head_gain(gheld, 0), head_gain(gheld, 16)

    def one_head(h, carry):
        cols = pl.ds(pl.multiple_of(h * HD, HD), HD)
        for source, gain, target in (
            (projq_ref, query_gain, query_ref), (projk_ref, key_gain, key_ref),
        ):
            values = source[:, cols]
            inverse = lax.rsqrt(jnp.mean(values * values, axis=1, keepdims=True) + EPSILON)
            target[:, cols] = rotate(values * inverse * gain, cosines, sines).astype(low)
        for start in range(0, 512, 256):
            rows = slice(start, start + 256)
            probs = head_probs(
                query_ref[rows, cols], key_ref[:, cols], seqc_ref[rows, :1], seqr_ref[:1, :]
            )
            ctx_ref[rows, cols] = jnp.dot(
                probs.astype(low), value_ref[:, cols], preferred_element_type=f32
            ).astype(low)
        return carry

    lax.fori_loop(0, heads // HD // 2, one_head, 0)
    gather_forward(gather, 2)
    lax.fori_loop(heads // HD // 2, heads // HD, one_head, 0)
    for k in range(4):
        rows = pl.ds(pl.multiple_of(line.zs[k] * 128, 128), 128)
        for start in range(0, width, 256):
            lanes = slice(start, start + 256)
            piece = jnp.dot(
                ctx_ref[rows, :256], wheld[lanes, 3 * heads : 3 * heads + 256],
                preferred_element_type=f32,
            ) + jnp.dot(
                ctx_ref[rows, 256:], wheld[lanes, 3 * heads + 256 : 4 * heads],
                preferred_element_type=f32,
            )
            if k < 3:
                line.blocks[k, :, lanes] = piece.astype(low)
            else:
                out_ref[:, lanes] = piece
        if k < 3:
            line.ready(k)
    gather.first(3)
    process(own_block)
    gather_process(gather, order, 1, process)
    gather.second(2)
    gather.third(1)
    line.onward(0)
    gather_process(gather, order, 2, process)
    line.onward(1)
    gather_process(gather, order, 3, process)
    gather_forward(gather, 4)
    line.onward(2)
    gather_process(gather, order, 4, process)
    gather_forward(gather, 5)
    line.last(out_ref)
    gather_process(gather, order, 5, process)
    picker.end()
    routes_ref[...] = metas[...]
    for copy in kept:
        copy.wait()
    for copies in sends:
        for copy in copies:
            copy.wait_send()
    for copy, cond in zsends:
        when_or_now(cond, functools.partial(copy.wait_send))
    gather.drain()
    line.drain()


def front(shards, tokens, cotangent, routes, gains, cosines, sines, seq_column, seq_row, heads):
    width = tokens.shape[1]
    rows = 4 * tokens.shape[0]
    f32, low = jnp.float32, jnp.bfloat16
    anywhere = pl.BlockSpec(memory_space=pl.ANY)
    vmem = pl.BlockSpec(memory_space=pltpu.VMEM)
    dma = pltpu.SemaphoreType.DMA
    narrow = jax.ShapeDtypeStruct((rows, heads), low)
    return pl.pallas_call(
        front_kernel,
        name="front",
        out_shape=(
            jax.ShapeDtypeStruct((width, 4 * heads + 128), low),
            jax.ShapeDtypeStruct((4, 128, width), low),
            jax.ShapeDtypeStruct((8, 576, width), low),
            jax.ShapeDtypeStruct((8, 8, 128), f32),
            jax.ShapeDtypeStruct((32, 256, 128), low),
            jax.ShapeDtypeStruct((32, 8, 128), f32),
            jax.ShapeDtypeStruct((rows, width), low),
            jax.ShapeDtypeStruct((rows, heads), f32),
            jax.ShapeDtypeStruct((rows, heads), f32),
            narrow, narrow, narrow, narrow,
            jax.ShapeDtypeStruct((128, width), f32),
        ),
        in_specs=[anywhere] * 5 + [vmem] * 8,
        out_specs=(anywhere,) * 3 + (vmem,) * 11,
        scratch_shapes=[
            pltpu.VMEM((width, 4 * heads + 128), low),
            pltpu.VMEM((4, 128, width), low),
            pltpu.VMEM((8, 8, 128), f32),
            pltpu.VMEM((32, 128, width), low),
            pltpu.VMEM((32, 8, 128), f32),
            pltpu.VMEM((2, 8, MAIN, width), low),
            pltpu.VMEM((4, 128, width), low),
            dma((9,)), dma((14,)), dma((8, 2)), dma((14,)), dma((8,)), dma((5,)), dma((4,)),
            dma((72,)), dma((32, 2)), dma((72,)), dma((32,)), dma((2,)), dma((6,)),
        ]
        + LineScatter.scratch(width),
        compiler_params=pltpu.CompilerParams(
            collective_id=0, has_side_effects=True, vmem_limit_bytes=VMEM_LIMIT
        ),
        cost_estimate=pl.CostEstimate(
            flops=5_000_000_000, bytes_accessed=100_000_000, transcendentals=2_000_000
        ),
    )(*shards, tokens, cotangent, routes, gains, cosines, sines, seq_column, seq_row)


def gather_kernel(
    x_ref, meta_ref, onehot_ref, routes_ref, slots_ref, gate_ref,
    held, metas, stage, spare, lsem, ssem, rsem, msem, mrsem, osem,
):
    dp, z, dc, dx, dy = place()
    own = dp * 4 + z
    gather = AllGather(held, held.at[own], ssem, rsem, metas, metas.at[own], msem, mrsem)
    order = arrival_order(gather)
    picker = Dispatcher(held, stage, spare, slots_ref, osem)
    local = [
        pltpu.make_async_copy(x_ref, held.at[own], lsem.at[0]),
        pltpu.make_async_copy(meta_ref, metas.at[own], lsem.at[1]),
    ]
    for copy in local:
        copy.start()
    greet(
        [(dp + dc, z), (dp + dx, z), (dp + dy, z), (dp, gather.zr)],
        (dp, gather.zo), gather.mid, z * (3 - z) // 2,
    )
    spare[...] = jnp.zeros_like(spare)
    gate_ref[:, 512:576, :] = jnp.zeros((8, 64, 128), jnp.float32)
    for copy in local:
        copy.wait()
    experts = (lax.broadcasted_iota(jnp.int32, (8, 128), 0) + dp * 8).astype(jnp.float32)

    def process(block):
        onehot = onehot_ref[block]
        gates_here = jnp.zeros((8, 128), jnp.float32)
        for j in range(TOPK):
            gates_here = gates_here + jnp.where(
                routes_ref[block, j : j + 1, :] == experts, metas[block, j : j + 1, :], 0.0
            )
        wide = jnp.broadcast_to(gates_here[:, None, :], (8, MAIN, 128)).reshape(128, 128)
        taken = onehot.astype(jnp.float32)
        main_gate = jnp.sum(taken[:128] * wide, axis=1, keepdims=True)
        spare_gate = jnp.sum(taken[128:] * wide, axis=1, keepdims=True)
        gate_ref[:, pl.ds(pl.multiple_of(block * MAIN, MAIN), MAIN), :] = jnp.broadcast_to(
            main_gate, (128, 128)
        ).reshape(8, MAIN, 128)
        spare_rows = pl.ds(pl.multiple_of(512 + (block // 8) * MAIN, MAIN), MAIN)
        gate_ref[:, spare_rows, :] = gate_ref[:, spare_rows, :] + jnp.broadcast_to(
            spare_gate, (128, 128)
        ).reshape(8, MAIN, 128)
        picker.block(block, onehot)

    for k in range(6):
        gather_forward(gather, k)
        gather_process(gather, order, k, process)
    picker.end()
    gather.drain()


def gather_slots(rows, meta, onehot, routes):
    count, width = rows.shape
    anywhere = pl.BlockSpec(memory_space=pl.ANY)
    vmem = pl.BlockSpec(memory_space=pltpu.VMEM)
    dma = pltpu.SemaphoreType.DMA
    return pl.pallas_call(
        gather_kernel,
        name="gather_x",
        out_shape=(
            jax.ShapeDtypeStruct((8, 576, width), jnp.bfloat16),
            jax.ShapeDtypeStruct((8, 576, 128), jnp.float32),
        ),
        in_specs=[anywhere, anywhere, vmem, vmem],
        out_specs=(anywhere, vmem),
        scratch_shapes=[
            pltpu.VMEM((32, count, width), jnp.bfloat16),
            pltpu.VMEM((32, 8, 128), jnp.float32),
            pltpu.VMEM((2, 8, MAIN, width), jnp.bfloat16),
            pltpu.VMEM((4, 128, width), jnp.bfloat16),
            dma((2,)), dma((72,)), dma((32, 2)), dma((72,)), dma((32,)), dma((2,)),
        ],
        compiler_params=pltpu.CompilerParams(
            collective_id=1, has_side_effects=True, vmem_limit_bytes=VMEM_LIMIT
        ),
        cost_estimate=pl.CostEstimate(
            flops=4_300_000_000, bytes_accessed=100_000_000, transcendentals=0
        ),
    )(rows, meta, onehot, routes)


def return_kernel(
    y_ref, g_ref, onehot_ref, outy_ref, outg_ref,
    rows_in, to_core, sums, ry0, rx1, rx0, ry1, rze, rzm, rzf,
    ysem, csend, crecv, xsend, xrecv, zsend, zrecv,
):
    dp, z, dc, dx, dy = place()
    zr, zo = z + 1 - 2 * (z % 2), 3 - z
    mid = z * (3 - z) > 0
    end = z * (3 - z) < 1
    half = 64
    sources, outs = (y_ref, g_ref), (outy_ref, outg_ref)
    zs = [3 - 3 * (z // 2), 2 - z // 2, zr, z]
    greet([(dp + dc, z), (dp + dx, z), (dp + dy, z), (dp, zr)], (dp, zo), mid, z * (3 - z) // 2)
    lo, hi = pl.ds(0, half), pl.ds(half, half)
    xsends, zsends = [[] for _ in range(8)], []

    def lanes_of(s):
        return pl.ds(0, sources[s // 4].shape[2])

    def tiles_of(s):
        width = sources[s // 4].shape[2]
        return [slice(i, min(i + 512, width)) for i in range(0, width, 512)]

    def dest(s, step):
        r = 3 - step % 4
        base = dp + dc - dc * (step // 4)
        return (base + (r % 2) * dx + (r // 2) * dy) * 4 + zs[s % 4]

    def fetch(s, block, slot):
        source, lanes = sources[s // 4], lanes_of(s)
        return [
            pltpu.make_async_copy(
                source.at[:, pl.ds(block * MAIN, MAIN), :],
                rows_in.at[slot, pl.ds(0, 8), :, lanes], ysem.at[slot, 0],
            ),
            pltpu.make_async_copy(
                source.at[:, pl.ds(512 + (block // 8) * MAIN, MAIN), :],
                rows_in.at[slot, pl.ds(8, 8), :, lanes], ysem.at[slot, 1],
            ),
        ]

    def partial_tile(block, slot, lanes):
        return lax.dot_general(
            onehot_ref[block], rows_in[slot, :, :, lanes].reshape(256, lanes.stop - lanes.start),
            (((0,), (0,)), ((), ())), preferred_element_type=jnp.float32,
        )

    def core_copy(r, s):
        lanes = lanes_of(s)
        return pltpu.make_async_remote_copy(
            to_core.at[s % 4, r, :, lanes], sums.at[s, r, :, lanes], csend.at[s, r], crecv.at[s, r],
            device_id=at(dp + dc, z), device_id_type=MESH,
        )

    def xy_copy(r, rows, target, index, s, dp_to):
        lanes = lanes_of(s)
        return pltpu.make_async_remote_copy(
            sums.at[s, r, rows, lanes], target.at[:, lanes], xsend.at[index, s], xrecv.at[index, s],
            device_id=at(dp_to, z), device_id_type=MESH,
        )

    def z_copy(s, target, index, z_to):
        lanes = lanes_of(s)
        index = 6 * (s // 4) + index
        return pltpu.make_async_remote_copy(
            sums.at[s, 0, :, lanes], target.at[:, lanes], zsend.at[index], zrecv.at[index],
            device_id=at(dp, z_to), device_id_type=MESH,
        )

    def add_to(s, r, rows, *others):
        lanes = lanes_of(s)
        total = sums[s, r, rows, lanes].astype(jnp.float32)
        for other in others:
            total = total + other[:, lanes].astype(jnp.float32)
        sums[s, r, rows, lanes] = total.astype(jnp.bfloat16)

    def stage_core(s):
        def load(block, slot, following=None):
            for copy in fetch(s, block, slot):
                copy.wait()
            if following is not None:
                for copy in fetch(s, following, 1 - slot):
                    copy.start()

        def partner(step, slot, following):
            r = 3 - step
            block = dest(s, step)
            load(block, slot, following)
            if s >= 4:
                core_copy(r, s - 4).wait_send()
            for lanes in tiles_of(s):
                to_core[s % 4, r, :, lanes] = partial_tile(block, slot, lanes).astype(jnp.bfloat16)
            core_copy(r, s).start()

        batch = [
            xy_copy(3, lo, ry0.at[1, s], 0, s, dp + dy),
            xy_copy(3, hi, rx1.at[1, s], 1, s, dp + dx),
            xy_copy(2, lo, ry0.at[0, s], 2, s, dp + dy),
            xy_copy(1, hi, rx1.at[0, s], 3, s, dp + dx),
        ]
        xsends[s].extend(batch)

        def both(i, carry):
            r = 3 - i
            block = dest(s, 4 + i)

            @pl.when(i < 3)
            def _():
                partner(i + 1, 1, block)

            late = i // 2
            following = (1 - late) * dest(s, i + 2) + late * dest(s, 5 + i)
            slot = i // 3
            load(block, slot)

            @pl.when(i < 3)
            def _():
                for copy in fetch(s, following, 1):
                    copy.start()

            if s < 7:

                @pl.when(i == 3)
                def _():
                    for copy in fetch(s + 1, dest(s + 1, 0), 0):
                        copy.start()

            core_copy(r, s).wait_recv()
            for lanes in tiles_of(s):
                sums[s, r, :, lanes] = (
                    partial_tile(block, slot, lanes) + sums[s, r, :, lanes].astype(jnp.float32)
                ).astype(jnp.bfloat16)
            for when, copies in enumerate((batch[:2], batch[2:3], batch[3:])):

                @pl.when(i == when)
                def _():
                    for copy in copies:
                        copy.start()

            return carry

        partner(0, 0, dest(s, 1))
        lax.fori_loop(0, 4, both, 0)

    def stage_cross(s):
        xsends[s][0].wait_recv()
        add_to(s, 1, lo, ry0.at[1, s])
        across = xy_copy(1, lo, rx0.at[s], 4, s, dp + dx)
        across.start()
        xsends[s][1].wait_recv()
        add_to(s, 2, hi, rx1.at[1, s])
        down = xy_copy(2, hi, ry1.at[s], 5, s, dp + dy)
        down.start()
        xsends[s].extend([across, down])

    def outward(s):
        return z_copy(s, rze.at[3 * (s // 4) + s % 4], s % 4, zr)

    def stage_line(s):
        for j in range(2, 6):
            xsends[s][j].wait_recv()
        if s % 4 < 3:
            add_to(s, 0, lo, ry0.at[0, s], rx0.at[s])
            add_to(s, 0, hi, rx1.at[0, s], ry1.at[s])
            copy = outward(s)
            zsends.append((copy, end))
            pl.when(end)(functools.partial(copy.start))
        else:
            out_ref, lanes = outs[s // 4], lanes_of(s)
            for rows, first, second in ((lo, ry0.at[0, s], rx0.at[s]), (hi, rx1.at[0, s], ry1.at[s])):
                out_ref[rows, :] = (
                    sums[s, 0, rows, lanes].astype(jnp.float32)
                    + first[:, lanes].astype(jnp.float32)
                    + second[:, lanes].astype(jnp.float32)
                )

    def stage_onward(s):
        p, k = s // 4, s % 4
        if k < 2:
            onward = z_copy(s, rzm.at[2 * p + k], 3 + k, zo)
        else:
            onward = z_copy(s, rzf.at[p], 5, zr)
        zsends.append((onward, mid))

        @pl.when(mid)
        def _():
            if k < 2:
                outward(s).wait_recv()
                add_to(s, 0, slice(None), rze.at[3 * p + k])
            else:
                z_copy(4 * p, rzm.at[2 * p], 3, zo).wait_recv()
                add_to(s, 0, slice(None), rzm.at[2 * p])
            onward.start()

    def stage_last(p):
        out_ref, lanes = outs[p], lanes_of(4 * p)

        @pl.when(end)
        def _():
            z_copy(4 * p + 2, rzf.at[p], 5, zr).wait_recv()
            out_ref[...] = out_ref[...] + rzf[p, :, lanes].astype(jnp.float32)

        @pl.when(mid)
        def _():
            outward(4 * p + 2).wait_recv()
            z_copy(4 * p + 1, rzm.at[2 * p + 1], 4, zo).wait_recv()
            out_ref[...] = (
                out_ref[...]
                + rze[3 * p + 2, :, lanes].astype(jnp.float32)
                + rzm[2 * p + 1, :, lanes].astype(jnp.float32)
            )

    for copy in fetch(0, dest(0, 0), 0):
        copy.start()
    for t in range(10):
        if t < 8:
            stage_core(t)
        if 1 <= t < 9:
            stage_cross(t - 1)
        if t >= 2:
            stage_line(t - 2)
        if t % 4 == 3:
            stage_onward(t - 3)
        if t >= 4 and t % 4 == 0:
            stage_onward(t - 2)
            stage_onward(t - 3)
        if t >= 5 and t % 4 == 1:
            stage_last(t // 4 - 1)
    for s in range(4, 8):
        for r in range(4):
            core_copy(r, s).wait_send()
    for batch in xsends:
        for copy in batch:
            copy.wait_send()
    for copy, cond in zsends:
        pl.when(cond)(functools.partial(copy.wait_send))


def return_rows(y_slots, gin_slots, onehot):
    width, narrow = y_slots.shape[2], gin_slots.shape[2]
    anywhere = pl.BlockSpec(memory_space=pl.ANY)
    vmem = pl.BlockSpec(memory_space=pltpu.VMEM)
    dma = pltpu.SemaphoreType.DMA
    low = jnp.bfloat16
    return pl.pallas_call(
        return_kernel,
        name="return_rows",
        out_shape=(
            jax.ShapeDtypeStruct((128, width), jnp.float32),
            jax.ShapeDtypeStruct((128, narrow), jnp.float32),
        ),
        in_specs=[anywhere, anywhere, vmem],
        out_specs=(vmem, vmem),
        scratch_shapes=[
            pltpu.VMEM((2, 16, MAIN, width), low),
            pltpu.VMEM((4, 4, 128, width), low),
            pltpu.VMEM((8, 4, 128, width), low),
            pltpu.VMEM((2, 8, 64, width), low),
            pltpu.VMEM((2, 8, 64, width), low),
            pltpu.VMEM((8, 64, width), low),
            pltpu.VMEM((8, 64, width), low),
            pltpu.VMEM((6, 128, width), low),
            pltpu.VMEM((4, 128, width), low),
            pltpu.VMEM((2, 128, width), low),
            dma((2, 2)), dma((8, 4)), dma((8, 4)), dma((6, 8)), dma((6, 8)), dma((12,)), dma((12,)),
        ],
        compiler_params=pltpu.CompilerParams(
            collective_id=2, has_side_effects=True, vmem_limit_bytes=VMEM_LIMIT
        ),
        cost_estimate=pl.CostEstimate(
            flops=8_600_000_000, bytes_accessed=300_000_000, transcendentals=0
        ),
    )(y_slots, gin_slots, onehot)


def finish_kernel(
    rows_ref, tok_ref, projq_ref, projk_ref, query_ref, key_ref, value_ref, ctx_ref, ga_ref, w_ref,
    gains_ref, cos_ref, sin_ref, seqc_ref, seqr_ref, side_ref, stat_ref, mid_ref,
    gwq_ref, gwk_ref, gwv_ref, gwo_ref, tokens_ref, small_ref,
    dx_ref, gqkv_ref, gctx_ref, dx_all, to_core, from_core, sums, ry0, rx1, rx0, ry1, gain, zside,
    csend, crecv, xsend, xrecv, ssend, srecv, *line_refs,
):
    dp, z, dc, dx, dy = place()
    line = LineScatter(dp, z, *line_refs)
    dxs = line.blocks
    f32, low = jnp.float32, jnp.bfloat16
    half = 128
    heads = query_ref.shape[1]
    width = rows_ref.shape[1]
    others = [(z + i) % 4 for i in (1, 2, 3)]
    greet([(dp + dc, z), (dp + dx, z), (dp + dy, z)] + [(dp, other) for other in others])
    nt = (((1,), (1,)), ((), ()))
    tn = (((0,), (0,)), ((), ()))
    lo, hi = pl.ds(0, half), pl.ds(half, half)
    early = 3 * heads + 128

    def mm(a, b, dims):
        return lax.dot_general(a, b, dims, preferred_element_type=f32)

    def dest(step):
        r = 3 - step % 4
        base = dp + dc - dc * (step // 4)
        return base + (r % 2) * dx + (r // 2) * dy

    def scatter(index, first, count, pieces):
        lanes = pl.ds(first, count)

        def core_copy(r):
            return pltpu.make_async_remote_copy(
                to_core.at[r, :, lanes], from_core.at[r, :, lanes],
                csend.at[index, r], crecv.at[index, r],
                device_id=at(dp + dc, z), device_id_type=MESH,
            )

        def xy_copy(r, rows, target, j, dp_to):
            return pltpu.make_async_remote_copy(
                sums.at[r, rows, lanes], target.at[:, lanes], xsend.at[index, j], xrecv.at[index, j],
                device_id=at(dp_to, z), device_id_type=MESH,
            )

        def add_to(r, rows, part):
            total = sums[r, rows, lanes].astype(f32) + part[:, lanes].astype(f32)
            sums[r, rows, lanes] = total.astype(low)

        copies = [
            xy_copy(3, lo, ry0.at[1], 0, dp + dy),
            xy_copy(3, hi, rx1.at[1], 1, dp + dx),
            xy_copy(2, lo, ry0.at[0], 2, dp + dy),
            xy_copy(1, hi, rx1.at[0], 3, dp + dx),
            xy_copy(1, lo, rx0, 4, dp + dx),
            xy_copy(2, hi, ry1, 5, dp + dy),
        ]

        def partner(step):
            r = 3 - step
            for part, value in pieces(dest(step)):
                to_core[r, :, part] = value.astype(low)
            core_copy(r).start()

        def both(i, carry):
            @pl.when(i < 3)
            def _():
                partner(i + 1)

            r = 3 - i
            core_copy(r).wait_recv()
            for part, value in pieces(dest(4 + i)):
                sums[r, :, part] = (value + from_core[r, :, part].astype(f32)).astype(low)
            for when, batch in enumerate((copies[:2], copies[2:3], copies[3:4])):

                @pl.when(i == when)
                def _():
                    for copy in batch:
                        copy.start()

            return carry

        def core():
            partner(0)
            lax.fori_loop(0, 4, both, 0)

        def cross():
            copies[0].wait_recv()
            add_to(1, lo, ry0.at[1])
            copies[4].start()
            copies[1].wait_recv()
            add_to(2, hi, rx1.at[1])
            copies[5].start()

        def wait():
            for copy in copies[2:]:
                copy.wait_recv()

        def drain():
            for r in range(4):
                core_copy(r).wait_send()
            for copy in copies:
                copy.wait_send()

        return core, cross, wait, drain

    def out_pieces(to):
        cols = pl.ds(pl.multiple_of(to * 256, 256), 256)
        out = mm(ctx_ref[...], ga_ref[:, cols], tn)
        yield slice(early, early + 256), out[:256]
        yield slice(early + 256, early + 512), out[256:]

    def head_pieces(to):
        cols = pl.ds(pl.multiple_of(to * 256, 256), 256)
        yield slice(0, 3 * heads), mm(rows_ref[:, cols], gqkv_ref[...], tn)
        yield slice(3 * heads, early), jnp.concatenate(
            [
                side_ref[to, :128, :].astype(f32),
                side_ref[to, 128:144, :].astype(f32) + gain[to],
                jnp.zeros((112, 128), f32),
            ],
            axis=0,
        )

    core_out, cross_out, wait_out, drain_out = scatter(0, early, heads, out_pieces)
    core_heads, cross_heads, wait_heads, drain_heads = scatter(1, 0, early, head_pieces)
    core_out()
    gain[...] = jnp.zeros_like(gain)
    cosines, sines = cos_ref[...], sin_ref[...]
    query_gain, key_gain = head_gain(gains_ref, 0), head_gain(gains_ref, 16)
    for i in range(2):
        column = 3 * heads + i * 256
        total_ctx = jnp.zeros((512, 256), f32)
        for start in range(0, width, 256):
            lanes = slice(start, start + 256)
            total_ctx = total_ctx + mm(ga_ref[:, lanes], w_ref[lanes, column : column + 256], nt)
        gctx_ref[:, i * 256 : i * 256 + 256] = total_ctx.astype(low)
    score_scale = HD ** (-0.5)

    def head_back(grad, source, rows, cols, gain_values, column):
        values = source[rows, cols]
        inverse = lax.rsqrt(jnp.mean(values * values, axis=1, keepdims=True) + EPSILON)
        turned = grad * cosines[rows] - pltpu.roll(grad, HD // 2, 1) * sines[rows]
        scaled = turned * gain_values
        inner = jnp.mean(scaled * values, axis=1, keepdims=True)
        target = pl.ds(pl.multiple_of(cols.start + column, HD), HD)
        gqkv_ref[rows, target] = ((scaled - values * inner * inverse * inverse) * inverse).astype(low)
        return jnp.sum(turned * values * inverse, axis=0, keepdims=True)

    def one_head(h, carry):
        query_part, key_part = carry
        cols = pl.ds(pl.multiple_of(h * HD, HD), HD)
        key, value = key_ref[:, cols], value_ref[:, cols]
        grad_key = jnp.zeros((key.shape[0], HD), f32)
        grad_value = jnp.zeros((key.shape[0], HD), f32)
        for start in range(0, 512, 256):
            rows = slice(start, start + 256)
            query, grad_ctx = query_ref[rows, cols], gctx_ref[rows, cols]
            probs = head_probs(query, key, seqc_ref[rows, :1], seqr_ref[:1, :])
            grad_value = grad_value + mm(probs.astype(low), grad_ctx, tn)
            grad_probs = mm(grad_ctx, value, nt)
            inner = jnp.sum(probs * grad_probs, axis=1, keepdims=True)
            grad_scores = (probs * (grad_probs - inner)).astype(low)
            grad_query = jnp.dot(grad_scores, key, preferred_element_type=f32) * score_scale
            grad_key = grad_key + mm(grad_scores, query, tn)
            query_part = query_part + head_back(
                grad_query, projq_ref, rows, cols, query_gain, 0
            )
        key_part = key_part + head_back(
            grad_key * score_scale, projk_ref, slice(0, 512), cols, key_gain, heads
        )
        target = pl.ds(pl.multiple_of(cols.start + 2 * heads, HD), HD)
        gqkv_ref[:, target] = grad_value.astype(low)
        return query_part, key_part

    zero_row = jnp.zeros((1, HD), f32)
    query_part, key_part = lax.fori_loop(0, heads // HD, one_head, (zero_row, zero_row))
    for to in range(8):
        gain[to, 4:5, :] = query_part
        gain[to, 5:6, :] = key_part
    cross_out()
    for start in range(0, width, 512):
        lanes = slice(start, start + 512)
        dx_all[:, lanes] = mm(gqkv_ref[...], w_ref[lanes, : 3 * heads], nt)
    for k in range(4):
        rows = pl.ds(pl.multiple_of(line.zs[k] * 128, 128), 128)
        square = jnp.zeros((128, 1), f32)
        for start in range(0, width, 512):
            values = tok_ref[rows, start : start + 512].astype(f32)
            square = square + jnp.sum(values * values, axis=1, keepdims=True)
        inverse = lax.rsqrt(square * (1.0 / width) + EPSILON)
        for start in range(0, width, 512):
            lanes = slice(start, start + 512)
            piece = dx_all[rows, lanes]
            scaled = tok_ref[rows, lanes].astype(f32) * inverse
            column = jnp.sum(piece * scaled, axis=0, keepdims=True)
            for j in range(4):
                to = start // 256 + j // 2
                row = slice(j % 2, j % 2 + 1)
                gain[to, row, :] = gain[to, row, :] + column[:, j * 128 : j * 128 + 128]
            if k < 3:
                dxs[k, :, lanes] = piece.astype(low)
            else:
                dx_ref[:, lanes] = piece
        if k < 3:
            line.ready(k)

    core_heads()
    line.onward(0)
    cross_heads()
    line.onward(1)
    line.onward(2)
    wait_out()
    wait_heads()

    def side_copy(i, source):
        return pltpu.make_async_remote_copy(
            zside.at[source], zside.at[source], ssend.at[i], srecv.at[source],
            device_id=at(dp, others[i]), device_id_type=MESH,
        )

    def total(part, lanes, first, second):
        return (
            sums[0, part, lanes].astype(f32)
            + first[:, lanes].astype(f32)
            + second[:, lanes].astype(f32)
        )

    sides = slice(3 * heads, early)
    zside[z, :128, :] = total(lo, sides, ry0.at[0], rx0)
    zside[z, 128:144, :] = total(hi, sides, rx1.at[0], ry1)[:16] + stat_ref[...]
    for i in range(3):
        side_copy(i, z).start()
    for rows, first, second in ((lo, ry0.at[0], rx0), (hi, rx1.at[0], ry1)):
        for i, target in enumerate((gwq_ref, gwk_ref, gwv_ref)):
            target[rows, :] = total(rows, slice(i * heads, i * heads + heads), first, second)
        gwo_ref[rows, :] = total(rows, slice(early, early + 256), first, second)
        below = pl.ds(256 + rows.start, half)
        gwo_ref[below, :] = total(rows, slice(early + 256, early + 512), first, second)

    line.last(dx_ref)
    scale = jnp.concatenate(
        [gains_ref[j // 2, j % 2 : j % 2 + 1, :] for j in range(width // 128)], axis=1
    )

    def norm_back(index, carry):
        rows = pl.ds(pl.multiple_of(index * 32, 32), 32)
        values = tok_ref[pl.ds(pl.multiple_of(z * 128 + index * 32, 32), 32), :].astype(f32)
        inverse = lax.rsqrt(jnp.mean(values * values, axis=1, keepdims=True) + EPSILON)
        scaled = dx_ref[rows, :] * scale
        inner = jnp.mean(scaled * values, axis=1, keepdims=True)
        back = (scaled - values * (inner * inverse * inverse)) * inverse
        tokens_ref[rows, :] = mid_ref[rows, :] + back
        return carry

    lax.fori_loop(0, 4, norm_back, 0)
    for i in range(3):
        side_copy(i, others[i]).wait_recv()
    small_ref[...] = (zside[0] + zside[1]) + (zside[2] + zside[3])
    drain_out()
    drain_heads()
    line.drain()
    for i in range(3):
        side_copy(i, z).wait_send()


def finish(rows, tok, attention, grad_attn, weights, tables, side, stats, grad_mid):
    width = rows.shape[1]
    heads = attention[0].shape[1]
    f32, low = jnp.float32, jnp.bfloat16
    vmem = pl.BlockSpec(memory_space=pltpu.VMEM)
    dma = pltpu.SemaphoreType.DMA
    packed = 4 * heads + 128
    return pl.pallas_call(
        finish_kernel,
        name="finish",
        out_shape=(
            jax.ShapeDtypeStruct((256, heads), f32),
            jax.ShapeDtypeStruct((256, heads), f32),
            jax.ShapeDtypeStruct((256, heads), f32),
            jax.ShapeDtypeStruct((heads, 256), f32),
            jax.ShapeDtypeStruct((128, width), f32),
            jax.ShapeDtypeStruct((144, 128), f32),
        ),
        in_specs=[vmem] * 18,
        out_specs=(vmem,) * 6,
        scratch_shapes=[
            pltpu.VMEM((128, width), f32),
            pltpu.VMEM((512, 3 * heads), low),
            pltpu.VMEM((512, heads), low),
            pltpu.VMEM((512, width), f32),
        ]
        + [
            pltpu.VMEM((4, 256, packed), low),
            pltpu.VMEM((4, 256, packed), low),
            pltpu.VMEM((4, 256, packed), low),
            pltpu.VMEM((2, 128, packed), low),
            pltpu.VMEM((2, 128, packed), low),
            pltpu.VMEM((128, packed), low),
            pltpu.VMEM((128, packed), low),
            pltpu.VMEM((8, 16, 128), f32),
            pltpu.VMEM((4, 144, 128), f32),
            dma((2, 4)), dma((2, 4)), dma((2, 6)), dma((2, 6)), dma((3,)), dma((4,)),
        ]
        + LineScatter.scratch(width),
        compiler_params=pltpu.CompilerParams(
            collective_id=4, has_side_effects=True, vmem_limit_bytes=VMEM_LIMIT
        ),
        cost_estimate=pl.CostEstimate(
            flops=8_000_000_000, bytes_accessed=100_000_000, transcendentals=0
        ),
    )(rows, tok, *attention, grad_attn, weights, *tables, side, stats, grad_mid)


def expert_kernel(
    x_ref, dy_ref, gate_ref, wg_ref, wu_ref, wd_ref, y_ref, gin_ref, dgate_ref, dup_ref, hgated_ref,
    gate_pre_ref, up_pre_ref, raw_ref,
):
    rows, ff = dgate_ref.shape[1:]
    width = x_ref.shape[2]
    expert = lax.axis_index("dp") * 8 + pl.program_id(0)
    nt = (((1,), (1,)), ((), ()))

    def mm(a, b, dims):
        return lax.dot_general(a, b, dims, preferred_element_type=jnp.float32)

    gate_pre_ref[...] = jnp.dot(x_ref[0], wg_ref[0], preferred_element_type=jnp.float32)
    up_pre_ref[...] = jnp.dot(x_ref[0], wu_ref[0], preferred_element_type=jnp.float32)
    raw_ref[...] = mm(dy_ref[0], wd_ref[0], nt)
    step = 96

    def pointwise(index, carry):
        part = pl.ds(pl.multiple_of(index * step, step), step)
        gate_pre, up_pre, raw = gate_pre_ref[part, :], up_pre_ref[part, :], raw_ref[part, :]
        weight = jnp.concatenate([gate_ref[0, part, :]] * (ff // 128), axis=1)
        sig = jax.nn.sigmoid(gate_pre)
        silu = gate_pre * sig
        hidden = silu * up_pre
        route_grad = jnp.sum(hidden * raw, axis=1, keepdims=True)
        grad_hidden = weight * raw
        lane = lax.broadcasted_iota(jnp.int32, (step, 128), 1)
        high = route_grad.astype(jnp.bfloat16).astype(jnp.float32)
        extra = jnp.where(lane == expert, high, 0.0) + jnp.where(
            lane == expert + 64, route_grad - high, 0.0
        )
        hgated_ref[0, part, :] = (weight * hidden).astype(jnp.bfloat16)
        dgate_ref[0, part, :] = (
            grad_hidden * up_pre * sig * (1.0 + gate_pre * (1.0 - sig))
        ).astype(jnp.bfloat16)
        dup_ref[0, part, :] = (grad_hidden * silu).astype(jnp.bfloat16)
        y_ref[0, part, width:] = extra.astype(jnp.bfloat16)
        return carry

    lax.fori_loop(0, rows // step, pointwise, 0)
    for start in range(0, width, 512):
        lanes = slice(start, start + 512)
        y_ref[0, :, lanes] = jnp.dot(
            hgated_ref[0], wd_ref[0, :, lanes], preferred_element_type=jnp.float32
        ).astype(jnp.bfloat16)
        gin_ref[0, :, lanes] = (
            mm(dgate_ref[0], wg_ref[0, lanes, :], nt) + mm(dup_ref[0], wu_ref[0, lanes, :], nt)
        ).astype(jnp.bfloat16)


def weights_kernel(x_ref, dy_ref, dgate_ref, dup_ref, hgated_ref, gwg_ref, gwu_ref, gwd_ref):
    width = x_ref.shape[2]
    tn = (((0,), (0,)), ((), ()))

    def mm(a, b):
        return lax.dot_general(a, b, tn, preferred_element_type=jnp.float32)

    for start in range(0, width, 512):
        part = slice(start, start + 512)
        gwd_ref[0, :, part] = mm(hgated_ref[0], dy_ref[0, :, part])
        xs = x_ref[0, :, part]
        gwg_ref[0, part, :] = mm(xs, dgate_ref[0])
        gwu_ref[0, part, :] = mm(xs, dup_ref[0])


def expert_spec(*shape):
    return pl.BlockSpec((1,) + shape, lambda e: (e, 0, 0))


def run_experts(x_slots, dy_slots, gate_slots, w_gate, w_up, w_down):
    experts, rows, width = x_slots.shape
    ff = w_gate.shape[2]
    spec, low = expert_spec, jnp.bfloat16
    middle = jax.ShapeDtypeStruct((experts, rows, ff), low)
    return pl.pallas_call(
        expert_kernel,
        name="experts",
        grid=(experts,),
        in_specs=[
            spec(rows, width), spec(rows, width), spec(rows, 128),
            spec(width, ff), spec(width, ff), spec(ff, width),
        ],
        out_specs=(spec(rows, width + 128), spec(rows, width)) + (spec(rows, ff),) * 3,
        out_shape=(
            jax.ShapeDtypeStruct((experts, rows, width + 128), low),
            jax.ShapeDtypeStruct((experts, rows, width), low),
            middle, middle, middle,
        ),
        scratch_shapes=[pltpu.VMEM((rows, ff), jnp.float32)] * 3,
        compiler_params=pltpu.CompilerParams(vmem_limit_bytes=VMEM_LIMIT),
        cost_estimate=pl.CostEstimate(
            flops=29_000_000_000, bytes_accessed=100_000_000, transcendentals=2_000_000
        ),
    )(x_slots, dy_slots, gate_slots, w_gate, w_up, w_down)


def run_weights(x_slots, dy_slots, dgate, dup, hgated):
    experts, rows, width = x_slots.shape
    ff = dgate.shape[2]
    spec, f32 = expert_spec, jnp.float32
    wide = jax.ShapeDtypeStruct((experts, width, ff), f32)
    return pl.pallas_call(
        weights_kernel,
        name="expert_weights",
        grid=(experts,),
        in_specs=[spec(rows, width)] * 2 + [spec(rows, ff)] * 3,
        out_specs=(spec(width, ff), spec(width, ff), spec(ff, width)),
        out_shape=(wide, wide, jax.ShapeDtypeStruct((experts, ff, width), f32)),
        compiler_params=pltpu.CompilerParams(vmem_limit_bytes=VMEM_LIMIT),
        cost_estimate=pl.CostEstimate(
            flops=15_000_000_000, bytes_accessed=100_000_000, transcendentals=0
        ),
    )(x_slots, dy_slots, dgate, dup, hgated)


def plain_onehot(routes_all, first_expert, local_experts):
    sources, rows = routes_all.shape[0], routes_all.shape[1]
    experts = jnp.arange(local_experts, dtype=jnp.int32) + first_expert
    member = jnp.any(routes_all[:, :, :, None] == experts, axis=2).astype(jnp.int32)
    rank = jnp.cumsum(member, axis=1) - member
    rank = jnp.where(member > 0, rank, -1)
    return (
        rank.transpose(0, 2, 1)[:, :, None, :] == jnp.arange(CAP, dtype=jnp.int32)[:, None]
    ).astype(jnp.bfloat16)


def plain_experts(moe_low, cotangent, routes, gates, w_gate, w_up, w_down):
    both = ("dp", "tensor")
    local_experts = w_gate.shape[0]
    width = moe_low.shape[1]
    f32 = jnp.float32
    routes_all = lax.all_gather(routes, both, axis=0)
    x_all = lax.all_gather(moe_low, both, axis=0)
    dy_all = lax.all_gather(cotangent, both, axis=0)
    gates_all = lax.all_gather(gates, both, axis=0)
    first_expert = lax.axis_index("dp") * local_experts
    onehot = plain_onehot(routes_all, first_expert, local_experts)
    take = functools.partial(jnp.einsum, "sect,std->escd")
    flat = (local_experts, -1, width)
    x_slots = take(onehot, x_all).reshape(flat)
    dy_slots = take(onehot, dy_all).reshape(flat)
    experts = jnp.arange(local_experts, dtype=jnp.int32) + first_expert
    gates_here = jnp.sum(
        jnp.where(routes_all[..., None] == experts, gates_all[..., None], 0.0), axis=2
    )
    weight = jnp.einsum(
        "sect,ste->esc", onehot.astype(f32), gates_here, precision=lax.Precision.HIGHEST
    ).reshape(local_experts, -1)[..., None]
    mm = functools.partial(jnp.einsum, preferred_element_type=f32)
    gate_pre = mm("ecd,edf->ecf", x_slots, w_gate)
    up_pre = mm("ecd,edf->ecf", x_slots, w_up)
    raw = mm("ecd,efd->ecf", dy_slots, w_down)
    sig = jax.nn.sigmoid(gate_pre)
    silu = gate_pre * sig
    hidden = silu * up_pre
    hgated = (weight * hidden).astype(jnp.bfloat16)
    route_grad = jnp.sum(hidden * raw, axis=2).reshape(local_experts, -1, CAP)
    grad_hidden = weight * raw
    dgate = (grad_hidden * up_pre * sig * (1.0 + gate_pre * (1.0 - sig))).astype(jnp.bfloat16)
    dup = (grad_hidden * silu).astype(jnp.bfloat16)
    y_slots = mm("ecf,efd->ecd", hgated, w_down).astype(jnp.bfloat16)
    gin_slots = (mm("ecf,edf->ecd", dgate, w_gate) + mm("ecf,edf->ecd", dup, w_up)).astype(
        jnp.bfloat16
    )
    grads = (
        mm("ecd,ecf->edf", x_slots, dgate),
        mm("ecd,ecf->edf", x_slots, dup),
        mm("ecf,ecd->efd", hgated, dy_slots),
    )

    def give_back(slots):
        slots = slots.reshape(local_experts, -1, CAP, width)
        rows = mm("sect,escd->std", onehot, slots).astype(jnp.bfloat16)
        return lax.psum_scatter(
            rows.reshape(-1, width), both, scatter_dimension=0, tiled=True
        ).astype(f32)

    here = jnp.einsum(
        "sect,esc->ste", onehot.astype(f32), route_grad, precision=lax.Precision.HIGHEST
    )
    spread = jnp.zeros(here.shape[:2] + (EXPERTS,), f32)
    spread = lax.dynamic_update_slice(spread, here, (0, 0, first_expert))
    grad_gates = lax.psum_scatter(
        spread.reshape(-1, EXPERTS), both, scatter_dimension=0, tiled=True
    )
    return (give_back(y_slots), grad_gates, give_back(gin_slots), lambda own_rows: grads)


def routed_experts(moe_low, cotangent, routes, gates, w_gate, w_up, w_down, dispatched):
    if dispatched is None:
        return plain_experts(moe_low, cotangent, routes, gates, w_gate, w_up, w_down)
    dy_slots, onehot, all_routes = dispatched
    width = moe_low.shape[1]
    x_slots, gate_slots = gather_slots(moe_low, gates.T, onehot, all_routes)
    y_slots, gin_slots, *middle = run_experts(
        x_slots, dy_slots, gate_slots, w_gate, w_up, w_down
    )
    sums, grad_in = return_rows(y_slots, gin_slots, onehot)
    grad_gates = sums[:, width : width + EXPERTS] + sums[:, width + EXPERTS :]

    def weight_grads(own_rows):
        hgated, unused = lax.optimization_barrier((middle[2], own_rows))
        return run_weights(x_slots, dy_slots, middle[0], middle[1], hgated)

    return (sums[:, :width], grad_gates, grad_in, weight_grads)


def own_kernels(tokens, w_gate):
    return (
        lax.axis_size("dp") == 8
        and lax.axis_size("tensor") == 4
        and tokens.shape == (128, 2048)
        and w_gate.shape[0] == 8
    )


def side_columns(pieces, rows):
    filled = [jnp.pad(p, ((0, rows - p.shape[0]), (0, 0))) for p in pieces]
    used = sum(p.shape[1] for p in filled)
    return jnp.concatenate(filled + [jnp.zeros((rows, 128 - used), filled[0].dtype)], axis=1)


def body(
    tokens,
    cotangent,
    lengths,
    seq_order,
    routes,
    attn_gain,
    w_query,
    w_key,
    w_value,
    w_output,
    query_gain,
    key_gain,
    ffn_gain,
    router,
    w_gate,
    w_up,
    w_down,
):
    tok_rows, model_width = tokens.shape
    tensor_count = lax.axis_size("tensor")
    data_count = lax.axis_size("dp")
    group_rows_count = tok_rows * tensor_count
    block_rows = min(group_rows_count, 512)
    shard = w_query.shape[0]
    heads_width = w_query.shape[1]
    gain_rows = query_gain.shape[0]
    low = jnp.bfloat16
    f32 = jnp.float32

    own = own_kernels(tokens, w_gate)

    seq_ids, positions = arrival_layout(lengths[0], seq_order[0])
    resid_in = tokens.astype(f32)
    if own:
        gains, filled = jnp.zeros((1024,), f32), 0
        for part in (attn_gain, ffn_gain, query_gain, key_gain):
            count = part.shape[0]
            gains = gains + jnp.pad(part.astype(f32), (filled, 1024 - filled - count))
            filled += count
        gains = gains.reshape(8, 128)
        shards = (w_query, w_key, w_value, w_output, jnp.pad(router, ((0, 0), (0, 128 - EXPERTS))))
        seq_float = seq_ids.astype(f32)
        lane = jnp.arange(HD, dtype=jnp.int32)
        frequency = THETA ** (-(lane % (HD // 2)).astype(f32) / (HD // 2))
        angles = positions.astype(f32)[:, None] * frequency[None, :]
        tables = (
            jnp.cos(angles),
            jnp.sin(angles) * jnp.where(lane < HD // 2, -1.0, 1.0),
            jnp.broadcast_to(seq_float[:, None], (group_rows_count, 128)),
            jnp.broadcast_to(seq_float[None, :], (8, group_rows_count)),
        )
        (
            weights, group_tokens, dy_slots, all_gains, onehot, all_routes, group_rows,
            *attention, attn_out,
        ) = front(shards, tokens, cotangent, routes.T.astype(f32), gains, *tables, heads_width)
        dispatched = (dy_slots, onehot, all_routes)
        group_tokens = group_tokens.reshape(-1, model_width)
        full_router = weights[:, 4 * heads_width : 4 * heads_width + EXPERTS]
        ffn_scale = all_gains[:, 2:4].reshape(-1)
    else:
        side = side_columns(
            [router, attn_gain[:, None], ffn_gain[:, None], query_gain[:, None], key_gain[:, None]],
            shard,
        )
        packed = jnp.concatenate([w_query, w_key, w_value, w_output.T, side], axis=1)
        weights = lax.all_gather(packed, "dp", axis=0, tiled=True)
        group_tokens = lax.all_gather(tokens, "tensor", axis=0, tiled=True)
        dispatched = None
        full_query = weights[:, :heads_width]
        full_key = weights[:, heads_width : 2 * heads_width]
        full_value = weights[:, 2 * heads_width : 3 * heads_width]
        output_t = weights[:, 3 * heads_width : 4 * heads_width]
        extras = weights[:, 4 * heads_width :]
        full_router = extras[:, :EXPERTS]
        attn_scale = extras[:, EXPERTS].astype(f32)
        ffn_scale = extras[:, EXPERTS + 1].astype(f32)
        gain_columns = extras.reshape(data_count, shard, 128)[:, :gain_rows, EXPERTS + 2 : EXPERTS + 4]
        query_scale = gain_columns[:, :, 0].reshape(-1).astype(f32)
        key_scale = gain_columns[:, :, 1].reshape(-1).astype(f32)

        cosines, sines = rope_tables(positions)
        group_rows = norm_apply(group_tokens.astype(f32), attn_scale).astype(low)
        proj_query = jnp.dot(group_rows, full_query, preferred_element_type=f32)
        proj_key = jnp.dot(group_rows, full_key, preferred_element_type=f32)
        value_flat = jnp.dot(group_rows, full_value, preferred_element_type=f32).astype(low)
        value_low = value_flat.reshape(group_rows_count, -1, HD)
        query_low = head_norm_rope(proj_query, query_scale, cosines, sines).astype(low)
        key_low = head_norm_rope(proj_key, key_scale, cosines, sines).astype(low)
        context, row_lse = attend(query_low, key_low, value_low, seq_ids, block_rows)
        context_low = context.reshape(group_rows_count, -1).astype(low)
        attn_out = lax.psum_scatter(
            lax.dot_general(
                context_low, output_t, (((1,), (1,)), ((), ())), preferred_element_type=f32
            ).astype(low),
            "tensor",
            scatter_dimension=0,
            tiled=True,
        ).astype(f32)
    resid_mid = resid_in + attn_out
    moe_low = norm_apply(resid_mid, ffn_scale).astype(low)
    logits = jnp.dot(moe_low, full_router, preferred_element_type=f32)
    route_match = routes[:, :, None] == jnp.arange(EXPERTS, dtype=jnp.int32)[None, None, :]
    picked_logits = jnp.sum(jnp.where(route_match, logits[:, None, :], 0.0), axis=-1)
    gate_peak = jnp.max(picked_logits, axis=1, keepdims=True)
    gate_raw = jnp.exp(picked_logits - gate_peak)
    gates = gate_raw / jnp.sum(gate_raw, axis=1, keepdims=True)
    dense_gates = jnp.sum(jnp.where(route_match, gates[:, :, None], 0.0), axis=1)

    moe_out, grad_gates, grad_from_experts, expert_weight_grads = routed_experts(
        moe_low, cotangent, routes, gates, w_gate, w_up, w_down, dispatched
    )
    layer_out = (resid_mid + moe_out).astype(low)
    stat_terms = jnp.stack(
        [jnp.sum(resid_mid * resid_mid), jnp.sum(attn_out * attn_out), jnp.sum(moe_out * moe_out)]
    )
    grad_out = cotangent.astype(f32)
    inner_gate = jnp.sum(dense_gates * grad_gates, axis=1, keepdims=True)
    grad_logits_low = (dense_gates * (grad_gates - inner_gate)).astype(low)
    grad_router_part = jnp.dot(moe_low.T, grad_logits_low, preferred_element_type=f32)
    grad_moe_in = grad_from_experts + jnp.dot(
        grad_logits_low, full_router.T, preferred_element_type=f32
    )
    unused_mid, ffn_back = jax.vjp(norm_apply, resid_mid, ffn_scale)
    grad_mid_norm, grad_ffn_part = ffn_back(grad_moe_in)
    grad_mid = grad_out + grad_mid_norm
    grad_attn_low = grad_mid.astype(low)
    grad_attn_rows = lax.all_gather(grad_attn_low, "tensor", axis=0, tiled=True)
    grad_gate_w, grad_up_w, grad_down = expert_weight_grads(grad_attn_low)
    tn = (((0,), (0,)), ((), ()))
    if own:
        router_side = grad_router_part.reshape(8, 2, 128, EXPERTS).swapaxes(1, 2).reshape(8, 128, 128)

        side = jnp.concatenate(
            [
                router_side,
                jnp.zeros((8, 2, 128), f32),
                grad_ffn_part.reshape(8, 2, 128),
                jnp.zeros((8, 12, 128), f32),
            ],
            axis=1,
        ).astype(low)
        stats = jnp.pad(stat_terms[None, :], ((6, 9), (0, 125)))
        *grads_qkv, grad_out_w, grad_tokens, small = finish(
            group_rows, group_tokens, attention, grad_attn_rows, weights, (all_gains,) + tables,
            side, stats, grad_mid,
        )
        grad_router = jnp.concatenate([small[:128, :EXPERTS], small[:128, EXPERTS:]], axis=0)
        grad_attn_gain = small[128:130].reshape(-1)
        grad_ffn_gain = small[130:132].reshape(-1)
        first_lane = lax.axis_index("dp") * gain_rows
        grad_query_gain = lax.dynamic_slice(small[132], (first_lane,), (gain_rows,))
        grad_key_gain = lax.dynamic_slice(small[133], (first_lane,), (gain_rows,))
        stat_totals = small[134, :3]
    else:
        grad_ctx_low = jnp.dot(grad_attn_rows, output_t, preferred_element_type=f32).astype(low)
        grad_query, grad_key, grad_value = attend_back(
            query_low,
            key_low,
            value_low,
            seq_ids,
            row_lse,
            grad_ctx_low.reshape(value_low.shape),
            block_rows,
        )
        grad_value_low = grad_value.reshape(group_rows_count, -1).astype(low)
        unused_query, query_back = jax.vjp(
            lambda projected, head_gain: head_norm_rope(projected, head_gain, cosines, sines),
            proj_query,
            query_scale,
        )
        grad_proj_query, grad_query_gain_part = query_back(grad_query)
        unused_key, key_back = jax.vjp(
            lambda projected, head_gain: head_norm_rope(projected, head_gain, cosines, sines),
            proj_key,
            key_scale,
        )
        grad_proj_key, grad_key_gain_part = key_back(grad_key)
        grad_query_low = grad_proj_query.astype(low)
        grad_key_low = grad_proj_key.astype(low)
        head_grads = (grad_query_low, grad_key_low, grad_value_low)
        weight_grads = [
            lax.dot_general(group_rows, part, tn, preferred_element_type=f32) for part in head_grads
        ]
        grad_output_t = lax.dot_general(grad_attn_rows, context_low, tn, preferred_element_type=f32)
        total_rows = jnp.dot(grad_query_low, full_query.T, preferred_element_type=f32)
        total_rows = total_rows + jnp.dot(grad_key_low, full_key.T, preferred_element_type=f32)
        total_rows = total_rows + jnp.dot(grad_value_low, full_value.T, preferred_element_type=f32)
        grad_normed = lax.psum_scatter(
            total_rows.astype(low), "tensor", scatter_dimension=0, tiled=True
        ).astype(f32)
        unused_in, attn_back = jax.vjp(norm_apply, resid_in, attn_scale)
        grad_in_norm, grad_attn_part = attn_back(grad_normed)

        def gain_column(part):
            cut = part.astype(low).reshape(data_count, gain_rows, 1)
            return jnp.pad(cut, ((0, 0), (0, shard - gain_rows), (0, 0))).reshape(-1, 1)

        side_grads = side_columns(
            [
                grad_router_part.astype(low),
                grad_attn_part.astype(low)[:, None],
                grad_ffn_part.astype(low)[:, None],
                gain_column(grad_query_gain_part),
                gain_column(grad_key_gain_part),
            ],
            model_width,
        )
        packed_grads = jnp.concatenate(
            [part.astype(low) for part in weight_grads] + [grad_output_t.astype(low), side_grads],
            axis=1,
        )
        reduced = lax.psum_scatter(packed_grads, "dp", scatter_dimension=0, tiled=True).astype(f32)
        side_total, stat_totals = lax.psum(
            (reduced[:, 4 * heads_width : 4 * heads_width + EXPERTS + 4], stat_terms), "tensor"
        )
        grads_qkv = [reduced[:, i * heads_width : (i + 1) * heads_width] for i in range(3)]
        grad_out_w = reduced[:, 3 * heads_width : 4 * heads_width].T
        grad_attn_gain = side_total[:, EXPERTS]
        grad_ffn_gain = side_total[:, EXPERTS + 1]
        grad_query_gain = side_total[:gain_rows, EXPERTS + 2]
        grad_key_gain = side_total[:gain_rows, EXPERTS + 3]
        grad_router = side_total[:, :EXPERTS]
        grad_tokens = grad_mid + grad_in_norm
    rms_stats = jnp.sqrt(stat_totals / (group_rows_count * model_width))[None, :]
    return (
        layer_out,
        grad_tokens,
        grad_attn_gain,
        *grads_qkv,
        grad_out_w,
        grad_query_gain,
        grad_key_gain,
        grad_ffn_gain,
        grad_router,
        grad_gate_w,
        grad_up_w,
        grad_down,
        rms_stats,
    )


def solution(mesh):
    in_specs = (
        P(("dp", "tensor"), None),
        P(("dp", "tensor"), None),
        P("dp", None),
        P("dp", None),
        P(("dp", "tensor"), None),
        P("dp"),
        P("dp", "tensor"),
        P("dp", "tensor"),
        P("dp", "tensor"),
        P("tensor", "dp"),
        P("dp"),
        P("dp"),
        P("dp"),
        P("dp", None),
        P("dp", None, "tensor"),
        P("dp", None, "tensor"),
        P("dp", "tensor", None),
    )
    out_specs = (
        P(("dp", "tensor"), None),
        P(("dp", "tensor"), None),
        P("dp"),
        P("dp", "tensor"),
        P("dp", "tensor"),
        P("dp", "tensor"),
        P("tensor", "dp"),
        P("dp"),
        P("dp"),
        P("dp"),
        P("dp", None),
        P("dp", None, "tensor"),
        P("dp", None, "tensor"),
        P("dp", "tensor", None),
        P("dp", None),
    )
    return jax.shard_map(body, mesh=mesh, in_specs=in_specs, out_specs=out_specs, check_vma=False)
```

```python
import functools

import jax
import jax.numpy as jnp
from jax import lax
from jax.experimental import pallas as pl
from jax.experimental.pallas import tpu as pltpu
from jax.sharding import PartitionSpec as P

HD = 128
EXPERTS = 64
TOPK = 8
CAP = 18


EPSILON = 1e-05
THETA = 10000.0
NEGATIVE = -1e30


def inv_rms(values):
    return lax.rsqrt(jnp.mean(values * values, axis=-1, keepdims=True) + EPSILON)


def norm_apply(values, scale_gain):
    return values * inv_rms(values) * scale_gain


def arrival_layout(seq_lengths, order_row):
    row_total = order_row.shape[0]
    placed = jnp.arange(row_total, dtype=jnp.int32)
    order = jnp.arange(seq_lengths.shape[0], dtype=jnp.int32)
    upto = order[None, :] <= order[:, None]
    seq_ends = jnp.sum(jnp.where(upto, seq_lengths[None, :], 0), axis=1)
    seq_starts = seq_ends - seq_lengths
    member = jnp.sum((placed[:, None] >= seq_ends[None, :]).astype(jnp.int32), axis=1)
    chosen = member[:, None] == jnp.arange(seq_lengths.shape[0], dtype=jnp.int32)[None, :]
    seq_begin = jnp.sum(jnp.where(chosen, seq_starts[None, :], 0), axis=1)
    here = order_row[None, :] == placed[:, None]
    seq_ids = jnp.sum(jnp.where(here, member[None, :], 0), axis=1)
    positions = jnp.sum(jnp.where(here, (placed - seq_begin)[None, :], 0), axis=1)
    return (seq_ids, positions)


def rope_tables(positions):
    half_dim = HD // 2
    frequency = THETA ** (-jnp.arange(half_dim, dtype=jnp.float32) / half_dim)
    angles = positions.astype(jnp.float32)[:, None] * frequency[None, :]
    return (jnp.cos(angles)[:, None, :], jnp.sin(angles)[:, None, :])


def head_norm_rope(projected, head_gain, cosines, sines):
    shaped = projected.reshape(projected.shape[0], -1, HD)
    normed_heads = norm_apply(shaped, head_gain)
    first_half = normed_heads[..., : HD // 2]
    second_half = normed_heads[..., HD // 2 :]
    return jnp.concatenate(
        [first_half * cosines - second_half * sines, second_half * cosines + first_half * sines],
        axis=-1,
    )


def masked_scores(query_block, key_low, seq_block, seq_ids):
    score_scale = HD ** (-0.5)
    scores = (
        jnp.einsum("qhd,khd->hqk", query_block, key_low, preferred_element_type=jnp.float32)
        * score_scale
    )
    same_seq = (seq_block[:, None] == seq_ids[None, :])[None]
    return jnp.where(same_seq, scores, NEGATIVE)


def attend(query_low, key_low, value_low, seq_ids, block_rows):
    num_blocks = query_low.shape[0] // block_rows
    query_blocks = query_low.reshape(num_blocks, block_rows, query_low.shape[1], HD)
    seq_blocks = seq_ids.reshape(num_blocks, block_rows)

    def one_block(inputs):
        query_block, seq_block = inputs
        scores = masked_scores(query_block, key_low, seq_block, seq_ids)
        row_peak = jnp.max(scores, axis=-1, keepdims=True)
        raised = jnp.exp(scores - row_peak)
        row_total = jnp.sum(raised, axis=-1, keepdims=True)
        probs_low = (raised / row_total).astype(jnp.bfloat16)
        context = jnp.einsum(
            "hqk,khd->qhd", probs_low, value_low, preferred_element_type=jnp.float32
        )
        return (context, row_peak + jnp.log(row_total))

    context, row_lse = lax.map(one_block, (query_blocks, seq_blocks))
    return (context.reshape(query_low.shape), row_lse)


def attend_back(query_low, key_low, value_low, seq_ids, row_lse, grad_ctx_low, block_rows):
    score_scale = HD ** (-0.5)
    num_blocks = query_low.shape[0] // block_rows
    block_shape = (num_blocks, block_rows, query_low.shape[1], HD)

    def one_block(carry, inputs):
        grad_key_sum, grad_value_sum = carry
        query_block, seq_block, lse_block, grad_block = inputs
        scores = masked_scores(query_block, key_low, seq_block, seq_ids)
        probs = jnp.exp(scores - lse_block)
        probs_low = probs.astype(jnp.bfloat16)
        grad_value_sum = grad_value_sum + jnp.einsum(
            "hqk,qhd->khd", probs_low, grad_block, preferred_element_type=jnp.float32
        )
        grad_probs = jnp.einsum(
            "qhd,khd->hqk", grad_block, value_low, preferred_element_type=jnp.float32
        )
        inner_sum = jnp.sum(probs * grad_probs, axis=-1, keepdims=True)
        grad_scores = (probs * (grad_probs - inner_sum)).astype(jnp.bfloat16)
        grad_query_block = (
            jnp.einsum("hqk,khd->qhd", grad_scores, key_low, preferred_element_type=jnp.float32)
            * score_scale
        )
        grad_key_sum = (
            grad_key_sum
            + jnp.einsum(
                "hqk,qhd->khd", grad_scores, query_block, preferred_element_type=jnp.float32
            )
            * score_scale
        )
        return ((grad_key_sum, grad_value_sum), grad_query_block)

    zeros_heads = jnp.zeros(query_low.shape, jnp.float32)
    carried, grad_query = lax.scan(
        one_block,
        (zeros_heads, zeros_heads),
        (
            query_low.reshape(block_shape),
            seq_ids.reshape(num_blocks, block_rows),
            row_lse,
            grad_ctx_low.reshape(block_shape),
        ),
    )
    return (grad_query.reshape(query_low.shape), carried[0], carried[1])


MESH = pl.DeviceIdType.MESH
VMEM_LIMIT = 60 * 1024 * 1024
MAIN = 16
SPARE = CAP - MAIN


def at(dp_index, z_index):
    return {"dp": dp_index, "tensor": z_index}


def place():
    dp = lax.axis_index("dp")
    z = lax.axis_index("tensor")
    core, x, y = dp % 2, (dp // 2) % 2, dp // 4
    return dp, z, 1 - 2 * core, 2 - 4 * x, 4 - 8 * y


def greet(peers, extra=None, has_extra=None, count=0):
    barrier = pltpu.get_barrier_semaphore()
    for peer in peers:
        pl.semaphore_signal(barrier, inc=1, device_id=at(*peer), device_id_type=MESH)
    if extra is not None:

        @pl.when(has_extra)
        def _():
            pl.semaphore_signal(barrier, inc=1, device_id=at(*extra), device_id_type=MESH)

    pl.semaphore_wait(barrier, len(peers) + count)


def when_or_now(cond, action):
    if cond is None:
        action()
    else:
        pl.when(cond)(action)


def slot_matrix(routes_block, source, first_expert):
    experts = lax.broadcasted_iota(jnp.int32, (8, 128), 0) + first_expert
    member = jnp.zeros((8, 128), jnp.float32)
    for j in range(TOPK):
        member = member + (routes_block[j : j + 1, :] == experts.astype(jnp.float32)).astype(jnp.float32)
    earlier = (
        lax.broadcasted_iota(jnp.int32, (128, 128), 0)
        < lax.broadcasted_iota(jnp.int32, (128, 128), 1)
    ).astype(jnp.bfloat16)
    rank = jnp.dot(member.astype(jnp.bfloat16), earlier, preferred_element_type=jnp.float32)
    rank = jnp.where(member > 0.5, rank, -1.0).astype(jnp.int32)
    spread = jnp.broadcast_to(rank[:, None, :], (8, MAIN, 128)).reshape(128, 128)
    row = lax.broadcasted_iota(jnp.int32, (128, 128), 0) % MAIN
    main = spread == row
    spare = jnp.logical_and(row // SPARE == source % 8, spread == MAIN + row % SPARE)
    return jnp.concatenate(
        [main.astype(jnp.float32), spare.astype(jnp.float32)], axis=0
    ).astype(jnp.bfloat16)


class LineScatter:
    def __init__(self, dp, z, blocks, rze, rzm, rzf, zsend, zrecv):
        self.dp, self.z = dp, z
        self.zr, self.zo = z + 1 - 2 * (z % 2), 3 - z
        self.mid, self.end = z * (3 - z) > 0, z * (3 - z) < 1
        self.zs = [3 - 3 * (z // 2), 2 - z // 2, self.zr, z]
        self.blocks, self.rze, self.rzm, self.rzf = blocks, rze, rzm, rzf
        self.zsend, self.zrecv = zsend, zrecv
        self.outward = [self.copy(blocks.at[k], rze.at[k], k, self.zr) for k in range(3)]
        self.sends = []

    def copy(self, src, dst, index, z_to):
        return pltpu.make_async_remote_copy(
            src, dst, self.zsend.at[index], self.zrecv.at[index],
            device_id=at(self.dp, z_to), device_id_type=MESH,
        )

    def ready(self, k):
        pl.when(self.end)(functools.partial(self.outward[k].start))
        self.sends.append((self.outward[k], self.end))

    def add(self, k, part):
        total = self.blocks[k].astype(jnp.float32) + part[...].astype(jnp.float32)
        self.blocks[k] = total.astype(jnp.bfloat16)

    def onward(self, k):
        if k < 2:
            copy = self.copy(self.blocks.at[k], self.rzm.at[k], 3 + k, self.zo)
        else:
            copy = self.copy(self.blocks.at[k], self.rzf, 5, self.zr)
        self.sends.append((copy, self.mid))

        @pl.when(self.mid)
        def _():
            if k < 2:
                self.outward[k].wait_recv()
                self.add(k, self.rze.at[k])
            else:
                self.copy(self.blocks.at[0], self.rzm.at[0], 3, self.zo).wait_recv()
                self.add(k, self.rzm.at[0])
            copy.start()

    def last(self, out_ref):
        @pl.when(self.end)
        def _():
            self.copy(self.blocks.at[2], self.rzf, 5, self.zr).wait_recv()
            out_ref[...] = out_ref[...] + self.rzf[...].astype(jnp.float32)

        @pl.when(self.mid)
        def _():
            self.outward[2].wait_recv()
            self.copy(self.blocks.at[1], self.rzm.at[1], 4, self.zo).wait_recv()
            out_ref[...] = (
                out_ref[...]
                + self.rze[2].astype(jnp.float32)
                + self.rzm[1].astype(jnp.float32)
            )

    def drain(self):
        for copy, cond in self.sends:
            pl.when(cond)(functools.partial(copy.wait_send))

    @staticmethod
    def scratch(width):
        low, dma = jnp.bfloat16, pltpu.SemaphoreType.DMA
        return [
            pltpu.VMEM((3, 128, width), low),
            pltpu.VMEM((3, 128, width), low),
            pltpu.VMEM((2, 128, width), low),
            pltpu.VMEM((128, width), low),
            dma((6,)),
            dma((6,)),
        ]


class AllGather:
    def __init__(self, held, own_ref, ssem, rsem, metas=None, own_meta=None, msem=None, mrsem=None):
        self.dp, self.z, self.dc, self.dx, self.dy = place()
        z = self.z
        self.zr, self.zo = z + 1 - 2 * (z % 2), 3 - z
        self.mid = z * (3 - z) > 0
        self.zs = [z, self.zr, 2 - z // 2, 3 - 3 * (z // 2)]
        self.held, self.own_ref, self.ssem, self.rsem = held, own_ref, ssem, rsem
        self.metas, self.own_meta, self.msem, self.mrsem = metas, own_meta, msem, mrsem
        self.sends = []

    def send(self, block, part, dp_to, z_to, cond=None, own=False):
        half = pl.ds(part * 64, 64)
        view = self.held.at[block, half]
        source = self.own_ref.at[half] if own else view
        index = len(self.sends)
        copies = [
            pltpu.make_async_remote_copy(
                source, view, self.ssem.at[index], self.rsem.at[block, part],
                device_id=at(dp_to, z_to), device_id_type=MESH,
            )
        ]
        if part == 0 and self.metas is not None:
            copies.append(
                pltpu.make_async_remote_copy(
                    self.own_meta if own else self.metas.at[block], self.metas.at[block],
                    self.msem.at[index], self.mrsem.at[block],
                    device_id=at(dp_to, z_to), device_id_type=MESH,
                )
            )
        self.sends.append((copies, cond))

        def go():
            for copy in copies:
                copy.start()

        when_or_now(cond, go)

    def arrive(self, block, part):
        view = self.held.at[block, pl.ds(part * 64, 64)]
        here = dict(device_id=at(self.dp, self.zr), device_id_type=MESH)
        pltpu.make_async_remote_copy(
            view, view, self.ssem.at[0], self.rsem.at[block, part], **here
        ).wait_recv()
        if part == 0 and self.metas is not None:
            pltpu.make_async_remote_copy(
                self.metas.at[block], self.metas.at[block], self.msem.at[0], self.mrsem.at[block],
                **here
            ).wait_recv()

    def first(self, k):
        dp, z, dx, dy, dc = self.dp, self.z, self.dx, self.dy, self.dc
        block = dp * 4 + self.zs[k]
        own = k == 0
        for part in (0, 1):
            if k > 0:
                self.arrive(block, part)
            if k == 0:
                self.send(block, part, dp, self.zr, None, own)
                self.send(block, part, dp, self.zo, self.mid, own)
            else:
                self.send(block, part, dp, self.zo if k == 1 else self.zr, self.mid)
            self.send(block, part, dp + (dx if part == 0 else dy), z, None, own)
        self.send(block, 1, dp + dx, z, None, own)
        self.send(block, 0, dp + dy, z, None, own)
        self.send(block, 0, dp + dc, z, None, own)
        self.send(block, 1, dp + dc, z, None, own)

    def second(self, k):
        dp, z, dx, dy, dc = self.dp, self.z, self.dx, self.dy, self.dc
        bx, by = (dp + dx) * 4 + self.zs[k], (dp + dy) * 4 + self.zs[k]
        self.arrive(bx, 0)
        self.send(bx, 0, dp + dy, z)
        self.send(bx, 0, dp + dc, z)
        self.arrive(by, 1)
        self.send(by, 1, dp + dx, z)
        self.send(by, 1, dp + dc, z)
        self.arrive(bx, 1)
        self.send(bx, 1, dp + dc, z)
        self.arrive(by, 0)
        self.send(by, 0, dp + dc, z)

    def third(self, k):
        block = (self.dp + self.dx + self.dy) * 4 + self.zs[k]
        for part in (0, 1):
            self.arrive(block, part)
            self.send(block, part, self.dp + self.dc, self.z)

    def across(self, k, step):
        block = (self.dp + self.dc + step) * 4 + self.zs[k]
        self.arrive(block, 0)
        self.arrive(block, 1)

    def drain(self):
        for copies, cond in self.sends:

            def done(copies=copies):
                for copy in copies:
                    copy.wait_send()

            when_or_now(cond, done)


class Dispatcher:
    def __init__(self, held, stage, spare, slots_ref, osem):
        self.held, self.stage, self.spare = held, stage, spare
        self.slots_ref, self.osem = slots_ref, osem
        self.count = 0

    def put(self, start, slot):
        return pltpu.make_async_copy(
            self.stage.at[slot], self.slots_ref.at[:, pl.ds(start, MAIN), :], self.osem.at[slot]
        )

    def block(self, block, onehot):
        slot, group = self.count % 2, block // 8
        width = self.held.shape[2]
        if self.count >= 2:
            self.put(block * MAIN, slot).wait()

        def tile(step, carry):
            lanes = pl.ds(pl.multiple_of(step * 1024, 1024), 1024)
            rows = jnp.dot(onehot, self.held[block, :, lanes], preferred_element_type=jnp.float32)
            self.stage[slot, :, :, lanes] = rows[:128].astype(jnp.bfloat16).reshape(8, MAIN, 1024)
            extra = rows[128:].astype(jnp.bfloat16)
            self.spare[group, :, lanes] = self.spare[group, :, lanes] + extra
            return carry

        lax.fori_loop(0, width // 1024, tile, 0)
        self.put(block * MAIN, slot).start()
        self.count += 1

    def end(self):
        width = self.held.shape[2]
        for group in range(4):
            slot = group % 2
            self.put(512 + group * MAIN, slot).wait()
            self.stage[slot] = self.spare[group].reshape(8, MAIN, width)
            self.put(512 + group * MAIN, slot).start()
        for slot in range(2):
            self.put(512, slot).wait()


def arrival_order(gather):
    dp, dc, dx, dy, zs = gather.dp, gather.dc, gather.dx, gather.dy, gather.zs
    order = []
    for k in range(6):
        column = []
        if k < 4:
            column.append((k, 0))
        if 1 <= k < 5:
            column += [(k - 1, dx), (k - 1, dy)]
        if k >= 2:
            column.append((k - 2, dx + dy))
        across = [(k - 1, dc)] if 1 <= k < 5 else []
        if k >= 2:
            across += [(k - 2, dc + step) for step in (dx, dy, dx + dy)]
        order.append([[(dp + to) * 4 + zs[j] for j, to in part] for part in (column, across)])
    return order


def gather_forward(gather, k):
    if k < 4:
        gather.first(k)
    if 1 <= k < 5:
        gather.second(k - 1)
    if k >= 2:
        gather.third(k - 2)


def gather_process(gather, order, k, process):
    for block in order[k][0]:
        process(block)
    for block in order[k][1]:
        gather.arrive(block, 0)
        gather.arrive(block, 1)
        process(block)


def rotate(values, cosines, sines):
    return values * cosines + pltpu.roll(values, HD // 2, 1) * sines


def head_probs(query, key, seq_column, seq_row):
    scores = lax.dot_general(
        query, key, (((1,), (1,)), ((), ())), preferred_element_type=jnp.float32
    ) * (HD ** (-0.5))
    scores = jnp.where(seq_column == seq_row, scores, NEGATIVE)
    raised = jnp.exp(scores - jnp.max(scores, axis=1, keepdims=True))
    return raised / jnp.sum(raised, axis=1, keepdims=True)


def head_gain(gains_ref, first):
    lane = lax.broadcasted_iota(jnp.int32, (8, 128), 1)
    keep = jnp.logical_and(lane >= first, lane < first + 16)
    total = jnp.zeros((8, 128), jnp.float32)
    for block in range(8):
        part = jnp.where(keep, jnp.broadcast_to(gains_ref[block, 4:5, :], (8, 128)), 0.0)
        shift = (16 * block - first) % 128
        total = total + (pltpu.roll(part, shift, 1) if shift else part)
    return total[:1]


def front_kernel(
    wq_ref, wk_ref, wv_ref, wo_ref, router_ref, tok_ref, cot_ref, routes_in, gains_in, cos_ref, sin_ref, seqc_ref, seqr_ref,
    weights_ref, group_ref, slots_ref, gains_ref, onehot_ref, routes_ref, normed_ref, projq_ref, projk_ref,
    query_ref, key_ref, value_ref, ctx_ref, out_ref,
    wheld, theld, gheld, held, metas, stage, spare, lsem, wsend, wrecv, gsend, grecv, zsend, zrecv,
    dsend, drecv, msend, mrecv, osem, fsem, *line_refs
):
    dp, z, dc, dx, dy = place()
    zr, zo = z + 1 - 2 * (z % 2), 3 - z
    mid = z * (3 - z) > 0
    f32, low = jnp.float32, jnp.bfloat16
    heads = query_ref.shape[1]
    width = tok_ref.shape[1]
    line = LineScatter(dp, z, *line_refs)
    gather = AllGather(held, cot_ref, dsend, drecv, metas, routes_in, msend, mrecv)
    order = arrival_order(gather)
    picker = Dispatcher(held, stage, spare, slots_ref, osem)
    own_block = dp * 4 + z
    own_rows = pl.ds(pl.multiple_of(dp * 256, 256), 256)
    fill = []
    for source, column, count in (
        (wq_ref, 0, heads), (wk_ref, heads, heads), (wv_ref, 2 * heads, heads),
        (wo_ref.at[pl.ds(0, 256)], 3 * heads, 256), (wo_ref.at[pl.ds(256, 256)], 3 * heads + 256, 256),
        (router_ref, 4 * heads, 128),
    ):
        target = wheld.at[own_rows, pl.ds(column, count)]
        fill.append(pltpu.make_async_copy(source, target, fsem.at[len(fill)]))
    for copy in fill:
        copy.start()
    greet([(dp + dc, z), (dp + dx, z), (dp + dy, z), (dp, zr)], (dp, zo), mid, z * (3 - z) // 2)
    sends = []

    def spot(block, part):
        return wheld.at[pl.ds(pl.multiple_of(block * 256 + part * 128, 128), 128)]

    def send(block, part, dp_to, own=False):
        source = spot(block, part)
        index = len(sends)
        copies = [
            pltpu.make_async_remote_copy(
                source, spot(block, part), wsend.at[index], wrecv.at[block, part],
                device_id=at(dp_to, z), device_id_type=MESH,
            )
        ]
        if part == 0:
            copies.append(
                pltpu.make_async_remote_copy(
                    gains_in if own else gheld.at[block], gheld.at[block],
                    gsend.at[index], grecv.at[block],
                    device_id=at(dp_to, z), device_id_type=MESH,
                )
            )
        for copy in copies:
            copy.start()
        sends.append(copies)

    def arrive(block, part):
        here = dict(device_id=at(dp + dx, z), device_id_type=MESH)
        pltpu.make_async_remote_copy(
            spot(block, part), spot(block, part), wsend.at[0], wrecv.at[block, part], **here
        ).wait_recv()
        if part == 0:
            pltpu.make_async_remote_copy(
                gheld.at[block], gheld.at[block], gsend.at[0], grecv.at[block], **here
            ).wait_recv()

    zsends = []

    def z_send(source, block, z_to, cond=None):
        copy = pltpu.make_async_remote_copy(
            source, theld.at[block], zsend.at[len(zsends)], zrecv.at[block],
            device_id=at(dp, z_to), device_id_type=MESH,
        )
        when_or_now(cond, functools.partial(copy.start))
        zsends.append((copy, cond))

    def z_arrive(block):
        pltpu.make_async_remote_copy(
            theld.at[block], theld.at[block], zsend.at[0], zrecv.at[block],
            device_id=at(dp, zr), device_id_type=MESH,
        ).wait_recv()

    z_send(tok_ref, z, zr)
    z_send(tok_ref, z, zo, mid)
    for copy in fill:
        copy.wait()
    send(dp, 0, dp + dx, True)
    send(dp, 1, dp + dy, True)
    send(dp, 1, dp + dx, True)
    send(dp, 0, dp + dy, True)
    send(dp, 0, dp + dc, True)
    send(dp, 1, dp + dc, True)
    local = [
        pltpu.make_async_copy(tok_ref, theld.at[z], lsem.at[1]),
        pltpu.make_async_copy(gains_in, gheld.at[dp], lsem.at[2]),
        pltpu.make_async_copy(cot_ref, held.at[own_block], lsem.at[3]),
        pltpu.make_async_copy(routes_in, metas.at[own_block], lsem.at[4]),
    ]
    for copy in local:
        copy.start()
    spare[...] = jnp.zeros_like(spare)
    z_arrive(zr)
    z_send(theld.at[zr], zr, zo, mid)
    bx, by, bxy = dp + dx, dp + dy, dp + dx + dy
    arrive(bx, 0)
    send(bx, 0, dp + dy)
    send(bx, 0, dp + dc)
    arrive(by, 1)
    send(by, 1, dp + dx)
    send(by, 1, dp + dc)
    gather.first(0)
    far = 2 - z // 2
    z_arrive(far)
    z_send(theld.at[far], far, zr, mid)
    arrive(bx, 1)
    send(bx, 1, dp + dc)
    arrive(by, 0)
    send(by, 0, dp + dc)
    last = 3 - 3 * (z // 2)
    z_arrive(last)
    z_send(theld.at[last], last, zr, mid)
    for part in (0, 1):
        arrive(bxy, part)
        send(bxy, part, dp + dc)
    for block in (dp, bx, by, bxy):
        for part in (0, 1):
            arrive(block + dc, part)
    for copy in local:
        copy.wait()
    kept = [
        pltpu.make_async_copy(wheld, weights_ref, lsem.at[0]),
        pltpu.make_async_copy(theld, group_ref, lsem.at[1]),
    ]
    for copy in kept:
        copy.start()

    def process(block):
        onehot = slot_matrix(metas[block], block, dp * 8)
        onehot_ref[block] = onehot
        picker.block(block, onehot)

    scale = jnp.concatenate(
        [gheld[j // 2, j % 2 : j % 2 + 1, :] for j in range(width // 128)], axis=1
    )

    def norm_rows(step, carry):
        values = theld[step].astype(f32)
        inverse = lax.rsqrt(jnp.mean(values * values, axis=1, keepdims=True) + EPSILON)
        rows = pl.ds(pl.multiple_of(step * 128, 128), 128)
        normed_ref[rows, :] = (values * inverse * scale).astype(low)
        return carry

    gains_ref[...] = gheld[...]
    lax.fori_loop(0, 4, norm_rows, 0)

    def project(column):
        cols = slice(column * heads, column * heads + heads)
        return jnp.dot(normed_ref[...], wheld[:, cols], preferred_element_type=f32)

    projq_ref[...] = project(0)
    projk_ref[...] = project(1)
    value_ref[...] = project(2).astype(low)
    gather_forward(gather, 1)
    cosines, sines = cos_ref[...], sin_ref[...]
    query_gain, key_gain = head_gain(gheld, 0), head_gain(gheld, 16)

    def one_head(h, carry):
        cols = pl.ds(pl.multiple_of(h * HD, HD), HD)
        for source, gain, target in (
            (projq_ref, query_gain, query_ref), (projk_ref, key_gain, key_ref),
        ):
            values = source[:, cols]
            inverse = lax.rsqrt(jnp.mean(values * values, axis=1, keepdims=True) + EPSILON)
            target[:, cols] = rotate(values * inverse * gain, cosines, sines).astype(low)
        for start in range(0, 512, 256):
            rows = slice(start, start + 256)
            probs = head_probs(
                query_ref[rows, cols], key_ref[:, cols], seqc_ref[rows, :1], seqr_ref[:1, :]
            )
            ctx_ref[rows, cols] = jnp.dot(
                probs.astype(low), value_ref[:, cols], preferred_element_type=f32
            ).astype(low)
        return carry

    lax.fori_loop(0, heads // HD // 2, one_head, 0)
    gather_forward(gather, 2)
    lax.fori_loop(heads // HD // 2, heads // HD, one_head, 0)
    for k in range(4):
        rows = pl.ds(pl.multiple_of(line.zs[k] * 128, 128), 128)
        for start in range(0, width, 256):
            lanes = slice(start, start + 256)
            piece = jnp.dot(
                ctx_ref[rows, :256], wheld[lanes, 3 * heads : 3 * heads + 256],
                preferred_element_type=f32,
            ) + jnp.dot(
                ctx_ref[rows, 256:], wheld[lanes, 3 * heads + 256 : 4 * heads],
                preferred_element_type=f32,
            )
            if k < 3:
                line.blocks[k, :, lanes] = piece.astype(low)
            else:
                out_ref[:, lanes] = piece
        if k < 3:
            line.ready(k)
    gather.first(3)
    process(own_block)
    gather_process(gather, order, 1, process)
    gather.second(2)
    gather.third(1)
    line.onward(0)
    gather_process(gather, order, 2, process)
    line.onward(1)
    gather_process(gather, order, 3, process)
    gather_forward(gather, 4)
    line.onward(2)
    gather_process(gather, order, 4, process)
    gather_forward(gather, 5)
    line.last(out_ref)
    gather_process(gather, order, 5, process)
    picker.end()
    routes_ref[...] = metas[...]
    for copy in kept:
        copy.wait()
    for copies in sends:
        for copy in copies:
            copy.wait_send()
    for copy, cond in zsends:
        when_or_now(cond, functools.partial(copy.wait_send))
    gather.drain()
    line.drain()


def front(shards, tokens, cotangent, routes, gains, cosines, sines, seq_column, seq_row, heads):
    width = tokens.shape[1]
    rows = 4 * tokens.shape[0]
    f32, low = jnp.float32, jnp.bfloat16
    anywhere = pl.BlockSpec(memory_space=pl.ANY)
    vmem = pl.BlockSpec(memory_space=pltpu.VMEM)
    dma = pltpu.SemaphoreType.DMA
    narrow = jax.ShapeDtypeStruct((rows, heads), low)
    return pl.pallas_call(
        front_kernel,
        name="front",
        out_shape=(
            jax.ShapeDtypeStruct((width, 4 * heads + 128), low),
            jax.ShapeDtypeStruct((4, 128, width), low),
            jax.ShapeDtypeStruct((8, 576, width), low),
            jax.ShapeDtypeStruct((8, 8, 128), f32),
            jax.ShapeDtypeStruct((32, 256, 128), low),
            jax.ShapeDtypeStruct((32, 8, 128), f32),
            jax.ShapeDtypeStruct((rows, width), low),
            jax.ShapeDtypeStruct((rows, heads), f32),
            jax.ShapeDtypeStruct((rows, heads), f32),
            narrow, narrow, narrow, narrow,
            jax.ShapeDtypeStruct((128, width), f32),
        ),
        in_specs=[anywhere] * 5 + [vmem] * 8,
        out_specs=(anywhere,) * 3 + (vmem,) * 11,
        scratch_shapes=[
            pltpu.VMEM((width, 4 * heads + 128), low),
            pltpu.VMEM((4, 128, width), low),
            pltpu.VMEM((8, 8, 128), f32),
            pltpu.VMEM((32, 128, width), low),
            pltpu.VMEM((32, 8, 128), f32),
            pltpu.VMEM((2, 8, MAIN, width), low),
            pltpu.VMEM((4, 128, width), low),
            dma((9,)), dma((14,)), dma((8, 2)), dma((14,)), dma((8,)), dma((5,)), dma((4,)),
            dma((72,)), dma((32, 2)), dma((72,)), dma((32,)), dma((2,)), dma((6,)),
        ]
        + LineScatter.scratch(width),
        compiler_params=pltpu.CompilerParams(
            collective_id=0, has_side_effects=True, vmem_limit_bytes=VMEM_LIMIT
        ),
        cost_estimate=pl.CostEstimate(
            flops=5_000_000_000, bytes_accessed=100_000_000, transcendentals=2_000_000
        ),
    )(*shards, tokens, cotangent, routes, gains, cosines, sines, seq_column, seq_row)


def gather_kernel(
    x_ref, meta_ref, onehot_ref, routes_ref, slots_ref, gate_ref,
    held, metas, stage, spare, lsem, ssem, rsem, msem, mrsem, osem,
):
    dp, z, dc, dx, dy = place()
    own = dp * 4 + z
    gather = AllGather(held, held.at[own], ssem, rsem, metas, metas.at[own], msem, mrsem)
    order = arrival_order(gather)
    picker = Dispatcher(held, stage, spare, slots_ref, osem)
    local = [
        pltpu.make_async_copy(x_ref, held.at[own], lsem.at[0]),
        pltpu.make_async_copy(meta_ref, metas.at[own], lsem.at[1]),
    ]
    for copy in local:
        copy.start()
    greet(
        [(dp + dc, z), (dp + dx, z), (dp + dy, z), (dp, gather.zr)],
        (dp, gather.zo), gather.mid, z * (3 - z) // 2,
    )
    spare[...] = jnp.zeros_like(spare)
    gate_ref[:, 512:576, :] = jnp.zeros((8, 64, 128), jnp.float32)
    for copy in local:
        copy.wait()
    experts = (lax.broadcasted_iota(jnp.int32, (8, 128), 0) + dp * 8).astype(jnp.float32)

    def process(block):
        onehot = onehot_ref[block]
        gates_here = jnp.zeros((8, 128), jnp.float32)
        for j in range(TOPK):
            gates_here = gates_here + jnp.where(
                routes_ref[block, j : j + 1, :] == experts, metas[block, j : j + 1, :], 0.0
            )
        wide = jnp.broadcast_to(gates_here[:, None, :], (8, MAIN, 128)).reshape(128, 128)
        taken = onehot.astype(jnp.float32)
        main_gate = jnp.sum(taken[:128] * wide, axis=1, keepdims=True)
        spare_gate = jnp.sum(taken[128:] * wide, axis=1, keepdims=True)
        gate_ref[:, pl.ds(pl.multiple_of(block * MAIN, MAIN), MAIN), :] = jnp.broadcast_to(
            main_gate, (128, 128)
        ).reshape(8, MAIN, 128)
        spare_rows = pl.ds(pl.multiple_of(512 + (block // 8) * MAIN, MAIN), MAIN)
        gate_ref[:, spare_rows, :] = gate_ref[:, spare_rows, :] + jnp.broadcast_to(
            spare_gate, (128, 128)
        ).reshape(8, MAIN, 128)
        picker.block(block, onehot)

    for k in range(6):
        gather_forward(gather, k)
        gather_process(gather, order, k, process)
    picker.end()
    gather.drain()


def gather_slots(rows, meta, onehot, routes):
    count, width = rows.shape
    anywhere = pl.BlockSpec(memory_space=pl.ANY)
    vmem = pl.BlockSpec(memory_space=pltpu.VMEM)
    dma = pltpu.SemaphoreType.DMA
    return pl.pallas_call(
        gather_kernel,
        name="gather_x",
        out_shape=(
            jax.ShapeDtypeStruct((8, 576, width), jnp.bfloat16),
            jax.ShapeDtypeStruct((8, 576, 128), jnp.float32),
        ),
        in_specs=[anywhere, anywhere, vmem, vmem],
        out_specs=(anywhere, vmem),
        scratch_shapes=[
            pltpu.VMEM((32, count, width), jnp.bfloat16),
            pltpu.VMEM((32, 8, 128), jnp.float32),
            pltpu.VMEM((2, 8, MAIN, width), jnp.bfloat16),
            pltpu.VMEM((4, 128, width), jnp.bfloat16),
            dma((2,)), dma((72,)), dma((32, 2)), dma((72,)), dma((32,)), dma((2,)),
        ],
        compiler_params=pltpu.CompilerParams(
            collective_id=1, has_side_effects=True, vmem_limit_bytes=VMEM_LIMIT
        ),
        cost_estimate=pl.CostEstimate(
            flops=4_300_000_000, bytes_accessed=100_000_000, transcendentals=0
        ),
    )(rows, meta, onehot, routes)


def return_kernel(
    y_ref, g_ref, onehot_ref, outy_ref, outg_ref,
    rows_in, to_core, sums, ry0, rx1, rx0, ry1, rze, rzm, rzf,
    ysem, csend, crecv, xsend, xrecv, zsend, zrecv,
):
    dp, z, dc, dx, dy = place()
    zr, zo = z + 1 - 2 * (z % 2), 3 - z
    mid = z * (3 - z) > 0
    end = z * (3 - z) < 1
    half = 64
    sources, outs = (y_ref, g_ref), (outy_ref, outg_ref)
    zs = [3 - 3 * (z // 2), 2 - z // 2, zr, z]
    greet([(dp + dc, z), (dp + dx, z), (dp + dy, z), (dp, zr)], (dp, zo), mid, z * (3 - z) // 2)
    lo, hi = pl.ds(0, half), pl.ds(half, half)
    xsends, zsends = [[] for _ in range(8)], []

    def lanes_of(s):
        return pl.ds(0, sources[s // 4].shape[2])

    def tiles_of(s):
        width = sources[s // 4].shape[2]
        return [slice(i, min(i + 512, width)) for i in range(0, width, 512)]

    def dest(s, step):
        r = 3 - step % 4
        base = dp + dc - dc * (step // 4)
        return (base + (r % 2) * dx + (r // 2) * dy) * 4 + zs[s % 4]

    def fetch(s, block, slot):
        source, lanes = sources[s // 4], lanes_of(s)
        return [
            pltpu.make_async_copy(
                source.at[:, pl.ds(block * MAIN, MAIN), :],
                rows_in.at[slot, pl.ds(0, 8), :, lanes], ysem.at[slot, 0],
            ),
            pltpu.make_async_copy(
                source.at[:, pl.ds(512 + (block // 8) * MAIN, MAIN), :],
                rows_in.at[slot, pl.ds(8, 8), :, lanes], ysem.at[slot, 1],
            ),
        ]

    def partial_tile(block, slot, lanes):
        return lax.dot_general(
            onehot_ref[block], rows_in[slot, :, :, lanes].reshape(256, lanes.stop - lanes.start),
            (((0,), (0,)), ((), ())), preferred_element_type=jnp.float32,
        )

    def core_copy(r, s):
        lanes = lanes_of(s)
        return pltpu.make_async_remote_copy(
            to_core.at[s % 4, r, :, lanes], sums.at[s, r, :, lanes], csend.at[s, r], crecv.at[s, r],
            device_id=at(dp + dc, z), device_id_type=MESH,
        )

    def xy_copy(r, rows, target, index, s, dp_to):
        lanes = lanes_of(s)
        return pltpu.make_async_remote_copy(
            sums.at[s, r, rows, lanes], target.at[:, lanes], xsend.at[index, s], xrecv.at[index, s],
            device_id=at(dp_to, z), device_id_type=MESH,
        )

    def z_copy(s, target, index, z_to):
        lanes = lanes_of(s)
        index = 6 * (s // 4) + index
        return pltpu.make_async_remote_copy(
            sums.at[s, 0, :, lanes], target.at[:, lanes], zsend.at[index], zrecv.at[index],
            device_id=at(dp, z_to), device_id_type=MESH,
        )

    def add_to(s, r, rows, *others):
        lanes = lanes_of(s)
        total = sums[s, r, rows, lanes].astype(jnp.float32)
        for other in others:
            total = total + other[:, lanes].astype(jnp.float32)
        sums[s, r, rows, lanes] = total.astype(jnp.bfloat16)

    def stage_core(s):
        def load(block, slot, following=None):
            for copy in fetch(s, block, slot):
                copy.wait()
            if following is not None:
                for copy in fetch(s, following, 1 - slot):
                    copy.start()

        def partner(step, slot, following):
            r = 3 - step
            block = dest(s, step)
            load(block, slot, following)
            if s >= 4:
                core_copy(r, s - 4).wait_send()
            for lanes in tiles_of(s):
                to_core[s % 4, r, :, lanes] = partial_tile(block, slot, lanes).astype(jnp.bfloat16)
            core_copy(r, s).start()

        batch = [
            xy_copy(3, lo, ry0.at[1, s], 0, s, dp + dy),
            xy_copy(3, hi, rx1.at[1, s], 1, s, dp + dx),
            xy_copy(2, lo, ry0.at[0, s], 2, s, dp + dy),
            xy_copy(1, hi, rx1.at[0, s], 3, s, dp + dx),
        ]
        xsends[s].extend(batch)

        def both(i, carry):
            r = 3 - i
            block = dest(s, 4 + i)

            @pl.when(i < 3)
            def _():
                partner(i + 1, 1, block)

            late = i // 2
            following = (1 - late) * dest(s, i + 2) + late * dest(s, 5 + i)
            slot = i // 3
            load(block, slot)

            @pl.when(i < 3)
            def _():
                for copy in fetch(s, following, 1):
                    copy.start()

            if s < 7:

                @pl.when(i == 3)
                def _():
                    for copy in fetch(s + 1, dest(s + 1, 0), 0):
                        copy.start()

            core_copy(r, s).wait_recv()
            for lanes in tiles_of(s):
                sums[s, r, :, lanes] = (
                    partial_tile(block, slot, lanes) + sums[s, r, :, lanes].astype(jnp.float32)
                ).astype(jnp.bfloat16)
            for when, copies in enumerate((batch[:2], batch[2:3], batch[3:])):

                @pl.when(i == when)
                def _():
                    for copy in copies:
                        copy.start()

            return carry

        partner(0, 0, dest(s, 1))
        lax.fori_loop(0, 4, both, 0)

    def stage_cross(s):
        xsends[s][0].wait_recv()
        add_to(s, 1, lo, ry0.at[1, s])
        across = xy_copy(1, lo, rx0.at[s], 4, s, dp + dx)
        across.start()
        xsends[s][1].wait_recv()
        add_to(s, 2, hi, rx1.at[1, s])
        down = xy_copy(2, hi, ry1.at[s], 5, s, dp + dy)
        down.start()
        xsends[s].extend([across, down])

    def outward(s):
        return z_copy(s, rze.at[3 * (s // 4) + s % 4], s % 4, zr)

    def stage_line(s):
        for j in range(2, 6):
            xsends[s][j].wait_recv()
        if s % 4 < 3:
            add_to(s, 0, lo, ry0.at[0, s], rx0.at[s])
            add_to(s, 0, hi, rx1.at[0, s], ry1.at[s])
            copy = outward(s)
            zsends.append((copy, end))
            pl.when(end)(functools.partial(copy.start))
        else:
            out_ref, lanes = outs[s // 4], lanes_of(s)
            for rows, first, second in ((lo, ry0.at[0, s], rx0.at[s]), (hi, rx1.at[0, s], ry1.at[s])):
                out_ref[rows, :] = (
                    sums[s, 0, rows, lanes].astype(jnp.float32)
                    + first[:, lanes].astype(jnp.float32)
                    + second[:, lanes].astype(jnp.float32)
                )

    def stage_onward(s):
        p, k = s // 4, s % 4
        if k < 2:
            onward = z_copy(s, rzm.at[2 * p + k], 3 + k, zo)
        else:
            onward = z_copy(s, rzf.at[p], 5, zr)
        zsends.append((onward, mid))

        @pl.when(mid)
        def _():
            if k < 2:
                outward(s).wait_recv()
                add_to(s, 0, slice(None), rze.at[3 * p + k])
            else:
                z_copy(4 * p, rzm.at[2 * p], 3, zo).wait_recv()
                add_to(s, 0, slice(None), rzm.at[2 * p])
            onward.start()

    def stage_last(p):
        out_ref, lanes = outs[p], lanes_of(4 * p)

        @pl.when(end)
        def _():
            z_copy(4 * p + 2, rzf.at[p], 5, zr).wait_recv()
            out_ref[...] = out_ref[...] + rzf[p, :, lanes].astype(jnp.float32)

        @pl.when(mid)
        def _():
            outward(4 * p + 2).wait_recv()
            z_copy(4 * p + 1, rzm.at[2 * p + 1], 4, zo).wait_recv()
            out_ref[...] = (
                out_ref[...]
                + rze[3 * p + 2, :, lanes].astype(jnp.float32)
                + rzm[2 * p + 1, :, lanes].astype(jnp.float32)
            )

    for copy in fetch(0, dest(0, 0), 0):
        copy.start()
    for t in range(10):
        if t < 8:
            stage_core(t)
        if 1 <= t < 9:
            stage_cross(t - 1)
        if t >= 2:
            stage_line(t - 2)
        if t % 4 == 3:
            stage_onward(t - 3)
        if t >= 4 and t % 4 == 0:
            stage_onward(t - 2)
            stage_onward(t - 3)
        if t >= 5 and t % 4 == 1:
            stage_last(t // 4 - 1)
    for s in range(4, 8):
        for r in range(4):
            core_copy(r, s).wait_send()
    for batch in xsends:
        for copy in batch:
            copy.wait_send()
    for copy, cond in zsends:
        pl.when(cond)(functools.partial(copy.wait_send))


def return_rows(y_slots, gin_slots, onehot):
    width, narrow = y_slots.shape[2], gin_slots.shape[2]
    anywhere = pl.BlockSpec(memory_space=pl.ANY)
    vmem = pl.BlockSpec(memory_space=pltpu.VMEM)
    dma = pltpu.SemaphoreType.DMA
    low = jnp.bfloat16
    return pl.pallas_call(
        return_kernel,
        name="return_rows",
        out_shape=(
            jax.ShapeDtypeStruct((128, width), jnp.float32),
            jax.ShapeDtypeStruct((128, narrow), jnp.float32),
        ),
        in_specs=[anywhere, anywhere, vmem],
        out_specs=(vmem, vmem),
        scratch_shapes=[
            pltpu.VMEM((2, 16, MAIN, width), low),
            pltpu.VMEM((4, 4, 128, width), low),
            pltpu.VMEM((8, 4, 128, width), low),
            pltpu.VMEM((2, 8, 64, width), low),
            pltpu.VMEM((2, 8, 64, width), low),
            pltpu.VMEM((8, 64, width), low),
            pltpu.VMEM((8, 64, width), low),
            pltpu.VMEM((6, 128, width), low),
            pltpu.VMEM((4, 128, width), low),
            pltpu.VMEM((2, 128, width), low),
            dma((2, 2)), dma((8, 4)), dma((8, 4)), dma((6, 8)), dma((6, 8)), dma((12,)), dma((12,)),
        ],
        compiler_params=pltpu.CompilerParams(
            collective_id=2, has_side_effects=True, vmem_limit_bytes=VMEM_LIMIT
        ),
        cost_estimate=pl.CostEstimate(
            flops=8_600_000_000, bytes_accessed=300_000_000, transcendentals=0
        ),
    )(y_slots, gin_slots, onehot)


def finish_kernel(
    rows_ref, tok_ref, projq_ref, projk_ref, query_ref, key_ref, value_ref, ctx_ref, ga_ref, w_ref,
    gains_ref, cos_ref, sin_ref, seqc_ref, seqr_ref, side_ref, stat_ref,
    gw_ref, gwo_ref, back_ref, small_ref,
    dx_ref, gqkv_ref, gctx_ref, dx_all, to_core, from_core, sums, ry0, rx1, rx0, ry1, gain, zside,
    csend, crecv, xsend, xrecv, ssend, srecv, *line_refs,
):
    dp, z, dc, dx, dy = place()
    line = LineScatter(dp, z, *line_refs)
    dxs = line.blocks
    f32, low = jnp.float32, jnp.bfloat16
    half = 128
    heads = query_ref.shape[1]
    width = rows_ref.shape[1]
    others = [(z + i) % 4 for i in (1, 2, 3)]
    greet([(dp + dc, z), (dp + dx, z), (dp + dy, z)] + [(dp, other) for other in others])
    nt = (((1,), (1,)), ((), ()))
    tn = (((0,), (0,)), ((), ()))
    lo, hi = pl.ds(0, half), pl.ds(half, half)
    early = 3 * heads + 128

    def mm(a, b, dims):
        return lax.dot_general(a, b, dims, preferred_element_type=f32)

    def dest(step):
        r = 3 - step % 4
        base = dp + dc - dc * (step // 4)
        return base + (r % 2) * dx + (r // 2) * dy

    def scatter(index, first, count, pieces):
        lanes = pl.ds(first, count)

        def core_copy(r):
            return pltpu.make_async_remote_copy(
                to_core.at[r, :, lanes], from_core.at[r, :, lanes],
                csend.at[index, r], crecv.at[index, r],
                device_id=at(dp + dc, z), device_id_type=MESH,
            )

        def xy_copy(r, rows, target, j, dp_to):
            return pltpu.make_async_remote_copy(
                sums.at[r, rows, lanes], target.at[:, lanes], xsend.at[index, j], xrecv.at[index, j],
                device_id=at(dp_to, z), device_id_type=MESH,
            )

        def add_to(r, rows, part):
            total = sums[r, rows, lanes].astype(f32) + part[:, lanes].astype(f32)
            sums[r, rows, lanes] = total.astype(low)

        copies = [
            xy_copy(3, lo, ry0.at[1], 0, dp + dy),
            xy_copy(3, hi, rx1.at[1], 1, dp + dx),
            xy_copy(2, lo, ry0.at[0], 2, dp + dy),
            xy_copy(1, hi, rx1.at[0], 3, dp + dx),
            xy_copy(1, lo, rx0, 4, dp + dx),
            xy_copy(2, hi, ry1, 5, dp + dy),
        ]

        def partner(step):
            r = 3 - step
            for part, value in pieces(dest(step)):
                to_core[r, :, part] = value.astype(low)
            core_copy(r).start()

        def both(i, carry):
            @pl.when(i < 3)
            def _():
                partner(i + 1)

            r = 3 - i
            core_copy(r).wait_recv()
            for part, value in pieces(dest(4 + i)):
                sums[r, :, part] = (value + from_core[r, :, part].astype(f32)).astype(low)
            for when, batch in enumerate((copies[:2], copies[2:3], copies[3:4])):

                @pl.when(i == when)
                def _():
                    for copy in batch:
                        copy.start()

            return carry

        def core():
            partner(0)
            lax.fori_loop(0, 4, both, 0)

        def cross():
            copies[0].wait_recv()
            add_to(1, lo, ry0.at[1])
            copies[4].start()
            copies[1].wait_recv()
            add_to(2, hi, rx1.at[1])
            copies[5].start()

        def wait():
            for copy in copies[2:]:
                copy.wait_recv()

        def drain():
            for r in range(4):
                core_copy(r).wait_send()
            for copy in copies:
                copy.wait_send()

        return core, cross, wait, drain

    def out_pieces(to):
        cols = pl.ds(pl.multiple_of(to * 256, 256), 256)
        out = mm(ctx_ref[...], ga_ref[:, cols], tn)
        yield slice(early, early + 256), out[:256]
        yield slice(early + 256, early + 512), out[256:]

    def head_pieces(to):
        cols = pl.ds(pl.multiple_of(to * 256, 256), 256)
        yield slice(0, 3 * heads), mm(rows_ref[:, cols], gqkv_ref[...], tn)
        yield slice(3 * heads, early), jnp.concatenate(
            [
                side_ref[to, :128, :].astype(f32),
                side_ref[to, 128:144, :].astype(f32) + gain[to],
                jnp.zeros((112, 128), f32),
            ],
            axis=0,
        )

    core_out, cross_out, wait_out, drain_out = scatter(0, early, heads, out_pieces)
    core_heads, cross_heads, wait_heads, drain_heads = scatter(1, 0, early, head_pieces)
    core_out()
    gain[...] = jnp.zeros_like(gain)
    cosines, sines = cos_ref[...], sin_ref[...]
    query_gain, key_gain = head_gain(gains_ref, 0), head_gain(gains_ref, 16)
    for i in range(2):
        column = 3 * heads + i * 256
        total_ctx = jnp.zeros((512, 256), f32)
        for start in range(0, width, 256):
            lanes = slice(start, start + 256)
            total_ctx = total_ctx + mm(ga_ref[:, lanes], w_ref[lanes, column : column + 256], nt)
        gctx_ref[:, i * 256 : i * 256 + 256] = total_ctx.astype(low)
    score_scale = HD ** (-0.5)

    def head_back(grad, source, rows, cols, gain_values, column):
        values = source[rows, cols]
        inverse = lax.rsqrt(jnp.mean(values * values, axis=1, keepdims=True) + EPSILON)
        turned = grad * cosines[rows] - pltpu.roll(grad, HD // 2, 1) * sines[rows]
        scaled = turned * gain_values
        inner = jnp.mean(scaled * values, axis=1, keepdims=True)
        target = pl.ds(pl.multiple_of(cols.start + column, HD), HD)
        gqkv_ref[rows, target] = ((scaled - values * inner * inverse * inverse) * inverse).astype(low)
        return jnp.sum(turned * values * inverse, axis=0, keepdims=True)

    def one_head(h, carry):
        query_part, key_part = carry
        cols = pl.ds(pl.multiple_of(h * HD, HD), HD)
        key, value = key_ref[:, cols], value_ref[:, cols]
        grad_key = jnp.zeros((key.shape[0], HD), f32)
        grad_value = jnp.zeros((key.shape[0], HD), f32)
        for start in range(0, 512, 256):
            rows = slice(start, start + 256)
            query, grad_ctx = query_ref[rows, cols], gctx_ref[rows, cols]
            probs = head_probs(query, key, seqc_ref[rows, :1], seqr_ref[:1, :])
            grad_value = grad_value + mm(probs.astype(low), grad_ctx, tn)
            grad_probs = mm(grad_ctx, value, nt)
            inner = jnp.sum(probs * grad_probs, axis=1, keepdims=True)
            grad_scores = (probs * (grad_probs - inner)).astype(low)
            grad_query = jnp.dot(grad_scores, key, preferred_element_type=f32) * score_scale
            grad_key = grad_key + mm(grad_scores, query, tn)
            query_part = query_part + head_back(
                grad_query, projq_ref, rows, cols, query_gain, 0
            )
        key_part = key_part + head_back(
            grad_key * score_scale, projk_ref, slice(0, 512), cols, key_gain, heads
        )
        target = pl.ds(pl.multiple_of(cols.start + 2 * heads, HD), HD)
        gqkv_ref[:, target] = grad_value.astype(low)
        return query_part, key_part

    zero_row = jnp.zeros((1, HD), f32)
    query_part, key_part = lax.fori_loop(0, heads // HD, one_head, (zero_row, zero_row))
    for to in range(8):
        gain[to, 4:5, :] = query_part
        gain[to, 5:6, :] = key_part
    cross_out()
    for start in range(0, width, 512):
        lanes = slice(start, start + 512)
        dx_all[:, lanes] = mm(gqkv_ref[...], w_ref[lanes, : 3 * heads], nt)
    for k in range(4):
        rows = pl.ds(pl.multiple_of(line.zs[k] * 128, 128), 128)
        square = jnp.zeros((128, 1), f32)
        for start in range(0, width, 512):
            values = tok_ref[rows, start : start + 512].astype(f32)
            square = square + jnp.sum(values * values, axis=1, keepdims=True)
        inverse = lax.rsqrt(square * (1.0 / width) + EPSILON)
        for start in range(0, width, 512):
            lanes = slice(start, start + 512)
            piece = dx_all[rows, lanes]
            scaled = tok_ref[rows, lanes].astype(f32) * inverse
            column = jnp.sum(piece * scaled, axis=0, keepdims=True)
            for j in range(4):
                to = start // 256 + j // 2
                row = slice(j % 2, j % 2 + 1)
                gain[to, row, :] = gain[to, row, :] + column[:, j * 128 : j * 128 + 128]
            if k < 3:
                dxs[k, :, lanes] = piece.astype(low)
            else:
                dx_ref[:, lanes] = piece
        if k < 3:
            line.ready(k)

    core_heads()
    line.onward(0)
    cross_heads()
    line.onward(1)
    line.onward(2)
    wait_out()
    wait_heads()

    def side_copy(i, source):
        return pltpu.make_async_remote_copy(
            zside.at[source], zside.at[source], ssend.at[i], srecv.at[source],
            device_id=at(dp, others[i]), device_id_type=MESH,
        )

    def total(part, lanes, first, second):
        return (
            sums[0, part, lanes].astype(f32)
            + first[:, lanes].astype(f32)
            + second[:, lanes].astype(f32)
        )

    sides = slice(3 * heads, early)
    zside[z, :128, :] = total(lo, sides, ry0.at[0], rx0)
    zside[z, 128:144, :] = total(hi, sides, rx1.at[0], ry1)[:16] + stat_ref[...]
    for i in range(3):
        side_copy(i, z).start()
    for rows, first, second in ((lo, ry0.at[0], rx0), (hi, rx1.at[0], ry1)):
        gw_ref[rows, :] = total(rows, slice(0, 3 * heads), first, second)
        gwo_ref[rows, :] = total(rows, slice(early, early + 256), first, second)
        below = pl.ds(256 + rows.start, half)
        gwo_ref[below, :] = total(rows, slice(early + 256, early + 512), first, second)

    line.last(dx_ref)
    scale = jnp.concatenate(
        [gains_ref[j // 2, j % 2 : j % 2 + 1, :] for j in range(width // 128)], axis=1
    )

    def norm_back(index, carry):
        rows = pl.ds(pl.multiple_of(index * 32, 32), 32)
        values = tok_ref[pl.ds(pl.multiple_of(z * 128 + index * 32, 32), 32), :].astype(f32)
        inverse = lax.rsqrt(jnp.mean(values * values, axis=1, keepdims=True) + EPSILON)
        scaled = dx_ref[rows, :] * scale
        inner = jnp.mean(scaled * values, axis=1, keepdims=True)
        back_ref[rows, :] = (scaled - values * (inner * inverse * inverse)) * inverse
        return carry

    lax.fori_loop(0, 4, norm_back, 0)
    for i in range(3):
        side_copy(i, others[i]).wait_recv()
    small_ref[...] = (zside[0] + zside[1]) + (zside[2] + zside[3])
    drain_out()
    drain_heads()
    line.drain()
    for i in range(3):
        side_copy(i, z).wait_send()


def finish(rows, tok, attention, grad_attn, weights, tables, side, stats):
    width = rows.shape[1]
    heads = attention[0].shape[1]
    f32, low = jnp.float32, jnp.bfloat16
    vmem = pl.BlockSpec(memory_space=pltpu.VMEM)
    dma = pltpu.SemaphoreType.DMA
    packed = 4 * heads + 128
    return pl.pallas_call(
        finish_kernel,
        name="finish",
        out_shape=(
            jax.ShapeDtypeStruct((256, 3 * heads), f32),
            jax.ShapeDtypeStruct((heads, 256), f32),
            jax.ShapeDtypeStruct((128, width), f32),
            jax.ShapeDtypeStruct((144, 128), f32),
        ),
        in_specs=[vmem] * 17,
        out_specs=(vmem,) * 4,
        scratch_shapes=[
            pltpu.VMEM((128, width), f32),
            pltpu.VMEM((512, 3 * heads), low),
            pltpu.VMEM((512, heads), low),
            pltpu.VMEM((512, width), f32),
        ]
        + [
            pltpu.VMEM((4, 256, packed), low),
            pltpu.VMEM((4, 256, packed), low),
            pltpu.VMEM((4, 256, packed), low),
            pltpu.VMEM((2, 128, packed), low),
            pltpu.VMEM((2, 128, packed), low),
            pltpu.VMEM((128, packed), low),
            pltpu.VMEM((128, packed), low),
            pltpu.VMEM((8, 16, 128), f32),
            pltpu.VMEM((4, 144, 128), f32),
            dma((2, 4)), dma((2, 4)), dma((2, 6)), dma((2, 6)), dma((3,)), dma((4,)),
        ]
        + LineScatter.scratch(width),
        compiler_params=pltpu.CompilerParams(
            collective_id=4, has_side_effects=True, vmem_limit_bytes=VMEM_LIMIT
        ),
        cost_estimate=pl.CostEstimate(
            flops=8_000_000_000, bytes_accessed=100_000_000, transcendentals=0
        ),
    )(rows, tok, *attention, grad_attn, weights, *tables, side, stats)


def expert_kernel(
    x_ref, dy_ref, gate_ref, wg_ref, wu_ref, wd_ref, y_ref, gin_ref, dgate_ref, dup_ref, hgated_ref,
    gate_pre_ref, up_pre_ref, raw_ref,
):
    rows, ff = dgate_ref.shape[1:]
    width = x_ref.shape[2]
    expert = lax.axis_index("dp") * 8 + pl.program_id(0)
    nt = (((1,), (1,)), ((), ()))

    def mm(a, b, dims):
        return lax.dot_general(a, b, dims, preferred_element_type=jnp.float32)

    gate_pre_ref[...] = jnp.dot(x_ref[0], wg_ref[0], preferred_element_type=jnp.float32)
    up_pre_ref[...] = jnp.dot(x_ref[0], wu_ref[0], preferred_element_type=jnp.float32)
    raw_ref[...] = mm(dy_ref[0], wd_ref[0], nt)
    step = 96

    def pointwise(index, carry):
        part = pl.ds(pl.multiple_of(index * step, step), step)
        gate_pre, up_pre, raw = gate_pre_ref[part, :], up_pre_ref[part, :], raw_ref[part, :]
        weight = jnp.concatenate([gate_ref[0, part, :]] * (ff // 128), axis=1)
        sig = jax.nn.sigmoid(gate_pre)
        silu = gate_pre * sig
        hidden = silu * up_pre
        route_grad = jnp.sum(hidden * raw, axis=1, keepdims=True)
        grad_hidden = weight * raw
        lane = lax.broadcasted_iota(jnp.int32, (step, 128), 1)
        high = route_grad.astype(jnp.bfloat16).astype(jnp.float32)
        extra = jnp.where(lane == expert, high, 0.0) + jnp.where(
            lane == expert + 64, route_grad - high, 0.0
        )
        hgated_ref[0, part, :] = (weight * hidden).astype(jnp.bfloat16)
        dgate_ref[0, part, :] = (
            grad_hidden * up_pre * sig * (1.0 + gate_pre * (1.0 - sig))
        ).astype(jnp.bfloat16)
        dup_ref[0, part, :] = (grad_hidden * silu).astype(jnp.bfloat16)
        y_ref[0, part, width:] = extra.astype(jnp.bfloat16)
        return carry

    lax.fori_loop(0, rows // step, pointwise, 0)
    for start in range(0, width, 512):
        lanes = slice(start, start + 512)
        y_ref[0, :, lanes] = jnp.dot(
            hgated_ref[0], wd_ref[0, :, lanes], preferred_element_type=jnp.float32
        ).astype(jnp.bfloat16)
        gin_ref[0, :, lanes] = (
            mm(dgate_ref[0], wg_ref[0, lanes, :], nt) + mm(dup_ref[0], wu_ref[0, lanes, :], nt)
        ).astype(jnp.bfloat16)


def weights_kernel(x_ref, dy_ref, dgate_ref, dup_ref, hgated_ref, gwg_ref, gwu_ref, gwd_ref):
    width = x_ref.shape[2]
    tn = (((0,), (0,)), ((), ()))

    def mm(a, b):
        return lax.dot_general(a, b, tn, preferred_element_type=jnp.float32)

    for start in range(0, width, 512):
        part = slice(start, start + 512)
        gwd_ref[0, :, part] = mm(hgated_ref[0], dy_ref[0, :, part])
        xs = x_ref[0, :, part]
        gwg_ref[0, part, :] = mm(xs, dgate_ref[0])
        gwu_ref[0, part, :] = mm(xs, dup_ref[0])


def expert_spec(*shape):
    return pl.BlockSpec((1,) + shape, lambda e: (e, 0, 0))


def run_experts(x_slots, dy_slots, gate_slots, w_gate, w_up, w_down):
    experts, rows, width = x_slots.shape
    ff = w_gate.shape[2]
    spec, low = expert_spec, jnp.bfloat16
    middle = jax.ShapeDtypeStruct((experts, rows, ff), low)
    return pl.pallas_call(
        expert_kernel,
        name="experts",
        grid=(experts,),
        in_specs=[
            spec(rows, width), spec(rows, width), spec(rows, 128),
            spec(width, ff), spec(width, ff), spec(ff, width),
        ],
        out_specs=(spec(rows, width + 128), spec(rows, width)) + (spec(rows, ff),) * 3,
        out_shape=(
            jax.ShapeDtypeStruct((experts, rows, width + 128), low),
            jax.ShapeDtypeStruct((experts, rows, width), low),
            middle, middle, middle,
        ),
        scratch_shapes=[pltpu.VMEM((rows, ff), jnp.float32)] * 3,
        compiler_params=pltpu.CompilerParams(vmem_limit_bytes=VMEM_LIMIT),
        cost_estimate=pl.CostEstimate(
            flops=29_000_000_000, bytes_accessed=100_000_000, transcendentals=2_000_000
        ),
    )(x_slots, dy_slots, gate_slots, w_gate, w_up, w_down)


def run_weights(x_slots, dy_slots, dgate, dup, hgated):
    experts, rows, width = x_slots.shape
    ff = dgate.shape[2]
    spec, f32 = expert_spec, jnp.float32
    wide = jax.ShapeDtypeStruct((experts, width, ff), f32)
    return pl.pallas_call(
        weights_kernel,
        name="expert_weights",
        grid=(experts,),
        in_specs=[spec(rows, width)] * 2 + [spec(rows, ff)] * 3,
        out_specs=(spec(width, ff), spec(width, ff), spec(ff, width)),
        out_shape=(wide, wide, jax.ShapeDtypeStruct((experts, ff, width), f32)),
        compiler_params=pltpu.CompilerParams(vmem_limit_bytes=VMEM_LIMIT),
        cost_estimate=pl.CostEstimate(
            flops=15_000_000_000, bytes_accessed=100_000_000, transcendentals=0
        ),
    )(x_slots, dy_slots, dgate, dup, hgated)


def plain_onehot(routes_all, first_expert, local_experts):
    sources, rows = routes_all.shape[0], routes_all.shape[1]
    experts = jnp.arange(local_experts, dtype=jnp.int32) + first_expert
    member = jnp.any(routes_all[:, :, :, None] == experts, axis=2).astype(jnp.int32)
    rank = jnp.cumsum(member, axis=1) - member
    rank = jnp.where(member > 0, rank, -1)
    return (
        rank.transpose(0, 2, 1)[:, :, None, :] == jnp.arange(CAP, dtype=jnp.int32)[:, None]
    ).astype(jnp.bfloat16)


def plain_experts(moe_low, cotangent, routes, gates, w_gate, w_up, w_down):
    both = ("dp", "tensor")
    local_experts = w_gate.shape[0]
    width = moe_low.shape[1]
    f32 = jnp.float32
    routes_all = lax.all_gather(routes, both, axis=0)
    x_all = lax.all_gather(moe_low, both, axis=0)
    dy_all = lax.all_gather(cotangent, both, axis=0)
    gates_all = lax.all_gather(gates, both, axis=0)
    first_expert = lax.axis_index("dp") * local_experts
    onehot = plain_onehot(routes_all, first_expert, local_experts)
    take = functools.partial(jnp.einsum, "sect,std->escd")
    flat = (local_experts, -1, width)
    x_slots = take(onehot, x_all).reshape(flat)
    dy_slots = take(onehot, dy_all).reshape(flat)
    experts = jnp.arange(local_experts, dtype=jnp.int32) + first_expert
    gates_here = jnp.sum(
        jnp.where(routes_all[..., None] == experts, gates_all[..., None], 0.0), axis=2
    )
    weight = jnp.einsum(
        "sect,ste->esc", onehot.astype(f32), gates_here, precision=lax.Precision.HIGHEST
    ).reshape(local_experts, -1)[..., None]
    mm = functools.partial(jnp.einsum, preferred_element_type=f32)
    gate_pre = mm("ecd,edf->ecf", x_slots, w_gate)
    up_pre = mm("ecd,edf->ecf", x_slots, w_up)
    raw = mm("ecd,efd->ecf", dy_slots, w_down)
    sig = jax.nn.sigmoid(gate_pre)
    silu = gate_pre * sig
    hidden = silu * up_pre
    hgated = (weight * hidden).astype(jnp.bfloat16)
    route_grad = jnp.sum(hidden * raw, axis=2).reshape(local_experts, -1, CAP)
    grad_hidden = weight * raw
    dgate = (grad_hidden * up_pre * sig * (1.0 + gate_pre * (1.0 - sig))).astype(jnp.bfloat16)
    dup = (grad_hidden * silu).astype(jnp.bfloat16)
    y_slots = mm("ecf,efd->ecd", hgated, w_down).astype(jnp.bfloat16)
    gin_slots = (mm("ecf,edf->ecd", dgate, w_gate) + mm("ecf,edf->ecd", dup, w_up)).astype(
        jnp.bfloat16
    )
    grads = (
        mm("ecd,ecf->edf", x_slots, dgate),
        mm("ecd,ecf->edf", x_slots, dup),
        mm("ecf,ecd->efd", hgated, dy_slots),
    )

    def give_back(slots):
        slots = slots.reshape(local_experts, -1, CAP, width)
        rows = mm("sect,escd->std", onehot, slots).astype(jnp.bfloat16)
        return lax.psum_scatter(
            rows.reshape(-1, width), both, scatter_dimension=0, tiled=True
        ).astype(f32)

    here = jnp.einsum(
        "sect,esc->ste", onehot.astype(f32), route_grad, precision=lax.Precision.HIGHEST
    )
    spread = jnp.zeros(here.shape[:2] + (EXPERTS,), f32)
    spread = lax.dynamic_update_slice(spread, here, (0, 0, first_expert))
    grad_gates = lax.psum_scatter(
        spread.reshape(-1, EXPERTS), both, scatter_dimension=0, tiled=True
    )
    return (give_back(y_slots), grad_gates, give_back(gin_slots), lambda own_rows: grads)


def routed_experts(moe_low, cotangent, routes, gates, w_gate, w_up, w_down, dispatched):
    if dispatched is None:
        return plain_experts(moe_low, cotangent, routes, gates, w_gate, w_up, w_down)
    dy_slots, onehot, all_routes = dispatched
    width = moe_low.shape[1]
    x_slots, gate_slots = gather_slots(moe_low, gates.T, onehot, all_routes)
    y_slots, gin_slots, *middle = run_experts(
        x_slots, dy_slots, gate_slots, w_gate, w_up, w_down
    )
    sums, grad_in = return_rows(y_slots, gin_slots, onehot)
    grad_gates = sums[:, width : width + EXPERTS] + sums[:, width + EXPERTS :]

    def weight_grads(own_rows):
        hgated, unused = lax.optimization_barrier((middle[2], own_rows))
        return run_weights(x_slots, dy_slots, middle[0], middle[1], hgated)

    return (sums[:, :width], grad_gates, grad_in, weight_grads)


def own_kernels(tokens, w_gate):
    return (
        lax.axis_size("dp") == 8
        and lax.axis_size("tensor") == 4
        and tokens.shape == (128, 2048)
        and w_gate.shape[0] == 8
    )


def side_columns(pieces, rows):
    filled = [jnp.pad(p, ((0, rows - p.shape[0]), (0, 0))) for p in pieces]
    used = sum(p.shape[1] for p in filled)
    return jnp.concatenate(filled + [jnp.zeros((rows, 128 - used), filled[0].dtype)], axis=1)


def body(
    tokens,
    cotangent,
    lengths,
    seq_order,
    routes,
    attn_gain,
    w_query,
    w_key,
    w_value,
    w_output,
    query_gain,
    key_gain,
    ffn_gain,
    router,
    w_gate,
    w_up,
    w_down,
):
    tok_rows, model_width = tokens.shape
    tensor_count = lax.axis_size("tensor")
    data_count = lax.axis_size("dp")
    group_rows_count = tok_rows * tensor_count
    block_rows = min(group_rows_count, 512)
    shard = w_query.shape[0]
    heads_width = w_query.shape[1]
    gain_rows = query_gain.shape[0]
    low = jnp.bfloat16
    f32 = jnp.float32

    own = own_kernels(tokens, w_gate)

    seq_ids, positions = arrival_layout(lengths[0], seq_order[0])
    resid_in = tokens.astype(f32)
    if own:
        gains, filled = jnp.zeros((1024,), f32), 0
        for part in (attn_gain, ffn_gain, query_gain, key_gain):
            count = part.shape[0]
            gains = gains + jnp.pad(part.astype(f32), (filled, 1024 - filled - count))
            filled += count
        gains = gains.reshape(8, 128)
        shards = (w_query, w_key, w_value, w_output, jnp.pad(router, ((0, 0), (0, 128 - EXPERTS))))
        seq_float = seq_ids.astype(f32)
        lane = jnp.arange(HD, dtype=jnp.int32)
        frequency = THETA ** (-(lane % (HD // 2)).astype(f32) / (HD // 2))
        angles = positions.astype(f32)[:, None] * frequency[None, :]
        tables = (
            jnp.cos(angles),
            jnp.sin(angles) * jnp.where(lane < HD // 2, -1.0, 1.0),
            jnp.broadcast_to(seq_float[:, None], (group_rows_count, 128)),
            jnp.broadcast_to(seq_float[None, :], (8, group_rows_count)),
        )
        (
            weights, group_tokens, dy_slots, all_gains, onehot, all_routes, group_rows,
            *attention, attn_out,
        ) = front(shards, tokens, cotangent, routes.T.astype(f32), gains, *tables, heads_width)
        dispatched = (dy_slots, onehot, all_routes)
        group_tokens = group_tokens.reshape(-1, model_width)
        full_router = weights[:, 4 * heads_width : 4 * heads_width + EXPERTS]
        ffn_scale = all_gains[:, 2:4].reshape(-1)
    else:
        side = side_columns(
            [router, attn_gain[:, None], ffn_gain[:, None], query_gain[:, None], key_gain[:, None]],
            shard,
        )
        packed = jnp.concatenate([w_query, w_key, w_value, w_output.T, side], axis=1)
        weights = lax.all_gather(packed, "dp", axis=0, tiled=True)
        group_tokens = lax.all_gather(tokens, "tensor", axis=0, tiled=True)
        dispatched = None
        full_query = weights[:, :heads_width]
        full_key = weights[:, heads_width : 2 * heads_width]
        full_value = weights[:, 2 * heads_width : 3 * heads_width]
        output_t = weights[:, 3 * heads_width : 4 * heads_width]
        extras = weights[:, 4 * heads_width :]
        full_router = extras[:, :EXPERTS]
        attn_scale = extras[:, EXPERTS].astype(f32)
        ffn_scale = extras[:, EXPERTS + 1].astype(f32)
        gain_columns = extras.reshape(data_count, shard, 128)[:, :gain_rows, EXPERTS + 2 : EXPERTS + 4]
        query_scale = gain_columns[:, :, 0].reshape(-1).astype(f32)
        key_scale = gain_columns[:, :, 1].reshape(-1).astype(f32)

        cosines, sines = rope_tables(positions)
        group_rows = norm_apply(group_tokens.astype(f32), attn_scale).astype(low)
        proj_query = jnp.dot(group_rows, full_query, preferred_element_type=f32)
        proj_key = jnp.dot(group_rows, full_key, preferred_element_type=f32)
        value_flat = jnp.dot(group_rows, full_value, preferred_element_type=f32).astype(low)
        value_low = value_flat.reshape(group_rows_count, -1, HD)
        query_low = head_norm_rope(proj_query, query_scale, cosines, sines).astype(low)
        key_low = head_norm_rope(proj_key, key_scale, cosines, sines).astype(low)
        context, row_lse = attend(query_low, key_low, value_low, seq_ids, block_rows)
        context_low = context.reshape(group_rows_count, -1).astype(low)
        attn_out = lax.psum_scatter(
            lax.dot_general(
                context_low, output_t, (((1,), (1,)), ((), ())), preferred_element_type=f32
            ).astype(low),
            "tensor",
            scatter_dimension=0,
            tiled=True,
        ).astype(f32)
    resid_mid = resid_in + attn_out
    moe_low = norm_apply(resid_mid, ffn_scale).astype(low)
    logits = jnp.dot(moe_low, full_router, preferred_element_type=f32)
    route_match = routes[:, :, None] == jnp.arange(EXPERTS, dtype=jnp.int32)[None, None, :]
    picked_logits = jnp.sum(jnp.where(route_match, logits[:, None, :], 0.0), axis=-1)
    gate_peak = jnp.max(picked_logits, axis=1, keepdims=True)
    gate_raw = jnp.exp(picked_logits - gate_peak)
    gates = gate_raw / jnp.sum(gate_raw, axis=1, keepdims=True)
    dense_gates = jnp.sum(jnp.where(route_match, gates[:, :, None], 0.0), axis=1)

    moe_out, grad_gates, grad_from_experts, expert_weight_grads = routed_experts(
        moe_low, cotangent, routes, gates, w_gate, w_up, w_down, dispatched
    )
    layer_out = (resid_mid + moe_out).astype(low)
    stat_terms = jnp.stack(
        [jnp.sum(resid_mid * resid_mid), jnp.sum(attn_out * attn_out), jnp.sum(moe_out * moe_out)]
    )
    grad_out = cotangent.astype(f32)
    inner_gate = jnp.sum(dense_gates * grad_gates, axis=1, keepdims=True)
    grad_logits_low = (dense_gates * (grad_gates - inner_gate)).astype(low)
    grad_router_part = jnp.dot(moe_low.T, grad_logits_low, preferred_element_type=f32)
    grad_moe_in = grad_from_experts + jnp.dot(
        grad_logits_low, full_router.T, preferred_element_type=f32
    )
    unused_mid, ffn_back = jax.vjp(norm_apply, resid_mid, ffn_scale)
    grad_mid_norm, grad_ffn_part = ffn_back(grad_moe_in)
    grad_mid = grad_out + grad_mid_norm
    grad_attn_low = grad_mid.astype(low)
    grad_attn_rows = lax.all_gather(grad_attn_low, "tensor", axis=0, tiled=True)
    grad_gate_w, grad_up_w, grad_down = expert_weight_grads(grad_attn_low)
    tn = (((0,), (0,)), ((), ()))
    if own:
        router_side = grad_router_part.reshape(8, 2, 128, EXPERTS).swapaxes(1, 2).reshape(8, 128, 128)

        side = jnp.concatenate(
            [
                router_side,
                jnp.zeros((8, 2, 128), f32),
                grad_ffn_part.reshape(8, 2, 128),
                jnp.zeros((8, 12, 128), f32),
            ],
            axis=1,
        ).astype(low)
        stats = jnp.pad(stat_terms[None, :], ((6, 9), (0, 125)))
        packed_grads, grad_out_w, grad_in_norm, small = finish(
            group_rows, group_tokens, attention, grad_attn_rows, weights, (all_gains,) + tables,
            side, stats,
        )
        grads_qkv = [packed_grads[:, i * heads_width : (i + 1) * heads_width] for i in range(3)]
        grad_router = jnp.concatenate([small[:128, :EXPERTS], small[:128, EXPERTS:]], axis=0)
        grad_attn_gain = small[128:130].reshape(-1)
        grad_ffn_gain = small[130:132].reshape(-1)
        first_lane = lax.axis_index("dp") * gain_rows
        grad_query_gain = lax.dynamic_slice(small[132], (first_lane,), (gain_rows,))
        grad_key_gain = lax.dynamic_slice(small[133], (first_lane,), (gain_rows,))
        stat_totals = small[134, :3]
    else:
        grad_ctx_low = jnp.dot(grad_attn_rows, output_t, preferred_element_type=f32).astype(low)
        grad_query, grad_key, grad_value = attend_back(
            query_low,
            key_low,
            value_low,
            seq_ids,
            row_lse,
            grad_ctx_low.reshape(value_low.shape),
            block_rows,
        )
        grad_value_low = grad_value.reshape(group_rows_count, -1).astype(low)
        unused_query, query_back = jax.vjp(
            lambda projected, head_gain: head_norm_rope(projected, head_gain, cosines, sines),
            proj_query,
            query_scale,
        )
        grad_proj_query, grad_query_gain_part = query_back(grad_query)
        unused_key, key_back = jax.vjp(
            lambda projected, head_gain: head_norm_rope(projected, head_gain, cosines, sines),
            proj_key,
            key_scale,
        )
        grad_proj_key, grad_key_gain_part = key_back(grad_key)
        grad_query_low = grad_proj_query.astype(low)
        grad_key_low = grad_proj_key.astype(low)
        head_grads = (grad_query_low, grad_key_low, grad_value_low)
        weight_grads = [
            lax.dot_general(group_rows, part, tn, preferred_element_type=f32) for part in head_grads
        ]
        grad_output_t = lax.dot_general(grad_attn_rows, context_low, tn, preferred_element_type=f32)
        total_rows = jnp.dot(grad_query_low, full_query.T, preferred_element_type=f32)
        total_rows = total_rows + jnp.dot(grad_key_low, full_key.T, preferred_element_type=f32)
        total_rows = total_rows + jnp.dot(grad_value_low, full_value.T, preferred_element_type=f32)
        grad_normed = lax.psum_scatter(
            total_rows.astype(low), "tensor", scatter_dimension=0, tiled=True
        ).astype(f32)
        unused_in, attn_back = jax.vjp(norm_apply, resid_in, attn_scale)
        grad_in_norm, grad_attn_part = attn_back(grad_normed)

        def gain_column(part):
            cut = part.astype(low).reshape(data_count, gain_rows, 1)
            return jnp.pad(cut, ((0, 0), (0, shard - gain_rows), (0, 0))).reshape(-1, 1)

        side_grads = side_columns(
            [
                grad_router_part.astype(low),
                grad_attn_part.astype(low)[:, None],
                grad_ffn_part.astype(low)[:, None],
                gain_column(grad_query_gain_part),
                gain_column(grad_key_gain_part),
            ],
            model_width,
        )
        packed_grads = jnp.concatenate(
            [part.astype(low) for part in weight_grads] + [grad_output_t.astype(low), side_grads],
            axis=1,
        )
        reduced = lax.psum_scatter(packed_grads, "dp", scatter_dimension=0, tiled=True).astype(f32)
        side_total, stat_totals = lax.psum(
            (reduced[:, 4 * heads_width : 4 * heads_width + EXPERTS + 4], stat_terms), "tensor"
        )
        grads_qkv = [reduced[:, i * heads_width : (i + 1) * heads_width] for i in range(3)]
        grad_out_w = reduced[:, 3 * heads_width : 4 * heads_width].T
        grad_attn_gain = side_total[:, EXPERTS]
        grad_ffn_gain = side_total[:, EXPERTS + 1]
        grad_query_gain = side_total[:gain_rows, EXPERTS + 2]
        grad_key_gain = side_total[:gain_rows, EXPERTS + 3]
        grad_router = side_total[:, :EXPERTS]
    grad_tokens = grad_mid + grad_in_norm
    rms_stats = jnp.sqrt(stat_totals / (group_rows_count * model_width))[None, :]
    return (
        layer_out,
        grad_tokens,
        grad_attn_gain,
        *grads_qkv,
        grad_out_w,
        grad_query_gain,
        grad_key_gain,
        grad_ffn_gain,
        grad_router,
        grad_gate_w,
        grad_up_w,
        grad_down,
        rms_stats,
    )


def solution(mesh):
    in_specs = (
        P(("dp", "tensor"), None),
        P(("dp", "tensor"), None),
        P("dp", None),
        P("dp", None),
        P(("dp", "tensor"), None),
        P("dp"),
        P("dp", "tensor"),
        P("dp", "tensor"),
        P("dp", "tensor"),
        P("tensor", "dp"),
        P("dp"),
        P("dp"),
        P("dp"),
        P("dp", None),
        P("dp", None, "tensor"),
        P("dp", None, "tensor"),
        P("dp", "tensor", None),
    )
    out_specs = (
        P(("dp", "tensor"), None),
        P(("dp", "tensor"), None),
        P("dp"),
        P("dp", "tensor"),
        P("dp", "tensor"),
        P("dp", "tensor"),
        P("tensor", "dp"),
        P("dp"),
        P("dp"),
        P("dp"),
        P("dp", None),
        P("dp", None, "tensor"),
        P("dp", None, "tensor"),
        P("dp", "tensor", None),
        P("dp", None),
    )
    return jax.shard_map(body, mesh=mesh, in_specs=in_specs, out_specs=out_specs, check_vma=False)
```

```python
import functools

import jax
import jax.numpy as jnp
from jax import lax
from jax.experimental import pallas as pl
from jax.experimental.pallas import tpu as pltpu
from jax.sharding import PartitionSpec as P

HD = 128
EXPERTS = 64
TOPK = 8
CAP = 18


EPSILON = 1e-05
THETA = 10000.0
NEGATIVE = -1e30


def inv_rms(values):
    return lax.rsqrt(jnp.mean(values * values, axis=-1, keepdims=True) + EPSILON)


def norm_apply(values, scale_gain):
    return values * inv_rms(values) * scale_gain


def arrival_layout(seq_lengths, order_row):
    row_total = order_row.shape[0]
    placed = jnp.arange(row_total, dtype=jnp.int32)
    order = jnp.arange(seq_lengths.shape[0], dtype=jnp.int32)
    upto = order[None, :] <= order[:, None]
    seq_ends = jnp.sum(jnp.where(upto, seq_lengths[None, :], 0), axis=1)
    seq_starts = seq_ends - seq_lengths
    member = jnp.sum((placed[:, None] >= seq_ends[None, :]).astype(jnp.int32), axis=1)
    chosen = member[:, None] == jnp.arange(seq_lengths.shape[0], dtype=jnp.int32)[None, :]
    seq_begin = jnp.sum(jnp.where(chosen, seq_starts[None, :], 0), axis=1)
    here = order_row[None, :] == placed[:, None]
    seq_ids = jnp.sum(jnp.where(here, member[None, :], 0), axis=1)
    positions = jnp.sum(jnp.where(here, (placed - seq_begin)[None, :], 0), axis=1)
    return (seq_ids, positions)


def rope_tables(positions):
    half_dim = HD // 2
    frequency = THETA ** (-jnp.arange(half_dim, dtype=jnp.float32) / half_dim)
    angles = positions.astype(jnp.float32)[:, None] * frequency[None, :]
    return (jnp.cos(angles)[:, None, :], jnp.sin(angles)[:, None, :])


def head_norm_rope(projected, head_gain, cosines, sines):
    shaped = projected.reshape(projected.shape[0], -1, HD)
    normed_heads = norm_apply(shaped, head_gain)
    first_half = normed_heads[..., : HD // 2]
    second_half = normed_heads[..., HD // 2 :]
    return jnp.concatenate(
        [first_half * cosines - second_half * sines, second_half * cosines + first_half * sines],
        axis=-1,
    )


def masked_scores(query_block, key_low, seq_block, seq_ids):
    score_scale = HD ** (-0.5)
    scores = (
        jnp.einsum("qhd,khd->hqk", query_block, key_low, preferred_element_type=jnp.float32)
        * score_scale
    )
    same_seq = (seq_block[:, None] == seq_ids[None, :])[None]
    return jnp.where(same_seq, scores, NEGATIVE)


def attend(query_low, key_low, value_low, seq_ids, block_rows):
    num_blocks = query_low.shape[0] // block_rows
    query_blocks = query_low.reshape(num_blocks, block_rows, query_low.shape[1], HD)
    seq_blocks = seq_ids.reshape(num_blocks, block_rows)

    def one_block(inputs):
        query_block, seq_block = inputs
        scores = masked_scores(query_block, key_low, seq_block, seq_ids)
        row_peak = jnp.max(scores, axis=-1, keepdims=True)
        raised = jnp.exp(scores - row_peak)
        row_total = jnp.sum(raised, axis=-1, keepdims=True)
        probs_low = (raised / row_total).astype(jnp.bfloat16)
        context = jnp.einsum(
            "hqk,khd->qhd", probs_low, value_low, preferred_element_type=jnp.float32
        )
        return (context, row_peak + jnp.log(row_total))

    context, row_lse = lax.map(one_block, (query_blocks, seq_blocks))
    return (context.reshape(query_low.shape), row_lse)


def attend_back(query_low, key_low, value_low, seq_ids, row_lse, grad_ctx_low, block_rows):
    score_scale = HD ** (-0.5)
    num_blocks = query_low.shape[0] // block_rows
    block_shape = (num_blocks, block_rows, query_low.shape[1], HD)

    def one_block(carry, inputs):
        grad_key_sum, grad_value_sum = carry
        query_block, seq_block, lse_block, grad_block = inputs
        scores = masked_scores(query_block, key_low, seq_block, seq_ids)
        probs = jnp.exp(scores - lse_block)
        probs_low = probs.astype(jnp.bfloat16)
        grad_value_sum = grad_value_sum + jnp.einsum(
            "hqk,qhd->khd", probs_low, grad_block, preferred_element_type=jnp.float32
        )
        grad_probs = jnp.einsum(
            "qhd,khd->hqk", grad_block, value_low, preferred_element_type=jnp.float32
        )
        inner_sum = jnp.sum(probs * grad_probs, axis=-1, keepdims=True)
        grad_scores = (probs * (grad_probs - inner_sum)).astype(jnp.bfloat16)
        grad_query_block = (
            jnp.einsum("hqk,khd->qhd", grad_scores, key_low, preferred_element_type=jnp.float32)
            * score_scale
        )
        grad_key_sum = (
            grad_key_sum
            + jnp.einsum(
                "hqk,qhd->khd", grad_scores, query_block, preferred_element_type=jnp.float32
            )
            * score_scale
        )
        return ((grad_key_sum, grad_value_sum), grad_query_block)

    zeros_heads = jnp.zeros(query_low.shape, jnp.float32)
    carried, grad_query = lax.scan(
        one_block,
        (zeros_heads, zeros_heads),
        (
            query_low.reshape(block_shape),
            seq_ids.reshape(num_blocks, block_rows),
            row_lse,
            grad_ctx_low.reshape(block_shape),
        ),
    )
    return (grad_query.reshape(query_low.shape), carried[0], carried[1])


MESH = pl.DeviceIdType.MESH
VMEM_LIMIT = 60 * 1024 * 1024
MAIN = 16
SPARE = CAP - MAIN


def at(dp_index, z_index):
    return {"dp": dp_index, "tensor": z_index}


def place():
    dp = lax.axis_index("dp")
    z = lax.axis_index("tensor")
    core, x, y = dp % 2, (dp // 2) % 2, dp // 4
    return dp, z, 1 - 2 * core, 2 - 4 * x, 4 - 8 * y


def greet(peers, extra=None, has_extra=None, count=0):
    barrier = pltpu.get_barrier_semaphore()
    for peer in peers:
        pl.semaphore_signal(barrier, inc=1, device_id=at(*peer), device_id_type=MESH)
    if extra is not None:

        @pl.when(has_extra)
        def _():
            pl.semaphore_signal(barrier, inc=1, device_id=at(*extra), device_id_type=MESH)

    pl.semaphore_wait(barrier, len(peers) + count)


def when_or_now(cond, action):
    if cond is None:
        action()
    else:
        pl.when(cond)(action)


def slot_matrix(routes_block, source, first_expert):
    experts = lax.broadcasted_iota(jnp.int32, (8, 128), 0) + first_expert
    member = jnp.zeros((8, 128), jnp.float32)
    for j in range(TOPK):
        member = member + (routes_block[j : j + 1, :] == experts.astype(jnp.float32)).astype(jnp.float32)
    earlier = (
        lax.broadcasted_iota(jnp.int32, (128, 128), 0)
        < lax.broadcasted_iota(jnp.int32, (128, 128), 1)
    ).astype(jnp.bfloat16)
    rank = jnp.dot(member.astype(jnp.bfloat16), earlier, preferred_element_type=jnp.float32)
    rank = jnp.where(member > 0.5, rank, -1.0).astype(jnp.int32)
    spread = jnp.broadcast_to(rank[:, None, :], (8, MAIN, 128)).reshape(128, 128)
    row = lax.broadcasted_iota(jnp.int32, (128, 128), 0) % MAIN
    main = spread == row
    spare = jnp.logical_and(row // SPARE == source % 8, spread == MAIN + row % SPARE)
    onehot = jnp.concatenate(
        [main.astype(jnp.float32), spare.astype(jnp.float32)], axis=0
    ).astype(jnp.bfloat16)
    compact = jnp.concatenate(
        [(rank == MAIN + c).astype(jnp.float32) for c in range(SPARE)], axis=0
    ).astype(jnp.bfloat16)
    return onehot, compact


class LineScatter:
    def __init__(self, dp, z, blocks, rze, rzm, rzf, zsend, zrecv):
        self.dp, self.z = dp, z
        self.zr, self.zo = z + 1 - 2 * (z % 2), 3 - z
        self.mid, self.end = z * (3 - z) > 0, z * (3 - z) < 1
        self.zs = [3 - 3 * (z // 2), 2 - z // 2, self.zr, z]
        self.blocks, self.rze, self.rzm, self.rzf = blocks, rze, rzm, rzf
        self.zsend, self.zrecv = zsend, zrecv
        self.outward = [self.copy(blocks.at[k], rze.at[k], k, self.zr) for k in range(3)]
        self.sends = []

    def copy(self, src, dst, index, z_to):
        return pltpu.make_async_remote_copy(
            src, dst, self.zsend.at[index], self.zrecv.at[index],
            device_id=at(self.dp, z_to), device_id_type=MESH,
        )

    def ready(self, k):
        pl.when(self.end)(functools.partial(self.outward[k].start))
        self.sends.append((self.outward[k], self.end))

    def add(self, k, part):
        total = self.blocks[k].astype(jnp.float32) + part[...].astype(jnp.float32)
        self.blocks[k] = total.astype(jnp.bfloat16)

    def onward(self, k):
        if k < 2:
            copy = self.copy(self.blocks.at[k], self.rzm.at[k], 3 + k, self.zo)
        else:
            copy = self.copy(self.blocks.at[k], self.rzf, 5, self.zr)
        self.sends.append((copy, self.mid))

        @pl.when(self.mid)
        def _():
            if k < 2:
                self.outward[k].wait_recv()
                self.add(k, self.rze.at[k])
            else:
                self.copy(self.blocks.at[0], self.rzm.at[0], 3, self.zo).wait_recv()
                self.add(k, self.rzm.at[0])
            copy.start()

    def last(self, out_ref):
        @pl.when(self.end)
        def _():
            self.copy(self.blocks.at[2], self.rzf, 5, self.zr).wait_recv()
            out_ref[...] = out_ref[...] + self.rzf[...].astype(jnp.float32)

        @pl.when(self.mid)
        def _():
            self.outward[2].wait_recv()
            self.copy(self.blocks.at[1], self.rzm.at[1], 4, self.zo).wait_recv()
            out_ref[...] = (
                out_ref[...]
                + self.rze[2].astype(jnp.float32)
                + self.rzm[1].astype(jnp.float32)
            )

    def drain(self):
        for copy, cond in self.sends:
            pl.when(cond)(functools.partial(copy.wait_send))

    @staticmethod
    def scratch(width):
        low, dma = jnp.bfloat16, pltpu.SemaphoreType.DMA
        return [
            pltpu.VMEM((3, 128, width), low),
            pltpu.VMEM((3, 128, width), low),
            pltpu.VMEM((2, 128, width), low),
            pltpu.VMEM((128, width), low),
            dma((6,)),
            dma((6,)),
        ]


class AllGather:
    def __init__(self, held, own_ref, ssem, rsem, metas=None, own_meta=None, msem=None, mrsem=None):
        self.dp, self.z, self.dc, self.dx, self.dy = place()
        z = self.z
        self.zr, self.zo = z + 1 - 2 * (z % 2), 3 - z
        self.mid = z * (3 - z) > 0
        self.zs = [z, self.zr, 2 - z // 2, 3 - 3 * (z // 2)]
        self.held, self.own_ref, self.ssem, self.rsem = held, own_ref, ssem, rsem
        self.metas, self.own_meta, self.msem, self.mrsem = metas, own_meta, msem, mrsem
        self.sends = []

    def send(self, block, part, dp_to, z_to, cond=None, own=False):
        half = pl.ds(part * 64, 64)
        view = self.held.at[block, half]
        source = self.own_ref.at[half] if own else view
        index = len(self.sends)
        copies = [
            pltpu.make_async_remote_copy(
                source, view, self.ssem.at[index], self.rsem.at[block, part],
                device_id=at(dp_to, z_to), device_id_type=MESH,
            )
        ]
        if part == 0 and self.metas is not None:
            copies.append(
                pltpu.make_async_remote_copy(
                    self.own_meta if own else self.metas.at[block], self.metas.at[block],
                    self.msem.at[index], self.mrsem.at[block],
                    device_id=at(dp_to, z_to), device_id_type=MESH,
                )
            )
        self.sends.append((copies, cond))

        def go():
            for copy in copies:
                copy.start()

        when_or_now(cond, go)

    def arrive(self, block, part):
        view = self.held.at[block, pl.ds(part * 64, 64)]
        here = dict(device_id=at(self.dp, self.zr), device_id_type=MESH)
        pltpu.make_async_remote_copy(
            view, view, self.ssem.at[0], self.rsem.at[block, part], **here
        ).wait_recv()
        if part == 0 and self.metas is not None:
            pltpu.make_async_remote_copy(
                self.metas.at[block], self.metas.at[block], self.msem.at[0], self.mrsem.at[block],
                **here
            ).wait_recv()

    def first(self, k):
        dp, z, dx, dy, dc = self.dp, self.z, self.dx, self.dy, self.dc
        block = dp * 4 + self.zs[k]
        own = k == 0
        for part in (0, 1):
            if k > 0:
                self.arrive(block, part)
            if k == 0:
                self.send(block, part, dp, self.zr, None, own)
                self.send(block, part, dp, self.zo, self.mid, own)
            else:
                self.send(block, part, dp, self.zo if k == 1 else self.zr, self.mid)
            self.send(block, part, dp + (dx if part == 0 else dy), z, None, own)
        self.send(block, 1, dp + dx, z, None, own)
        self.send(block, 0, dp + dy, z, None, own)
        self.send(block, 0, dp + dc, z, None, own)
        self.send(block, 1, dp + dc, z, None, own)

    def second(self, k):
        dp, z, dx, dy, dc = self.dp, self.z, self.dx, self.dy, self.dc
        bx, by = (dp + dx) * 4 + self.zs[k], (dp + dy) * 4 + self.zs[k]
        self.arrive(bx, 0)
        self.send(bx, 0, dp + dy, z)
        self.send(bx, 0, dp + dc, z)
        self.arrive(by, 1)
        self.send(by, 1, dp + dx, z)
        self.send(by, 1, dp + dc, z)
        self.arrive(bx, 1)
        self.send(bx, 1, dp + dc, z)
        self.arrive(by, 0)
        self.send(by, 0, dp + dc, z)

    def third(self, k):
        block = (self.dp + self.dx + self.dy) * 4 + self.zs[k]
        for part in (0, 1):
            self.arrive(block, part)
            self.send(block, part, self.dp + self.dc, self.z)

    def across(self, k, step):
        block = (self.dp + self.dc + step) * 4 + self.zs[k]
        self.arrive(block, 0)
        self.arrive(block, 1)

    def drain(self):
        for copies, cond in self.sends:

            def done(copies=copies):
                for copy in copies:
                    copy.wait_send()

            when_or_now(cond, done)


class Dispatcher:
    def __init__(self, held, stage, spare, slots_ref, osem):
        self.held, self.stage, self.spare = held, stage, spare
        self.slots_ref, self.osem = slots_ref, osem
        self.count = 0

    def put(self, start, slot):
        return pltpu.make_async_copy(
            self.stage.at[slot], self.slots_ref.at[:, pl.ds(start, MAIN), :], self.osem.at[slot]
        )

    def block(self, block, onehot, compact):
        slot = self.count % 2
        picked = jnp.concatenate([onehot[:128], compact], axis=0)
        width = self.held.shape[2]
        if self.count >= 2:
            self.put(block * MAIN, slot).wait()

        def tile(step, carry):
            lanes = pl.ds(pl.multiple_of(step * 1024, 1024), 1024)
            rows = jnp.dot(picked, self.held[block, :, lanes], preferred_element_type=jnp.float32)
            self.stage[slot, :, :, lanes] = rows[:128].astype(jnp.bfloat16).reshape(8, MAIN, 1024)
            self.spare[block, :, lanes] = rows[128:].astype(jnp.bfloat16)
            return carry

        lax.fori_loop(0, width // 1024, tile, 0)
        self.put(block * MAIN, slot).start()
        self.count += 1

    def end(self):
        width = self.held.shape[2]
        row = lax.broadcasted_iota(jnp.int32, (128, 128), 0)
        column = lax.broadcasted_iota(jnp.int32, (128, 128), 1)
        source = (row // SPARE) % 8 * 16 + row % SPARE * 8 + row // MAIN
        turn = (column == source).astype(jnp.float32).astype(jnp.bfloat16)
        for group in range(4):
            slot = group % 2
            self.put(512 + group * MAIN, slot).wait()
            for start in range(0, width, 512):
                lanes = slice(start, start + 512)
                kept = self.spare[group * 8 : group * 8 + 8, :, lanes].reshape(128, 512)
                rows = jnp.dot(turn, kept, preferred_element_type=jnp.float32)
                self.stage[slot, :, :, lanes] = rows.astype(jnp.bfloat16).reshape(8, MAIN, 512)
            self.put(512 + group * MAIN, slot).start()
        for slot in range(2):
            self.put(512, slot).wait()


def arrival_order(gather):
    dp, dc, dx, dy, zs = gather.dp, gather.dc, gather.dx, gather.dy, gather.zs
    order = []
    for k in range(6):
        column = []
        if k < 4:
            column.append((k, 0))
        if 1 <= k < 5:
            column += [(k - 1, dx), (k - 1, dy)]
        if k >= 2:
            column.append((k - 2, dx + dy))
        across = [(k - 1, dc)] if 1 <= k < 5 else []
        if k >= 2:
            across += [(k - 2, dc + step) for step in (dx, dy, dx + dy)]
        order.append([[(dp + to) * 4 + zs[j] for j, to in part] for part in (column, across)])
    return order


def gather_forward(gather, k):
    if k < 4:
        gather.first(k)
    if 1 <= k < 5:
        gather.second(k - 1)
    if k >= 2:
        gather.third(k - 2)


def gather_process(gather, order, k, process):
    for block in order[k][0]:
        process(block)
    for block in order[k][1]:
        gather.arrive(block, 0)
        gather.arrive(block, 1)
        process(block)


def rotate(values, cosines, sines):
    return values * cosines + pltpu.roll(values, HD // 2, 1) * sines


def head_probs(query, key, seq_column, seq_row):
    scores = lax.dot_general(
        query, key, (((1,), (1,)), ((), ())), preferred_element_type=jnp.float32
    ) * (HD ** (-0.5))
    scores = jnp.where(seq_column == seq_row, scores, NEGATIVE)
    raised = jnp.exp(scores - jnp.max(scores, axis=1, keepdims=True))
    return raised / jnp.sum(raised, axis=1, keepdims=True)


def head_gain(gains_ref, first):
    lane = lax.broadcasted_iota(jnp.int32, (8, 128), 1)
    keep = jnp.logical_and(lane >= first, lane < first + 16)
    total = jnp.zeros((8, 128), jnp.float32)
    for block in range(8):
        part = jnp.where(keep, jnp.broadcast_to(gains_ref[block, 4:5, :], (8, 128)), 0.0)
        shift = (16 * block - first) % 128
        total = total + (pltpu.roll(part, shift, 1) if shift else part)
    return total[:1]


def front_kernel(
    wq_ref, wk_ref, wv_ref, wo_ref, router_ref, tok_ref, cot_ref, routes_in, gains_in, cos_ref, sin_ref, seqc_ref, seqr_ref,
    weights_ref, group_ref, slots_ref, gains_ref, onehot_ref, compact_ref, routes_ref, normed_ref, projq_ref, projk_ref,
    query_ref, key_ref, value_ref, ctx_ref, out_ref,
    wheld, theld, gheld, held, metas, stage, spare, lsem, wsend, wrecv, gsend, grecv, zsend, zrecv,
    dsend, drecv, msend, mrecv, osem, fsem, *line_refs
):
    dp, z, dc, dx, dy = place()
    zr, zo = z + 1 - 2 * (z % 2), 3 - z
    mid = z * (3 - z) > 0
    f32, low = jnp.float32, jnp.bfloat16
    heads = query_ref.shape[1]
    width = tok_ref.shape[1]
    line = LineScatter(dp, z, *line_refs)
    gather = AllGather(held, cot_ref, dsend, drecv, metas, routes_in, msend, mrecv)
    order = arrival_order(gather)
    picker = Dispatcher(held, stage, spare, slots_ref, osem)
    own_block = dp * 4 + z
    own_rows = pl.ds(pl.multiple_of(dp * 256, 256), 256)
    fill = []
    for source, column, count in (
        (wq_ref, 0, heads), (wk_ref, heads, heads), (wv_ref, 2 * heads, heads),
        (wo_ref.at[pl.ds(0, 256)], 3 * heads, 256), (wo_ref.at[pl.ds(256, 256)], 3 * heads + 256, 256),
        (router_ref, 4 * heads, 128),
    ):
        target = wheld.at[own_rows, pl.ds(column, count)]
        fill.append(pltpu.make_async_copy(source, target, fsem.at[len(fill)]))
    for copy in fill:
        copy.start()
    greet([(dp + dc, z), (dp + dx, z), (dp + dy, z), (dp, zr)], (dp, zo), mid, z * (3 - z) // 2)
    sends = []

    def spot(block, part):
        return wheld.at[pl.ds(pl.multiple_of(block * 256 + part * 128, 128), 128)]

    def send(block, part, dp_to, own=False):
        source = spot(block, part)
        index = len(sends)
        copies = [
            pltpu.make_async_remote_copy(
                source, spot(block, part), wsend.at[index], wrecv.at[block, part],
                device_id=at(dp_to, z), device_id_type=MESH,
            )
        ]
        if part == 0:
            copies.append(
                pltpu.make_async_remote_copy(
                    gains_in if own else gheld.at[block], gheld.at[block],
                    gsend.at[index], grecv.at[block],
                    device_id=at(dp_to, z), device_id_type=MESH,
                )
            )
        for copy in copies:
            copy.start()
        sends.append(copies)

    def arrive(block, part):
        here = dict(device_id=at(dp + dx, z), device_id_type=MESH)
        pltpu.make_async_remote_copy(
            spot(block, part), spot(block, part), wsend.at[0], wrecv.at[block, part], **here
        ).wait_recv()
        if part == 0:
            pltpu.make_async_remote_copy(
                gheld.at[block], gheld.at[block], gsend.at[0], grecv.at[block], **here
            ).wait_recv()

    zsends = []

    def z_send(source, block, z_to, cond=None):
        copy = pltpu.make_async_remote_copy(
            source, theld.at[block], zsend.at[len(zsends)], zrecv.at[block],
            device_id=at(dp, z_to), device_id_type=MESH,
        )
        when_or_now(cond, functools.partial(copy.start))
        zsends.append((copy, cond))

    def z_arrive(block):
        pltpu.make_async_remote_copy(
            theld.at[block], theld.at[block], zsend.at[0], zrecv.at[block],
            device_id=at(dp, zr), device_id_type=MESH,
        ).wait_recv()

    z_send(tok_ref, z, zr)
    z_send(tok_ref, z, zo, mid)
    for copy in fill:
        copy.wait()
    send(dp, 0, dp + dx, True)
    send(dp, 1, dp + dy, True)
    send(dp, 1, dp + dx, True)
    send(dp, 0, dp + dy, True)
    send(dp, 0, dp + dc, True)
    send(dp, 1, dp + dc, True)
    local = [
        pltpu.make_async_copy(tok_ref, theld.at[z], lsem.at[1]),
        pltpu.make_async_copy(gains_in, gheld.at[dp], lsem.at[2]),
        pltpu.make_async_copy(cot_ref, held.at[own_block], lsem.at[3]),
        pltpu.make_async_copy(routes_in, metas.at[own_block], lsem.at[4]),
    ]
    for copy in local:
        copy.start()
    z_arrive(zr)
    z_send(theld.at[zr], zr, zo, mid)
    bx, by, bxy = dp + dx, dp + dy, dp + dx + dy
    arrive(bx, 0)
    send(bx, 0, dp + dy)
    send(bx, 0, dp + dc)
    arrive(by, 1)
    send(by, 1, dp + dx)
    send(by, 1, dp + dc)
    gather.first(0)
    far = 2 - z // 2
    z_arrive(far)
    z_send(theld.at[far], far, zr, mid)
    arrive(bx, 1)
    send(bx, 1, dp + dc)
    arrive(by, 0)
    send(by, 0, dp + dc)
    last = 3 - 3 * (z // 2)
    z_arrive(last)
    z_send(theld.at[last], last, zr, mid)
    for part in (0, 1):
        arrive(bxy, part)
        send(bxy, part, dp + dc)
    for block in (dp, bx, by, bxy):
        for part in (0, 1):
            arrive(block + dc, part)
    for copy in local:
        copy.wait()
    kept = [
        pltpu.make_async_copy(wheld, weights_ref, lsem.at[0]),
        pltpu.make_async_copy(theld, group_ref, lsem.at[1]),
    ]
    for copy in kept:
        copy.start()

    def process(block):
        onehot, compact = slot_matrix(metas[block], block, dp * 8)
        onehot_ref[block] = onehot
        compact_ref[block] = compact
        picker.block(block, onehot, compact)

    scale = jnp.concatenate(
        [gheld[j // 2, j % 2 : j % 2 + 1, :] for j in range(width // 128)], axis=1
    )

    def norm_rows(step, carry):
        values = theld[step].astype(f32)
        inverse = lax.rsqrt(jnp.mean(values * values, axis=1, keepdims=True) + EPSILON)
        rows = pl.ds(pl.multiple_of(step * 128, 128), 128)
        normed_ref[rows, :] = (values * inverse * scale).astype(low)
        return carry

    gains_ref[...] = gheld[...]
    lax.fori_loop(0, 4, norm_rows, 0)

    def project(column):
        cols = slice(column * heads, column * heads + heads)
        return jnp.dot(normed_ref[...], wheld[:, cols], preferred_element_type=f32)

    projq_ref[...] = project(0)
    projk_ref[...] = project(1)
    value_ref[...] = project(2).astype(low)
    gather_forward(gather, 1)
    cosines, sines = cos_ref[...], sin_ref[...]
    query_gain, key_gain = head_gain(gheld, 0), head_gain(gheld, 16)

    def one_head(h, carry):
        cols = pl.ds(pl.multiple_of(h * HD, HD), HD)
        for source, gain, target in (
            (projq_ref, query_gain, query_ref), (projk_ref, key_gain, key_ref),
        ):
            values = source[:, cols]
            inverse = lax.rsqrt(jnp.mean(values * values, axis=1, keepdims=True) + EPSILON)
            target[:, cols] = rotate(values * inverse * gain, cosines, sines).astype(low)
        for start in range(0, 512, 256):
            rows = slice(start, start + 256)
            probs = head_probs(
                query_ref[rows, cols], key_ref[:, cols], seqc_ref[rows, :1], seqr_ref[:1, :]
            )
            ctx_ref[rows, cols] = jnp.dot(
                probs.astype(low), value_ref[:, cols], preferred_element_type=f32
            ).astype(low)
        return carry

    lax.fori_loop(0, heads // HD // 2, one_head, 0)
    gather_forward(gather, 2)
    lax.fori_loop(heads // HD // 2, heads // HD, one_head, 0)
    for k in range(4):
        rows = pl.ds(pl.multiple_of(line.zs[k] * 128, 128), 128)
        for start in range(0, width, 256):
            lanes = slice(start, start + 256)
            piece = jnp.dot(
                ctx_ref[rows, :256], wheld[lanes, 3 * heads : 3 * heads + 256],
                preferred_element_type=f32,
            ) + jnp.dot(
                ctx_ref[rows, 256:], wheld[lanes, 3 * heads + 256 : 4 * heads],
                preferred_element_type=f32,
            )
            if k < 3:
                line.blocks[k, :, lanes] = piece.astype(low)
            else:
                out_ref[:, lanes] = piece
        if k < 3:
            line.ready(k)
    gather.first(3)
    process(own_block)
    gather_process(gather, order, 1, process)
    gather.second(2)
    gather.third(1)
    line.onward(0)
    gather_process(gather, order, 2, process)
    line.onward(1)
    gather_process(gather, order, 3, process)
    gather_forward(gather, 4)
    line.onward(2)
    gather_process(gather, order, 4, process)
    gather_forward(gather, 5)
    line.last(out_ref)
    gather_process(gather, order, 5, process)
    picker.end()
    routes_ref[...] = metas[...]
    for copy in kept:
        copy.wait()
    for copies in sends:
        for copy in copies:
            copy.wait_send()
    for copy, cond in zsends:
        when_or_now(cond, functools.partial(copy.wait_send))
    gather.drain()
    line.drain()


def front(shards, tokens, cotangent, routes, gains, cosines, sines, seq_column, seq_row, heads):
    width = tokens.shape[1]
    rows = 4 * tokens.shape[0]
    f32, low = jnp.float32, jnp.bfloat16
    anywhere = pl.BlockSpec(memory_space=pl.ANY)
    vmem = pl.BlockSpec(memory_space=pltpu.VMEM)
    dma = pltpu.SemaphoreType.DMA
    narrow = jax.ShapeDtypeStruct((rows, heads), low)
    return pl.pallas_call(
        front_kernel,
        name="front",
        out_shape=(
            jax.ShapeDtypeStruct((width, 4 * heads + 128), low),
            jax.ShapeDtypeStruct((4, 128, width), low),
            jax.ShapeDtypeStruct((8, 576, width), low),
            jax.ShapeDtypeStruct((8, 8, 128), f32),
            jax.ShapeDtypeStruct((32, 256, 128), low),
            jax.ShapeDtypeStruct((32, 16, 128), low),
            jax.ShapeDtypeStruct((32, 8, 128), f32),
            jax.ShapeDtypeStruct((rows, width), low),
            jax.ShapeDtypeStruct((rows, heads), f32),
            jax.ShapeDtypeStruct((rows, heads), f32),
            narrow, narrow, narrow, narrow,
            jax.ShapeDtypeStruct((128, width), f32),
        ),
        in_specs=[anywhere] * 5 + [vmem] * 8,
        out_specs=(anywhere,) * 3 + (vmem,) * 12,
        scratch_shapes=[
            pltpu.VMEM((width, 4 * heads + 128), low),
            pltpu.VMEM((4, 128, width), low),
            pltpu.VMEM((8, 8, 128), f32),
            pltpu.VMEM((32, 128, width), low),
            pltpu.VMEM((32, 8, 128), f32),
            pltpu.VMEM((2, 8, MAIN, width), low),
            pltpu.VMEM((32, 16, width), low),
            dma((9,)), dma((14,)), dma((8, 2)), dma((14,)), dma((8,)), dma((5,)), dma((4,)),
            dma((72,)), dma((32, 2)), dma((72,)), dma((32,)), dma((2,)), dma((6,)),
        ]
        + LineScatter.scratch(width),
        compiler_params=pltpu.CompilerParams(
            collective_id=0, has_side_effects=True, vmem_limit_bytes=VMEM_LIMIT
        ),
        cost_estimate=pl.CostEstimate(
            flops=5_000_000_000, bytes_accessed=100_000_000, transcendentals=2_000_000
        ),
    )(*shards, tokens, cotangent, routes, gains, cosines, sines, seq_column, seq_row)


def gather_kernel(
    x_ref, meta_ref, onehot_ref, compact_ref, routes_ref, slots_ref, gate_ref,
    held, metas, stage, spare, lsem, ssem, rsem, msem, mrsem, osem,
):
    dp, z, dc, dx, dy = place()
    own = dp * 4 + z
    gather = AllGather(held, held.at[own], ssem, rsem, metas, metas.at[own], msem, mrsem)
    order = arrival_order(gather)
    picker = Dispatcher(held, stage, spare, slots_ref, osem)
    local = [
        pltpu.make_async_copy(x_ref, held.at[own], lsem.at[0]),
        pltpu.make_async_copy(meta_ref, metas.at[own], lsem.at[1]),
    ]
    for copy in local:
        copy.start()
    greet(
        [(dp + dc, z), (dp + dx, z), (dp + dy, z), (dp, gather.zr)],
        (dp, gather.zo), gather.mid, z * (3 - z) // 2,
    )
    gate_ref[:, 512:576, :] = jnp.zeros((8, 64, 128), jnp.float32)
    for copy in local:
        copy.wait()
    experts = (lax.broadcasted_iota(jnp.int32, (8, 128), 0) + dp * 8).astype(jnp.float32)

    def process(block):
        onehot = onehot_ref[block]
        gates_here = jnp.zeros((8, 128), jnp.float32)
        for j in range(TOPK):
            gates_here = gates_here + jnp.where(
                routes_ref[block, j : j + 1, :] == experts, metas[block, j : j + 1, :], 0.0
            )
        wide = jnp.broadcast_to(gates_here[:, None, :], (8, MAIN, 128)).reshape(128, 128)
        taken = onehot.astype(jnp.float32)
        main_gate = jnp.sum(taken[:128] * wide, axis=1, keepdims=True)
        spare_gate = jnp.sum(taken[128:] * wide, axis=1, keepdims=True)
        gate_ref[:, pl.ds(pl.multiple_of(block * MAIN, MAIN), MAIN), :] = jnp.broadcast_to(
            main_gate, (128, 128)
        ).reshape(8, MAIN, 128)
        spare_rows = pl.ds(pl.multiple_of(512 + (block // 8) * MAIN, MAIN), MAIN)
        gate_ref[:, spare_rows, :] = gate_ref[:, spare_rows, :] + jnp.broadcast_to(
            spare_gate, (128, 128)
        ).reshape(8, MAIN, 128)
        picker.block(block, onehot, compact_ref[block])

    for k in range(6):
        gather_forward(gather, k)
        gather_process(gather, order, k, process)
    picker.end()
    gather.drain()


def gather_slots(rows, meta, onehot, compact, routes):
    count, width = rows.shape
    anywhere = pl.BlockSpec(memory_space=pl.ANY)
    vmem = pl.BlockSpec(memory_space=pltpu.VMEM)
    dma = pltpu.SemaphoreType.DMA
    return pl.pallas_call(
        gather_kernel,
        name="gather_x",
        out_shape=(
            jax.ShapeDtypeStruct((8, 576, width), jnp.bfloat16),
            jax.ShapeDtypeStruct((8, 576, 128), jnp.float32),
        ),
        in_specs=[anywhere, anywhere, vmem, vmem, vmem],
        out_specs=(anywhere, vmem),
        scratch_shapes=[
            pltpu.VMEM((32, count, width), jnp.bfloat16),
            pltpu.VMEM((32, 8, 128), jnp.float32),
            pltpu.VMEM((2, 8, MAIN, width), jnp.bfloat16),
            pltpu.VMEM((32, 16, width), jnp.bfloat16),
            dma((2,)), dma((72,)), dma((32, 2)), dma((72,)), dma((32,)), dma((2,)),
        ],
        compiler_params=pltpu.CompilerParams(
            collective_id=1, has_side_effects=True, vmem_limit_bytes=VMEM_LIMIT
        ),
        cost_estimate=pl.CostEstimate(
            flops=4_300_000_000, bytes_accessed=100_000_000, transcendentals=0
        ),
    )(rows, meta, onehot, compact, routes)


def return_kernel(
    y_ref, g_ref, onehot_ref, outy_ref, outg_ref,
    rows_in, to_core, sums, ry0, rx1, rx0, ry1, rze, rzm, rzf,
    ysem, csend, crecv, xsend, xrecv, zsend, zrecv,
):
    dp, z, dc, dx, dy = place()
    zr, zo = z + 1 - 2 * (z % 2), 3 - z
    mid = z * (3 - z) > 0
    end = z * (3 - z) < 1
    half = 64
    sources, outs = (y_ref, g_ref), (outy_ref, outg_ref)
    zs = [3 - 3 * (z // 2), 2 - z // 2, zr, z]
    greet([(dp + dc, z), (dp + dx, z), (dp + dy, z), (dp, zr)], (dp, zo), mid, z * (3 - z) // 2)
    lo, hi = pl.ds(0, half), pl.ds(half, half)
    xsends, zsends = [[] for _ in range(8)], []

    def lanes_of(s):
        return pl.ds(0, sources[s // 4].shape[2])

    def tiles_of(s):
        width = sources[s // 4].shape[2]
        return [slice(i, min(i + 512, width)) for i in range(0, width, 512)]

    def dest(s, step):
        r = 3 - step % 4
        base = dp + dc - dc * (step // 4)
        return (base + (r % 2) * dx + (r // 2) * dy) * 4 + zs[s % 4]

    def fetch(s, block, slot):
        source, lanes = sources[s // 4], lanes_of(s)
        return [
            pltpu.make_async_copy(
                source.at[:, pl.ds(block * MAIN, MAIN), :],
                rows_in.at[slot, pl.ds(0, 8), :, lanes], ysem.at[slot, 0],
            ),
            pltpu.make_async_copy(
                source.at[:, pl.ds(512 + (block // 8) * MAIN, MAIN), :],
                rows_in.at[slot, pl.ds(8, 8), :, lanes], ysem.at[slot, 1],
            ),
        ]

    def partial_tile(block, slot, lanes):
        return lax.dot_general(
            onehot_ref[block], rows_in[slot, :, :, lanes].reshape(256, lanes.stop - lanes.start),
            (((0,), (0,)), ((), ())), preferred_element_type=jnp.float32,
        )

    def core_copy(r, s):
        lanes = lanes_of(s)
        return pltpu.make_async_remote_copy(
            to_core.at[s % 4, r, :, lanes], sums.at[s, r, :, lanes], csend.at[s, r], crecv.at[s, r],
            device_id=at(dp + dc, z), device_id_type=MESH,
        )

    def xy_copy(r, rows, target, index, s, dp_to):
        lanes = lanes_of(s)
        return pltpu.make_async_remote_copy(
            sums.at[s, r, rows, lanes], target.at[:, lanes], xsend.at[index, s], xrecv.at[index, s],
            device_id=at(dp_to, z), device_id_type=MESH,
        )

    def z_copy(s, target, index, z_to):
        lanes = lanes_of(s)
        index = 6 * (s // 4) + index
        return pltpu.make_async_remote_copy(
            sums.at[s, 0, :, lanes], target.at[:, lanes], zsend.at[index], zrecv.at[index],
            device_id=at(dp, z_to), device_id_type=MESH,
        )

    def add_to(s, r, rows, *others):
        lanes = lanes_of(s)
        total = sums[s, r, rows, lanes].astype(jnp.float32)
        for other in others:
            total = total + other[:, lanes].astype(jnp.float32)
        sums[s, r, rows, lanes] = total.astype(jnp.bfloat16)

    def stage_core(s):
        def load(block, slot, following=None):
            for copy in fetch(s, block, slot):
                copy.wait()
            if following is not None:
                for copy in fetch(s, following, 1 - slot):
                    copy.start()

        def partner(step, slot, following):
            r = 3 - step
            block = dest(s, step)
            load(block, slot, following)
            if s >= 4:
                core_copy(r, s - 4).wait_send()
            for lanes in tiles_of(s):
                to_core[s % 4, r, :, lanes] = partial_tile(block, slot, lanes).astype(jnp.bfloat16)
            core_copy(r, s).start()

        batch = [
            xy_copy(3, lo, ry0.at[1, s], 0, s, dp + dy),
            xy_copy(3, hi, rx1.at[1, s], 1, s, dp + dx),
            xy_copy(2, lo, ry0.at[0, s], 2, s, dp + dy),
            xy_copy(1, hi, rx1.at[0, s], 3, s, dp + dx),
        ]
        xsends[s].extend(batch)

        def both(i, carry):
            r = 3 - i
            block = dest(s, 4 + i)

            @pl.when(i < 3)
            def _():
                partner(i + 1, 1, block)

            late = i // 2
            following = (1 - late) * dest(s, i + 2) + late * dest(s, 5 + i)
            slot = i // 3
            load(block, slot)

            @pl.when(i < 3)
            def _():
                for copy in fetch(s, following, 1):
                    copy.start()

            if s < 7:

                @pl.when(i == 3)
                def _():
                    for copy in fetch(s + 1, dest(s + 1, 0), 0):
                        copy.start()

            core_copy(r, s).wait_recv()
            for lanes in tiles_of(s):
                sums[s, r, :, lanes] = (
                    partial_tile(block, slot, lanes) + sums[s, r, :, lanes].astype(jnp.float32)
                ).astype(jnp.bfloat16)
            for when, copies in enumerate((batch[:2], batch[2:3], batch[3:])):

                @pl.when(i == when)
                def _():
                    for copy in copies:
                        copy.start()

            return carry

        partner(0, 0, dest(s, 1))
        lax.fori_loop(0, 4, both, 0)

    def stage_cross(s):
        xsends[s][0].wait_recv()
        add_to(s, 1, lo, ry0.at[1, s])
        across = xy_copy(1, lo, rx0.at[s], 4, s, dp + dx)
        across.start()
        xsends[s][1].wait_recv()
        add_to(s, 2, hi, rx1.at[1, s])
        down = xy_copy(2, hi, ry1.at[s], 5, s, dp + dy)
        down.start()
        xsends[s].extend([across, down])

    def outward(s):
        return z_copy(s, rze.at[3 * (s // 4) + s % 4], s % 4, zr)

    def stage_line(s):
        for j in range(2, 6):
            xsends[s][j].wait_recv()
        if s % 4 < 3:
            add_to(s, 0, lo, ry0.at[0, s], rx0.at[s])
            add_to(s, 0, hi, rx1.at[0, s], ry1.at[s])
            copy = outward(s)
            zsends.append((copy, end))
            pl.when(end)(functools.partial(copy.start))
        else:
            out_ref, lanes = outs[s // 4], lanes_of(s)
            for rows, first, second in ((lo, ry0.at[0, s], rx0.at[s]), (hi, rx1.at[0, s], ry1.at[s])):
                out_ref[rows, :] = (
                    sums[s, 0, rows, lanes].astype(jnp.float32)
                    + first[:, lanes].astype(jnp.float32)
                    + second[:, lanes].astype(jnp.float32)
                )

    def stage_onward(s):
        p, k = s // 4, s % 4
        if k < 2:
            onward = z_copy(s, rzm.at[2 * p + k], 3 + k, zo)
        else:
            onward = z_copy(s, rzf.at[p], 5, zr)
        zsends.append((onward, mid))

        @pl.when(mid)
        def _():
            if k < 2:
                outward(s).wait_recv()
                add_to(s, 0, slice(None), rze.at[3 * p + k])
            else:
                z_copy(4 * p, rzm.at[2 * p], 3, zo).wait_recv()
                add_to(s, 0, slice(None), rzm.at[2 * p])
            onward.start()

    def stage_last(p):
        out_ref, lanes = outs[p], lanes_of(4 * p)

        @pl.when(end)
        def _():
            z_copy(4 * p + 2, rzf.at[p], 5, zr).wait_recv()
            out_ref[...] = out_ref[...] + rzf[p, :, lanes].astype(jnp.float32)

        @pl.when(mid)
        def _():
            outward(4 * p + 2).wait_recv()
            z_copy(4 * p + 1, rzm.at[2 * p + 1], 4, zo).wait_recv()
            out_ref[...] = (
                out_ref[...]
                + rze[3 * p + 2, :, lanes].astype(jnp.float32)
                + rzm[2 * p + 1, :, lanes].astype(jnp.float32)
            )

    for copy in fetch(0, dest(0, 0), 0):
        copy.start()
    for t in range(10):
        if t < 8:
            stage_core(t)
        if 1 <= t < 9:
            stage_cross(t - 1)
        if t >= 2:
            stage_line(t - 2)
        if t % 4 == 3:
            stage_onward(t - 3)
        if t >= 4 and t % 4 == 0:
            stage_onward(t - 2)
            stage_onward(t - 3)
        if t >= 5 and t % 4 == 1:
            stage_last(t // 4 - 1)
    for s in range(4, 8):
        for r in range(4):
            core_copy(r, s).wait_send()
    for batch in xsends:
        for copy in batch:
            copy.wait_send()
    for copy, cond in zsends:
        pl.when(cond)(functools.partial(copy.wait_send))


def return_rows(y_slots, gin_slots, onehot):
    width, narrow = y_slots.shape[2], gin_slots.shape[2]
    anywhere = pl.BlockSpec(memory_space=pl.ANY)
    vmem = pl.BlockSpec(memory_space=pltpu.VMEM)
    dma = pltpu.SemaphoreType.DMA
    low = jnp.bfloat16
    return pl.pallas_call(
        return_kernel,
        name="return_rows",
        out_shape=(
            jax.ShapeDtypeStruct((128, width), jnp.float32),
            jax.ShapeDtypeStruct((128, narrow), jnp.float32),
        ),
        in_specs=[anywhere, anywhere, vmem],
        out_specs=(vmem, vmem),
        scratch_shapes=[
            pltpu.VMEM((2, 16, MAIN, width), low),
            pltpu.VMEM((4, 4, 128, width), low),
            pltpu.VMEM((8, 4, 128, width), low),
            pltpu.VMEM((2, 8, 64, width), low),
            pltpu.VMEM((2, 8, 64, width), low),
            pltpu.VMEM((8, 64, width), low),
            pltpu.VMEM((8, 64, width), low),
            pltpu.VMEM((6, 128, width), low),
            pltpu.VMEM((4, 128, width), low),
            pltpu.VMEM((2, 128, width), low),
            dma((2, 2)), dma((8, 4)), dma((8, 4)), dma((6, 8)), dma((6, 8)), dma((12,)), dma((12,)),
        ],
        compiler_params=pltpu.CompilerParams(
            collective_id=2, has_side_effects=True, vmem_limit_bytes=VMEM_LIMIT
        ),
        cost_estimate=pl.CostEstimate(
            flops=8_600_000_000, bytes_accessed=300_000_000, transcendentals=0
        ),
    )(y_slots, gin_slots, onehot)


def finish_kernel(
    rows_ref, tok_ref, projq_ref, projk_ref, query_ref, key_ref, value_ref, ctx_ref, ga_ref, w_ref,
    gains_ref, cos_ref, sin_ref, seqc_ref, seqr_ref, side_ref, stat_ref,
    gw_ref, gwo_ref, back_ref, small_ref,
    dx_ref, gqkv_ref, gctx_ref, dx_all, to_core, from_core, sums, ry0, rx1, rx0, ry1, gain, zside,
    csend, crecv, xsend, xrecv, ssend, srecv, *line_refs,
):
    dp, z, dc, dx, dy = place()
    line = LineScatter(dp, z, *line_refs)
    dxs = line.blocks
    f32, low = jnp.float32, jnp.bfloat16
    half = 128
    heads = query_ref.shape[1]
    width = rows_ref.shape[1]
    others = [(z + i) % 4 for i in (1, 2, 3)]
    greet([(dp + dc, z), (dp + dx, z), (dp + dy, z)] + [(dp, other) for other in others])
    nt = (((1,), (1,)), ((), ()))
    tn = (((0,), (0,)), ((), ()))
    lo, hi = pl.ds(0, half), pl.ds(half, half)
    early = 3 * heads + 128

    def mm(a, b, dims):
        return lax.dot_general(a, b, dims, preferred_element_type=f32)

    def dest(step):
        r = 3 - step % 4
        base = dp + dc - dc * (step // 4)
        return base + (r % 2) * dx + (r // 2) * dy

    def scatter(index, first, count, pieces):
        lanes = pl.ds(first, count)

        def core_copy(r):
            return pltpu.make_async_remote_copy(
                to_core.at[r, :, lanes], from_core.at[r, :, lanes],
                csend.at[index, r], crecv.at[index, r],
                device_id=at(dp + dc, z), device_id_type=MESH,
            )

        def xy_copy(r, rows, target, j, dp_to):
            return pltpu.make_async_remote_copy(
                sums.at[r, rows, lanes], target.at[:, lanes], xsend.at[index, j], xrecv.at[index, j],
                device_id=at(dp_to, z), device_id_type=MESH,
            )

        def add_to(r, rows, part):
            total = sums[r, rows, lanes].astype(f32) + part[:, lanes].astype(f32)
            sums[r, rows, lanes] = total.astype(low)

        copies = [
            xy_copy(3, lo, ry0.at[1], 0, dp + dy),
            xy_copy(3, hi, rx1.at[1], 1, dp + dx),
            xy_copy(2, lo, ry0.at[0], 2, dp + dy),
            xy_copy(1, hi, rx1.at[0], 3, dp + dx),
            xy_copy(1, lo, rx0, 4, dp + dx),
            xy_copy(2, hi, ry1, 5, dp + dy),
        ]

        def partner(step):
            r = 3 - step
            for part, value in pieces(dest(step)):
                to_core[r, :, part] = value.astype(low)
            core_copy(r).start()

        def both(i, carry):
            @pl.when(i < 3)
            def _():
                partner(i + 1)

            r = 3 - i
            core_copy(r).wait_recv()
            for part, value in pieces(dest(4 + i)):
                sums[r, :, part] = (value + from_core[r, :, part].astype(f32)).astype(low)
            for when, batch in enumerate((copies[:2], copies[2:3], copies[3:4])):

                @pl.when(i == when)
                def _():
                    for copy in batch:
                        copy.start()

            return carry

        def core():
            partner(0)
            lax.fori_loop(0, 4, both, 0)

        def cross():
            copies[0].wait_recv()
            add_to(1, lo, ry0.at[1])
            copies[4].start()
            copies[1].wait_recv()
            add_to(2, hi, rx1.at[1])
            copies[5].start()

        def wait():
            for copy in copies[2:]:
                copy.wait_recv()

        def drain():
            for r in range(4):
                core_copy(r).wait_send()
            for copy in copies:
                copy.wait_send()

        return core, cross, wait, drain

    def out_pieces(to):
        cols = pl.ds(pl.multiple_of(to * 256, 256), 256)
        out = mm(ctx_ref[...], ga_ref[:, cols], tn)
        yield slice(early, early + 256), out[:256]
        yield slice(early + 256, early + 512), out[256:]

    def head_pieces(to):
        cols = pl.ds(pl.multiple_of(to * 256, 256), 256)
        yield slice(0, 3 * heads), mm(rows_ref[:, cols], gqkv_ref[...], tn)
        yield slice(3 * heads, early), jnp.concatenate(
            [
                side_ref[to, :128, :].astype(f32),
                side_ref[to, 128:144, :].astype(f32) + gain[to],
                jnp.zeros((112, 128), f32),
            ],
            axis=0,
        )

    core_out, cross_out, wait_out, drain_out = scatter(0, early, heads, out_pieces)
    core_heads, cross_heads, wait_heads, drain_heads = scatter(1, 0, early, head_pieces)
    core_out()
    gain[...] = jnp.zeros_like(gain)
    cosines, sines = cos_ref[...], sin_ref[...]
    query_gain, key_gain = head_gain(gains_ref, 0), head_gain(gains_ref, 16)
    for i in range(2):
        column = 3 * heads + i * 256
        total_ctx = jnp.zeros((512, 256), f32)
        for start in range(0, width, 256):
            lanes = slice(start, start + 256)
            total_ctx = total_ctx + mm(ga_ref[:, lanes], w_ref[lanes, column : column + 256], nt)
        gctx_ref[:, i * 256 : i * 256 + 256] = total_ctx.astype(low)
    score_scale = HD ** (-0.5)

    def head_back(grad, source, rows, cols, gain_values, column):
        values = source[rows, cols]
        inverse = lax.rsqrt(jnp.mean(values * values, axis=1, keepdims=True) + EPSILON)
        turned = grad * cosines[rows] - pltpu.roll(grad, HD // 2, 1) * sines[rows]
        scaled = turned * gain_values
        inner = jnp.mean(scaled * values, axis=1, keepdims=True)
        target = pl.ds(pl.multiple_of(cols.start + column, HD), HD)
        gqkv_ref[rows, target] = ((scaled - values * inner * inverse * inverse) * inverse).astype(low)
        return jnp.sum(turned * values * inverse, axis=0, keepdims=True)

    def one_head(h, carry):
        query_part, key_part = carry
        cols = pl.ds(pl.multiple_of(h * HD, HD), HD)
        key, value = key_ref[:, cols], value_ref[:, cols]
        grad_key = jnp.zeros((key.shape[0], HD), f32)
        grad_value = jnp.zeros((key.shape[0], HD), f32)
        for start in range(0, 512, 256):
            rows = slice(start, start + 256)
            query, grad_ctx = query_ref[rows, cols], gctx_ref[rows, cols]
            probs = head_probs(query, key, seqc_ref[rows, :1], seqr_ref[:1, :])
            grad_value = grad_value + mm(probs.astype(low), grad_ctx, tn)
            grad_probs = mm(grad_ctx, value, nt)
            inner = jnp.sum(probs * grad_probs, axis=1, keepdims=True)
            grad_scores = (probs * (grad_probs - inner)).astype(low)
            grad_query = jnp.dot(grad_scores, key, preferred_element_type=f32) * score_scale
            grad_key = grad_key + mm(grad_scores, query, tn)
            query_part = query_part + head_back(
                grad_query, projq_ref, rows, cols, query_gain, 0
            )
        key_part = key_part + head_back(
            grad_key * score_scale, projk_ref, slice(0, 512), cols, key_gain, heads
        )
        target = pl.ds(pl.multiple_of(cols.start + 2 * heads, HD), HD)
        gqkv_ref[:, target] = grad_value.astype(low)
        return query_part, key_part

    zero_row = jnp.zeros((1, HD), f32)
    query_part, key_part = lax.fori_loop(0, heads // HD, one_head, (zero_row, zero_row))
    for to in range(8):
        gain[to, 4:5, :] = query_part
        gain[to, 5:6, :] = key_part
    cross_out()
    for start in range(0, width, 512):
        lanes = slice(start, start + 512)
        dx_all[:, lanes] = mm(gqkv_ref[...], w_ref[lanes, : 3 * heads], nt)
    for k in range(4):
        rows = pl.ds(pl.multiple_of(line.zs[k] * 128, 128), 128)
        square = jnp.zeros((128, 1), f32)
        for start in range(0, width, 512):
            values = tok_ref[rows, start : start + 512].astype(f32)
            square = square + jnp.sum(values * values, axis=1, keepdims=True)
        inverse = lax.rsqrt(square * (1.0 / width) + EPSILON)
        for start in range(0, width, 512):
            lanes = slice(start, start + 512)
            piece = dx_all[rows, lanes]
            scaled = tok_ref[rows, lanes].astype(f32) * inverse
            column = jnp.sum(piece * scaled, axis=0, keepdims=True)
            for j in range(4):
                to = start // 256 + j // 2
                row = slice(j % 2, j % 2 + 1)
                gain[to, row, :] = gain[to, row, :] + column[:, j * 128 : j * 128 + 128]
            if k < 3:
                dxs[k, :, lanes] = piece.astype(low)
            else:
                dx_ref[:, lanes] = piece
        if k < 3:
            line.ready(k)

    core_heads()
    line.onward(0)
    cross_heads()
    line.onward(1)
    line.onward(2)
    wait_out()
    wait_heads()

    def side_copy(i, source):
        return pltpu.make_async_remote_copy(
            zside.at[source], zside.at[source], ssend.at[i], srecv.at[source],
            device_id=at(dp, others[i]), device_id_type=MESH,
        )

    def total(part, lanes, first, second):
        return (
            sums[0, part, lanes].astype(f32)
            + first[:, lanes].astype(f32)
            + second[:, lanes].astype(f32)
        )

    sides = slice(3 * heads, early)
    zside[z, :128, :] = total(lo, sides, ry0.at[0], rx0)
    zside[z, 128:144, :] = total(hi, sides, rx1.at[0], ry1)[:16] + stat_ref[...]
    for i in range(3):
        side_copy(i, z).start()
    for rows, first, second in ((lo, ry0.at[0], rx0), (hi, rx1.at[0], ry1)):
        gw_ref[rows, :] = total(rows, slice(0, 3 * heads), first, second)
        gwo_ref[rows, :] = total(rows, slice(early, early + 256), first, second)
        below = pl.ds(256 + rows.start, half)
        gwo_ref[below, :] = total(rows, slice(early + 256, early + 512), first, second)

    line.last(dx_ref)
    scale = jnp.concatenate(
        [gains_ref[j // 2, j % 2 : j % 2 + 1, :] for j in range(width // 128)], axis=1
    )

    def norm_back(index, carry):
        rows = pl.ds(pl.multiple_of(index * 32, 32), 32)
        values = tok_ref[pl.ds(pl.multiple_of(z * 128 + index * 32, 32), 32), :].astype(f32)
        inverse = lax.rsqrt(jnp.mean(values * values, axis=1, keepdims=True) + EPSILON)
        scaled = dx_ref[rows, :] * scale
        inner = jnp.mean(scaled * values, axis=1, keepdims=True)
        back_ref[rows, :] = (scaled - values * (inner * inverse * inverse)) * inverse
        return carry

    lax.fori_loop(0, 4, norm_back, 0)
    for i in range(3):
        side_copy(i, others[i]).wait_recv()
    small_ref[...] = (zside[0] + zside[1]) + (zside[2] + zside[3])
    drain_out()
    drain_heads()
    line.drain()
    for i in range(3):
        side_copy(i, z).wait_send()


def finish(rows, tok, attention, grad_attn, weights, tables, side, stats):
    width = rows.shape[1]
    heads = attention[0].shape[1]
    f32, low = jnp.float32, jnp.bfloat16
    vmem = pl.BlockSpec(memory_space=pltpu.VMEM)
    dma = pltpu.SemaphoreType.DMA
    packed = 4 * heads + 128
    return pl.pallas_call(
        finish_kernel,
        name="finish",
        out_shape=(
            jax.ShapeDtypeStruct((256, 3 * heads), f32),
            jax.ShapeDtypeStruct((heads, 256), f32),
            jax.ShapeDtypeStruct((128, width), f32),
            jax.ShapeDtypeStruct((144, 128), f32),
        ),
        in_specs=[vmem] * 17,
        out_specs=(vmem,) * 4,
        scratch_shapes=[
            pltpu.VMEM((128, width), f32),
            pltpu.VMEM((512, 3 * heads), low),
            pltpu.VMEM((512, heads), low),
            pltpu.VMEM((512, width), f32),
        ]
        + [
            pltpu.VMEM((4, 256, packed), low),
            pltpu.VMEM((4, 256, packed), low),
            pltpu.VMEM((4, 256, packed), low),
            pltpu.VMEM((2, 128, packed), low),
            pltpu.VMEM((2, 128, packed), low),
            pltpu.VMEM((128, packed), low),
            pltpu.VMEM((128, packed), low),
            pltpu.VMEM((8, 16, 128), f32),
            pltpu.VMEM((4, 144, 128), f32),
            dma((2, 4)), dma((2, 4)), dma((2, 6)), dma((2, 6)), dma((3,)), dma((4,)),
        ]
        + LineScatter.scratch(width),
        compiler_params=pltpu.CompilerParams(
            collective_id=4, has_side_effects=True, vmem_limit_bytes=VMEM_LIMIT
        ),
        cost_estimate=pl.CostEstimate(
            flops=8_000_000_000, bytes_accessed=100_000_000, transcendentals=0
        ),
    )(rows, tok, *attention, grad_attn, weights, *tables, side, stats)


def expert_kernel(
    x_ref, dy_ref, gate_ref, wg_ref, wu_ref, wd_ref, y_ref, gin_ref, dgate_ref, dup_ref, hgated_ref,
    gate_pre_ref, up_pre_ref, raw_ref,
):
    rows, ff = dgate_ref.shape[1:]
    width = x_ref.shape[2]
    expert = lax.axis_index("dp") * 8 + pl.program_id(0)
    nt = (((1,), (1,)), ((), ()))

    def mm(a, b, dims):
        return lax.dot_general(a, b, dims, preferred_element_type=jnp.float32)

    gate_pre_ref[...] = jnp.dot(x_ref[0], wg_ref[0], preferred_element_type=jnp.float32)
    up_pre_ref[...] = jnp.dot(x_ref[0], wu_ref[0], preferred_element_type=jnp.float32)
    raw_ref[...] = mm(dy_ref[0], wd_ref[0], nt)
    step = 96

    def pointwise(index, carry):
        part = pl.ds(pl.multiple_of(index * step, step), step)
        gate_pre, up_pre, raw = gate_pre_ref[part, :], up_pre_ref[part, :], raw_ref[part, :]
        weight = jnp.concatenate([gate_ref[0, part, :]] * (ff // 128), axis=1)
        sig = jax.nn.sigmoid(gate_pre)
        silu = gate_pre * sig
        hidden = silu * up_pre
        route_grad = jnp.sum(hidden * raw, axis=1, keepdims=True)
        grad_hidden = weight * raw
        lane = lax.broadcasted_iota(jnp.int32, (step, 128), 1)
        high = route_grad.astype(jnp.bfloat16).astype(jnp.float32)
        extra = jnp.where(lane == expert, high, 0.0) + jnp.where(
            lane == expert + 64, route_grad - high, 0.0
        )
        hgated_ref[0, part, :] = (weight * hidden).astype(jnp.bfloat16)
        dgate_ref[0, part, :] = (
            grad_hidden * up_pre * sig * (1.0 + gate_pre * (1.0 - sig))
        ).astype(jnp.bfloat16)
        dup_ref[0, part, :] = (grad_hidden * silu).astype(jnp.bfloat16)
        y_ref[0, part, width:] = extra.astype(jnp.bfloat16)
        return carry

    lax.fori_loop(0, rows // step, pointwise, 0)
    for start in range(0, width, 512):
        lanes = slice(start, start + 512)
        y_ref[0, :, lanes] = jnp.dot(
            hgated_ref[0], wd_ref[0, :, lanes], preferred_element_type=jnp.float32
        ).astype(jnp.bfloat16)
        gin_ref[0, :, lanes] = (
            mm(dgate_ref[0], wg_ref[0, lanes, :], nt) + mm(dup_ref[0], wu_ref[0, lanes, :], nt)
        ).astype(jnp.bfloat16)


def weights_kernel(x_ref, dy_ref, dgate_ref, dup_ref, hgated_ref, gwg_ref, gwu_ref, gwd_ref):
    width = x_ref.shape[2]
    tn = (((0,), (0,)), ((), ()))

    def mm(a, b):
        return lax.dot_general(a, b, tn, preferred_element_type=jnp.float32)

    for start in range(0, width, 512):
        part = slice(start, start + 512)
        gwd_ref[0, :, part] = mm(hgated_ref[0], dy_ref[0, :, part])
        xs = x_ref[0, :, part]
        gwg_ref[0, part, :] = mm(xs, dgate_ref[0])
        gwu_ref[0, part, :] = mm(xs, dup_ref[0])


def expert_spec(*shape):
    return pl.BlockSpec((1,) + shape, lambda e: (e, 0, 0))


def run_experts(x_slots, dy_slots, gate_slots, w_gate, w_up, w_down):
    experts, rows, width = x_slots.shape
    ff = w_gate.shape[2]
    spec, low = expert_spec, jnp.bfloat16
    middle = jax.ShapeDtypeStruct((experts, rows, ff), low)
    return pl.pallas_call(
        expert_kernel,
        name="experts",
        grid=(experts,),
        in_specs=[
            spec(rows, width), spec(rows, width), spec(rows, 128),
            spec(width, ff), spec(width, ff), spec(ff, width),
        ],
        out_specs=(spec(rows, width + 128), spec(rows, width)) + (spec(rows, ff),) * 3,
        out_shape=(
            jax.ShapeDtypeStruct((experts, rows, width + 128), low),
            jax.ShapeDtypeStruct((experts, rows, width), low),
            middle, middle, middle,
        ),
        scratch_shapes=[pltpu.VMEM((rows, ff), jnp.float32)] * 3,
        compiler_params=pltpu.CompilerParams(vmem_limit_bytes=VMEM_LIMIT),
        cost_estimate=pl.CostEstimate(
            flops=29_000_000_000, bytes_accessed=100_000_000, transcendentals=2_000_000
        ),
    )(x_slots, dy_slots, gate_slots, w_gate, w_up, w_down)


def run_weights(x_slots, dy_slots, dgate, dup, hgated):
    experts, rows, width = x_slots.shape
    ff = dgate.shape[2]
    spec, f32 = expert_spec, jnp.float32
    wide = jax.ShapeDtypeStruct((experts, width, ff), f32)
    return pl.pallas_call(
        weights_kernel,
        name="expert_weights",
        grid=(experts,),
        in_specs=[spec(rows, width)] * 2 + [spec(rows, ff)] * 3,
        out_specs=(spec(width, ff), spec(width, ff), spec(ff, width)),
        out_shape=(wide, wide, jax.ShapeDtypeStruct((experts, ff, width), f32)),
        compiler_params=pltpu.CompilerParams(vmem_limit_bytes=VMEM_LIMIT),
        cost_estimate=pl.CostEstimate(
            flops=15_000_000_000, bytes_accessed=100_000_000, transcendentals=0
        ),
    )(x_slots, dy_slots, dgate, dup, hgated)


def plain_onehot(routes_all, first_expert, local_experts):
    sources, rows = routes_all.shape[0], routes_all.shape[1]
    experts = jnp.arange(local_experts, dtype=jnp.int32) + first_expert
    member = jnp.any(routes_all[:, :, :, None] == experts, axis=2).astype(jnp.int32)
    rank = jnp.cumsum(member, axis=1) - member
    rank = jnp.where(member > 0, rank, -1)
    return (
        rank.transpose(0, 2, 1)[:, :, None, :] == jnp.arange(CAP, dtype=jnp.int32)[:, None]
    ).astype(jnp.bfloat16)


def plain_experts(moe_low, cotangent, routes, gates, w_gate, w_up, w_down):
    both = ("dp", "tensor")
    local_experts = w_gate.shape[0]
    width = moe_low.shape[1]
    f32 = jnp.float32
    routes_all = lax.all_gather(routes, both, axis=0)
    x_all = lax.all_gather(moe_low, both, axis=0)
    dy_all = lax.all_gather(cotangent, both, axis=0)
    gates_all = lax.all_gather(gates, both, axis=0)
    first_expert = lax.axis_index("dp") * local_experts
    onehot = plain_onehot(routes_all, first_expert, local_experts)
    take = functools.partial(jnp.einsum, "sect,std->escd")
    flat = (local_experts, -1, width)
    x_slots = take(onehot, x_all).reshape(flat)
    dy_slots = take(onehot, dy_all).reshape(flat)
    experts = jnp.arange(local_experts, dtype=jnp.int32) + first_expert
    gates_here = jnp.sum(
        jnp.where(routes_all[..., None] == experts, gates_all[..., None], 0.0), axis=2
    )
    weight = jnp.einsum(
        "sect,ste->esc", onehot.astype(f32), gates_here, precision=lax.Precision.HIGHEST
    ).reshape(local_experts, -1)[..., None]
    mm = functools.partial(jnp.einsum, preferred_element_type=f32)
    gate_pre = mm("ecd,edf->ecf", x_slots, w_gate)
    up_pre = mm("ecd,edf->ecf", x_slots, w_up)
    raw = mm("ecd,efd->ecf", dy_slots, w_down)
    sig = jax.nn.sigmoid(gate_pre)
    silu = gate_pre * sig
    hidden = silu * up_pre
    hgated = (weight * hidden).astype(jnp.bfloat16)
    route_grad = jnp.sum(hidden * raw, axis=2).reshape(local_experts, -1, CAP)
    grad_hidden = weight * raw
    dgate = (grad_hidden * up_pre * sig * (1.0 + gate_pre * (1.0 - sig))).astype(jnp.bfloat16)
    dup = (grad_hidden * silu).astype(jnp.bfloat16)
    y_slots = mm("ecf,efd->ecd", hgated, w_down).astype(jnp.bfloat16)
    gin_slots = (mm("ecf,edf->ecd", dgate, w_gate) + mm("ecf,edf->ecd", dup, w_up)).astype(
        jnp.bfloat16
    )
    grads = (
        mm("ecd,ecf->edf", x_slots, dgate),
        mm("ecd,ecf->edf", x_slots, dup),
        mm("ecf,ecd->efd", hgated, dy_slots),
    )

    def give_back(slots):
        slots = slots.reshape(local_experts, -1, CAP, width)
        rows = mm("sect,escd->std", onehot, slots).astype(jnp.bfloat16)
        return lax.psum_scatter(
            rows.reshape(-1, width), both, scatter_dimension=0, tiled=True
        ).astype(f32)

    here = jnp.einsum(
        "sect,esc->ste", onehot.astype(f32), route_grad, precision=lax.Precision.HIGHEST
    )
    spread = jnp.zeros(here.shape[:2] + (EXPERTS,), f32)
    spread = lax.dynamic_update_slice(spread, here, (0, 0, first_expert))
    grad_gates = lax.psum_scatter(
        spread.reshape(-1, EXPERTS), both, scatter_dimension=0, tiled=True
    )
    return (give_back(y_slots), grad_gates, give_back(gin_slots), lambda own_rows: grads)


def routed_experts(moe_low, cotangent, routes, gates, w_gate, w_up, w_down, dispatched):
    if dispatched is None:
        return plain_experts(moe_low, cotangent, routes, gates, w_gate, w_up, w_down)
    dy_slots, onehot, compact, all_routes = dispatched
    width = moe_low.shape[1]
    x_slots, gate_slots = gather_slots(moe_low, gates.T, onehot, compact, all_routes)
    y_slots, gin_slots, *middle = run_experts(
        x_slots, dy_slots, gate_slots, w_gate, w_up, w_down
    )
    sums, grad_in = return_rows(y_slots, gin_slots, onehot)
    grad_gates = sums[:, width : width + EXPERTS] + sums[:, width + EXPERTS :]

    def weight_grads(own_rows):
        hgated, unused = lax.optimization_barrier((middle[2], own_rows))
        return run_weights(x_slots, dy_slots, middle[0], middle[1], hgated)

    return (sums[:, :width], grad_gates, grad_in, weight_grads)


def own_kernels(tokens, w_gate):
    return (
        lax.axis_size("dp") == 8
        and lax.axis_size("tensor") == 4
        and tokens.shape == (128, 2048)
        and w_gate.shape[0] == 8
    )


def side_columns(pieces, rows):
    filled = [jnp.pad(p, ((0, rows - p.shape[0]), (0, 0))) for p in pieces]
    used = sum(p.shape[1] for p in filled)
    return jnp.concatenate(filled + [jnp.zeros((rows, 128 - used), filled[0].dtype)], axis=1)


def body(
    tokens,
    cotangent,
    lengths,
    seq_order,
    routes,
    attn_gain,
    w_query,
    w_key,
    w_value,
    w_output,
    query_gain,
    key_gain,
    ffn_gain,
    router,
    w_gate,
    w_up,
    w_down,
):
    tok_rows, model_width = tokens.shape
    tensor_count = lax.axis_size("tensor")
    data_count = lax.axis_size("dp")
    group_rows_count = tok_rows * tensor_count
    block_rows = min(group_rows_count, 512)
    shard = w_query.shape[0]
    heads_width = w_query.shape[1]
    gain_rows = query_gain.shape[0]
    low = jnp.bfloat16
    f32 = jnp.float32

    own = own_kernels(tokens, w_gate)

    seq_ids, positions = arrival_layout(lengths[0], seq_order[0])
    resid_in = tokens.astype(f32)
    if own:
        gains, filled = jnp.zeros((1024,), f32), 0
        for part in (attn_gain, ffn_gain, query_gain, key_gain):
            count = part.shape[0]
            gains = gains + jnp.pad(part.astype(f32), (filled, 1024 - filled - count))
            filled += count
        gains = gains.reshape(8, 128)
        shards = (w_query, w_key, w_value, w_output, jnp.pad(router, ((0, 0), (0, 128 - EXPERTS))))
        seq_float = seq_ids.astype(f32)
        lane = jnp.arange(HD, dtype=jnp.int32)
        frequency = THETA ** (-(lane % (HD // 2)).astype(f32) / (HD // 2))
        angles = positions.astype(f32)[:, None] * frequency[None, :]
        tables = (
            jnp.cos(angles),
            jnp.sin(angles) * jnp.where(lane < HD // 2, -1.0, 1.0),
            jnp.broadcast_to(seq_float[:, None], (group_rows_count, 128)),
            jnp.broadcast_to(seq_float[None, :], (8, group_rows_count)),
        )
        (
            weights, group_tokens, dy_slots, all_gains, onehot, compact, all_routes, group_rows,
            *attention, attn_out,
        ) = front(shards, tokens, cotangent, routes.T.astype(f32), gains, *tables, heads_width)
        dispatched = (dy_slots, onehot, compact, all_routes)
        group_tokens = group_tokens.reshape(-1, model_width)
        full_router = weights[:, 4 * heads_width : 4 * heads_width + EXPERTS]
        ffn_scale = all_gains[:, 2:4].reshape(-1)
    else:
        side = side_columns(
            [router, attn_gain[:, None], ffn_gain[:, None], query_gain[:, None], key_gain[:, None]],
            shard,
        )
        packed = jnp.concatenate([w_query, w_key, w_value, w_output.T, side], axis=1)
        weights = lax.all_gather(packed, "dp", axis=0, tiled=True)
        group_tokens = lax.all_gather(tokens, "tensor", axis=0, tiled=True)
        dispatched = None
        full_query = weights[:, :heads_width]
        full_key = weights[:, heads_width : 2 * heads_width]
        full_value = weights[:, 2 * heads_width : 3 * heads_width]
        output_t = weights[:, 3 * heads_width : 4 * heads_width]
        extras = weights[:, 4 * heads_width :]
        full_router = extras[:, :EXPERTS]
        attn_scale = extras[:, EXPERTS].astype(f32)
        ffn_scale = extras[:, EXPERTS + 1].astype(f32)
        gain_columns = extras.reshape(data_count, shard, 128)[:, :gain_rows, EXPERTS + 2 : EXPERTS + 4]
        query_scale = gain_columns[:, :, 0].reshape(-1).astype(f32)
        key_scale = gain_columns[:, :, 1].reshape(-1).astype(f32)

        cosines, sines = rope_tables(positions)
        group_rows = norm_apply(group_tokens.astype(f32), attn_scale).astype(low)
        proj_query = jnp.dot(group_rows, full_query, preferred_element_type=f32)
        proj_key = jnp.dot(group_rows, full_key, preferred_element_type=f32)
        value_flat = jnp.dot(group_rows, full_value, preferred_element_type=f32).astype(low)
        value_low = value_flat.reshape(group_rows_count, -1, HD)
        query_low = head_norm_rope(proj_query, query_scale, cosines, sines).astype(low)
        key_low = head_norm_rope(proj_key, key_scale, cosines, sines).astype(low)
        context, row_lse = attend(query_low, key_low, value_low, seq_ids, block_rows)
        context_low = context.reshape(group_rows_count, -1).astype(low)
        attn_out = lax.psum_scatter(
            lax.dot_general(
                context_low, output_t, (((1,), (1,)), ((), ())), preferred_element_type=f32
            ).astype(low),
            "tensor",
            scatter_dimension=0,
            tiled=True,
        ).astype(f32)
    resid_mid = resid_in + attn_out
    moe_low = norm_apply(resid_mid, ffn_scale).astype(low)
    logits = jnp.dot(moe_low, full_router, preferred_element_type=f32)
    route_match = routes[:, :, None] == jnp.arange(EXPERTS, dtype=jnp.int32)[None, None, :]
    picked_logits = jnp.sum(jnp.where(route_match, logits[:, None, :], 0.0), axis=-1)
    gate_peak = jnp.max(picked_logits, axis=1, keepdims=True)
    gate_raw = jnp.exp(picked_logits - gate_peak)
    gates = gate_raw / jnp.sum(gate_raw, axis=1, keepdims=True)
    dense_gates = jnp.sum(jnp.where(route_match, gates[:, :, None], 0.0), axis=1)

    moe_out, grad_gates, grad_from_experts, expert_weight_grads = routed_experts(
        moe_low, cotangent, routes, gates, w_gate, w_up, w_down, dispatched
    )
    layer_out = (resid_mid + moe_out).astype(low)
    stat_terms = jnp.stack(
        [jnp.sum(resid_mid * resid_mid), jnp.sum(attn_out * attn_out), jnp.sum(moe_out * moe_out)]
    )
    grad_out = cotangent.astype(f32)
    inner_gate = jnp.sum(dense_gates * grad_gates, axis=1, keepdims=True)
    grad_logits_low = (dense_gates * (grad_gates - inner_gate)).astype(low)
    grad_router_part = jnp.dot(moe_low.T, grad_logits_low, preferred_element_type=f32)
    grad_moe_in = grad_from_experts + jnp.dot(
        grad_logits_low, full_router.T, preferred_element_type=f32
    )
    unused_mid, ffn_back = jax.vjp(norm_apply, resid_mid, ffn_scale)
    grad_mid_norm, grad_ffn_part = ffn_back(grad_moe_in)
    grad_mid = grad_out + grad_mid_norm
    grad_attn_low = grad_mid.astype(low)
    grad_attn_rows = lax.all_gather(grad_attn_low, "tensor", axis=0, tiled=True)
    grad_gate_w, grad_up_w, grad_down = expert_weight_grads(grad_attn_low)
    tn = (((0,), (0,)), ((), ()))
    if own:
        router_side = grad_router_part.reshape(8, 2, 128, EXPERTS).swapaxes(1, 2).reshape(8, 128, 128)

        side = jnp.concatenate(
            [
                router_side,
                jnp.zeros((8, 2, 128), f32),
                grad_ffn_part.reshape(8, 2, 128),
                jnp.zeros((8, 12, 128), f32),
            ],
            axis=1,
        ).astype(low)
        stats = jnp.pad(stat_terms[None, :], ((6, 9), (0, 125)))
        packed_grads, grad_out_w, grad_in_norm, small = finish(
            group_rows, group_tokens, attention, grad_attn_rows, weights, (all_gains,) + tables,
            side, stats,
        )
        grads_qkv = [packed_grads[:, i * heads_width : (i + 1) * heads_width] for i in range(3)]
        grad_router = jnp.concatenate([small[:128, :EXPERTS], small[:128, EXPERTS:]], axis=0)
        grad_attn_gain = small[128:130].reshape(-1)
        grad_ffn_gain = small[130:132].reshape(-1)
        first_lane = lax.axis_index("dp") * gain_rows
        grad_query_gain = lax.dynamic_slice(small[132], (first_lane,), (gain_rows,))
        grad_key_gain = lax.dynamic_slice(small[133], (first_lane,), (gain_rows,))
        stat_totals = small[134, :3]
    else:
        grad_ctx_low = jnp.dot(grad_attn_rows, output_t, preferred_element_type=f32).astype(low)
        grad_query, grad_key, grad_value = attend_back(
            query_low,
            key_low,
            value_low,
            seq_ids,
            row_lse,
            grad_ctx_low.reshape(value_low.shape),
            block_rows,
        )
        grad_value_low = grad_value.reshape(group_rows_count, -1).astype(low)
        unused_query, query_back = jax.vjp(
            lambda projected, head_gain: head_norm_rope(projected, head_gain, cosines, sines),
            proj_query,
            query_scale,
        )
        grad_proj_query, grad_query_gain_part = query_back(grad_query)
        unused_key, key_back = jax.vjp(
            lambda projected, head_gain: head_norm_rope(projected, head_gain, cosines, sines),
            proj_key,
            key_scale,
        )
        grad_proj_key, grad_key_gain_part = key_back(grad_key)
        grad_query_low = grad_proj_query.astype(low)
        grad_key_low = grad_proj_key.astype(low)
        head_grads = (grad_query_low, grad_key_low, grad_value_low)
        weight_grads = [
            lax.dot_general(group_rows, part, tn, preferred_element_type=f32) for part in head_grads
        ]
        grad_output_t = lax.dot_general(grad_attn_rows, context_low, tn, preferred_element_type=f32)
        total_rows = jnp.dot(grad_query_low, full_query.T, preferred_element_type=f32)
        total_rows = total_rows + jnp.dot(grad_key_low, full_key.T, preferred_element_type=f32)
        total_rows = total_rows + jnp.dot(grad_value_low, full_value.T, preferred_element_type=f32)
        grad_normed = lax.psum_scatter(
            total_rows.astype(low), "tensor", scatter_dimension=0, tiled=True
        ).astype(f32)
        unused_in, attn_back = jax.vjp(norm_apply, resid_in, attn_scale)
        grad_in_norm, grad_attn_part = attn_back(grad_normed)

        def gain_column(part):
            cut = part.astype(low).reshape(data_count, gain_rows, 1)
            return jnp.pad(cut, ((0, 0), (0, shard - gain_rows), (0, 0))).reshape(-1, 1)

        side_grads = side_columns(
            [
                grad_router_part.astype(low),
                grad_attn_part.astype(low)[:, None],
                grad_ffn_part.astype(low)[:, None],
                gain_column(grad_query_gain_part),
                gain_column(grad_key_gain_part),
            ],
            model_width,
        )
        packed_grads = jnp.concatenate(
            [part.astype(low) for part in weight_grads] + [grad_output_t.astype(low), side_grads],
            axis=1,
        )
        reduced = lax.psum_scatter(packed_grads, "dp", scatter_dimension=0, tiled=True).astype(f32)
        side_total, stat_totals = lax.psum(
            (reduced[:, 4 * heads_width : 4 * heads_width + EXPERTS + 4], stat_terms), "tensor"
        )
        grads_qkv = [reduced[:, i * heads_width : (i + 1) * heads_width] for i in range(3)]
        grad_out_w = reduced[:, 3 * heads_width : 4 * heads_width].T
        grad_attn_gain = side_total[:, EXPERTS]
        grad_ffn_gain = side_total[:, EXPERTS + 1]
        grad_query_gain = side_total[:gain_rows, EXPERTS + 2]
        grad_key_gain = side_total[:gain_rows, EXPERTS + 3]
        grad_router = side_total[:, :EXPERTS]
    grad_tokens = grad_mid + grad_in_norm
    rms_stats = jnp.sqrt(stat_totals / (group_rows_count * model_width))[None, :]
    return (
        layer_out,
        grad_tokens,
        grad_attn_gain,
        *grads_qkv,
        grad_out_w,
        grad_query_gain,
        grad_key_gain,
        grad_ffn_gain,
        grad_router,
        grad_gate_w,
        grad_up_w,
        grad_down,
        rms_stats,
    )


def solution(mesh):
    in_specs = (
        P(("dp", "tensor"), None),
        P(("dp", "tensor"), None),
        P("dp", None),
        P("dp", None),
        P(("dp", "tensor"), None),
        P("dp"),
        P("dp", "tensor"),
        P("dp", "tensor"),
        P("dp", "tensor"),
        P("tensor", "dp"),
        P("dp"),
        P("dp"),
        P("dp"),
        P("dp", None),
        P("dp", None, "tensor"),
        P("dp", None, "tensor"),
        P("dp", "tensor", None),
    )
    out_specs = (
        P(("dp", "tensor"), None),
        P(("dp", "tensor"), None),
        P("dp"),
        P("dp", "tensor"),
        P("dp", "tensor"),
        P("dp", "tensor"),
        P("tensor", "dp"),
        P("dp"),
        P("dp"),
        P("dp"),
        P("dp", None),
        P("dp", None, "tensor"),
        P("dp", None, "tensor"),
        P("dp", "tensor", None),
        P("dp", None),
    )
    return jax.shard_map(body, mesh=mesh, in_specs=in_specs, out_specs=out_specs, check_vma=False)
```
